32 devices in a mesh: dp: 16 (over z, y, x), mlp: 2 (over core).
Axes of the slice: x: 2, y: 2, z: 4, core: 2. Of those that a mesh axis runs over, the one named last changes fastest.
Arguments:
- tokens: bfloat16 [65536, 384], P('dp'), may hold values from -6 to 6
- cotangent: bfloat16 [65536, 384], P('dp')
- image_bucket: int32 [256], P('dp'), may hold values from 0 to 3
- bucket_width: int32 [4], replicated, may hold values from 384 to 1536, as said below
- bucket_heads: int32 [4], replicated, may hold values from 3 to 6, as said below
- w_qkv: float32 [3, 384, 384], P(None, 'mlp', 'dp'), may hold values from -0.3125 to 0.3125
- w_out: float32 [384, 384], P('mlp', 'dp'), may hold values from -1.75 to 1.75
- w_fc1: float32 [1536, 384], P('mlp', 'dp'), may hold values from -0.3125 to 0.3125
- w_fc2: float32 [1536, 384], P('mlp', 'dp'), may hold values from -0.3125 to 0.3125
- vectors: float32 [6, 384], P(None, 'dp')
- mom_qkv: float32 [3, 384, 384], P(None, 'mlp', 'dp'), may hold values from -1536 to 1536
- mom_out: float32 [384, 384], P('mlp', 'dp'), may hold values from -448 to 448
- mom_fc1: float32 [1536, 384], P('mlp', 'dp'), may hold values from -1536 to 1536
- mom_fc2: float32 [1536, 384], P('mlp', 'dp'), may hold values from -896 to 896
- vec_first: float32 [6, 384], P(None, 'dp'), may hold values from -160 to 160
- vec_second: float32 [6, 384], P(None, 'dp'), may hold values from 3276.8 to 13107.2
Outputs:
- output: float32 [65536, 384], P('dp')
- grad_tokens: float32 [65536, 384], P('dp')
- grad_w_qkv: float32 [3, 384, 384], P(None, 'mlp', 'dp')
- grad_w_out: float32 [384, 384], P('mlp', 'dp')
- grad_w_fc1: float32 [1536, 384], P('mlp', 'dp')
- grad_w_fc2: float32 [1536, 384], P('mlp', 'dp')
- grad_vectors: float32 [6, 384], P(None, 'dp')
- mom_qkv_new: float32 [3, 384, 384], P(None, 'mlp', 'dp')
- mom_out_new: float32 [384, 384], P('mlp', 'dp')
- mom_fc1_new: float32 [1536, 384], P('mlp', 'dp')
- mom_fc2_new: float32 [1536, 384], P('mlp', 'dp')
- w_qkv_new: float32 [3, 384, 384], P(None, 'mlp', 'dp')
- w_out_new: float32 [384, 384], P('mlp', 'dp')
- w_fc1_new: float32 [1536, 384], P('mlp', 'dp')
- w_fc2_new: float32 [1536, 384], P('mlp', 'dp')
- vectors_new: float32 [6, 384], P(None, 'dp')
- vec_first_new: float32 [6, 384], P(None, 'dp')
- vec_second_new: float32 [6, 384], P(None, 'dp')
- grad_norms: float32 [5], replicated
The draws below stay inside these ranges and needn't reach their ends.
Inputs may be any that keep to these rules, and one draw needn't show every extreme that they name: `bucket_width`: multiples of 192; some bucket uses all 1536 and some 1536 / 4. `bucket_heads`: some bucket uses all 6 and some 6 / 2.
All inputs are finite; a program needn't handle non-finite values.
Results may differ from the reference program's by a relative error of at most 0.017.
Values may be sent and summed in bfloat16 or wider, within the bound.
A program may use at most 192 MiB of HBM per device.

```python
import math
import jax
import jax.numpy as jnp
from jax import lax

D = 384
HEADS = 6
HD = 64
MLP = 1536
IMG_LEN = 256
IMG_DEV = 16
NB = 4
NS_ITERS = 5
STEP = 10
IMAGES = 256
TOKENS = 65536
N_DP = 16


def draw_cotangent(key, part):
    ramp = 0.6 + 1.2 * jnp.arange(D, dtype=jnp.float32) / D
    values = jax.random.normal(key, (TOKENS, D), jnp.float32) * ramp[None, :]
    return values.astype(jnp.bfloat16)


def draw_vectors(key, part):
    gain_key = jax.random.fold_in(key, 11)
    bias_key = jax.random.fold_in(key, 13)
    ramp = 0.6 + 1.2 * jnp.arange(D, dtype=jnp.float32) / D
    gains = ramp[None, :] * jax.random.uniform(gain_key, (6, D), jnp.float32, 0.8, 1.2)
    biases = 0.3 * jax.random.normal(bias_key, (6, D), jnp.float32)
    row_ids = jnp.arange(6)
    is_gain = (row_ids == 0) | (row_ids == 2)
    return jnp.where(is_gain[:, None], gains, biases)


def draw_bucket_width(key, part):
    pick_key = jax.random.fold_in(key, 17)
    order_key = jax.random.fold_in(key, 19)
    eighths = jax.random.randint(pick_key, (NB,), 2, 9)
    order = jax.random.permutation(order_key, NB)
    eighths = eighths.at[order[0]].set(8).at[order[1]].set(2)
    return (eighths * (MLP // 8)).astype(jnp.int32)


def draw_bucket_heads(key, part):
    pick_key = jax.random.fold_in(key, 23)
    order_key = jax.random.fold_in(key, 29)
    counts = jax.random.randint(pick_key, (NB,), HEADS // 2, HEADS + 1)
    order = jax.random.permutation(order_key, NB)
    counts = counts.at[order[0]].set(HEADS).at[order[1]].set(HEADS // 2)
    return counts.astype(jnp.int32)


def with_ends(entries, own_key, smallest, top_value):
    longest = entries.shape.index(max(entries.shape))
    spots = []
    for shift in (0, 1):
        where = [jax.random.randint(jax.random.fold_in(own_key, axis), (), 0, length) for axis, length in enumerate(entries.shape)]
        where[longest] = (where[longest] + shift) % entries.shape[longest]
        spots.append(tuple(where))
    return entries.at[spots[0]].set(smallest).at[spots[1]].set(top_value)


def block_levels(key, extent, cuts, least, largest):
    gain = 1.0
    for dim, blocks in cuts:
        heights = jax.random.uniform(jax.random.fold_in(jax.random.fold_in(key, 6), dim), (blocks,), jnp.float32, least / len(cuts), largest / len(cuts))
        gain = gain * jnp.repeat(jnp.exp(heights), extent[dim] // blocks).reshape((-1,) + (1,) * (len(extent) - 1 - dim))
    return gain


def bell_draw(key, extent, width, most, shards=(), kind=jnp.bfloat16):
    loudness = block_levels(key, extent, shards, -0.22, 0.18) if shards else 1.0
    array = jax.random.normal(key, extent, jnp.float32) * width * loudness
    return jnp.minimum(jnp.maximum(array, -most), most).astype(kind)


def setup_inputs(seed: int = 0) -> dict:
    arg_keys = jax.random.split(jax.random.key(seed), 17)
    tokens = bell_draw(arg_keys[0], (TOKENS, D), 1.0, 6.0, ((0, 16),))
    cotangent = draw_cotangent(jax.random.fold_in(arg_keys[16], 71), 0)
    image_bucket = with_ends(jax.random.randint(arg_keys[2], (IMAGES,), 0, NB), jax.random.fold_in(arg_keys[2], 1), 0, NB - 1).astype(jnp.int32)
    bucket_width = draw_bucket_width(jax.random.fold_in(arg_keys[16], 71), 0)
    bucket_heads = draw_bucket_heads(jax.random.fold_in(arg_keys[16], 71), 0)
    w_qkv = bell_draw(arg_keys[5], (3, D, D), D ** -0.5, 0.3125, ((1, 2), (2, 16)), jnp.float32)
    w_out = bell_draw(arg_keys[6], (D, D), (D // 32) ** -0.5, 1.75, ((0, 2), (1, 16)), jnp.float32)
    w_fc1 = bell_draw(arg_keys[7], (MLP, D), D ** -0.5, 0.3125, ((0, 2), (1, 16)), jnp.float32)
    w_fc2 = bell_draw(arg_keys[8], (MLP, D), (MLP // 4) ** -0.5, 0.3125, ((0, 2), (1, 16)), jnp.float32)
    vectors = draw_vectors(jax.random.fold_in(arg_keys[16], 71), 0)
    mom_qkv = bell_draw(arg_keys[10], (3, D, D), (TOKENS ** 0.5), 1536.0, ((1, 2), (2, 16)), jnp.float32)
    mom_out = bell_draw(arg_keys[11], (D, D), (0.3 * TOKENS ** 0.5), 448.0, ((0, 2), (1, 16)), jnp.float32)
    mom_fc1 = bell_draw(arg_keys[12], (MLP, D), (TOKENS ** 0.5), 1536.0, ((0, 2), (1, 16)), jnp.float32)
    mom_fc2 = bell_draw(arg_keys[13], (MLP, D), (0.6 * TOKENS ** 0.5), 896.0, ((0, 2), (1, 16)), jnp.float32)
    vec_first = bell_draw(arg_keys[14], (6, D), (0.11 * TOKENS ** 0.5), 160.0, ((1, 16),), jnp.float32)
    vec_second = jnp.clip(jnp.exp(math.log(13107.2) - 1.3862944 * jax.random.uniform(arg_keys[15], (6, D), jnp.float32) ** block_levels(arg_keys[15], (6, D), ((1, 16),), -0.2, 0.2)), 3276.8, 13107.2)
    return dict(tokens=tokens, cotangent=cotangent, image_bucket=image_bucket, bucket_width=bucket_width, bucket_heads=bucket_heads, w_qkv=w_qkv, w_out=w_out, w_fc1=w_fc1, w_fc2=w_fc2, vectors=vectors, mom_qkv=mom_qkv, mom_out=mom_out, mom_fc1=mom_fc1, mom_fc2=mom_fc2, vec_first=vec_first, vec_second=vec_second)


@jax.custom_vjp
def low(v):
    return lax.optimization_barrier(v.astype(jnp.bfloat16)).astype(jnp.float32)

@jax.custom_vjp
def low_back(v):
    return v

def low_keep(v):
    return (low(v), None)

def low_pass(kept, grad):
    return (grad,)

def back_keep(v):
    return (v, None)

def back_low(kept, grad):
    return (low(grad),)
low.defvjp(low_keep, low_pass)
low_back.defvjp(back_keep, back_low)
EPSILON = 1e-06
PRECISE = lax.Precision.HIGHEST

def layer_norm(values):
    center = values - lax.optimization_barrier(jnp.mean(values, axis=-1, keepdims=True))
    return center * lax.rsqrt(lax.optimization_barrier(jnp.mean(center * center, axis=-1, keepdims=True)) + EPSILON)

def block_rows(rows_in, query_weight, out_weight, fc_one, fc_two, params, width_img, heads_img):
    count = rows_in.shape[0]
    images = count // IMG_LEN
    width_tok = jnp.repeat(width_img, IMG_LEN)
    heads_tok = jnp.repeat(heads_img, IMG_LEN)
    unit_mask = (jnp.arange(MLP, dtype=jnp.int32)[None, :] < width_tok[:, None]).astype(jnp.float32)
    head_ids = jnp.arange(D, dtype=jnp.int32) // HD
    head_mask = (head_ids[None, :] < heads_tok[:, None]).astype(jnp.float32)
    hidden_one = low(layer_norm(rows_in) * params[0] + params[1])
    proj = low(low_back(jnp.einsum('td,cjd->ctj', hidden_one, query_weight, precision=PRECISE)))
    shaped = proj.reshape(3, images, IMG_LEN, HEADS, HD)
    scores = low_back(jnp.einsum('iqhe,ikhe->ihqk', shaped[0], shaped[1], precision=PRECISE) * 0.125)
    probs = jax.nn.softmax(scores, axis=-1)
    attended = jnp.einsum('ihqk,ikhe->iqhe', low(probs), shaped[2], precision=PRECISE).reshape(count, D)
    mixed = low(low_back(attended * head_mask))
    resid = rows_in + low_back(jnp.dot(mixed, out_weight, precision=PRECISE)) + params[4]
    hidden_two = low(layer_norm(resid) * params[2] + params[3])
    pre_act = low_back(jnp.dot(hidden_two, fc_one.T, precision=PRECISE))
    act = low(jax.nn.gelu(pre_act, approximate=False) * unit_mask)
    return resid + jnp.dot(act, fc_two, precision=PRECISE) + params[5]

def reference(tokens, cotangent, image_bucket, bucket_width, bucket_heads, w_qkv, w_out, w_fc1, w_fc2, vectors, mom_qkv, mom_out, mom_fc1, mom_fc2, vec_first, vec_second):
    width_img = bucket_width[image_bucket].astype(jnp.int32).reshape(N_DP, IMG_DEV)
    heads_img = bucket_heads[image_bucket].astype(jnp.int32).reshape(N_DP, IMG_DEV)

    def forward(rows_all, weight_qkv, weight_out, weight_one, weight_two, params):
        query_weight = low(weight_qkv)
        out_weight = low(weight_out)
        fc_one = low(weight_one)
        fc_two = low(weight_two)
        params_low = low(params)

        def group_fn(pieces):
            return block_rows(pieces[0], query_weight, out_weight, fc_one, fc_two, params_low, pieces[1], pieces[2])
        groups = rows_all.reshape(N_DP, IMG_DEV * IMG_LEN, D)
        result = lax.map(jax.checkpoint(group_fn), (groups, width_img, heads_img))
        return result.reshape(TOKENS, D)
    output, pullback = jax.vjp(forward, tokens.astype(jnp.float32), w_qkv, w_out, w_fc1, w_fc2, vectors)
    grad_tokens, grad_qkv, grad_out, grad_fc1, grad_fc2, grad_vec = pullback(cotangent.astype(jnp.float32))
    grads = (grad_qkv, grad_out, grad_fc1, grad_fc2)
    olds = (mom_qkv, mom_out, mom_fc1, mom_fc2)
    weights = (w_qkv, w_out, w_fc1, w_fc2)
    rates = (math.sqrt(3.0), math.sqrt(32.0), math.sqrt(MLP / D), 2.0)
    moments = tuple((0.95 * old_m + gradient for old_m, gradient in zip(olds, grads)))
    news = []
    for weight, moment, rate in zip(weights, moments, rates):
        start = moment.reshape(-1, D)
        current = start / (jnp.sqrt(jnp.sum(start * start)) + 1e-07)
        for sweep in range(NS_ITERS):
            gram_sum = jnp.dot(current.T, current, precision=PRECISE)
            polynomial = -4.775 * gram_sum + 2.0315 * jnp.dot(gram_sum, gram_sum, precision=PRECISE)
            current = 3.4445 * current + jnp.dot(current, polynomial, precision=PRECISE)
        news.append(0.999 * weight - rate * current.reshape(weight.shape))
    norms = jnp.sqrt(jnp.stack([jnp.sum(gradient * gradient) for gradient in grads + (grad_vec,)]))
    first = 0.9 * vec_first + 0.1 * grad_vec
    second = 0.95 * vec_second + 0.05 * grad_vec * grad_vec
    vectors_new = vectors - 0.5 * (first / (1.0 - 0.9 ** STEP)) / (jnp.sqrt(second / (1.0 - 0.95 ** STEP)) + 1e-08)
    return (output, grad_tokens, grad_qkv, grad_out, grad_fc1, grad_fc2, grad_vec, moments[0], moments[1], moments[2], moments[3], news[0], news[1], news[2], news[3], vectors_new, first, second, norms)
```

```python
import functools
import math

import jax
import jax.numpy as jnp
from jax import lax
from jax.experimental import pallas as pl
from jax.experimental.pallas import tpu as pltpu
from jax.sharding import PartitionSpec as P

HD = 64
NS_ITERS = 5
STEP = 10
EPSILON = 1e-06
F32 = jnp.float32
BF16 = jnp.bfloat16
NN = (((1,), (0,)), ((), ()))
NT = (((1,), (1,)), ((), ()))
TN = (((0,), (0,)), ((), ()))

FC1, FC2, QKV, OUT, VEC, PACK = 0, 768, 1536, 2304, 2560, 2688
SLOT = 256
CHUNK = 256


def mm(a, b, dims):
    return lax.dot_general(a, b, dims, preferred_element_type=F32)


def lane_sum(v):
    return jnp.sum(v, axis=-1, keepdims=True)


def norm_rows(v):
    inv = 1.0 / v.shape[-1]
    center = v - lane_sum(v) * inv
    factor = lax.rsqrt(lane_sum(center * center) * inv + EPSILON)
    return center * factor, factor


def norm_back(g, n, factor):
    inv = 1.0 / g.shape[-1]
    return factor * (g - lane_sum(g) * inv - n * (lane_sum(g * n) * inv))


def image_kernel(
    half_ref, bucket_ref, widths_ref, counts_ref,
    tok_ref, cot_ref, w_ref,
    out_ref, gtok_ref, grad_ref,
    acc_ref, vec_ref, gvec_ref, q_ref, k_ref, v_ref, mixed_ref, probs_ref, low_ref,
    att_ref, dq_ref, dk_ref, dv_ref, y_ref, gh_ref,
):
    step = pl.program_id(0)
    rows, model = tok_ref.shape
    heads_half = 3
    bucket = bucket_ref[half_ref[0] * pl.num_programs(0) + step]
    width = widths_ref[bucket]
    count = counts_ref[bucket]

    @pl.when(step == 0)
    def _():
        acc_ref[...] = jnp.zeros_like(acc_ref)
        gvec_ref[...] = jnp.zeros_like(gvec_ref)
        turned = w_ref[0, :, VEC:PACK].astype(F32).T
        vec_ref[...] = turned[0:8]

    def head_lanes(s, values):
        lanes = lax.broadcasted_iota(jnp.int32, values.shape, 1)
        return jnp.where((lanes >= s * HD) & (lanes < (s + 1) * HD), values, jnp.zeros_like(values))

    x = tok_ref[...].astype(F32)
    normed_one, factor_one = norm_rows(x)
    hidden_one = (normed_one * vec_ref[0:1] + vec_ref[1:2]).astype(BF16)
    for half in range(2):
        for ref, which in ((q_ref, 0), (k_ref, 1), (v_ref, 2)):
            lanes = slice(QKV + which * SLOT, QKV + (which + 1) * SLOT)
            ref[half] = mm(hidden_one, w_ref[half, :, lanes], NN).astype(BF16)
        att_ref[...] = jnp.zeros_like(att_ref)
        for s in range(heads_half):
            head = half * heads_half + s

            @pl.when(count > head)
            def _():
                scores = mm(head_lanes(s, q_ref[half]), k_ref[half], NT) * 0.125
                top = jnp.max(scores, axis=-1, keepdims=True)
                grown = jnp.exp(scores - top)
                probs = grown * (1.0 / lane_sum(grown))
                low = probs.astype(BF16)
                probs_ref[head] = probs
                low_ref[head] = low
                att_ref[...] += mm(low, head_lanes(s, v_ref[half]), NN)

        mixed_ref[half] = att_ref[...].astype(BF16)
    branch = mm(mixed_ref[0], w_ref[0, :, OUT:VEC], NT) + mm(mixed_ref[1], w_ref[1, :, OUT:VEC], NT)
    resid = x + branch + vec_ref[4:5]
    normed_two, factor_two = norm_rows(resid)
    hidden_two = (normed_two * vec_ref[2:3] + vec_ref[3:4]).astype(BF16)
    cot = cot_ref[...]
    hidden_two_t = hidden_two.T
    cot_t = cot.T
    y_ref[...] = resid + vec_ref[5:6]
    gh_ref[...] = jnp.zeros_like(gh_ref)
    per_half = FC2 // CHUNK
    for chunk in range(2 * per_half):
        half, part = divmod(chunk, per_half)
        one = slice(FC1 + part * CHUNK, FC1 + (part + 1) * CHUNK)
        two = slice(FC2 + part * CHUNK, FC2 + (part + 1) * CHUNK)

        @pl.when(width > chunk * CHUNK)
        def _():
            pre = mm(hidden_two, w_ref[half, :, one], NN)
            units = chunk * CHUNK + lax.broadcasted_iota(jnp.int32, pre.shape, 1)
            cumulative = 0.5 + 0.5 * lax.erf(pre * 0.7071067811865476)
            density = jnp.exp(-0.5 * pre * pre) * 0.3989422804014327
            cumulative = jnp.where(units < width, cumulative, 0.0)
            density = jnp.where(units < width, density, 0.0)
            act = (pre * cumulative).astype(BF16)
            grad_act = mm(cot, w_ref[half, :, two], NN)
            grad_pre = (grad_act * (cumulative + pre * density)).astype(BF16)
            y_ref[...] += mm(act, w_ref[half, :, two], NT)
            gh_ref[...] += mm(grad_pre, w_ref[half, :, one], NT)
            acc_ref[half, :, two] += mm(cot_t, act, NN)
            acc_ref[half, :, one] += mm(hidden_two_t, grad_pre, NN)

    out_ref[...] = y_ref[...]
    grad_hidden_two = gh_ref[...]
    cot_f = cot.astype(F32)
    grad_resid = cot_f + norm_back(grad_hidden_two * vec_ref[2:3], normed_two, factor_two)
    resid_low = grad_resid.astype(BF16)
    resid_low_t = resid_low.T
    hidden_one_t = hidden_one.T
    grad_hidden_one = None
    for half in range(2):
        acc_ref[half, :, OUT:VEC] += mm(resid_low_t, mixed_ref[half], NN)
        grad_heads = mm(resid_low, w_ref[half, :, OUT:VEC], NN).astype(BF16)
        dq_ref[...] = jnp.zeros_like(dq_ref)
        dk_ref[...] = jnp.zeros_like(dk_ref)
        dv_ref[...] = jnp.zeros_like(dv_ref)
        for s in range(heads_half):
            head = half * heads_half + s

            @pl.when(count > head)
            def _():
                own = head_lanes(s, grad_heads)
                grad_probs = mm(own, v_ref[half], NT)
                probs = probs_ref[head]
                weighed = probs * grad_probs
                grad_scores = (weighed - probs * lane_sum(weighed)).astype(BF16)
                dq_ref[...] += mm(grad_scores, head_lanes(s, k_ref[half]), NN)
                dk_ref[...] += mm(grad_scores, head_lanes(s, q_ref[half]), TN)
                dv_ref[...] += mm(low_ref[head], own, TN)

        for which, ref, scale in ((0, dq_ref, 0.125), (1, dk_ref, 0.125), (2, dv_ref, 1.0)):
            lanes = slice(QKV + which * SLOT, QKV + (which + 1) * SLOT)
            grad_proj = (ref[...] * scale).astype(BF16)
            acc_ref[half, :, lanes] += mm(hidden_one_t, grad_proj, NN)
            term = mm(grad_proj, w_ref[half, :, lanes], NT)
            grad_hidden_one = term if grad_hidden_one is None else grad_hidden_one + term
    gtok_ref[...] = grad_resid + norm_back(grad_hidden_one * vec_ref[0:1], normed_one, factor_one)
    sums = (
        grad_hidden_one * normed_one,
        grad_hidden_one,
        grad_hidden_two * normed_two,
        grad_hidden_two,
        grad_resid,
        cot_f,
    )
    for row, values in enumerate(sums):
        gvec_ref[row : row + 1] += jnp.sum(values, axis=0, keepdims=True)

    @pl.when(step == pl.num_programs(0) - 1)
    def _():
        grad_ref[0, :, 0:VEC] = acc_ref[0].astype(BF16)
        grad_ref[1, :, 0:VEC] = acc_ref[1].astype(BF16)
        columns = gvec_ref[...].T.astype(BF16)
        grad_ref[0, :, VEC:PACK] = columns
        grad_ref[1, :, VEC:PACK] = columns


def image_pass(half, bucket, widths, counts, tokens, cotangent, packed):
    images = bucket.shape[0] // 2
    model = tokens.shape[1]
    seq = tokens.shape[0] // bucket.shape[0]
    rows = images * seq
    picked = pl.BlockSpec((seq, model), lambda i, h, b, w, c: (h[0] * images + i, 0))
    placed = pl.BlockSpec((seq, model), lambda i, h, b, w, c: (i, 0))
    whole = pl.BlockSpec(
        (2, model, PACK), lambda i, h, b, w, c: (0, 0, 0), pipeline_mode=pl.Buffered(1)
    )
    heads = 6
    flops = 2 * rows * model * (3 * 4 * model + 3 * 8 * model)
    return pl.pallas_call(
        image_kernel,
        out_shape=(
            jax.ShapeDtypeStruct((rows, model), F32),
            jax.ShapeDtypeStruct((rows, model), F32),
            jax.ShapeDtypeStruct((2, model, PACK), BF16),
        ),
        grid_spec=pltpu.PrefetchScalarGridSpec(
            num_scalar_prefetch=4,
            grid=(images,),
            in_specs=[picked, picked, whole],
            out_specs=[placed, placed, whole],
            scratch_shapes=[
                pltpu.VMEM((2, model, VEC), F32),
                pltpu.VMEM((8, model), F32),
                pltpu.VMEM((128, model), F32),
                pltpu.VMEM((2, seq, SLOT), BF16),
                pltpu.VMEM((2, seq, SLOT), BF16),
                pltpu.VMEM((2, seq, SLOT), BF16),
                pltpu.VMEM((2, seq, SLOT), BF16),
                pltpu.VMEM((heads, seq, seq), F32),
                pltpu.VMEM((heads, seq, seq), BF16),
                pltpu.VMEM((seq, SLOT), F32),
                pltpu.VMEM((seq, SLOT), F32),
                pltpu.VMEM((seq, SLOT), F32),
                pltpu.VMEM((seq, SLOT), F32),
                pltpu.VMEM((seq, model), F32),
                pltpu.VMEM((seq, model), F32),
            ],
        ),
        compiler_params=pltpu.CompilerParams(vmem_limit_bytes=56 * 1024 * 1024),
        cost_estimate=pl.CostEstimate(flops=flops, bytes_accessed=20 * rows * model, transcendentals=rows * 6144),
        name="image_pass",
    )(half, bucket, widths, counts, tokens, cotangent, packed)


MESH = pl.DeviceIdType.MESH
CUT = 1408


class Place:
    def __init__(self):
        dp = lax.axis_index("dp")
        self.half = lax.axis_index("mlp")
        self.z = dp // 4
        self.y = (dp // 2) % 2
        self.x = dp % 2
        self.dp = dp

    def index(self, z, y, x):
        return z * 4 + y * 2 + x

    def at_z(self, z):
        return (self.index(z, self.y, self.x), self.half)

    @property
    def y_peer(self):
        return (self.index(self.z, 1 - self.y, self.x), self.half)

    @property
    def x_peer(self):
        return (self.index(self.z, self.y, 1 - self.x), self.half)

    @property
    def sibling(self):
        return (self.dp, 1 - self.half)


def meet(place):
    barrier = pltpu.get_barrier_semaphore()
    peers = [place.at_z((place.z + j) % 4) for j in range(1, 4)]
    peers += [place.y_peer, place.x_peer, place.sibling]
    for peer in peers:
        pl.semaphore_signal(barrier, inc=1, device_id=peer, device_id_type=MESH)
    pl.semaphore_wait(barrier, len(peers))


class Sender:
    def __init__(self, send_sem, recv_sem):
        self.send_sem, self.recv_sem = send_sem, recv_sem
        self.copies = {}

    def start(self, slot, src, dst, peer):
        copy = pltpu.make_async_remote_copy(
            src_ref=src,
            dst_ref=dst,
            send_sem=self.send_sem.at[slot],
            recv_sem=self.recv_sem.at[slot],
            device_id=peer,
            device_id_type=MESH,
        )
        copy.start()
        self.copies[slot] = copy

    def arrived(self, slot):
        self.copies[slot].wait_recv()

    def drain(self):
        for copy in self.copies.values():
            copy.wait_send()


GATHER_SLOTS = 35


def gather_flow(place, sender, own, buf, base=0):
    half = place.half
    other_y, other_x = 1 - place.y, 1 - place.x

    def shard(z, y, x):
        return place.index(z, y, x)

    def send(slot, src, dp, peer, lanes=None):
        dst = buf.at[half, dp] if lanes is None else buf.at[half, dp, :, lanes]
        sender.start(base + slot, src, dst, peer)

    def forward(slot, dp, peer, lanes=None):
        src = buf.at[half, dp] if lanes is None else buf.at[half, dp, :, lanes]
        send(slot, src, dp, peer, lanes)

    cut_a, cut_b = pl.ds(0, CUT), pl.ds(CUT, PACK - CUT)
    me = place.dp
    for j in range(1, 4):
        send(j - 1, own, me, place.at_z((place.z + j) % 4))
    send(3, own, me, place.y_peer)
    send(7, own, me, place.x_peer)
    send(19, own, me, place.sibling)
    for k in range(1, 5):
        if k < 4:
            sender.arrived(base + k - 1)
            dp = shard((place.z + 4 - k) % 4, place.y, place.x)
            forward(3 + k, dp, place.y_peer)
            forward(7 + k, dp, place.x_peer)
            forward(19 + k, dp, place.sibling)
        z = (place.z + 5 - k) % 4
        sender.arrived(base + 3 + k - 1)
        dp = shard(z, other_y, place.x)
        forward(11 + k - 1, dp, place.x_peer, cut_a)
        forward(23 + k - 1, dp, place.sibling)
        sender.arrived(base + 7 + k - 1)
        dp = shard(z, place.y, other_x)
        forward(15 + k - 1, dp, place.y_peer, cut_b)
        forward(27 + k - 1, dp, place.sibling)
    for k in range(4):
        sender.arrived(base + 11 + k)
        sender.arrived(base + 15 + k)
        forward(31 + k, shard((place.z + 4 - k) % 4, other_y, other_x), place.sibling)
    for k in range(16):
        sender.arrived(base + 19 + k)


def weights_kernel(fc1_ref, fc2_ref, qkv_ref, out_ref, vec_ref, buf_ref, own_ref, send_sem, recv_sem, local_sem):
    place = Place()
    own_ref[...] = jnp.zeros_like(own_ref)
    own_ref[:, FC1:FC2] = fc1_ref[...].astype(BF16)
    own_ref[:, FC2:QKV] = fc2_ref[...].astype(BF16)
    for which in range(3):
        start = QKV + which * SLOT
        own_ref[:, start : start + qkv_ref.shape[2]] = qkv_ref[which].astype(BF16)
    own_ref[:, OUT : OUT + out_ref.shape[1]] = out_ref[...].astype(BF16)
    own_ref[:, VEC:PACK] = vec_ref[...].astype(BF16)
    local = pltpu.make_async_copy(own_ref, buf_ref.at[place.half, place.dp], local_sem)
    local.start()
    meet(place)
    sender = Sender(send_sem, recv_sem)
    gather_flow(place, sender, own_ref, buf_ref)
    sender.drain()
    local.wait()


def gather_weights(parts, ranks):
    rows = parts[0].shape[0]
    vmem = pl.BlockSpec(memory_space=pltpu.VMEM)
    return pl.pallas_call(
        weights_kernel,
        out_shape=jax.ShapeDtypeStruct((2, ranks, rows, PACK), BF16),
        in_specs=[vmem] * 5,
        out_specs=pl.BlockSpec(memory_space=pl.ANY),
        scratch_shapes=[
            pltpu.VMEM((rows, PACK), BF16),
            pltpu.SemaphoreType.DMA((GATHER_SLOTS,)),
            pltpu.SemaphoreType.DMA((GATHER_SLOTS,)),
            pltpu.SemaphoreType.DMA,
        ],
        compiler_params=pltpu.CompilerParams(collective_id=0, has_side_effects=True),
        name="gather_weights",
    )(*parts)


SCATTER_SLOTS = 43
Z_ORDER = (2, 1, 3, 0)


def scatter_flow(place, sender, parts, hold, first_a, first_b, second_a, second_b, last):
    half, z, y, x = place.half, place.z, place.y, place.x
    other_y, other_x = 1 - y, 1 - x
    cut_a, cut_b = pl.ds(0, CUT), pl.ds(CUT, PACK - CUT)
    columns = ((other_y, other_x), (y, other_x), (other_y, x), (y, x))

    def shard(k, column):
        return place.index((z + Z_ORDER[k]) % 4, *column)

    for c, column in enumerate(columns):
        for k in range(4):
            dp = shard(k, column)
            sender.start(4 * c + k, parts.at[1 - half, dp], hold.at[dp], place.sibling)

    def settle(c, k):
        dp = shard(k, columns[c])
        sender.arrived(4 * c + k)
        hold[dp] = (hold[dp].astype(F32) + parts[half, dp].astype(F32)).astype(BF16)
        return dp

    def add(dp, lanes, arrived):
        hold[dp, :, lanes] = (hold[dp, :, lanes].astype(F32) + arrived.astype(F32)).astype(BF16)

    for k in range(4):
        dp = settle(0, k)
        sender.start(16 + k, hold.at[dp, :, cut_a], first_a.at[k], place.x_peer)
        sender.start(24 + k, hold.at[dp, :, cut_b], first_b.at[k], place.y_peer)
    for k in range(4):
        dp = settle(1, k)
        sender.start(20 + k, hold.at[dp, :, cut_a], first_a.at[4 + k], place.x_peer)
        dp = settle(2, k)
        sender.start(28 + k, hold.at[dp, :, cut_b], first_b.at[4 + k], place.y_peer)
    for k in range(4):
        settle(3, k)
    for k in range(4):
        sender.arrived(16 + k)
        dp = shard(k, columns[2])
        add(dp, cut_a, first_a[k])
        sender.start(32 + k, hold.at[dp, :, cut_a], second_a.at[k], place.y_peer)
        sender.arrived(24 + k)
        dp = shard(k, columns[1])
        add(dp, cut_b, first_b[k])
        sender.start(36 + k, hold.at[dp, :, cut_b], second_b.at[k], place.x_peer)
    total = None
    for k in range(4):
        dp = shard(k, columns[3])
        sender.arrived(20 + k)
        sender.arrived(32 + k)
        own_a = hold[dp, :, cut_a].astype(F32) + first_a[4 + k].astype(F32) + second_a[k].astype(F32)
        sender.arrived(28 + k)
        sender.arrived(36 + k)
        own_b = hold[dp, :, cut_b].astype(F32) + first_b[4 + k].astype(F32) + second_b[k].astype(F32)
        if Z_ORDER[k]:
            hold[dp, :, cut_a] = own_a.astype(BF16)
            hold[dp, :, cut_b] = own_b.astype(BF16)
            j = Z_ORDER[k]
            sender.start(40 + j - 1, hold.at[dp], last.at[j - 1], place.at_z((z + j) % 4))
        else:
            total = (own_a, own_b)
    for j in range(3):
        sender.arrived(40 + j)
    total_a, total_b = total
    for j in range(3):
        total_a = total_a + last[j, :, cut_a].astype(F32)
        total_b = total_b + last[j, :, cut_b].astype(F32)
    return total_a, total_b


def moments_kernel(
    parts, fc1_ref, fc2_ref, qkv_ref, wo_ref, out_half, gtok_half,
    grad_ref, mom_ref, buf_ref, out_other, gtok_other,
    hold, first_a, first_b, second_a, second_b, last, own_ref,
    send_sem, recv_sem, local_sem,
):
    place = Place()
    mom_ref[...] = jnp.zeros_like(mom_ref)
    mom_ref[:, FC1:FC2] = 0.95 * fc1_ref[...]
    mom_ref[:, FC2:QKV] = 0.95 * fc2_ref[...]
    for which in range(3):
        start = QKV + which * SLOT
        mom_ref[:, start : start + qkv_ref.shape[2]] = 0.95 * qkv_ref[which]
    mom_ref[:, OUT : OUT + wo_ref.shape[1]] = 0.95 * wo_ref[...]
    meet(place)
    sender = Sender(send_sem, recv_sem)
    total_a, total_b = scatter_flow(
        place, sender, parts, hold, first_a, first_b, second_a, second_b, last
    )
    base = SCATTER_SLOTS + GATHER_SLOTS
    sender.start(base, out_half, out_other, place.sibling)
    sender.start(base + 1, gtok_half, gtok_other, place.sibling)
    grad_ref[:, 0:CUT] = total_a
    grad_ref[:, CUT:PACK] = total_b
    mom_ref[...] = mom_ref[...] + grad_ref[:, 0:VEC]
    own_ref[:, 0:VEC] = mom_ref[...].astype(BF16)
    lanes = lax.broadcasted_iota(jnp.int32, (own_ref.shape[0], 128), 1)
    tile = jnp.zeros(lanes.shape, F32)
    for number, (start, stop) in enumerate(((QKV, OUT), (OUT, VEC), (FC1, FC2), (FC2, QKV), (VEC, PACK))):
        piece = grad_ref[:, start:stop]
        square = jnp.sum(lane_sum(piece * piece), axis=0, keepdims=True)
        square = jnp.broadcast_to(square * (0.5 if start == VEC else 1.0), lanes.shape)
        high = square.astype(BF16).astype(F32)
        tile = jnp.where(lanes == number, high, tile)
        tile = jnp.where(lanes == 64 + number, square - high, tile)
    own_ref[:, VEC:PACK] = tile.astype(BF16)
    local = pltpu.make_async_copy(own_ref, buf_ref.at[place.half, place.dp], local_sem)
    local.start()
    gather_flow(place, sender, own_ref, buf_ref, SCATTER_SLOTS)
    sender.arrived(base)
    sender.arrived(base + 1)
    sender.drain()
    local.wait()


def exchange_moments(parts, moms, out_half, gtok_half):
    _, ranks, rows, _ = parts.shape
    vmem = pl.BlockSpec(memory_space=pltpu.VMEM)
    anywhere = pl.BlockSpec(memory_space=pl.ANY)
    slots = SCATTER_SLOTS + GATHER_SLOTS + 2
    return pl.pallas_call(
        moments_kernel,
        out_shape=(
            jax.ShapeDtypeStruct((rows, PACK), F32),
            jax.ShapeDtypeStruct((rows, VEC), F32),
            jax.ShapeDtypeStruct((2, ranks, rows, PACK), BF16),
            jax.ShapeDtypeStruct(out_half.shape, F32),
            jax.ShapeDtypeStruct(gtok_half.shape, F32),
        ),
        in_specs=[vmem] * 5 + [anywhere] * 2,
        out_specs=(vmem, vmem, anywhere, anywhere, anywhere),
        scratch_shapes=[
            pltpu.VMEM((ranks, rows, PACK), BF16),
            pltpu.VMEM((8, rows, CUT), BF16),
            pltpu.VMEM((8, rows, PACK - CUT), BF16),
            pltpu.VMEM((4, rows, CUT), BF16),
            pltpu.VMEM((4, rows, PACK - CUT), BF16),
            pltpu.VMEM((3, rows, PACK), BF16),
            pltpu.VMEM((rows, PACK), BF16),
            pltpu.SemaphoreType.DMA((slots,)),
            pltpu.SemaphoreType.DMA((slots,)),
            pltpu.SemaphoreType.DMA,
        ],
        compiler_params=pltpu.CompilerParams(
            collective_id=1, has_side_effects=True, vmem_limit_bytes=40 * 1024 * 1024
        ),
        name="exchange_moments",
    )(parts, *moms, out_half, gtok_half)


QUINTIC = (3.4445, -4.775, 2.0315)
RATES = (2.0, 2.0, math.sqrt(3.0), math.sqrt(32.0))
RANGES = ((FC1, FC2), (FC2, QKV), (QKV, OUT), (OUT, VEC))


def mm3(a, b):
    return lax.dot_general(a, b, NN, precision=lax.Precision.HIGH, preferred_element_type=F32)


def eye_mask(n):
    return lax.broadcasted_iota(jnp.int32, (n, n), 0) == lax.broadcasted_iota(jnp.int32, (n, n), 1)


def chain_kernel(
    which_ref, buf_ref, grad_ref, mom_ref, vec_ref, first_ref, second_ref,
    out_half, out_other, gtok_half, gtok_other,
    root_ref, norm_ref, gfc1, gfc2, gqkv, gwo, gvec, mfc1, mfc2, mqkv, mwo,
    vec_new, first_new, second_new, out_ref, gtok_ref,
    gram_ref, poly_ref, turn_ref, sems,
):
    rows = out_half.shape[0]
    half = which_ref[1]
    mine = pl.ds(pl.multiple_of(half * rows, 8), rows)
    others = pl.ds(pl.multiple_of((1 - half) * rows, 8), rows)
    copies = [
        pltpu.make_async_copy(out_half, out_ref.at[mine], sems.at[0]),
        pltpu.make_async_copy(out_other, out_ref.at[others], sems.at[1]),
        pltpu.make_async_copy(gtok_half, gtok_ref.at[mine], sems.at[2]),
        pltpu.make_async_copy(gtok_other, gtok_ref.at[others], sems.at[3]),
    ]
    for copy in copies:
        copy.start()
    model = buf_ref.shape[1]
    for number, (start, stop) in enumerate(RANGES):

        @pl.when(which_ref[0] == number)
        def _():
            lower, upper = buf_ref[0, :, start:stop], buf_ref[1, :, start:stop]
            gram_ref[...] = mm(lower, lower, NT) + mm(upper, upper, NT)

    eye = eye_mask(model)
    gram = gram_ref[...]
    total = jnp.sum(lane_sum(jnp.where(eye, gram, 0.0)), axis=0, keepdims=True)
    scale = 1.0 / (jnp.sqrt(total) + 1e-07)
    gram_ref[...] = gram * (scale * scale)
    a, b, c = QUINTIC

    def polynomial():
        gram = gram_ref[...]
        return jnp.where(eye, a, 0.0) + b * gram + c * mm3(gram, gram)

    def advance(poly):
        gram_ref[...] = mm3(mm3(gram_ref[...], poly), poly)

    poly = polynomial()
    poly_ref[...] = poly
    advance(poly)

    def sweep(_, carry):
        poly = polynomial()
        poly_ref[...] = mm3(poly_ref[...], poly)
        advance(poly)
        return carry

    lax.fori_loop(0, NS_ITERS - 2, sweep, 0)
    root_ref[...] = mm3(poly_ref[...], polynomial()) * scale

    for grad, mom, lanes in ((gfc1, mfc1, FC1), (gfc2, mfc2, FC2), (gwo, mwo, OUT)):
        grad[...] = grad_ref[:, lanes : lanes + grad.shape[1]]
        mom[...] = mom_ref[:, lanes : lanes + grad.shape[1]]
    for part in range(3):
        start = QKV + part * SLOT
        gqkv[part] = grad_ref[:, start : start + gqkv.shape[2]]
        mqkv[part] = mom_ref[:, start : start + gqkv.shape[2]]
    own = grad_ref.shape[0]
    turn_ref[...] = jnp.zeros_like(turn_ref)
    turn_ref[0:own] = grad_ref[:, VEC:PACK]
    columns = vec_ref.shape[1]
    turned = turn_ref[...].T[0:6, 0:columns]
    first = 0.9 * first_ref[...] + 0.1 * turned
    second = 0.95 * second_ref[...] + 0.05 * turned * turned
    gvec[...] = turned
    first_new[...] = first
    second_new[...] = second
    vec_new[...] = vec_ref[...] - 0.5 * (first / (1.0 - 0.9**STEP)) / (
        jnp.sqrt(second / (1.0 - 0.95**STEP)) + 1e-08
    )
    tiles = buf_ref[0, :, VEC:PACK].astype(F32) + buf_ref[1, :, VEC:PACK].astype(F32)
    leads = lax.broadcasted_iota(jnp.int32, tiles.shape, 0) % own == 0
    squares = jnp.sum(jnp.where(leads, tiles, 0.0), axis=0, keepdims=True)
    norm_ref[...] = jnp.sqrt(squares + pltpu.roll(squares, 64, 1))
    for copy in copies:
        copy.wait()


def run_chain(which, buf, grad, mom, vectors, first, second, halves):
    model = buf.shape[1]
    own, columns = grad.shape[0], vectors.shape[1]
    full = (2 * halves[0].shape[0], model)
    vmem = pl.BlockSpec(memory_space=pltpu.VMEM)
    anywhere = pl.BlockSpec(memory_space=pl.ANY)
    shapes = [(own, 768), (own, 768), (3, own, 192), (own, 192)]
    outs = [(model, model), (1, 128)] + shapes + [(6, columns)] + shapes + [(6, columns)] * 3 + [full] * 2
    return pl.pallas_call(
        chain_kernel,
        out_shape=tuple(jax.ShapeDtypeStruct(shape, F32) for shape in outs),
        in_specs=[pl.BlockSpec(memory_space=pltpu.SMEM)] + [vmem] * 6 + [anywhere] * 4,
        out_specs=tuple([vmem] * (len(outs) - 2) + [anywhere] * 2),
        scratch_shapes=[
            pltpu.VMEM((model, model), F32),
            pltpu.VMEM((model, model), F32),
            pltpu.VMEM((128, 128), F32),
            pltpu.SemaphoreType.DMA((4,)),
        ],
        compiler_params=pltpu.CompilerParams(vmem_limit_bytes=40 * 1024 * 1024),
        name="run_chain",
    )(which, buf, grad, mom, vectors, first, second, *halves)


def roots_kernel(root_ref, buf_ref, fc1_ref, fc2_ref, qkv_ref, wo_ref, nfc1, nfc2, nqkv, nwo, rows_ref, send_sem, recv_sem):
    place = Place()
    x, half = place.x, place.half
    barrier = pltpu.get_barrier_semaphore()
    peers = [(1 - x, half), (x, 1 - half), (1 - x, 1 - half)]
    ids = [(place.index(place.z, place.y, px), ph) for px, ph in peers]
    for peer in ids:
        pl.semaphore_signal(barrier, inc=1, device_id=peer, device_id_type=MESH)
    pl.semaphore_wait(barrier, 3)
    sender = Sender(send_sem, recv_sem)
    mine = 2 * x + half
    for slot, peer in enumerate(ids):
        sender.start(slot, root_ref.at[peer[0]], rows_ref.at[mine], peer)
    rows_ref[mine] = root_ref[place.dp]
    for slot in range(3):
        sender.arrived(slot)
    for number, (start, stop) in enumerate(RANGES):
        rows = rows_ref[number]
        high = rows.astype(BF16)
        low = (rows - high.astype(F32)).astype(BF16)
        moment = buf_ref[half, :, start:stop]
        step = RATES[number] * (mm(high, moment, NN) + mm(low, moment, NN))
        if number == 2:
            for part in range(3):
                nqkv[part] = 0.999 * qkv_ref[part] - step[:, part * SLOT : part * SLOT + nqkv.shape[2]]
        else:
            new, old = ((nfc1, fc1_ref), (nfc2, fc2_ref), None, (nwo, wo_ref))[number]
            new[...] = 0.999 * old[...] - step[:, 0 : new.shape[1]]
    sender.drain()


def apply_roots(root, buf, weights):
    ranks, rows, model = root.shape
    vmem = pl.BlockSpec(memory_space=pltpu.VMEM)
    return pl.pallas_call(
        roots_kernel,
        out_shape=tuple(jax.ShapeDtypeStruct(w.shape, F32) for w in weights),
        in_specs=[vmem] * 6,
        out_specs=(vmem,) * 4,
        scratch_shapes=[
            pltpu.VMEM((4, rows, model), F32),
            pltpu.SemaphoreType.DMA((3,)),
            pltpu.SemaphoreType.DMA((3,)),
        ],
        compiler_params=pltpu.CompilerParams(
            collective_id=2, has_side_effects=True, vmem_limit_bytes=40 * 1024 * 1024
        ),
        name="apply_roots",
    )(root, buf, *weights)


def flat(part):
    return part.T if part.ndim == 2 else jnp.transpose(part, (0, 2, 1))


def pack(fc1, fc2, qkv, out):
    pad = ((0, 0), (0, SLOT - out.shape[1]))
    return jnp.concatenate([fc1, fc2] + [jnp.pad(part, pad) for part in (*qkv, out)], axis=1)


def unpack(packed, like):
    fc1, fc2, qkv, out = like
    split = jnp.stack([packed[:, QKV + part * SLOT :][:, : qkv.shape[2]] for part in range(3)])
    return packed[:, FC1:FC2], packed[:, FC2:QKV], split, packed[:, OUT : OUT + out.shape[1]]


def root_of(gram):
    a, b, c = QUINTIC
    eye = eye_mask(gram.shape[0])
    scale = 1.0 / (jnp.sqrt(jnp.sum(jnp.where(eye, gram, 0.0))) + 1e-07)
    gram = gram * (scale * scale)
    root = jnp.where(eye, scale, 0.0)
    for _ in range(NS_ITERS):
        poly = jnp.where(eye, a, 0.0) + b * gram + c * mm3(gram, gram)
        root = mm3(root, poly)
        gram = mm3(mm3(gram, poly), poly)
    return root


def general(half, bucket, widths, counts, tokens, cotangent, weights, moms, vectors, vec_first, vec_second):
    dp = lax.axis_index("dp")
    rows = weights[0].shape[0]
    vec = jnp.pad(vectors.T, ((0, 0), (0, PACK - VEC - vectors.shape[0])))
    own = jnp.concatenate([pack(*weights), vec], axis=1).astype(BF16)
    packed = lax.all_gather(lax.all_gather(own, "dp", axis=0, tiled=True), "mlp")
    out_half, gtok_half, grads = image_pass(half.reshape(1), bucket, widths, counts, tokens, cotangent, packed)
    output = lax.all_gather(out_half, "mlp", axis=0, tiled=True)
    gtok = lax.all_gather(gtok_half, "mlp", axis=0, tiled=True)
    grad = lax.psum_scatter(grads.astype(F32), "mlp", scatter_dimension=0)
    grad = lax.psum_scatter(grad, "dp", scatter_dimension=0, tiled=True)
    mom = 0.95 * pack(*moms) + grad[:, 0:VEC]
    ranges = (RANGES[2], RANGES[3], RANGES[0], RANGES[1])
    squares = [jnp.sum(jnp.square(grad[:, start:stop])) for start, stop in ranges]
    squares.append(0.5 * jnp.sum(jnp.square(grad[:, VEC:PACK])))
    norms = jnp.sqrt(lax.psum(jnp.stack(squares), ("dp", "mlp")))
    buf = lax.all_gather(lax.all_gather(mom.astype(BF16), "dp", axis=0, tiled=True), "mlp")
    ours = lax.dynamic_index_in_dim(buf, half, 0, keepdims=False)
    steps = []
    for (start, stop), rate in zip(RANGES, RATES):
        root = root_of(sum(mm(buf[h, :, start:stop], buf[h, :, start:stop], NT) for h in range(2)))
        root = lax.dynamic_slice_in_dim(root, dp * rows, rows, 0)
        high = root.astype(BF16)
        low = (root - high.astype(F32)).astype(BF16)
        steps.append(rate * (mm(high, ours[:, start:stop], NN) + mm(low, ours[:, start:stop], NN)))
    moved = unpack(jnp.concatenate(steps, axis=1), weights)
    gvec = grad[:, VEC : VEC + vectors.shape[0]].T
    first = 0.9 * vec_first + 0.1 * gvec
    second = 0.95 * vec_second + 0.05 * gvec * gvec
    vec_new = vectors - 0.5 * (first / (1.0 - 0.9**STEP)) / (
        jnp.sqrt(second / (1.0 - 0.95**STEP)) + 1e-08
    )

    def ordered(parts):
        fc1, fc2, qkv, out = parts
        return flat(qkv), flat(out), flat(fc1), flat(fc2)

    news = [0.999 * w - move for w, move in zip(weights, moved)]
    return (
        output, gtok, *ordered(unpack(grad, weights)), gvec,
        *ordered(unpack(mom, weights)), *ordered(news), vec_new, first, second, norms,
    )


def body(
    tokens, cotangent, image_bucket, bucket_width, bucket_heads,
    w_qkv, w_out, w_fc1, w_fc2, vectors,
    mom_qkv, mom_out, mom_fc1, mom_fc2, vec_first, vec_second,
):
    half = lax.axis_index("mlp").astype(jnp.int32)
    dp = lax.axis_index("dp").astype(jnp.int32)
    ranks = lax.axis_size("dp")
    model = tokens.shape[1]
    rows = w_fc1.shape[1]
    weights = [flat(w) for w in (w_fc1, w_fc2, w_qkv, w_out)]
    moms = [flat(m) for m in (mom_fc1, mom_fc2, mom_qkv, mom_out)]
    if ranks != 16:
        return general(
            half, image_bucket, bucket_width, bucket_heads, tokens, cotangent,
            weights, moms, vectors, vec_first, vec_second,
        )
    vec = jnp.pad(vectors.T, ((0, 0), (0, PACK - VEC - vectors.shape[0])))
    packed = gather_weights(weights + [vec], ranks)
    out_half, gtok_half, grads = image_pass(
        half.reshape(1), image_bucket, bucket_width, bucket_heads,
        tokens, cotangent, packed.reshape(2, model, PACK),
    )
    grad, mom, buf, out_other, gtok_other = exchange_moments(
        grads.reshape(2, ranks, rows, PACK), moms, out_half, gtok_half
    )
    which = jnp.stack([2 * (dp % 2) + half, half])
    buf = buf.reshape(2, model, PACK)
    (root, norms, gfc1, gfc2, gqkv, gwo, gvec, mfc1, mfc2, mqkv, mwo, vec_new, first, second, output, gtok) = run_chain(
        which, buf, grad, mom, vectors, vec_first, vec_second,
        (out_half, out_other, gtok_half, gtok_other),
    )
    nfc1, nfc2, nqkv, nwo = apply_roots(root.reshape(ranks, rows, model), buf, weights)
    return (
        output, gtok,
        flat(gqkv), flat(gwo), flat(gfc1), flat(gfc2), gvec,
        flat(mqkv), flat(mwo), flat(mfc1), flat(mfc2),
        flat(nqkv), flat(nwo), flat(nfc1), flat(nfc2),
        vec_new, first, second, norms[0, 0:5],
    )


def solution(mesh):
    halves, columns = P("mlp", "dp"), P(None, "dp")
    blocks = P(None, "mlp", "dp")
    matrices = (blocks, halves, halves, halves)
    placed = (P("dp", None), P("dp", None), P("dp"), P(), P()) + matrices + (columns,) + matrices + (columns, columns)
    outs = (P("dp", None), P("dp", None)) + matrices + (columns,) + matrices + matrices + (columns,) * 3 + (P(),)
    return jax.shard_map(body, mesh=mesh, in_specs=placed, out_specs=outs, check_vma=False)
```

```python
import functools
import math

import jax
import jax.numpy as jnp
from jax import lax
from jax.experimental import pallas as pl
from jax.experimental.pallas import tpu as pltpu
from jax.sharding import PartitionSpec as P

HD = 64
NS_ITERS = 5
STEP = 10
EPSILON = 1e-06
F32 = jnp.float32
BF16 = jnp.bfloat16
NN = (((1,), (0,)), ((), ()))
NT = (((1,), (1,)), ((), ()))
TN = (((0,), (0,)), ((), ()))

FC1, FC2, QKV, OUT, VEC, PACK = 0, 768, 1536, 2304, 2560, 2688
SLOT = 256
SEQ = 256
PAIR = 2
CHUNK = 256


def mm(a, b, dims):
    return lax.dot_general(a, b, dims, preferred_element_type=F32)


def lane_sum(v):
    return jnp.sum(v, axis=-1, keepdims=True)


def norm_rows(v):
    inv = 1.0 / v.shape[-1]
    center = v - lane_sum(v) * inv
    factor = lax.rsqrt(lane_sum(center * center) * inv + EPSILON)
    return center * factor, factor


def norm_back(g, n, factor):
    inv = 1.0 / g.shape[-1]
    return factor * (g - lane_sum(g) * inv - n * (lane_sum(g * n) * inv))


def image_kernel(
    half_ref, bucket_ref, widths_ref, counts_ref,
    tok_ref, cot_ref, w_ref,
    out_ref, gtok_ref, grad_ref,
    acc_ref, vec_ref, gvec_ref, q_ref, k_ref, v_ref, mixed_ref, probs_ref, low_ref,
    y_ref, gh_ref,
):
    step = pl.program_id(0)
    rows, model = tok_ref.shape
    heads_half = 3
    pack = rows // SEQ
    first = (half_ref[0] * pl.num_programs(0) + step) * pack
    buckets = [bucket_ref[first + image] for image in range(pack)]
    widths = [widths_ref[bucket] for bucket in buckets]
    counts = [counts_ref[bucket] for bucket in buckets]
    width, count = widths[0], counts[0]
    for image in range(1, pack):
        width, count = jnp.maximum(width, widths[image]), jnp.maximum(count, counts[image])
    row_ids = lax.broadcasted_iota(jnp.int32, (rows, 1), 0)
    row_width = jnp.full((rows, 1), widths[0], jnp.int32)
    for image in range(1, pack):
        row_width = jnp.where(row_ids >= image * SEQ, widths[image], row_width)

    @pl.when(step == 0)
    def _():
        acc_ref[...] = jnp.zeros_like(acc_ref)
        gvec_ref[...] = jnp.zeros_like(gvec_ref)
        turned = w_ref[0, :, VEC:PACK].astype(F32).T
        vec_ref[...] = turned[0:8]

    lane_head = lax.broadcasted_iota(jnp.int32, (1, SLOT), 1) // HD
    masks = [(lane_head == s).astype(F32).astype(BF16) for s in range(heads_half)]

    def used_heads(image):
        return (lane_head < counts[image] - heads_half).astype(F32)

    def spans():
        return [slice(image * SEQ, (image + 1) * SEQ) for image in range(pack)]

    x = tok_ref[...].astype(F32)
    normed_one, factor_one = norm_rows(x)
    hidden_one = (normed_one * vec_ref[0:1] + vec_ref[1:2]).astype(BF16)
    for half in range(2):
        for ref, which in ((q_ref, 0), (k_ref, 1), (v_ref, 2)):
            lanes = slice(QKV + which * SLOT, QKV + (which + 1) * SLOT)
            ref[half] = mm(hidden_one, w_ref[half, :, lanes], NN).astype(BF16)

        def attend():
            for image, span in enumerate(spans()):
                total = None
                for s in range(heads_half):
                    slot = (image * 2 + half) * heads_half + s
                    scores = mm(q_ref[half, span] * masks[s], k_ref[half, span], NT) * 0.125
                    top = jnp.max(scores, axis=-1, keepdims=True)
                    grown = jnp.exp(scores - top)
                    probs = grown * (1.0 / lane_sum(grown))
                    low = probs.astype(BF16)
                    probs_ref[slot] = probs
                    low_ref[slot] = low
                    term = mm(low, v_ref[half, span] * masks[s], NN)
                    total = term if total is None else total + term
                if half:
                    total = total * used_heads(image)
                mixed_ref[half, span] = total.astype(BF16)

        if half == 0:
            attend()
        else:
            mixed_ref[half] = jnp.zeros_like(mixed_ref[half])
            pl.when(count > heads_half)(attend)

    branch = mm(mixed_ref[0], w_ref[0, :, OUT:VEC], NT) + mm(mixed_ref[1], w_ref[1, :, OUT:VEC], NT)
    resid = x + branch + vec_ref[4:5]
    normed_two, factor_two = norm_rows(resid)
    hidden_two = (normed_two * vec_ref[2:3] + vec_ref[3:4]).astype(BF16)
    cot = cot_ref[...]
    hidden_two_t = hidden_two.T
    cot_t = cot.T
    y_ref[...] = resid + vec_ref[5:6]
    gh_ref[...] = jnp.zeros_like(gh_ref)
    per_half = FC2 // CHUNK
    for chunk in range(2 * per_half):
        half, part = divmod(chunk, per_half)
        one = slice(FC1 + part * CHUNK, FC1 + (part + 1) * CHUNK)
        two = slice(FC2 + part * CHUNK, FC2 + (part + 1) * CHUNK)

        def units_pass():
            pre = mm(hidden_two, w_ref[half, :, one], NN)
            units = chunk * CHUNK + lax.broadcasted_iota(jnp.int32, pre.shape, 1)
            cumulative = 0.5 + 0.5 * lax.erf(pre * 0.7071067811865476)
            density = jnp.exp(-0.5 * pre * pre) * 0.3989422804014327
            cumulative = jnp.where(units < row_width, cumulative, 0.0)
            density = jnp.where(units < row_width, density, 0.0)
            act = (pre * cumulative).astype(BF16)
            grad_act = mm(cot, w_ref[half, :, two], NN)
            grad_pre = (grad_act * (cumulative + pre * density)).astype(BF16)
            y_ref[...] += mm(act, w_ref[half, :, two], NT)
            gh_ref[...] += mm(grad_pre, w_ref[half, :, one], NT)
            acc_ref[half, :, two] += mm(cot_t, act, NN)
            acc_ref[half, :, one] += mm(hidden_two_t, grad_pre, NN)

        if chunk < 2:
            units_pass()
        else:
            pl.when(width > chunk * CHUNK)(units_pass)

    out_ref[...] = y_ref[...]
    grad_hidden_two = gh_ref[...]
    cot_f = cot.astype(F32)
    grad_resid = cot_f + norm_back(grad_hidden_two * vec_ref[2:3], normed_two, factor_two)
    resid_low = grad_resid.astype(BF16)
    resid_low_t = resid_low.T
    hidden_one_t = hidden_one.T
    for half in range(2):
        acc_ref[half, :, OUT:VEC] += mm(resid_low_t, mixed_ref[half], NN)

        def back():
            grad_heads = mm(resid_low, w_ref[half, :, OUT:VEC], NN).astype(BF16)
            parts = []
            for image, span in enumerate(spans()):
                heads = grad_heads[span]
                if half:
                    heads = heads * used_heads(image).astype(BF16)
                sums = [None, None, None]
                for s in range(heads_half):
                    slot = (image * 2 + half) * heads_half + s
                    own = heads * masks[s]
                    grad_probs = mm(own, v_ref[half, span], NT)
                    probs = probs_ref[slot]
                    weighed = probs * grad_probs
                    grad_scores = (weighed - probs * lane_sum(weighed)).astype(BF16)
                    terms = (
                        mm(grad_scores, k_ref[half, span] * masks[s], NN),
                        mm(grad_scores, q_ref[half, span] * masks[s], TN),
                        mm(low_ref[slot], own, TN),
                    )
                    sums = [t if o is None else o + t for o, t in zip(sums, terms)]
                parts.append([(v * c).astype(BF16) for v, c in zip(sums, (0.125, 0.125, 1.0))])
            total = None
            for which in range(3):
                lanes = slice(QKV + which * SLOT, QKV + (which + 1) * SLOT)
                grad_proj = jnp.concatenate([part[which] for part in parts], axis=0)
                acc_ref[half, :, lanes] += mm(hidden_one_t, grad_proj, NN)
                term = mm(grad_proj, w_ref[half, :, lanes], NT)
                total = term if total is None else total + term
            return total

        if half == 0:
            gh_ref[...] = back()
        else:

            @pl.when(count > heads_half)
            def _():
                gh_ref[...] += back()

    grad_hidden_one = gh_ref[...]
    gtok_ref[...] = grad_resid + norm_back(grad_hidden_one * vec_ref[0:1], normed_one, factor_one)
    sums = (
        grad_hidden_one * normed_one,
        grad_hidden_one,
        grad_hidden_two * normed_two,
        grad_hidden_two,
        grad_resid,
        cot_f,
    )
    for row, values in enumerate(sums):
        gvec_ref[row : row + 1] += jnp.sum(values, axis=0, keepdims=True)

    @pl.when(step == pl.num_programs(0) - 1)
    def _():
        grad_ref[0, :, 0:VEC] = acc_ref[0].astype(BF16)
        grad_ref[1, :, 0:VEC] = acc_ref[1].astype(BF16)
        columns = gvec_ref[...].T.astype(BF16)
        grad_ref[0, :, VEC:PACK] = columns
        grad_ref[1, :, VEC:PACK] = columns


def image_pass(half, bucket, widths, counts, tokens, cotangent, packed):
    images = bucket.shape[0] // 2
    model = tokens.shape[1]
    rows = images * SEQ
    images = images // PAIR
    seq = PAIR * SEQ
    picked = pl.BlockSpec((seq, model), lambda i, h, b, w, c: (h[0] * images + i, 0))
    placed = pl.BlockSpec((seq, model), lambda i, h, b, w, c: (i, 0))
    whole = pl.BlockSpec(
        (2, model, PACK), lambda i, h, b, w, c: (0, 0, 0), pipeline_mode=pl.Buffered(1)
    )
    heads = 6
    flops = 2 * rows * model * (3 * 4 * model + 3 * 8 * model)
    return pl.pallas_call(
        image_kernel,
        out_shape=(
            jax.ShapeDtypeStruct((rows, model), F32),
            jax.ShapeDtypeStruct((rows, model), F32),
            jax.ShapeDtypeStruct((2, model, PACK), BF16),
        ),
        grid_spec=pltpu.PrefetchScalarGridSpec(
            num_scalar_prefetch=4,
            grid=(images,),
            in_specs=[picked, picked, whole],
            out_specs=[placed, placed, whole],
            scratch_shapes=[
                pltpu.VMEM((2, model, VEC), F32),
                pltpu.VMEM((8, model), F32),
                pltpu.VMEM((128, model), F32),
                pltpu.VMEM((2, seq, SLOT), BF16),
                pltpu.VMEM((2, seq, SLOT), BF16),
                pltpu.VMEM((2, seq, SLOT), BF16),
                pltpu.VMEM((2, seq, SLOT), BF16),
                pltpu.VMEM((PAIR * heads, SEQ, SEQ), F32),
                pltpu.VMEM((PAIR * heads, SEQ, SEQ), BF16),
                pltpu.VMEM((seq, model), F32),
                pltpu.VMEM((seq, model), F32),
            ],
        ),
        compiler_params=pltpu.CompilerParams(vmem_limit_bytes=56 * 1024 * 1024),
        cost_estimate=pl.CostEstimate(flops=flops, bytes_accessed=20 * rows * model, transcendentals=rows * 6144),
        name="image_pass",
    )(half, bucket, widths, counts, tokens, cotangent, packed)


MESH = pl.DeviceIdType.MESH
CUT = 1408


class Place:
    def __init__(self):
        dp = lax.axis_index("dp")
        self.half = lax.axis_index("mlp")
        self.z = dp // 4
        self.y = (dp // 2) % 2
        self.x = dp % 2
        self.dp = dp

    def index(self, z, y, x):
        return z * 4 + y * 2 + x

    def at_z(self, z):
        return (self.index(z, self.y, self.x), self.half)

    @property
    def y_peer(self):
        return (self.index(self.z, 1 - self.y, self.x), self.half)

    @property
    def x_peer(self):
        return (self.index(self.z, self.y, 1 - self.x), self.half)

    @property
    def sibling(self):
        return (self.dp, 1 - self.half)


def meet(place):
    barrier = pltpu.get_barrier_semaphore()
    peers = [place.at_z((place.z + j) % 4) for j in range(1, 4)]
    peers += [place.y_peer, place.x_peer, place.sibling]
    for peer in peers:
        pl.semaphore_signal(barrier, inc=1, device_id=peer, device_id_type=MESH)
    pl.semaphore_wait(barrier, len(peers))


class Sender:
    def __init__(self, send_sem, recv_sem):
        self.send_sem, self.recv_sem = send_sem, recv_sem
        self.copies = {}

    def start(self, slot, src, dst, peer):
        copy = pltpu.make_async_remote_copy(
            src_ref=src,
            dst_ref=dst,
            send_sem=self.send_sem.at[slot],
            recv_sem=self.recv_sem.at[slot],
            device_id=peer,
            device_id_type=MESH,
        )
        copy.start()
        self.copies[slot] = copy

    def arrived(self, slot):
        self.copies[slot].wait_recv()

    def drain(self):
        for copy in self.copies.values():
            copy.wait_send()


GATHER_SLOTS = 35


def gather_flow(place, sender, own, buf, base=0):
    half = place.half
    other_y, other_x = 1 - place.y, 1 - place.x

    def shard(z, y, x):
        return place.index(z, y, x)

    def send(slot, src, dp, peer, lanes=None):
        dst = buf.at[half, dp] if lanes is None else buf.at[half, dp, :, lanes]
        sender.start(base + slot, src, dst, peer)

    def forward(slot, dp, peer, lanes=None):
        src = buf.at[half, dp] if lanes is None else buf.at[half, dp, :, lanes]
        send(slot, src, dp, peer, lanes)

    cut_a, cut_b = pl.ds(0, CUT), pl.ds(CUT, PACK - CUT)
    me = place.dp
    for j in range(1, 4):
        send(j - 1, own, me, place.at_z((place.z + j) % 4))
    send(3, own, me, place.y_peer)
    send(7, own, me, place.x_peer)
    send(19, own, me, place.sibling)
    for k in range(1, 5):
        if k < 4:
            sender.arrived(base + k - 1)
            dp = shard((place.z + 4 - k) % 4, place.y, place.x)
            forward(3 + k, dp, place.y_peer)
            forward(7 + k, dp, place.x_peer)
            forward(19 + k, dp, place.sibling)
        z = (place.z + 5 - k) % 4
        sender.arrived(base + 3 + k - 1)
        dp = shard(z, other_y, place.x)
        forward(11 + k - 1, dp, place.x_peer, cut_a)
        forward(23 + k - 1, dp, place.sibling)
        sender.arrived(base + 7 + k - 1)
        dp = shard(z, place.y, other_x)
        forward(15 + k - 1, dp, place.y_peer, cut_b)
        forward(27 + k - 1, dp, place.sibling)
    for k in range(4):
        sender.arrived(base + 11 + k)
        sender.arrived(base + 15 + k)
        forward(31 + k, shard((place.z + 4 - k) % 4, other_y, other_x), place.sibling)
    for k in range(16):
        sender.arrived(base + 19 + k)


def weights_kernel(fc1_ref, fc2_ref, qkv_ref, out_ref, vec_ref, buf_ref, own_ref, send_sem, recv_sem, local_sem):
    place = Place()
    own_ref[...] = jnp.zeros_like(own_ref)
    own_ref[:, FC1:FC2] = fc1_ref[...].astype(BF16)
    own_ref[:, FC2:QKV] = fc2_ref[...].astype(BF16)
    for which in range(3):
        start = QKV + which * SLOT
        own_ref[:, start : start + qkv_ref.shape[2]] = qkv_ref[which].astype(BF16)
    own_ref[:, OUT : OUT + out_ref.shape[1]] = out_ref[...].astype(BF16)
    own_ref[:, VEC:PACK] = vec_ref[...].astype(BF16)
    local = pltpu.make_async_copy(own_ref, buf_ref.at[place.half, place.dp], local_sem)
    local.start()
    meet(place)
    sender = Sender(send_sem, recv_sem)
    gather_flow(place, sender, own_ref, buf_ref)
    sender.drain()
    local.wait()


def gather_weights(parts, ranks):
    rows = parts[0].shape[0]
    vmem = pl.BlockSpec(memory_space=pltpu.VMEM)
    return pl.pallas_call(
        weights_kernel,
        out_shape=jax.ShapeDtypeStruct((2, ranks, rows, PACK), BF16),
        in_specs=[vmem] * 5,
        out_specs=pl.BlockSpec(memory_space=pl.ANY),
        scratch_shapes=[
            pltpu.VMEM((rows, PACK), BF16),
            pltpu.SemaphoreType.DMA((GATHER_SLOTS,)),
            pltpu.SemaphoreType.DMA((GATHER_SLOTS,)),
            pltpu.SemaphoreType.DMA,
        ],
        compiler_params=pltpu.CompilerParams(collective_id=0, has_side_effects=True),
        name="gather_weights",
    )(*parts)


SCATTER_SLOTS = 43
Z_ORDER = (2, 1, 3, 0)


def scatter_flow(place, sender, parts, hold, first_a, first_b, second_a, second_b, last):
    half, z, y, x = place.half, place.z, place.y, place.x
    other_y, other_x = 1 - y, 1 - x
    cut_a, cut_b = pl.ds(0, CUT), pl.ds(CUT, PACK - CUT)
    columns = ((other_y, other_x), (y, other_x), (other_y, x), (y, x))

    def shard(k, column):
        return place.index((z + Z_ORDER[k]) % 4, *column)

    for c, column in enumerate(columns):
        for k in range(4):
            dp = shard(k, column)
            sender.start(4 * c + k, parts.at[1 - half, dp], hold.at[dp], place.sibling)

    def settle(c, k):
        dp = shard(k, columns[c])
        sender.arrived(4 * c + k)
        hold[dp] = (hold[dp].astype(F32) + parts[half, dp].astype(F32)).astype(BF16)
        return dp

    def add(dp, lanes, arrived):
        hold[dp, :, lanes] = (hold[dp, :, lanes].astype(F32) + arrived.astype(F32)).astype(BF16)

    for k in range(4):
        dp = settle(0, k)
        sender.start(16 + k, hold.at[dp, :, cut_a], first_a.at[k], place.x_peer)
        sender.start(24 + k, hold.at[dp, :, cut_b], first_b.at[k], place.y_peer)
    for k in range(4):
        dp = settle(1, k)
        sender.start(20 + k, hold.at[dp, :, cut_a], first_a.at[4 + k], place.x_peer)
        dp = settle(2, k)
        sender.start(28 + k, hold.at[dp, :, cut_b], first_b.at[4 + k], place.y_peer)
    for k in range(4):
        settle(3, k)
    for k in range(4):
        sender.arrived(16 + k)
        dp = shard(k, columns[2])
        add(dp, cut_a, first_a[k])
        sender.start(32 + k, hold.at[dp, :, cut_a], second_a.at[k], place.y_peer)
        sender.arrived(24 + k)
        dp = shard(k, columns[1])
        add(dp, cut_b, first_b[k])
        sender.start(36 + k, hold.at[dp, :, cut_b], second_b.at[k], place.x_peer)
    total = None
    for k in range(4):
        dp = shard(k, columns[3])
        sender.arrived(20 + k)
        sender.arrived(32 + k)
        own_a = hold[dp, :, cut_a].astype(F32) + first_a[4 + k].astype(F32) + second_a[k].astype(F32)
        sender.arrived(28 + k)
        sender.arrived(36 + k)
        own_b = hold[dp, :, cut_b].astype(F32) + first_b[4 + k].astype(F32) + second_b[k].astype(F32)
        if Z_ORDER[k]:
            hold[dp, :, cut_a] = own_a.astype(BF16)
            hold[dp, :, cut_b] = own_b.astype(BF16)
            j = Z_ORDER[k]
            sender.start(40 + j - 1, hold.at[dp], last.at[j - 1], place.at_z((z + j) % 4))
        else:
            total = (own_a, own_b)
    for j in range(3):
        sender.arrived(40 + j)
    total_a, total_b = total
    for j in range(3):
        total_a = total_a + last[j, :, cut_a].astype(F32)
        total_b = total_b + last[j, :, cut_b].astype(F32)
    return total_a, total_b


def moments_kernel(
    parts, fc1_ref, fc2_ref, qkv_ref, wo_ref, out_half, gtok_half,
    grad_ref, mom_ref, buf_ref, out_other, gtok_other,
    hold, first_a, first_b, second_a, second_b, last, own_ref,
    send_sem, recv_sem, local_sem,
):
    place = Place()
    mom_ref[...] = jnp.zeros_like(mom_ref)
    mom_ref[:, FC1:FC2] = 0.95 * fc1_ref[...]
    mom_ref[:, FC2:QKV] = 0.95 * fc2_ref[...]
    for which in range(3):
        start = QKV + which * SLOT
        mom_ref[:, start : start + qkv_ref.shape[2]] = 0.95 * qkv_ref[which]
    mom_ref[:, OUT : OUT + wo_ref.shape[1]] = 0.95 * wo_ref[...]
    meet(place)
    sender = Sender(send_sem, recv_sem)
    total_a, total_b = scatter_flow(
        place, sender, parts, hold, first_a, first_b, second_a, second_b, last
    )
    base = SCATTER_SLOTS + GATHER_SLOTS
    sender.start(base, out_half, out_other, place.sibling)
    sender.start(base + 1, gtok_half, gtok_other, place.sibling)
    grad_ref[:, 0:CUT] = total_a
    grad_ref[:, CUT:PACK] = total_b
    mom_ref[...] = mom_ref[...] + grad_ref[:, 0:VEC]
    own_ref[:, 0:VEC] = mom_ref[...].astype(BF16)
    lanes = lax.broadcasted_iota(jnp.int32, (own_ref.shape[0], 128), 1)
    tile = jnp.zeros(lanes.shape, F32)
    for number, (start, stop) in enumerate(((QKV, OUT), (OUT, VEC), (FC1, FC2), (FC2, QKV), (VEC, PACK))):
        piece = grad_ref[:, start:stop]
        square = jnp.sum(lane_sum(piece * piece), axis=0, keepdims=True)
        square = jnp.broadcast_to(square * (0.5 if start == VEC else 1.0), lanes.shape)
        high = square.astype(BF16).astype(F32)
        tile = jnp.where(lanes == number, high, tile)
        tile = jnp.where(lanes == 64 + number, square - high, tile)
    own_ref[:, VEC:PACK] = tile.astype(BF16)
    local = pltpu.make_async_copy(own_ref, buf_ref.at[place.half, place.dp], local_sem)
    local.start()
    gather_flow(place, sender, own_ref, buf_ref, SCATTER_SLOTS)
    sender.arrived(base)
    sender.arrived(base + 1)
    sender.drain()
    local.wait()


def exchange_moments(parts, moms, out_half, gtok_half):
    _, ranks, rows, _ = parts.shape
    vmem = pl.BlockSpec(memory_space=pltpu.VMEM)
    anywhere = pl.BlockSpec(memory_space=pltpu.HBM)
    slots = SCATTER_SLOTS + GATHER_SLOTS + 2
    return pl.pallas_call(
        moments_kernel,
        out_shape=(
            jax.ShapeDtypeStruct((rows, PACK), F32),
            jax.ShapeDtypeStruct((rows, VEC), F32),
            jax.ShapeDtypeStruct((2, ranks, rows, PACK), BF16),
            jax.ShapeDtypeStruct(out_half.shape, F32),
            jax.ShapeDtypeStruct(gtok_half.shape, F32),
        ),
        in_specs=[vmem] * 5 + [anywhere] * 2,
        out_specs=(vmem, vmem, anywhere, anywhere, anywhere),
        scratch_shapes=[
            pltpu.VMEM((ranks, rows, PACK), BF16),
            pltpu.VMEM((8, rows, CUT), BF16),
            pltpu.VMEM((8, rows, PACK - CUT), BF16),
            pltpu.VMEM((4, rows, CUT), BF16),
            pltpu.VMEM((4, rows, PACK - CUT), BF16),
            pltpu.VMEM((3, rows, PACK), BF16),
            pltpu.VMEM((rows, PACK), BF16),
            pltpu.SemaphoreType.DMA((slots,)),
            pltpu.SemaphoreType.DMA((slots,)),
            pltpu.SemaphoreType.DMA,
        ],
        compiler_params=pltpu.CompilerParams(
            collective_id=1, has_side_effects=True, vmem_limit_bytes=58 * 1024 * 1024
        ),
        name="exchange_moments",
    )(parts, *moms, out_half, gtok_half)


QUINTIC = (3.4445, -4.775, 2.0315)
RATES = (2.0, 2.0, math.sqrt(3.0), math.sqrt(32.0))
RANGES = ((FC1, FC2), (FC2, QKV), (QKV, OUT), (OUT, VEC))


def mm3(a, b):
    return lax.dot_general(a, b, NN, precision=lax.Precision.HIGH, preferred_element_type=F32)


def eye_mask(n):
    return lax.broadcasted_iota(jnp.int32, (n, n), 0) == lax.broadcasted_iota(jnp.int32, (n, n), 1)


def chain_kernel(
    which_ref, buf_ref, grad_ref, mom_ref, vec_ref, first_ref, second_ref,
    out_half, out_other, gtok_half, gtok_other,
    root_ref, norm_ref, gfc1, gfc2, gqkv, gwo, gvec, mfc1, mfc2, mqkv, mwo,
    vec_new, first_new, second_new, out_ref, gtok_ref,
    gram_ref, poly_ref, turn_ref, sems,
):
    rows = out_half.shape[0]
    half = which_ref[1]
    mine = pl.ds(pl.multiple_of(half * rows, 8), rows)
    others = pl.ds(pl.multiple_of((1 - half) * rows, 8), rows)
    copies = [
        pltpu.make_async_copy(out_half, out_ref.at[mine], sems.at[0]),
        pltpu.make_async_copy(out_other, out_ref.at[others], sems.at[1]),
        pltpu.make_async_copy(gtok_half, gtok_ref.at[mine], sems.at[2]),
        pltpu.make_async_copy(gtok_other, gtok_ref.at[others], sems.at[3]),
    ]
    for copy in copies:
        copy.start()
    model = buf_ref.shape[1]
    for number, (start, stop) in enumerate(RANGES):

        @pl.when(which_ref[0] == number)
        def _():
            lower, upper = buf_ref[0, :, start:stop], buf_ref[1, :, start:stop]
            gram_ref[...] = mm(lower, lower, NT) + mm(upper, upper, NT)

    eye = eye_mask(model)
    gram = gram_ref[...]
    total = jnp.sum(lane_sum(jnp.where(eye, gram, 0.0)), axis=0, keepdims=True)
    scale = 1.0 / (jnp.sqrt(total) + 1e-07)
    gram_ref[...] = gram * (scale * scale)
    a, b, c = QUINTIC

    def polynomial():
        gram = gram_ref[...]
        return jnp.where(eye, a, 0.0) + b * gram + c * mm3(gram, gram)

    def advance(poly):
        gram_ref[...] = mm3(mm3(gram_ref[...], poly), poly)

    poly = polynomial()
    poly_ref[...] = poly
    advance(poly)

    def sweep(_, carry):
        poly = polynomial()
        poly_ref[...] = mm3(poly_ref[...], poly)
        advance(poly)
        return carry

    lax.fori_loop(0, NS_ITERS - 2, sweep, 0)
    root_ref[...] = mm3(poly_ref[...], polynomial()) * scale

    for grad, mom, lanes in ((gfc1, mfc1, FC1), (gfc2, mfc2, FC2), (gwo, mwo, OUT)):
        grad[...] = grad_ref[:, lanes : lanes + grad.shape[1]]
        mom[...] = mom_ref[:, lanes : lanes + grad.shape[1]]
    for part in range(3):
        start = QKV + part * SLOT
        gqkv[part] = grad_ref[:, start : start + gqkv.shape[2]]
        mqkv[part] = mom_ref[:, start : start + gqkv.shape[2]]
    own = grad_ref.shape[0]
    turn_ref[...] = jnp.zeros_like(turn_ref)
    turn_ref[0:own] = grad_ref[:, VEC:PACK]
    columns = vec_ref.shape[1]
    turned = turn_ref[...].T[0:6, 0:columns]
    first = 0.9 * first_ref[...] + 0.1 * turned
    second = 0.95 * second_ref[...] + 0.05 * turned * turned
    gvec[...] = turned
    first_new[...] = first
    second_new[...] = second
    vec_new[...] = vec_ref[...] - 0.5 * (first / (1.0 - 0.9**STEP)) / (
        jnp.sqrt(second / (1.0 - 0.95**STEP)) + 1e-08
    )
    tiles = buf_ref[0, :, VEC:PACK].astype(F32) + buf_ref[1, :, VEC:PACK].astype(F32)
    leads = lax.broadcasted_iota(jnp.int32, tiles.shape, 0) % own == 0
    squares = jnp.sum(jnp.where(leads, tiles, 0.0), axis=0, keepdims=True)
    norm_ref[...] = jnp.sqrt(squares + pltpu.roll(squares, 64, 1))
    for copy in copies:
        copy.wait()


def run_chain(which, buf, grad, mom, vectors, first, second, halves):
    model = buf.shape[1]
    own, columns = grad.shape[0], vectors.shape[1]
    full = (2 * halves[0].shape[0], model)
    vmem = pl.BlockSpec(memory_space=pltpu.VMEM)
    anywhere = pl.BlockSpec(memory_space=pltpu.HBM)
    shapes = [(own, 768), (own, 768), (3, own, 192), (own, 192)]
    outs = [(model, model), (1, 128)] + shapes + [(6, columns)] + shapes + [(6, columns)] * 3 + [full] * 2
    return pl.pallas_call(
        chain_kernel,
        out_shape=tuple(jax.ShapeDtypeStruct(shape, F32) for shape in outs),
        in_specs=[pl.BlockSpec(memory_space=pltpu.SMEM)] + [vmem] * 6 + [anywhere] * 4,
        out_specs=tuple([vmem] * (len(outs) - 2) + [anywhere] * 2),
        scratch_shapes=[
            pltpu.VMEM((model, model), F32),
            pltpu.VMEM((model, model), F32),
            pltpu.VMEM((128, 128), F32),
            pltpu.SemaphoreType.DMA((4,)),
        ],
        compiler_params=pltpu.CompilerParams(vmem_limit_bytes=58 * 1024 * 1024),
        name="run_chain",
    )(which, buf, grad, mom, vectors, first, second, *halves)


def roots_kernel(root_ref, buf_ref, fc1_ref, fc2_ref, qkv_ref, wo_ref, nfc1, nfc2, nqkv, nwo, rows_ref, send_sem, recv_sem):
    place = Place()
    x, half = place.x, place.half
    barrier = pltpu.get_barrier_semaphore()
    peers = [(1 - x, half), (x, 1 - half), (1 - x, 1 - half)]
    ids = [(place.index(place.z, place.y, px), ph) for px, ph in peers]
    for peer in ids:
        pl.semaphore_signal(barrier, inc=1, device_id=peer, device_id_type=MESH)
    pl.semaphore_wait(barrier, 3)
    sender = Sender(send_sem, recv_sem)
    mine = 2 * x + half
    for slot, peer in enumerate(ids):
        sender.start(slot, root_ref.at[peer[0]], rows_ref.at[mine], peer)
    rows_ref[mine] = root_ref[place.dp]
    for slot in range(3):
        sender.arrived(slot)
    for number, (start, stop) in enumerate(RANGES):
        rows = rows_ref[number]
        high = rows.astype(BF16)
        low = (rows - high.astype(F32)).astype(BF16)
        moment = buf_ref[half, :, start:stop]
        step = RATES[number] * (mm(high, moment, NN) + mm(low, moment, NN))
        if number == 2:
            for part in range(3):
                nqkv[part] = 0.999 * qkv_ref[part] - step[:, part * SLOT : part * SLOT + nqkv.shape[2]]
        else:
            new, old = ((nfc1, fc1_ref), (nfc2, fc2_ref), None, (nwo, wo_ref))[number]
            new[...] = 0.999 * old[...] - step[:, 0 : new.shape[1]]
    sender.drain()


def apply_roots(root, buf, weights):
    ranks, rows, model = root.shape
    vmem = pl.BlockSpec(memory_space=pltpu.VMEM)
    return pl.pallas_call(
        roots_kernel,
        out_shape=tuple(jax.ShapeDtypeStruct(w.shape, F32) for w in weights),
        in_specs=[vmem] * 6,
        out_specs=(vmem,) * 4,
        scratch_shapes=[
            pltpu.VMEM((4, rows, model), F32),
            pltpu.SemaphoreType.DMA((3,)),
            pltpu.SemaphoreType.DMA((3,)),
        ],
        compiler_params=pltpu.CompilerParams(
            collective_id=2, has_side_effects=True, vmem_limit_bytes=40 * 1024 * 1024
        ),
        name="apply_roots",
    )(root, buf, *weights)


def flat(part):
    return part.T if part.ndim == 2 else jnp.transpose(part, (0, 2, 1))


def pack(fc1, fc2, qkv, out):
    pad = ((0, 0), (0, SLOT - out.shape[1]))
    return jnp.concatenate([fc1, fc2] + [jnp.pad(part, pad) for part in (*qkv, out)], axis=1)


def unpack(packed, like):
    fc1, fc2, qkv, out = like
    split = jnp.stack([packed[:, QKV + part * SLOT :][:, : qkv.shape[2]] for part in range(3)])
    return packed[:, FC1:FC2], packed[:, FC2:QKV], split, packed[:, OUT : OUT + out.shape[1]]


def root_of(gram):
    a, b, c = QUINTIC
    eye = eye_mask(gram.shape[0])
    scale = 1.0 / (jnp.sqrt(jnp.sum(jnp.where(eye, gram, 0.0))) + 1e-07)
    gram = gram * (scale * scale)
    root = jnp.where(eye, scale, 0.0)
    for _ in range(NS_ITERS):
        poly = jnp.where(eye, a, 0.0) + b * gram + c * mm3(gram, gram)
        root = mm3(root, poly)
        gram = mm3(mm3(gram, poly), poly)
    return root


def general(half, bucket, widths, counts, tokens, cotangent, weights, moms, vectors, vec_first, vec_second):
    dp = lax.axis_index("dp")
    rows = weights[0].shape[0]
    vec = jnp.pad(vectors.T, ((0, 0), (0, PACK - VEC - vectors.shape[0])))
    own = jnp.concatenate([pack(*weights), vec], axis=1).astype(BF16)
    packed = lax.all_gather(lax.all_gather(own, "dp", axis=0, tiled=True), "mlp")
    out_half, gtok_half, grads = image_pass(half.reshape(1), bucket, widths, counts, tokens, cotangent, packed)
    output = lax.all_gather(out_half, "mlp", axis=0, tiled=True)
    gtok = lax.all_gather(gtok_half, "mlp", axis=0, tiled=True)
    grad = lax.psum_scatter(grads.astype(F32), "mlp", scatter_dimension=0)
    grad = lax.psum_scatter(grad, "dp", scatter_dimension=0, tiled=True)
    mom = 0.95 * pack(*moms) + grad[:, 0:VEC]
    ranges = (RANGES[2], RANGES[3], RANGES[0], RANGES[1])
    squares = [jnp.sum(jnp.square(grad[:, start:stop])) for start, stop in ranges]
    squares.append(0.5 * jnp.sum(jnp.square(grad[:, VEC:PACK])))
    norms = jnp.sqrt(lax.psum(jnp.stack(squares), ("dp", "mlp")))
    buf = lax.all_gather(lax.all_gather(mom.astype(BF16), "dp", axis=0, tiled=True), "mlp")
    ours = lax.dynamic_index_in_dim(buf, half, 0, keepdims=False)
    steps = []
    for (start, stop), rate in zip(RANGES, RATES):
        root = root_of(sum(mm(buf[h, :, start:stop], buf[h, :, start:stop], NT) for h in range(2)))
        root = lax.dynamic_slice_in_dim(root, dp * rows, rows, 0)
        high = root.astype(BF16)
        low = (root - high.astype(F32)).astype(BF16)
        steps.append(rate * (mm(high, ours[:, start:stop], NN) + mm(low, ours[:, start:stop], NN)))
    moved = unpack(jnp.concatenate(steps, axis=1), weights)
    gvec = grad[:, VEC : VEC + vectors.shape[0]].T
    first = 0.9 * vec_first + 0.1 * gvec
    second = 0.95 * vec_second + 0.05 * gvec * gvec
    vec_new = vectors - 0.5 * (first / (1.0 - 0.9**STEP)) / (
        jnp.sqrt(second / (1.0 - 0.95**STEP)) + 1e-08
    )

    def ordered(parts):
        fc1, fc2, qkv, out = parts
        return flat(qkv), flat(out), flat(fc1), flat(fc2)

    news = [0.999 * w - move for w, move in zip(weights, moved)]
    return (
        output, gtok, *ordered(unpack(grad, weights)), gvec,
        *ordered(unpack(mom, weights)), *ordered(news), vec_new, first, second, norms,
    )


def body(
    tokens, cotangent, image_bucket, bucket_width, bucket_heads,
    w_qkv, w_out, w_fc1, w_fc2, vectors,
    mom_qkv, mom_out, mom_fc1, mom_fc2, vec_first, vec_second,
):
    half = lax.axis_index("mlp").astype(jnp.int32)
    dp = lax.axis_index("dp").astype(jnp.int32)
    ranks = lax.axis_size("dp")
    model = tokens.shape[1]
    rows = w_fc1.shape[1]
    weights = [flat(w) for w in (w_fc1, w_fc2, w_qkv, w_out)]
    moms = [flat(m) for m in (mom_fc1, mom_fc2, mom_qkv, mom_out)]
    if ranks != 16:
        return general(
            half, image_bucket, bucket_width, bucket_heads, tokens, cotangent,
            weights, moms, vectors, vec_first, vec_second,
        )
    vec = jnp.pad(vectors.T, ((0, 0), (0, PACK - VEC - vectors.shape[0])))
    packed = gather_weights(weights + [vec], ranks)
    out_half, gtok_half, grads = image_pass(
        half.reshape(1), image_bucket, bucket_width, bucket_heads,
        tokens, cotangent, packed.reshape(2, model, PACK),
    )
    grad, mom, buf, out_other, gtok_other = exchange_moments(
        grads.reshape(2, ranks, rows, PACK), moms, out_half, gtok_half
    )
    which = jnp.stack([2 * (dp % 2) + half, half])
    buf = buf.reshape(2, model, PACK)
    (root, norms, gfc1, gfc2, gqkv, gwo, gvec, mfc1, mfc2, mqkv, mwo, vec_new, first, second, output, gtok) = run_chain(
        which, buf, grad, mom, vectors, vec_first, vec_second,
        (out_half, out_other, gtok_half, gtok_other),
    )
    nfc1, nfc2, nqkv, nwo = apply_roots(root.reshape(ranks, rows, model), buf, weights)
    return (
        output, gtok,
        flat(gqkv), flat(gwo), flat(gfc1), flat(gfc2), gvec,
        flat(mqkv), flat(mwo), flat(mfc1), flat(mfc2),
        flat(nqkv), flat(nwo), flat(nfc1), flat(nfc2),
        vec_new, first, second, norms[0, 0:5],
    )


def solution(mesh):
    halves, columns = P("mlp", "dp"), P(None, "dp")
    blocks = P(None, "mlp", "dp")
    matrices = (blocks, halves, halves, halves)
    placed = (P("dp", None), P("dp", None), P("dp"), P(), P()) + matrices + (columns,) + matrices + (columns, columns)
    outs = (P("dp", None), P("dp", None)) + matrices + (columns,) + matrices + matrices + (columns,) * 3 + (P(),)
    return jax.shard_map(body, mesh=mesh, in_specs=placed, out_specs=outs, check_vma=False)
```

```python
import functools
import math

import jax
import jax.numpy as jnp
from jax import lax
from jax.experimental import pallas as pl
from jax.experimental.pallas import tpu as pltpu
from jax.sharding import PartitionSpec as P

HD = 64
NS_ITERS = 5
STEP = 10
EPSILON = 1e-06
F32 = jnp.float32
BF16 = jnp.bfloat16
NN = (((1,), (0,)), ((), ()))
NT = (((1,), (1,)), ((), ()))
TN = (((0,), (0,)), ((), ()))

FC1, FC2, QKV, OUT, VEC, PACK = 0, 768, 1536, 2304, 2560, 2688
SLOT = 256
SEQ = 256
PAIR = 2
CHUNK = 256


def mm(a, b, dims):
    return lax.dot_general(a, b, dims, preferred_element_type=F32)


def lane_sum(v):
    return jnp.sum(v, axis=-1, keepdims=True)


def norm_rows(v):
    inv = 1.0 / v.shape[-1]
    center = v - lane_sum(v) * inv
    factor = lax.rsqrt(lane_sum(center * center) * inv + EPSILON)
    return center * factor, factor


def norm_back(g, n, factor):
    inv = 1.0 / g.shape[-1]
    return factor * (g - lane_sum(g) * inv - n * (lane_sum(g * n) * inv))


def image_kernel(
    half_ref, bucket_ref, widths_ref, counts_ref,
    tok_ref, cot_ref, w_ref,
    out_ref, gtok_ref, grad_ref,
    acc_ref, vec_ref, gvec_ref, q_ref, k_ref, v_ref, mixed_ref, probs_ref, low_ref,
    y_ref, gh_ref,
):
    step = pl.program_id(0)
    rows, model = tok_ref.shape
    heads_half = 3
    pack = rows // SEQ
    first = (half_ref[0] * pl.num_programs(0) + step) * pack
    buckets = [bucket_ref[first + image] for image in range(pack)]
    widths = [widths_ref[bucket] for bucket in buckets]
    counts = [counts_ref[bucket] for bucket in buckets]
    width, count = widths[0], counts[0]
    for image in range(1, pack):
        width, count = jnp.maximum(width, widths[image]), jnp.maximum(count, counts[image])
    row_ids = lax.broadcasted_iota(jnp.int32, (rows, 1), 0)
    row_width = jnp.full((rows, 1), widths[0], jnp.int32)
    for image in range(1, pack):
        row_width = jnp.where(row_ids >= image * SEQ, widths[image], row_width)

    @pl.when(step == 0)
    def _():
        acc_ref[...] = jnp.zeros_like(acc_ref)
        gvec_ref[...] = jnp.zeros_like(gvec_ref)
        turned = w_ref[0, :, VEC:PACK].astype(F32).T
        vec_ref[...] = turned[0:8]

    lane_head = lax.broadcasted_iota(jnp.int32, (1, SLOT), 1) // HD
    masks = [(lane_head == s).astype(F32).astype(BF16) for s in range(heads_half)]

    def used_heads(image):
        return (lane_head < counts[image] - heads_half).astype(F32)

    def spans():
        return [slice(image * SEQ, (image + 1) * SEQ) for image in range(pack)]

    x = tok_ref[...].astype(F32)
    normed_one, factor_one = norm_rows(x)
    hidden_one = (normed_one * vec_ref[0:1] + vec_ref[1:2]).astype(BF16)
    for half in range(2):
        for ref, which in ((q_ref, 0), (k_ref, 1), (v_ref, 2)):
            lanes = slice(QKV + which * SLOT, QKV + (which + 1) * SLOT)
            ref[half] = mm(hidden_one, w_ref[half, :, lanes], NN).astype(BF16)

        def attend():
            for image, span in enumerate(spans()):
                total = None
                for s in range(heads_half):
                    slot = (image * 2 + half) * heads_half + s
                    scores = mm(q_ref[half, span] * masks[s], k_ref[half, span], NT) * 0.125
                    top = jnp.max(scores, axis=-1, keepdims=True)
                    grown = jnp.exp(scores - top)
                    probs = grown * (1.0 / lane_sum(grown))
                    low = probs.astype(BF16)
                    probs_ref[slot] = probs
                    low_ref[slot] = low
                    term = mm(low, v_ref[half, span] * masks[s], NN)
                    total = term if total is None else total + term
                if half:
                    total = total * used_heads(image)
                mixed_ref[half, span] = total.astype(BF16)

        if half == 0:
            attend()
        else:
            mixed_ref[half] = jnp.zeros_like(mixed_ref[half])
            pl.when(count > heads_half)(attend)

    branch = mm(mixed_ref[0], w_ref[0, :, OUT:VEC], NT) + mm(mixed_ref[1], w_ref[1, :, OUT:VEC], NT)
    resid = x + branch + vec_ref[4:5]
    normed_two, factor_two = norm_rows(resid)
    hidden_two = (normed_two * vec_ref[2:3] + vec_ref[3:4]).astype(BF16)
    cot = cot_ref[...]
    hidden_two_t = hidden_two.T
    cot_t = cot.T
    y_ref[...] = resid + vec_ref[5:6]
    gh_ref[...] = jnp.zeros_like(gh_ref)
    per_half = FC2 // CHUNK
    for chunk in range(2 * per_half):
        half, part = divmod(chunk, per_half)
        one = slice(FC1 + part * CHUNK, FC1 + (part + 1) * CHUNK)
        two = slice(FC2 + part * CHUNK, FC2 + (part + 1) * CHUNK)

        def units_pass():
            pre = mm(hidden_two, w_ref[half, :, one], NN)
            units = chunk * CHUNK + lax.broadcasted_iota(jnp.int32, pre.shape, 1)
            cumulative = 0.5 + 0.5 * lax.erf(pre * 0.7071067811865476)
            density = jnp.exp(-0.5 * pre * pre) * 0.3989422804014327
            cumulative = jnp.where(units < row_width, cumulative, 0.0)
            density = jnp.where(units < row_width, density, 0.0)
            act = (pre * cumulative).astype(BF16)
            grad_act = mm(cot, w_ref[half, :, two], NN)
            grad_pre = (grad_act * (cumulative + pre * density)).astype(BF16)
            y_ref[...] += mm(act, w_ref[half, :, two], NT)
            gh_ref[...] += mm(grad_pre, w_ref[half, :, one], NT)
            acc_ref[half, :, two] += mm(cot_t, act, NN)
            acc_ref[half, :, one] += mm(hidden_two_t, grad_pre, NN)

        if chunk < 2:
            units_pass()
        else:
            pl.when(width > chunk * CHUNK)(units_pass)

    out_ref[...] = y_ref[...]
    grad_hidden_two = gh_ref[...]
    cot_f = cot.astype(F32)
    grad_resid = cot_f + norm_back(grad_hidden_two * vec_ref[2:3], normed_two, factor_two)
    resid_low = grad_resid.astype(BF16)
    resid_low_t = resid_low.T
    hidden_one_t = hidden_one.T
    for half in range(2):
        acc_ref[half, :, OUT:VEC] += mm(resid_low_t, mixed_ref[half], NN)

        def back():
            grad_heads = mm(resid_low, w_ref[half, :, OUT:VEC], NN).astype(BF16)
            parts = []
            for image, span in enumerate(spans()):
                heads = grad_heads[span]
                if half:
                    heads = heads * used_heads(image).astype(BF16)
                sums = [None, None, None]
                for s in range(heads_half):
                    slot = (image * 2 + half) * heads_half + s
                    own = heads * masks[s]
                    grad_probs = mm(own, v_ref[half, span], NT)
                    probs = probs_ref[slot]
                    weighed = probs * grad_probs
                    grad_scores = (weighed - probs * lane_sum(weighed)).astype(BF16)
                    terms = (
                        mm(grad_scores, k_ref[half, span] * masks[s], NN),
                        mm(grad_scores, q_ref[half, span] * masks[s], TN),
                        mm(low_ref[slot], own, TN),
                    )
                    sums = [t if o is None else o + t for o, t in zip(sums, terms)]
                parts.append([(v * c).astype(BF16) for v, c in zip(sums, (0.125, 0.125, 1.0))])
            total = None
            for which in range(3):
                lanes = slice(QKV + which * SLOT, QKV + (which + 1) * SLOT)
                grad_proj = jnp.concatenate([part[which] for part in parts], axis=0)
                acc_ref[half, :, lanes] += mm(hidden_one_t, grad_proj, NN)
                term = mm(grad_proj, w_ref[half, :, lanes], NT)
                total = term if total is None else total + term
            return total

        if half == 0:
            gh_ref[...] = back()
        else:

            @pl.when(count > heads_half)
            def _():
                gh_ref[...] += back()

    grad_hidden_one = gh_ref[...]
    gtok_ref[...] = grad_resid + norm_back(grad_hidden_one * vec_ref[0:1], normed_one, factor_one)
    sums = (
        grad_hidden_one * normed_one,
        grad_hidden_one,
        grad_hidden_two * normed_two,
        grad_hidden_two,
        grad_resid,
        cot_f,
    )
    for row, values in enumerate(sums):
        gvec_ref[row : row + 1] += jnp.sum(values, axis=0, keepdims=True)

    @pl.when(step == pl.num_programs(0) - 1)
    def _():
        grad_ref[0, :, 0:VEC] = acc_ref[0].astype(BF16)
        grad_ref[1, :, 0:VEC] = acc_ref[1].astype(BF16)
        columns = gvec_ref[...].T.astype(BF16)
        grad_ref[0, :, VEC:PACK] = columns
        grad_ref[1, :, VEC:PACK] = columns


def image_pass(half, bucket, widths, counts, tokens, cotangent, packed):
    images = bucket.shape[0] // 2
    model = tokens.shape[1]
    rows = images * SEQ
    images = images // PAIR
    seq = PAIR * SEQ
    picked = pl.BlockSpec((seq, model), lambda i, h, b, w, c: (h[0] * images + i, 0))
    placed = pl.BlockSpec((seq, model), lambda i, h, b, w, c: (i, 0))
    whole = pl.BlockSpec(
        (2, model, PACK), lambda i, h, b, w, c: (0, 0, 0), pipeline_mode=pl.Buffered(1)
    )
    heads = 6
    flops = 2 * rows * model * (3 * 4 * model + 3 * 8 * model)
    return pl.pallas_call(
        image_kernel,
        out_shape=(
            jax.ShapeDtypeStruct((rows, model), F32),
            jax.ShapeDtypeStruct((rows, model), F32),
            jax.ShapeDtypeStruct((2, model, PACK), BF16),
        ),
        grid_spec=pltpu.PrefetchScalarGridSpec(
            num_scalar_prefetch=4,
            grid=(images,),
            in_specs=[picked, picked, whole],
            out_specs=[placed, placed, whole],
            scratch_shapes=[
                pltpu.VMEM((2, model, VEC), F32),
                pltpu.VMEM((8, model), F32),
                pltpu.VMEM((128, model), F32),
                pltpu.VMEM((2, seq, SLOT), BF16),
                pltpu.VMEM((2, seq, SLOT), BF16),
                pltpu.VMEM((2, seq, SLOT), BF16),
                pltpu.VMEM((2, seq, SLOT), BF16),
                pltpu.VMEM((PAIR * heads, SEQ, SEQ), F32),
                pltpu.VMEM((PAIR * heads, SEQ, SEQ), BF16),
                pltpu.VMEM((seq, model), F32),
                pltpu.VMEM((seq, model), F32),
            ],
        ),
        compiler_params=pltpu.CompilerParams(vmem_limit_bytes=56 * 1024 * 1024),
        cost_estimate=pl.CostEstimate(flops=flops, bytes_accessed=20 * rows * model, transcendentals=rows * 6144),
        name="image_pass",
    )(half, bucket, widths, counts, tokens, cotangent, packed)


MESH = pl.DeviceIdType.MESH
AT_OUT, AT_VEC, AT = 768, 1024, 1152
FC = 1536


class Place:
    def __init__(self):
        dp = lax.axis_index("dp")
        self.half = lax.axis_index("mlp")
        self.z = dp // 4
        self.y = (dp // 2) % 2
        self.x = dp % 2
        self.dp = dp
        self.y_peer = (self.index(self.z, 1 - self.y, self.x), self.half)
        self.x_peer = (self.index(self.z, self.y, 1 - self.x), self.half)
        self.sibling = (self.dp, 1 - self.half)

    def index(self, z, y, x):
        return z * 4 + y * 2 + x

    def at_z(self, z):
        return (self.index(z, self.y, self.x), self.half)


def meet(place):
    barrier = pltpu.get_barrier_semaphore()
    peers = [place.at_z((place.z + j) % 4) for j in range(1, 4)]
    peers += [place.y_peer, place.x_peer, place.sibling]
    for peer in peers:
        pl.semaphore_signal(barrier, inc=1, device_id=peer, device_id_type=MESH)
    pl.semaphore_wait(barrier, len(peers))


class Mail:
    def __init__(self, place, send_sem, recv_sem):
        self.place, self.send_sem, self.recv_sem = place, send_sem, recv_sem

    def copy(self, slot, src, dst, peer):
        return pltpu.make_async_remote_copy(
            src_ref=src,
            dst_ref=dst,
            send_sem=self.send_sem.at[slot],
            recv_sem=self.recv_sem.at[slot],
            device_id=peer,
            device_id_type=MESH,
        )

    def start(self, slot, src, dst, peer):
        self.copy(slot, src, dst, peer).start()

    def arrived(self, slot, like):
        self.copy(slot, like, like, self.place.sibling).wait_recv()

    def left(self, slot, like):
        self.copy(slot, like, like, self.place.sibling).wait_send()


GATHER_SLOTS = 35


class Gather:
    def __init__(self, place, own, buf, cut, send_sem, recv_sem):
        self.place, self.own, self.buf = place, own, buf
        self.mail = Mail(place, send_sem, recv_sem)
        self.pieces = (pl.ds(0, cut), pl.ds(cut, own.shape[1] - cut))

    def shard(self, k, y, x):
        return self.place.index((self.place.z + 4 - k) % 4, y, x)

    def forward(self, slot, dp, peer, piece=None):
        ref = self.buf.at[self.place.half, dp]
        if piece is not None:
            ref = ref.at[:, self.pieces[piece]]
        self.mail.start(slot, ref, ref, peer)

    def like(self, piece=None):
        ref = self.buf.at[0, 0]
        return ref if piece is None else ref.at[:, self.pieces[piece]]

    def start(self):
        place = self.place
        home = self.buf.at[place.half, place.dp]
        for j in range(1, 4):
            self.mail.start(j - 1, self.own, home, place.at_z((place.z + j) % 4))
        self.mail.start(3, self.own, home, place.y_peer)
        self.mail.start(7, self.own, home, place.x_peer)
        self.mail.start(19, self.own, home, place.sibling)

    def column(self, k):
        place = self.place
        self.mail.arrived(k - 1, self.like())
        dp = self.shard(k, place.y, place.x)
        self.forward(3 + k, dp, place.y_peer)
        self.forward(7 + k, dp, place.x_peer)
        self.forward(19 + k, dp, place.sibling)

    def plane(self, k):
        place = self.place
        self.mail.arrived(3 + k, self.like())
        dp = self.shard(k, 1 - place.y, place.x)
        self.forward(11 + k, dp, place.x_peer, 0)
        self.forward(23 + k, dp, place.sibling)
        self.mail.arrived(7 + k, self.like())
        dp = self.shard(k, place.y, 1 - place.x)
        self.forward(15 + k, dp, place.y_peer, 1)
        self.forward(27 + k, dp, place.sibling)

    def corner(self, k):
        place = self.place
        self.mail.arrived(11 + k, self.like(0))
        self.mail.arrived(15 + k, self.like(1))
        self.forward(31 + k, self.shard(k, 1 - place.y, 1 - place.x), place.sibling)

    def finish(self):
        for k in range(16):
            self.mail.arrived(19 + k, self.like())
        for slot in range(GATHER_SLOTS):
            piece = 0 if 11 <= slot < 15 else 1 if 15 <= slot < 19 else None
            self.mail.left(slot, self.like(piece))

    def rest(self):
        for k in range(1, 4):
            self.column(k)
            self.plane(k - 1)
        self.plane(3)
        for k in range(4):
            self.corner(k)


SCATTER_SLOTS = 43
Z_ORDER = (2, 1, 3, 0)


class Scatter:
    def __init__(self, place, parts, hold, firsts, seconds, last, cut, send_sem, recv_sem):
        self.place, self.parts, self.hold = place, parts, hold
        self.firsts, self.seconds, self.last = firsts, seconds, last
        self.mail = Mail(place, send_sem, recv_sem)
        self.pieces = (pl.ds(0, cut), pl.ds(cut, hold.shape[2] - cut))

    def shard(self, c, k):
        y, x = self.place.y, self.place.x
        column = ((1 - y, 1 - x), (y, 1 - x), (1 - y, x), (y, x))[c]
        return self.place.index((self.place.z + Z_ORDER[k]) % 4, *column)

    def piece(self, dp, p):
        return self.hold.at[dp, :, self.pieces[p]]

    def load(self, dp, p):
        return self.hold[dp, :, self.pieces[p]].astype(F32)

    def start(self):
        half = self.place.half
        for c in range(4):
            for k in range(4):
                dp = self.shard(c, k)
                self.mail.start(4 * c + k, self.parts.at[1 - half, dp], self.hold.at[dp], self.place.sibling)

    def settle(self, c, k):
        dp = self.shard(c, k)
        self.mail.arrived(4 * c + k, self.hold.at[0])
        total = self.hold[dp].astype(F32) + self.parts[self.place.half, dp].astype(F32)
        self.hold[dp] = total.astype(BF16)
        return dp

    def first_hop(self):
        place, (first_a, first_b) = self.place, self.firsts
        for k in range(4):
            dp = self.settle(0, k)
            self.mail.start(16 + k, self.piece(dp, 0), first_a.at[k], place.x_peer)
            self.mail.start(24 + k, self.piece(dp, 1), first_b.at[k], place.y_peer)
        for k in range(4):
            dp = self.settle(1, k)
            self.mail.start(20 + k, self.piece(dp, 0), first_a.at[4 + k], place.x_peer)
            dp = self.settle(2, k)
            self.mail.start(28 + k, self.piece(dp, 1), first_b.at[4 + k], place.y_peer)
        for k in range(4):
            self.settle(3, k)

    def second_hop(self):
        place, firsts, seconds = self.place, self.firsts, self.seconds
        for k in range(4):
            for p, slot, column, out, peer in ((0, 16, 2, 32, place.y_peer), (1, 24, 1, 36, place.x_peer)):
                self.mail.arrived(slot + k, firsts[p].at[0])
                dp = self.shard(column, k)
                total = self.load(dp, p) + firsts[p][k].astype(F32)
                self.hold[dp, :, self.pieces[p]] = total.astype(BF16)
                self.mail.start(out + k, self.piece(dp, p), seconds[p].at[k], peer)

    def last_hop(self, keep):
        place = self.place
        for k in range(4):
            dp = self.shard(3, k)
            totals = []
            for p, slot, second in ((0, 20, 32), (1, 28, 36)):
                self.mail.arrived(slot + k, self.firsts[p].at[0])
                self.mail.arrived(second + k, self.seconds[p].at[0])
                totals.append(self.load(dp, p) + self.firsts[p][4 + k].astype(F32) + self.seconds[p][k].astype(F32))
            for p in range(2):
                if Z_ORDER[k]:
                    self.hold[dp, :, self.pieces[p]] = totals[p].astype(BF16)
                else:
                    keep[:, self.pieces[p]] = totals[p]
            if Z_ORDER[k]:
                j = Z_ORDER[k]
                self.mail.start(40 + j - 1, self.hold.at[dp], self.last.at[j - 1], place.at_z((place.z + j) % 4))

    def finish(self, keep):
        for j in range(3):
            self.mail.arrived(40 + j, self.last.at[0])
            keep[...] = keep[...] + self.last[j].astype(F32)
        for slot in range(SCATTER_SLOTS):
            if slot < 16 or slot >= 40:
                like = self.hold.at[0]
            elif slot < 32:
                like = self.firsts[(slot - 16) // 8].at[0]
            else:
                like = self.seconds[(slot - 32) // 4].at[0]
            self.mail.left(slot, like)


def scatter_scratch(ranks, rows, lanes, cut):
    return [
        pltpu.VMEM((ranks, rows, lanes), BF16),
        pltpu.VMEM((8, rows, cut), BF16),
        pltpu.VMEM((8, rows, lanes - cut), BF16),
        pltpu.VMEM((4, rows, cut), BF16),
        pltpu.VMEM((4, rows, lanes - cut), BF16),
        pltpu.VMEM((3, rows, lanes), BF16),
    ]


def dma(count):
    return [pltpu.SemaphoreType.DMA((count,))] * 2


AT_CUT, FC_CUT = 640, 768


def head_masks():
    lane_head = lax.broadcasted_iota(jnp.int32, (1, SLOT), 1) // HD
    return [(lane_head == s).astype(F32).astype(BF16) for s in range(3)]


def used_lanes(counts_ref, image, half):
    lane_head = lax.broadcasted_iota(jnp.int32, (1, SLOT), 1) // HD
    row = counts_ref[pl.ds(image, 1)]
    return jnp.where(lane_head < row[:, 0:1] - 3 * half, 1.0, 0.0)


def token_copy(place, tokens_ref, tok_own, sem):
    count = tok_own.shape[0]
    start = pl.multiple_of(place.half * count, count)
    return pltpu.make_async_copy(tokens_ref.at[pl.ds(start, count)], tok_own, sem)


def own_block(step, rows):
    return pl.ds(pl.multiple_of(step * rows, rows), rows)


def attend_kernel(
    counts_ref, tokens_ref, fc1_ref, fc2_ref, qkv_ref, wo_ref, vecs_ref,
    resid_ref, proj_ref, low_ref, mixed_ref, wt_ref, vec_ref, fc_buf,
    own_at, own_fc, at_buf, tok_own, at_send, at_recv, fc_send, fc_recv, local_sem, tok_sem,
):
    place = Place()
    step = pl.program_id(0)
    steps = pl.num_programs(0)
    rows, model = resid_ref.shape
    pack = rows // SEQ
    tok_copy = token_copy(place, tokens_ref, tok_own, tok_sem)
    slices = Gather(place, own_at, at_buf, AT_CUT, at_send, at_recv)
    units = Gather(place, own_fc, fc_buf, FC_CUT, fc_send, fc_recv)
    local = pltpu.make_async_copy(own_fc, fc_buf.at[place.half, place.dp], local_sem)

    @pl.when(step == 0)
    def _():
        tok_copy.start()
        own_at[...] = jnp.zeros_like(own_at)
        for which in range(3):
            own_at[:, which * SLOT : which * SLOT + qkv_ref.shape[2]] = qkv_ref[which].astype(BF16)
        own_at[:, AT_OUT : AT_OUT + wo_ref.shape[1]] = wo_ref[...].astype(BF16)
        own_at[:, AT_VEC:AT] = vecs_ref[...].astype(BF16)
        own_fc[:, 0 : FC // 2] = fc1_ref[...].astype(BF16)
        own_fc[:, FC // 2 : FC] = fc2_ref[...].astype(BF16)
        at_buf[place.half, place.dp] = own_at[...]
        local.start()
        meet(place)
        slices.start()
        slices.rest()
        units.start()
        slices.finish()
        for half in range(2):
            wt_ref[half] = at_buf[half].astype(F32).reshape(model, AT).astype(BF16)
        vec_ref[...] = wt_ref[0, :, AT_VEC:AT].astype(F32).T[0:8]
        tok_copy.wait()

    @pl.when(step == 1)
    def _():
        for k in range(1, 4):
            units.column(k)

    @pl.when(step == 2)
    def _():
        for k in range(4):
            units.plane(k)

    @pl.when(step == steps - 1)
    def _():
        for k in range(4):
            units.corner(k)

    masks = head_masks()
    x = tok_own[own_block(step, rows)].astype(F32)
    normed_one, _ = norm_rows(x)
    hidden_one = (normed_one * vec_ref[0:1] + vec_ref[1:2]).astype(BF16)
    branch = None
    for half in range(2):
        base = half * 3 * SLOT
        proj = []
        for which in range(3):
            part = mm(hidden_one, wt_ref[half, :, which * SLOT : (which + 1) * SLOT], NN).astype(BF16)
            proj_ref[:, base + which * SLOT : base + (which + 1) * SLOT] = part
            proj.append(part)
        mixes = []
        for image in range(pack):
            span = slice(image * SEQ, (image + 1) * SEQ)
            queries, keys, values = (part[span] for part in proj)
            total = None
            for s in range(3):
                scores = mm(queries * masks[s], keys, NT) * 0.125
                top = jnp.max(scores, axis=-1, keepdims=True)
                grown = jnp.exp(scores - top)
                low = (grown * (1.0 / lane_sum(grown))).astype(BF16)
                low_ref[(image * 2 + half) * 3 + s] = low
                term = mm(low, values * masks[s], NN)
                total = term if total is None else total + term
            mixes.append((total * used_lanes(counts_ref, step * pack + image, half)).astype(BF16))
        mixed = jnp.concatenate(mixes, axis=0)
        mixed_ref[:, half * SLOT : (half + 1) * SLOT] = mixed
        term = mm(mixed, wt_ref[half, :, AT_OUT:AT_VEC], NT)
        branch = term if branch is None else branch + term
    resid_ref[...] = x + branch + vec_ref[4:5]

    @pl.when(step == steps - 1)
    def _():
        units.finish()
        local.wait()


def const(shape, **kw):
    return pl.BlockSpec(shape, lambda i, *_: (0,) * len(shape), **kw)


def once(shape):
    return const(shape, pipeline_mode=pl.Buffered(1))


def attend_pass(counts, tokens, weights, vec, ranks):
    model = tokens.shape[1]
    images = counts.shape[0]
    rows = weights[0].shape[0]
    count = images * SEQ
    steps = images // PAIR
    block = PAIR * SEQ

    def by_step(lanes):
        return pl.BlockSpec((block, lanes), lambda i: (i, 0))

    return pl.pallas_call(
        attend_kernel,
        out_shape=(
            jax.ShapeDtypeStruct((count, model), F32),
            jax.ShapeDtypeStruct((count, 6 * SLOT), BF16),
            jax.ShapeDtypeStruct((images * 6, SEQ, SEQ), BF16),
            jax.ShapeDtypeStruct((count, 2 * SLOT), BF16),
            jax.ShapeDtypeStruct((2, model, AT), BF16),
            jax.ShapeDtypeStruct((8, model), F32),
            jax.ShapeDtypeStruct((2, ranks, rows, FC), BF16),
        ),
        grid_spec=pltpu.PrefetchScalarGridSpec(
            num_scalar_prefetch=0,
            grid=(steps,),
            in_specs=[once(counts.shape), pl.BlockSpec(memory_space=pl.ANY)]
            + [once(w.shape) for w in weights]
            + [once(vec.shape)],
            out_specs=[
                by_step(model),
                by_step(6 * SLOT),
                pl.BlockSpec((PAIR * 6, SEQ, SEQ), lambda i: (i, 0, 0)),
                by_step(2 * SLOT),
                once((2, model, AT)),
                once((8, model)),
                pl.BlockSpec(memory_space=pl.ANY),
            ],
            scratch_shapes=[
                pltpu.VMEM((rows, AT), BF16),
                pltpu.VMEM((rows, FC), BF16),
                pltpu.VMEM((2, ranks, rows, AT), BF16),
                pltpu.VMEM((count, model), BF16),
            ]
            + dma(GATHER_SLOTS)
            + dma(GATHER_SLOTS)
            + [pltpu.SemaphoreType.DMA] * 2,
        ),
        compiler_params=pltpu.CompilerParams(
            collective_id=0, has_side_effects=True, vmem_limit_bytes=56 * 1024 * 1024
        ),
        name="attend_pass",
    )(counts, tokens, *weights, vec)


def units_kernel(
    half_ref, bucket_ref, widths_ref, resid_ref, cot_ref, w_ref, vec_ref,
    out_ref, gres_ref, grad_ref, gvec_ref, acc_ref, y_ref, gh_ref,
):
    step = pl.program_id(0)
    rows, model = resid_ref.shape
    pack = rows // SEQ
    first = (half_ref[0] * pl.num_programs(0) + step) * pack
    widths = [widths_ref[bucket_ref[first + image]] for image in range(pack)]
    row_ids = lax.broadcasted_iota(jnp.int32, (rows, 1), 0)
    width, row_width = widths[0], jnp.full((rows, 1), widths[0], jnp.int32)
    for image in range(1, pack):
        width = jnp.maximum(width, widths[image])
        row_width = jnp.where(row_ids >= image * SEQ, widths[image], row_width)

    @pl.when(step == 0)
    def _():
        acc_ref[...] = jnp.zeros_like(acc_ref)
        gvec_ref[...] = jnp.zeros_like(gvec_ref)

    resid = resid_ref[...]
    normed_two, factor_two = norm_rows(resid)
    hidden_two = (normed_two * vec_ref[2:3] + vec_ref[3:4]).astype(BF16)
    cot = cot_ref[...]
    hidden_two_t = hidden_two.T
    cot_t = cot.T
    y_ref[...] = resid + vec_ref[5:6]
    gh_ref[...] = jnp.zeros_like(gh_ref)
    per_half = FC2 // CHUNK
    for chunk in range(2 * per_half):
        half, part = divmod(chunk, per_half)
        one = slice(FC1 + part * CHUNK, FC1 + (part + 1) * CHUNK)
        two = slice(FC2 + part * CHUNK, FC2 + (part + 1) * CHUNK)

        def units_pass():
            pre = mm(hidden_two, w_ref[half, :, one], NN)
            units = chunk * CHUNK + lax.broadcasted_iota(jnp.int32, pre.shape, 1)
            cumulative = 0.5 + 0.5 * lax.erf(pre * 0.7071067811865476)
            density = jnp.exp(-0.5 * pre * pre) * 0.3989422804014327
            cumulative = jnp.where(units < row_width, cumulative, 0.0)
            density = jnp.where(units < row_width, density, 0.0)
            act = (pre * cumulative).astype(BF16)
            grad_act = mm(cot, w_ref[half, :, two], NN)
            grad_pre = (grad_act * (cumulative + pre * density)).astype(BF16)
            y_ref[...] += mm(act, w_ref[half, :, two], NT)
            gh_ref[...] += mm(grad_pre, w_ref[half, :, one], NT)
            acc_ref[half, :, two] += mm(cot_t, act, NN)
            acc_ref[half, :, one] += mm(hidden_two_t, grad_pre, NN)

        if chunk < 2:
            units_pass()
        else:
            pl.when(width > chunk * CHUNK)(units_pass)

    out_ref[...] = y_ref[...]
    grad_hidden_two = gh_ref[...]
    cot_f = cot.astype(F32)
    grad_resid = cot_f + norm_back(grad_hidden_two * vec_ref[2:3], normed_two, factor_two)
    gres_ref[...] = grad_resid
    sums = (grad_hidden_two * normed_two, grad_hidden_two, grad_resid, cot_f)
    for row, values in enumerate(sums):
        gvec_ref[2 + row : 3 + row] += jnp.sum(values, axis=0, keepdims=True)

    @pl.when(step == pl.num_programs(0) - 1)
    def _():
        grad_ref[...] = acc_ref[...].astype(BF16)


def units_pass(half, bucket, widths, resid, cotangent, packed, vec):
    count, model = resid.shape
    block = PAIR * SEQ
    steps = count // block
    placed = pl.BlockSpec((block, model), lambda i, h, b, w: (i, 0))
    picked = pl.BlockSpec((block, model), lambda i, h, b, w: (h[0] * steps + i, 0))
    return pl.pallas_call(
        units_kernel,
        out_shape=(
            jax.ShapeDtypeStruct((count, model), F32),
            jax.ShapeDtypeStruct((count, model), F32),
            jax.ShapeDtypeStruct((2, model, FC), BF16),
            jax.ShapeDtypeStruct((8, model), F32),
        ),
        grid_spec=pltpu.PrefetchScalarGridSpec(
            num_scalar_prefetch=3,
            grid=(steps,),
            in_specs=[placed, picked, once(packed.shape), once(vec.shape)],
            out_specs=[placed, placed, once((2, model, FC)), once((8, model))],
            scratch_shapes=[
                pltpu.VMEM((2, model, FC), F32),
                pltpu.VMEM((block, model), F32),
                pltpu.VMEM((block, model), F32),
            ],
        ),
        compiler_params=pltpu.CompilerParams(vmem_limit_bytes=56 * 1024 * 1024),
        name="units_pass",
    )(half, bucket, widths, resid, cotangent, packed, vec)


def back_kernel(
    counts_ref, tokens_ref, gres_ref, proj_ref, low_ref, mixed_ref, wt_ref, vec_ref, gvec_ref,
    fc_parts, fc1_ref, fc2_ref, qkv_ref, wo_ref, out_half,
    gtok_ref, grad_fc, mom_fc, grad_at, mom_at, fc_buf, at_buf, out_other,
    acc_ref, sums_ref, gtok_own, at_parts, own_fc, own_at, tok_own,
    fc_hold, fc_first_a, fc_first_b, fc_second_a, fc_second_b, fc_last,
    at_hold, at_first_a, at_first_b, at_second_a, at_second_b, at_last,
    fcs_send, fcs_recv, ats_send, ats_recv, fcg_send, fcg_recv, atg_send, atg_recv,
    side_send, side_recv, local_sems,
):
    place = Place()
    step = pl.program_id(0)
    steps = pl.num_programs(0)
    rows, model = gres_ref.shape
    tok_copy = token_copy(place, tokens_ref, tok_own, local_sems.at[0])
    pack = rows // SEQ
    count = gtok_ref.shape[0] // 2
    fc_sum = Scatter(
        place, fc_parts, fc_hold, (fc_first_a, fc_first_b), (fc_second_a, fc_second_b), fc_last,
        FC_CUT, fcs_send, fcs_recv,
    )
    at_sum = Scatter(
        place, at_parts, at_hold, (at_first_a, at_first_b), (at_second_a, at_second_b), at_last,
        AT_CUT, ats_send, ats_recv,
    )
    fc_all = Gather(place, own_fc, fc_buf, FC_CUT, fcg_send, fcg_recv)
    at_all = Gather(place, own_at, at_buf, AT_CUT, atg_send, atg_recv)
    side = Mail(place, side_send, side_recv)
    fc_home = pltpu.make_async_copy(own_fc, fc_buf.at[place.half, place.dp], local_sems.at[1])
    at_home = pltpu.make_async_copy(own_at, at_buf.at[place.half, place.dp], local_sems.at[2])

    @pl.when(step == 0)
    def _():
        tok_copy.start()
        meet(place)
        fc_sum.start()
        tok_copy.wait()
        side.start(0, out_half, out_other, place.sibling)
        acc_ref[...] = jnp.zeros_like(acc_ref)
        sums_ref[...] = jnp.zeros_like(sums_ref)
        sums_ref[0:8] = gvec_ref[...]

    @pl.when(step == 1)
    def _():
        fc_sum.second_hop()

    @pl.when(step == 2)
    def _():
        fc_sum.last_hop(grad_fc)

    @pl.when(step == 3)
    def _():
        fc_all.column(1)
        fc_all.column(2)
        fc_all.column(3)

    masks = head_masks()
    normed_one, factor_one = norm_rows(tok_own[own_block(step, rows)].astype(F32))
    hidden_one_t = (normed_one * vec_ref[0:1] + vec_ref[1:2]).astype(BF16).T
    grad_resid = gres_ref[...]
    resid_low = grad_resid.astype(BF16)
    resid_low_t = resid_low.T
    grad_hidden_one = None
    for half in range(2):
        base = half * 3 * SLOT
        mixed = mixed_ref[:, half * SLOT : (half + 1) * SLOT]
        acc_ref[half, :, AT_OUT:AT_VEC] += mm(resid_low_t, mixed, NN)
        grad_heads = mm(resid_low, wt_ref[half, :, AT_OUT:AT_VEC], NN).astype(BF16)
        parts = []
        for image in range(pack):
            span = slice(image * SEQ, (image + 1) * SEQ)
            used = used_lanes(counts_ref, step * pack + image, half).astype(BF16)
            heads = grad_heads[span] * used
            queries, keys, values = (
                proj_ref[span, base + which * SLOT : base + (which + 1) * SLOT] for which in range(3)
            )
            sums = [None, None, None]
            for s in range(3):
                own = heads * masks[s]
                low = low_ref[(image * 2 + half) * 3 + s]
                grad_probs = mm(own, values, NT)
                probs = low.astype(F32)
                weighed = probs * grad_probs
                grad_scores = (weighed - probs * lane_sum(weighed)).astype(BF16)
                terms = (
                    mm(grad_scores, keys * masks[s], NN),
                    mm(grad_scores, queries * masks[s], TN),
                    mm(low, own, TN),
                )
                sums = [t if o is None else o + t for o, t in zip(sums, terms)]
            parts.append([(v * c).astype(BF16) for v, c in zip(sums, (0.125, 0.125, 1.0))])
        for which in range(3):
            lanes = slice(which * SLOT, (which + 1) * SLOT)
            grad_proj = jnp.concatenate([part[which] for part in parts], axis=0)
            acc_ref[half, :, lanes] += mm(hidden_one_t, grad_proj, NN)
            term = mm(grad_proj, wt_ref[half, :, lanes], NT)
            grad_hidden_one = term if grad_hidden_one is None else grad_hidden_one + term
        if half == 0:

            @pl.when(step == 0)
            def _():
                fc_sum.first_hop()

            @pl.when(step == 2)
            def _():
                fc_sum.finish(grad_fc)
                mom_fc[:, 0 : FC // 2] = 0.95 * fc1_ref[...]
                mom_fc[:, FC // 2 : FC] = 0.95 * fc2_ref[...]
                mom_fc[...] = mom_fc[...] + grad_fc[...]
                own_fc[...] = mom_fc[...].astype(BF16)
                fc_home.start()
                fc_all.start()

            @pl.when(step == 3)
            def _():
                for k in range(4):
                    fc_all.plane(k)

    gtok_own[step] = grad_resid + norm_back(grad_hidden_one * vec_ref[0:1], normed_one, factor_one)
    sums_ref[0:1] += jnp.sum(grad_hidden_one * normed_one, axis=0, keepdims=True)
    sums_ref[1:2] += jnp.sum(grad_hidden_one, axis=0, keepdims=True)

    def own_rows(index):
        start = place.half * count + index * rows
        return gtok_ref.at[pl.ds(pl.multiple_of(start, rows), rows)]

    @pl.when(step == steps - 1)
    def _():
        columns = sums_ref[...].T
        ranks, own = at_parts.shape[1], at_parts.shape[2]
        for half in range(2):
            for dp in range(ranks):
                span = slice(dp * own, (dp + 1) * own)
                at_parts[half, dp, :, 0:AT_VEC] = acc_ref[half, span].astype(BF16)
                at_parts[half, dp, :, AT_VEC:AT] = columns[span].astype(BF16)
        at_sum.start()
        at_sum.first_hop()
        for index in range(gtok_own.shape[0]):
            side.start(1 + index, gtok_own.at[index], own_rows(index), place.sibling)
            pltpu.make_async_copy(gtok_own.at[index], own_rows(index), local_sems.at[3 + index]).start()
        for k in range(4):
            fc_all.corner(k)
        mom_at[...] = jnp.zeros_like(mom_at)
        for which in range(3):
            mom_at[:, which * SLOT : which * SLOT + qkv_ref.shape[2]] = 0.95 * qkv_ref[which]
        mom_at[:, AT_OUT : AT_OUT + wo_ref.shape[1]] = 0.95 * wo_ref[...]
        at_sum.second_hop()
        at_sum.last_hop(grad_at)
        at_sum.finish(grad_at)
        mom_at[...] = mom_at[...] + grad_at[:, 0:AT_VEC]
        own_at[:, 0:AT_VEC] = mom_at[...].astype(BF16)
        lanes = lax.broadcasted_iota(jnp.int32, (own, 128), 1)
        tile = jnp.zeros(lanes.shape, F32)
        pieces = (
            grad_at[:, 0:AT_OUT], grad_at[:, AT_OUT:AT_VEC], grad_fc[:, 0 : FC // 2],
            grad_fc[:, FC // 2 : FC], grad_at[:, AT_VEC:AT],
        )
        for number, piece in enumerate(pieces):
            square = jnp.sum(lane_sum(piece * piece), axis=0, keepdims=True)
            square = jnp.broadcast_to(square * (0.5 if number == 4 else 1.0), lanes.shape)
            high = square.astype(BF16).astype(F32)
            tile = jnp.where(lanes == number, high, tile)
            tile = jnp.where(lanes == 64 + number, square - high, tile)
        own_at[:, AT_VEC:AT] = tile.astype(BF16)
        at_home.start()
        at_all.start()
        at_all.rest()
        at_all.finish()
        fc_all.finish()
        side.arrived(0, out_half)
        side.left(0, out_half)
        for index in range(gtok_own.shape[0]):
            side.arrived(1 + index, gtok_own.at[0])
            side.left(1 + index, gtok_own.at[0])
            pltpu.make_async_copy(gtok_own.at[index], own_rows(index), local_sems.at[3 + index]).wait()
        fc_home.wait()
        at_home.wait()


def back_pass(counts, tokens, gres, proj, low, mixed, wt, vec, gvec, fc_parts, moms, out_half):
    count, model = gres.shape
    _, ranks, rows, _ = fc_parts.shape
    block = PAIR * SEQ
    steps = count // block

    def by_step(lanes):
        return pl.BlockSpec((block, lanes), lambda i: (i, 0))

    anywhere = pl.BlockSpec(memory_space=pl.ANY)
    return pl.pallas_call(
        back_kernel,
        out_shape=(
            jax.ShapeDtypeStruct((2 * count, model), F32),
            jax.ShapeDtypeStruct((rows, FC), F32),
            jax.ShapeDtypeStruct((rows, FC), F32),
            jax.ShapeDtypeStruct((rows, AT), F32),
            jax.ShapeDtypeStruct((rows, AT_VEC), F32),
            jax.ShapeDtypeStruct((2, ranks, rows, FC), BF16),
            jax.ShapeDtypeStruct((2, ranks, rows, AT), BF16),
            jax.ShapeDtypeStruct((count, model), F32),
        ),
        grid_spec=pltpu.PrefetchScalarGridSpec(
            num_scalar_prefetch=0,
            grid=(steps,),
            in_specs=[
                once(counts.shape),
                anywhere,
                by_step(model),
                by_step(6 * SLOT),
                pl.BlockSpec((PAIR * 6, SEQ, SEQ), lambda i: (i, 0, 0)),
                by_step(2 * SLOT),
                once(wt.shape),
                once(vec.shape),
                once(gvec.shape),
                once(fc_parts.shape),
            ]
            + [once(m.shape) for m in moms]
            + [anywhere],
            out_specs=[
                anywhere,
                once((rows, FC)),
                once((rows, FC)),
                once((rows, AT)),
                once((rows, AT_VEC)),
                anywhere,
                anywhere,
                anywhere,
            ],
            scratch_shapes=[
                pltpu.VMEM((2, model, AT_VEC), F32),
                pltpu.VMEM((128, model), F32),
                pltpu.VMEM((steps, block, model), F32),
                pltpu.VMEM((2, ranks, rows, AT), BF16),
                pltpu.VMEM((rows, FC), BF16),
                pltpu.VMEM((rows, AT), BF16),
                pltpu.VMEM((count, model), BF16),
            ]
            + scatter_scratch(ranks, rows, FC, FC_CUT)
            + scatter_scratch(ranks, rows, AT, AT_CUT)
            + dma(SCATTER_SLOTS)
            + dma(SCATTER_SLOTS)
            + dma(GATHER_SLOTS)
            + dma(GATHER_SLOTS)
            + dma(1 + steps)
            + [pltpu.SemaphoreType.DMA((3 + steps,))],
        ),
        compiler_params=pltpu.CompilerParams(
            collective_id=1, has_side_effects=True, vmem_limit_bytes=60 * 1024 * 1024
        ),
        name="back_pass",
    )(counts, tokens, gres, proj, low, mixed, wt, vec, gvec, fc_parts, *moms, out_half)


QUINTIC = (3.4445, -4.775, 2.0315)
RATES = (2.0, 2.0, math.sqrt(3.0), math.sqrt(32.0))
RANGES = ((0, FC // 2), (FC // 2, FC), (0, AT_OUT), (AT_OUT, AT_VEC))


def mm3(a, b):
    return lax.dot_general(a, b, NN, precision=lax.Precision.HIGH, preferred_element_type=F32)


def eye_mask(n):
    return lax.broadcasted_iota(jnp.int32, (n, n), 0) == lax.broadcasted_iota(jnp.int32, (n, n), 1)


def chain_kernel(
    which_ref, fc_ref, at_ref, grad_fc, mom_fc, grad_at, mom_at, vec_ref, first_ref, second_ref,
    out_half, out_other, gtok_both,
    root_ref, norm_ref, gfc1, gfc2, gqkv, gwo, gvec, mfc1, mfc2, mqkv, mwo,
    vec_new, first_new, second_new, out_ref, gtok_ref,
    gram_ref, poly_ref, turn_ref, out_hold, gtok_hold, sems,
):
    count = out_half.shape[0]
    half = which_ref[1]
    sources = ((out_half, out_hold.at[0]), (out_other, out_hold.at[1]), (gtok_both, gtok_hold))
    loads = [pltpu.make_async_copy(src, hold, sems.at[i]) for i, (src, hold) in enumerate(sources)]
    stores = []
    for i, part in enumerate((half, 1 - half)):
        rows = pl.ds(pl.multiple_of(part * count, 8), count)
        stores.append(pltpu.make_async_copy(out_hold.at[i], out_ref.at[rows], sems.at[3 + i]))
    stores.append(pltpu.make_async_copy(gtok_hold, gtok_ref, sems.at[5]))
    for load in loads:
        load.start()
    model = fc_ref.shape[1]
    for number, (start, stop) in enumerate(RANGES):
        buf = fc_ref if number < 2 else at_ref

        @pl.when(which_ref[0] == number)
        def _():
            lower, upper = buf[0, :, start:stop], buf[1, :, start:stop]
            gram_ref[...] = mm(lower, lower, NT) + mm(upper, upper, NT)

    eye = eye_mask(model)
    gram = gram_ref[...]
    total = jnp.sum(lane_sum(jnp.where(eye, gram, 0.0)), axis=0, keepdims=True)
    scale = 1.0 / (jnp.sqrt(total) + 1e-07)
    gram_ref[...] = gram * (scale * scale)
    a, b, c = QUINTIC

    def polynomial():
        gram = gram_ref[...]
        return jnp.where(eye, a, 0.0) + b * gram + c * mm3(gram, gram)

    def advance(poly):
        gram_ref[...] = mm3(mm3(gram_ref[...], poly), poly)

    poly = polynomial()
    poly_ref[...] = poly
    advance(poly)
    for load, store in zip(loads, stores):
        load.wait()
        store.start()

    def sweep(_, carry):
        poly = polynomial()
        poly_ref[...] = mm3(poly_ref[...], poly)
        advance(poly)
        return carry

    lax.fori_loop(0, NS_ITERS - 2, sweep, 0)
    root_ref[...] = mm3(poly_ref[...], polynomial()) * scale

    wide = FC // 2
    gfc1[...], gfc2[...] = grad_fc[:, 0:wide], grad_fc[:, wide:FC]
    mfc1[...], mfc2[...] = mom_fc[:, 0:wide], mom_fc[:, wide:FC]
    narrow = gwo.shape[1]
    gwo[...] = grad_at[:, AT_OUT : AT_OUT + narrow]
    mwo[...] = mom_at[:, AT_OUT : AT_OUT + narrow]
    for part in range(3):
        gqkv[part] = grad_at[:, part * SLOT : part * SLOT + narrow]
        mqkv[part] = mom_at[:, part * SLOT : part * SLOT + narrow]
    own = grad_at.shape[0]
    turn_ref[...] = jnp.zeros_like(turn_ref)
    turn_ref[0:own] = grad_at[:, AT_VEC:AT]
    turned = turn_ref[...].T[0:6, 0 : vec_ref.shape[1]]
    first = 0.9 * first_ref[...] + 0.1 * turned
    second = 0.95 * second_ref[...] + 0.05 * turned * turned
    gvec[...] = turned
    first_new[...] = first
    second_new[...] = second
    vec_new[...] = vec_ref[...] - 0.5 * (first / (1.0 - 0.9**STEP)) / (
        jnp.sqrt(second / (1.0 - 0.95**STEP)) + 1e-08
    )
    tiles = at_ref[0, :, AT_VEC:AT].astype(F32) + at_ref[1, :, AT_VEC:AT].astype(F32)
    leads = lax.broadcasted_iota(jnp.int32, tiles.shape, 0) % own == 0
    squares = jnp.sum(jnp.where(leads, tiles, 0.0), axis=0, keepdims=True)
    norm_ref[...] = jnp.sqrt(squares + pltpu.roll(squares, 64, 1))
    for store in stores:
        store.wait()


def run_chain(which, fc_buf, at_buf, grad_fc, mom_fc, grad_at, mom_at, vectors, first, second, wholes):
    model = fc_buf.shape[1]
    own, columns = grad_fc.shape[0], vectors.shape[1]
    count = wholes[0].shape[0]
    full = (2 * count, model)
    vmem = pl.BlockSpec(memory_space=pltpu.VMEM)
    anywhere = pl.BlockSpec(memory_space=pl.ANY)
    shapes = [(own, 768), (own, 768), (3, own, 192), (own, 192)]
    outs = [(model, model), (1, 128)] + shapes + [(6, columns)] + shapes + [(6, columns)] * 3 + [full] * 2
    return pl.pallas_call(
        chain_kernel,
        out_shape=tuple(jax.ShapeDtypeStruct(shape, F32) for shape in outs),
        in_specs=[pl.BlockSpec(memory_space=pltpu.SMEM)] + [vmem] * 9 + [anywhere] * 3,
        out_specs=tuple([vmem] * (len(outs) - 2) + [anywhere] * 2),
        scratch_shapes=[
            pltpu.VMEM((model, model), F32),
            pltpu.VMEM((model, model), F32),
            pltpu.VMEM((128, 128), F32),
            pltpu.VMEM((2, count, model), F32),
            pltpu.VMEM(full, F32),
            pltpu.SemaphoreType.DMA((6,)),
        ],
        compiler_params=pltpu.CompilerParams(vmem_limit_bytes=60 * 1024 * 1024),
        name="run_chain",
    )(which, fc_buf, at_buf, grad_fc, mom_fc, grad_at, mom_at, vectors, first, second, *wholes)


def roots_kernel(
    root_ref, fc_ref, at_ref, fc1_ref, fc2_ref, qkv_ref, wo_ref,
    nfc1, nfc2, nqkv, nwo, rows_ref, send_sem, recv_sem,
):
    place = Place()
    x, half = place.x, place.half
    barrier = pltpu.get_barrier_semaphore()
    peers = [(1 - x, half), (x, 1 - half), (1 - x, 1 - half)]
    ids = [(place.index(place.z, place.y, px), ph) for px, ph in peers]
    for peer in ids:
        pl.semaphore_signal(barrier, inc=1, device_id=peer, device_id_type=MESH)
    pl.semaphore_wait(barrier, 3)
    mail = Mail(place, send_sem, recv_sem)
    mine = 2 * x + half
    for slot, peer in enumerate(ids):
        mail.start(slot, root_ref.at[peer[0]], rows_ref.at[mine], peer)
    rows_ref[mine] = root_ref[place.dp]
    for slot in range(3):
        mail.arrived(slot, rows_ref.at[0])
    for number, (start, stop) in enumerate(RANGES):
        rows = rows_ref[number]
        high = rows.astype(BF16)
        low = (rows - high.astype(F32)).astype(BF16)
        moment = (fc_ref if number < 2 else at_ref)[half, :, start:stop]
        step = RATES[number] * (mm(high, moment, NN) + mm(low, moment, NN))
        if number == 2:
            for part in range(3):
                nqkv[part] = 0.999 * qkv_ref[part] - step[:, part * SLOT : part * SLOT + nqkv.shape[2]]
        else:
            new, old = ((nfc1, fc1_ref), (nfc2, fc2_ref), None, (nwo, wo_ref))[number]
            new[...] = 0.999 * old[...] - step[:, 0 : new.shape[1]]
    for slot in range(3):
        mail.left(slot, rows_ref.at[0])


def apply_roots(root, fc_buf, at_buf, weights):
    ranks, rows, model = root.shape
    vmem = pl.BlockSpec(memory_space=pltpu.VMEM)
    return pl.pallas_call(
        roots_kernel,
        out_shape=tuple(jax.ShapeDtypeStruct(w.shape, F32) for w in weights),
        in_specs=[vmem] * 7,
        out_specs=(vmem,) * 4,
        scratch_shapes=[pltpu.VMEM((4, rows, model), F32)] + dma(3),
        compiler_params=pltpu.CompilerParams(
            collective_id=2, has_side_effects=True, vmem_limit_bytes=40 * 1024 * 1024
        ),
        name="apply_roots",
    )(root, fc_buf, at_buf, *weights)


def flat(part):
    return part.T if part.ndim == 2 else jnp.transpose(part, (0, 2, 1))


def pack(fc1, fc2, qkv, out):
    pad = ((0, 0), (0, SLOT - out.shape[1]))
    return jnp.concatenate([fc1, fc2] + [jnp.pad(part, pad) for part in (*qkv, out)], axis=1)


def unpack(packed, like):
    fc1, fc2, qkv, out = like
    split = jnp.stack([packed[:, QKV + part * SLOT :][:, : qkv.shape[2]] for part in range(3)])
    return packed[:, FC1:FC2], packed[:, FC2:QKV], split, packed[:, OUT : OUT + out.shape[1]]


def root_of(gram):
    a, b, c = QUINTIC
    eye = eye_mask(gram.shape[0])
    scale = 1.0 / (jnp.sqrt(jnp.sum(jnp.where(eye, gram, 0.0))) + 1e-07)
    gram = gram * (scale * scale)
    root = jnp.where(eye, scale, 0.0)
    for _ in range(NS_ITERS):
        poly = jnp.where(eye, a, 0.0) + b * gram + c * mm3(gram, gram)
        root = mm3(root, poly)
        gram = mm3(mm3(gram, poly), poly)
    return root


def general(half, bucket, widths, counts, tokens, cotangent, weights, moms, vectors, vec_first, vec_second):
    dp = lax.axis_index("dp")
    rows = weights[0].shape[0]
    vec = jnp.pad(vectors.T, ((0, 0), (0, PACK - VEC - vectors.shape[0])))
    own = jnp.concatenate([pack(*weights), vec], axis=1).astype(BF16)
    packed = lax.all_gather(lax.all_gather(own, "dp", axis=0, tiled=True), "mlp")
    out_half, gtok_half, grads = image_pass(half.reshape(1), bucket, widths, counts, tokens, cotangent, packed)
    output = lax.all_gather(out_half, "mlp", axis=0, tiled=True)
    gtok = lax.all_gather(gtok_half, "mlp", axis=0, tiled=True)
    grad = lax.psum_scatter(grads.astype(F32), "mlp", scatter_dimension=0)
    grad = lax.psum_scatter(grad, "dp", scatter_dimension=0, tiled=True)
    mom = 0.95 * pack(*moms) + grad[:, 0:VEC]
    spans = ((FC1, FC2), (FC2, QKV), (QKV, OUT), (OUT, VEC))
    squares = [jnp.sum(jnp.square(grad[:, start:stop])) for start, stop in spans[2:] + spans[:2]]
    squares.append(0.5 * jnp.sum(jnp.square(grad[:, VEC:PACK])))
    norms = jnp.sqrt(lax.psum(jnp.stack(squares), ("dp", "mlp")))
    buf = lax.all_gather(lax.all_gather(mom.astype(BF16), "dp", axis=0, tiled=True), "mlp")
    ours = lax.dynamic_index_in_dim(buf, half, 0, keepdims=False)
    steps = []
    for (start, stop), rate in zip(spans, RATES):
        root = root_of(sum(mm(buf[h, :, start:stop], buf[h, :, start:stop], NT) for h in range(2)))
        root = lax.dynamic_slice_in_dim(root, dp * rows, rows, 0)
        high = root.astype(BF16)
        low = (root - high.astype(F32)).astype(BF16)
        steps.append(rate * (mm(high, ours[:, start:stop], NN) + mm(low, ours[:, start:stop], NN)))
    moved = unpack(jnp.concatenate(steps, axis=1), weights)
    gvec = grad[:, VEC : VEC + vectors.shape[0]].T
    first = 0.9 * vec_first + 0.1 * gvec
    second = 0.95 * vec_second + 0.05 * gvec * gvec
    vec_new = vectors - 0.5 * (first / (1.0 - 0.9**STEP)) / (
        jnp.sqrt(second / (1.0 - 0.95**STEP)) + 1e-08
    )

    def ordered(parts):
        fc1, fc2, qkv, out = parts
        return flat(qkv), flat(out), flat(fc1), flat(fc2)

    news = [0.999 * w - move for w, move in zip(weights, moved)]
    return (
        output, gtok, *ordered(unpack(grad, weights)), gvec,
        *ordered(unpack(mom, weights)), *ordered(news), vec_new, first, second, norms,
    )


def body(
    tokens, cotangent, image_bucket, bucket_width, bucket_heads,
    w_qkv, w_out, w_fc1, w_fc2, vectors,
    mom_qkv, mom_out, mom_fc1, mom_fc2, vec_first, vec_second,
):
    half = lax.axis_index("mlp").astype(jnp.int32)
    dp = lax.axis_index("dp").astype(jnp.int32)
    ranks = lax.axis_size("dp")
    model = tokens.shape[1]
    rows = w_fc1.shape[1]
    weights = [flat(w) for w in (w_fc1, w_fc2, w_qkv, w_out)]
    moms = [flat(m) for m in (mom_fc1, mom_fc2, mom_qkv, mom_out)]
    images = image_bucket.shape[0] // 2
    if ranks != 16 or images != 4 * PAIR:
        return general(
            half, image_bucket, bucket_width, bucket_heads, tokens, cotangent,
            weights, moms, vectors, vec_first, vec_second,
        )
    vec = jnp.pad(vectors.T, ((0, 0), (0, PACK - VEC - vectors.shape[0])))
    own_buckets = lax.dynamic_slice_in_dim(image_bucket, half * images, images)
    chosen = own_buckets[:, None] == jnp.arange(bucket_heads.shape[0], dtype=jnp.int32)[None, :]
    counts = jnp.sum(jnp.where(chosen, bucket_heads[None, :], 0), axis=1, keepdims=True)
    resid, proj, low, mixed, wt, vec_rows, fc_weights = attend_pass(counts, tokens, weights, vec, ranks)
    out_half, gres, fc_parts, gvec_rows = units_pass(
        half.reshape(1), image_bucket, bucket_width, resid, cotangent,
        fc_weights.reshape(2, model, FC), vec_rows,
    )
    gtok_both, grad_fc, mom_fc_new, grad_at, mom_at_new, fc_buf, at_buf, out_other = back_pass(
        counts, tokens, gres, proj, low, mixed, wt, vec_rows, gvec_rows,
        fc_parts.reshape(2, ranks, rows, FC), moms, out_half,
    )
    which = jnp.stack([2 * (dp % 2) + half, half])
    fc_buf, at_buf = fc_buf.reshape(2, model, FC), at_buf.reshape(2, model, AT)
    (root, norms, gfc1, gfc2, gqkv, gwo, gvec, mfc1, mfc2, mqkv, mwo, vec_new, first, second, output, gtok) = run_chain(
        which, fc_buf, at_buf, grad_fc, mom_fc_new, grad_at, mom_at_new, vectors, vec_first, vec_second,
        (out_half, out_other, gtok_both),
    )
    nfc1, nfc2, nqkv, nwo = apply_roots(root.reshape(ranks, rows, model), fc_buf, at_buf, weights)
    return (
        output, gtok,
        flat(gqkv), flat(gwo), flat(gfc1), flat(gfc2), gvec,
        flat(mqkv), flat(mwo), flat(mfc1), flat(mfc2),
        flat(nqkv), flat(nwo), flat(nfc1), flat(nfc2),
        vec_new, first, second, norms[0, 0:5],
    )


def solution(mesh):
    halves, columns = P("mlp", "dp"), P(None, "dp")
    blocks = P(None, "mlp", "dp")
    matrices = (blocks, halves, halves, halves)
    placed = (P("dp", None), P("dp", None), P("dp"), P(), P()) + matrices + (columns,) + matrices + (columns, columns)
    outs = (P("dp", None), P("dp", None)) + matrices + (columns,) + matrices + matrices + (columns,) * 3 + (P(),)
    return jax.shard_map(body, mesh=mesh, in_specs=placed, out_specs=outs, check_vma=False)
```

```python
import functools
import math

import jax
import jax.numpy as jnp
from jax import lax
from jax.experimental import pallas as pl
from jax.experimental.pallas import tpu as pltpu
from jax.sharding import PartitionSpec as P

HD = 64
NS_ITERS = 5
STEP = 10
EPSILON = 1e-06
F32 = jnp.float32
BF16 = jnp.bfloat16
NN = (((1,), (0,)), ((), ()))
NT = (((1,), (1,)), ((), ()))
TN = (((0,), (0,)), ((), ()))

FC1, FC2, QKV, OUT, VEC, PACK = 0, 768, 1536, 2304, 2560, 2688
SLOT = 256
SEQ = 256
PAIR = 2
CHUNK = 256


def mm(a, b, dims):
    return lax.dot_general(a, b, dims, preferred_element_type=F32)


def lane_sum(v):
    return jnp.sum(v, axis=-1, keepdims=True)


def norm_rows(v):
    inv = 1.0 / v.shape[-1]
    center = v - lane_sum(v) * inv
    factor = lax.rsqrt(lane_sum(center * center) * inv + EPSILON)
    return center * factor, factor


def norm_back(g, n, factor):
    inv = 1.0 / g.shape[-1]
    return factor * (g - lane_sum(g) * inv - n * (lane_sum(g * n) * inv))


def image_kernel(
    half_ref, bucket_ref, widths_ref, counts_ref,
    tok_ref, cot_ref, w_ref,
    out_ref, gtok_ref, grad_ref,
    acc_ref, vec_ref, gvec_ref, q_ref, k_ref, v_ref, mixed_ref, probs_ref, low_ref,
    y_ref, gh_ref,
):
    step = pl.program_id(0)
    rows, model = tok_ref.shape
    heads_half = 3
    pack = rows // SEQ
    first = (half_ref[0] * pl.num_programs(0) + step) * pack
    buckets = [bucket_ref[first + image] for image in range(pack)]
    widths = [widths_ref[bucket] for bucket in buckets]
    counts = [counts_ref[bucket] for bucket in buckets]
    width, count = widths[0], counts[0]
    for image in range(1, pack):
        width, count = jnp.maximum(width, widths[image]), jnp.maximum(count, counts[image])
    row_ids = lax.broadcasted_iota(jnp.int32, (rows, 1), 0)
    row_width = jnp.full((rows, 1), widths[0], jnp.int32)
    for image in range(1, pack):
        row_width = jnp.where(row_ids >= image * SEQ, widths[image], row_width)

    @pl.when(step == 0)
    def _():
        acc_ref[...] = jnp.zeros_like(acc_ref)
        gvec_ref[...] = jnp.zeros_like(gvec_ref)
        turned = w_ref[0, :, VEC:PACK].astype(F32).T
        vec_ref[...] = turned[0:8]

    lane_head = lax.broadcasted_iota(jnp.int32, (1, SLOT), 1) // HD
    masks = [(lane_head == s).astype(F32).astype(BF16) for s in range(heads_half)]

    def used_heads(image):
        return (lane_head < counts[image] - heads_half).astype(F32)

    def spans():
        return [slice(image * SEQ, (image + 1) * SEQ) for image in range(pack)]

    x = tok_ref[...].astype(F32)
    normed_one, factor_one = norm_rows(x)
    hidden_one = (normed_one * vec_ref[0:1] + vec_ref[1:2]).astype(BF16)
    for half in range(2):
        for ref, which in ((q_ref, 0), (k_ref, 1), (v_ref, 2)):
            lanes = slice(QKV + which * SLOT, QKV + (which + 1) * SLOT)
            ref[half] = mm(hidden_one, w_ref[half, :, lanes], NN).astype(BF16)

        def attend():
            for image, span in enumerate(spans()):
                total = None
                for s in range(heads_half):
                    slot = (image * 2 + half) * heads_half + s
                    scores = mm(q_ref[half, span] * masks[s], k_ref[half, span], NT) * 0.125
                    top = jnp.max(scores, axis=-1, keepdims=True)
                    grown = jnp.exp(scores - top)
                    probs = grown * (1.0 / lane_sum(grown))
                    low = probs.astype(BF16)
                    probs_ref[slot] = probs
                    low_ref[slot] = low
                    term = mm(low, v_ref[half, span] * masks[s], NN)
                    total = term if total is None else total + term
                if half:
                    total = total * used_heads(image)
                mixed_ref[half, span] = total.astype(BF16)

        if half == 0:
            attend()
        else:
            mixed_ref[half] = jnp.zeros_like(mixed_ref[half])
            pl.when(count > heads_half)(attend)

    branch = mm(mixed_ref[0], w_ref[0, :, OUT:VEC], NT) + mm(mixed_ref[1], w_ref[1, :, OUT:VEC], NT)
    resid = x + branch + vec_ref[4:5]
    normed_two, factor_two = norm_rows(resid)
    hidden_two = (normed_two * vec_ref[2:3] + vec_ref[3:4]).astype(BF16)
    cot = cot_ref[...]
    hidden_two_t = hidden_two.T
    cot_t = cot.T
    y_ref[...] = resid + vec_ref[5:6]
    gh_ref[...] = jnp.zeros_like(gh_ref)
    per_half = FC2 // CHUNK
    for chunk in range(2 * per_half):
        half, part = divmod(chunk, per_half)
        one = slice(FC1 + part * CHUNK, FC1 + (part + 1) * CHUNK)
        two = slice(FC2 + part * CHUNK, FC2 + (part + 1) * CHUNK)

        def units_pass():
            pre = mm(hidden_two, w_ref[half, :, one], NN)
            units = chunk * CHUNK + lax.broadcasted_iota(jnp.int32, pre.shape, 1)
            cumulative = 0.5 + 0.5 * lax.erf(pre * 0.7071067811865476)
            density = jnp.exp(-0.5 * pre * pre) * 0.3989422804014327
            cumulative = jnp.where(units < row_width, cumulative, 0.0)
            density = jnp.where(units < row_width, density, 0.0)
            act = (pre * cumulative).astype(BF16)
            grad_act = mm(cot, w_ref[half, :, two], NN)
            grad_pre = (grad_act * (cumulative + pre * density)).astype(BF16)
            y_ref[...] += mm(act, w_ref[half, :, two], NT)
            gh_ref[...] += mm(grad_pre, w_ref[half, :, one], NT)
            acc_ref[half, :, two] += mm(cot_t, act, NN)
            acc_ref[half, :, one] += mm(hidden_two_t, grad_pre, NN)

        if chunk < 2:
            units_pass()
        else:
            pl.when(width > chunk * CHUNK)(units_pass)

    out_ref[...] = y_ref[...]
    grad_hidden_two = gh_ref[...]
    cot_f = cot.astype(F32)
    grad_resid = cot_f + norm_back(grad_hidden_two * vec_ref[2:3], normed_two, factor_two)
    resid_low = grad_resid.astype(BF16)
    resid_low_t = resid_low.T
    hidden_one_t = hidden_one.T
    for half in range(2):
        acc_ref[half, :, OUT:VEC] += mm(resid_low_t, mixed_ref[half], NN)

        def back():
            grad_heads = mm(resid_low, w_ref[half, :, OUT:VEC], NN).astype(BF16)
            parts = []
            for image, span in enumerate(spans()):
                heads = grad_heads[span]
                if half:
                    heads = heads * used_heads(image).astype(BF16)
                sums = [None, None, None]
                for s in range(heads_half):
                    slot = (image * 2 + half) * heads_half + s
                    own = heads * masks[s]
                    grad_probs = mm(own, v_ref[half, span], NT)
                    probs = probs_ref[slot]
                    weighed = probs * grad_probs
                    grad_scores = (weighed - probs * lane_sum(weighed)).astype(BF16)
                    terms = (
                        mm(grad_scores, k_ref[half, span] * masks[s], NN),
                        mm(grad_scores, q_ref[half, span] * masks[s], TN),
                        mm(low_ref[slot], own, TN),
                    )
                    sums = [t if o is None else o + t for o, t in zip(sums, terms)]
                parts.append([(v * c).astype(BF16) for v, c in zip(sums, (0.125, 0.125, 1.0))])
            total = None
            for which in range(3):
                lanes = slice(QKV + which * SLOT, QKV + (which + 1) * SLOT)
                grad_proj = jnp.concatenate([part[which] for part in parts], axis=0)
                acc_ref[half, :, lanes] += mm(hidden_one_t, grad_proj, NN)
                term = mm(grad_proj, w_ref[half, :, lanes], NT)
                total = term if total is None else total + term
            return total

        if half == 0:
            gh_ref[...] = back()
        else:

            @pl.when(count > heads_half)
            def _():
                gh_ref[...] += back()

    grad_hidden_one = gh_ref[...]
    gtok_ref[...] = grad_resid + norm_back(grad_hidden_one * vec_ref[0:1], normed_one, factor_one)
    sums = (
        grad_hidden_one * normed_one,
        grad_hidden_one,
        grad_hidden_two * normed_two,
        grad_hidden_two,
        grad_resid,
        cot_f,
    )
    for row, values in enumerate(sums):
        gvec_ref[row : row + 1] += jnp.sum(values, axis=0, keepdims=True)

    @pl.when(step == pl.num_programs(0) - 1)
    def _():
        grad_ref[0, :, 0:VEC] = acc_ref[0].astype(BF16)
        grad_ref[1, :, 0:VEC] = acc_ref[1].astype(BF16)
        columns = gvec_ref[...].T.astype(BF16)
        grad_ref[0, :, VEC:PACK] = columns
        grad_ref[1, :, VEC:PACK] = columns


def image_pass(half, bucket, widths, counts, tokens, cotangent, packed):
    images = bucket.shape[0] // 2
    model = tokens.shape[1]
    rows = images * SEQ
    images = images // PAIR
    seq = PAIR * SEQ
    picked = pl.BlockSpec((seq, model), lambda i, h, b, w, c: (h[0] * images + i, 0))
    placed = pl.BlockSpec((seq, model), lambda i, h, b, w, c: (i, 0))
    whole = pl.BlockSpec(
        (2, model, PACK), lambda i, h, b, w, c: (0, 0, 0), pipeline_mode=pl.Buffered(1)
    )
    heads = 6
    flops = 2 * rows * model * (3 * 4 * model + 3 * 8 * model)
    return pl.pallas_call(
        image_kernel,
        out_shape=(
            jax.ShapeDtypeStruct((rows, model), F32),
            jax.ShapeDtypeStruct((rows, model), F32),
            jax.ShapeDtypeStruct((2, model, PACK), BF16),
        ),
        grid_spec=pltpu.PrefetchScalarGridSpec(
            num_scalar_prefetch=4,
            grid=(images,),
            in_specs=[picked, picked, whole],
            out_specs=[placed, placed, whole],
            scratch_shapes=[
                pltpu.VMEM((2, model, VEC), F32),
                pltpu.VMEM((8, model), F32),
                pltpu.VMEM((128, model), F32),
                pltpu.VMEM((2, seq, SLOT), BF16),
                pltpu.VMEM((2, seq, SLOT), BF16),
                pltpu.VMEM((2, seq, SLOT), BF16),
                pltpu.VMEM((2, seq, SLOT), BF16),
                pltpu.VMEM((PAIR * heads, SEQ, SEQ), F32),
                pltpu.VMEM((PAIR * heads, SEQ, SEQ), BF16),
                pltpu.VMEM((seq, model), F32),
                pltpu.VMEM((seq, model), F32),
            ],
        ),
        compiler_params=pltpu.CompilerParams(vmem_limit_bytes=56 * 1024 * 1024),
        cost_estimate=pl.CostEstimate(flops=flops, bytes_accessed=20 * rows * model, transcendentals=rows * 6144),
        name="image_pass",
    )(half, bucket, widths, counts, tokens, cotangent, packed)


MESH = pl.DeviceIdType.MESH
AT_OUT, AT_VEC, AT = 768, 1024, 1152
HEADS = 192
AT_SENT = 896
FC = 1536
EARLY = FC + SLOT
TAIL, LATE = 3 * HEADS, 640


class Place:
    def __init__(self):
        dp = lax.axis_index("dp")
        self.half = lax.axis_index("mlp")
        self.z = dp // 4
        self.y = (dp // 2) % 2
        self.x = dp % 2
        self.dp = dp
        self.y_peer = (self.index(self.z, 1 - self.y, self.x), self.half)
        self.x_peer = (self.index(self.z, self.y, 1 - self.x), self.half)
        self.sibling = (self.dp, 1 - self.half)

    def index(self, z, y, x):
        return z * 4 + y * 2 + x

    def at_z(self, z):
        return (self.index(z, self.y, self.x), self.half)


def meet(place):
    barrier = pltpu.get_barrier_semaphore()
    peers = [place.at_z((place.z + j) % 4) for j in range(1, 4)]
    peers += [place.y_peer, place.x_peer, place.sibling]
    for peer in peers:
        pl.semaphore_signal(barrier, inc=1, device_id=peer, device_id_type=MESH)
    pl.semaphore_wait(barrier, len(peers))


class Mail:
    def __init__(self, place, send_sem, recv_sem):
        self.place, self.send_sem, self.recv_sem = place, send_sem, recv_sem

    def copy(self, slot, src, dst, peer):
        return pltpu.make_async_remote_copy(
            src_ref=src,
            dst_ref=dst,
            send_sem=self.send_sem.at[slot],
            recv_sem=self.recv_sem.at[slot],
            device_id=peer,
            device_id_type=MESH,
        )

    def start(self, slot, src, dst, peer):
        self.copy(slot, src, dst, peer).start()

    def arrived(self, slot, like):
        self.copy(slot, like, like, self.place.sibling).wait_recv()

    def left(self, slot, like):
        self.copy(slot, like, like, self.place.sibling).wait_send()


GATHER_SLOTS = 35
NEAR_FIRST = (1, 3, 2)


class Gather:
    def __init__(self, place, own, buf, cut, send_sem, recv_sem):
        self.place, self.own, self.buf = place, own, buf
        self.mail = Mail(place, send_sem, recv_sem)
        self.pieces = (pl.ds(0, cut), pl.ds(cut, own.shape[1] - cut))

    def shard(self, k, y, x):
        return self.place.index((self.place.z + 4 - k) % 4, y, x)

    def forward(self, slot, dp, peer, piece=None):
        ref = self.buf.at[self.place.half, dp]
        if piece is not None:
            ref = ref.at[:, self.pieces[piece]]
        self.mail.start(slot, ref, ref, peer)

    def like(self, piece=None):
        ref = self.buf.at[0, 0]
        return ref if piece is None else ref.at[:, self.pieces[piece]]

    def start_column(self):
        place = self.place
        home = self.buf.at[place.half, place.dp]
        for j in NEAR_FIRST:
            self.mail.start(j - 1, self.own, home, place.at_z((place.z + j) % 4))

    def start_plane(self):
        place = self.place
        home = self.buf.at[place.half, place.dp]
        self.mail.start(3, self.own, home, place.y_peer)
        self.mail.start(7, self.own, home, place.x_peer)
        self.mail.start(19, self.own, home, place.sibling)

    def column(self, k):
        place = self.place
        self.mail.arrived(k - 1, self.like())
        dp = self.shard(k, place.y, place.x)
        self.forward(3 + k, dp, place.y_peer)
        self.forward(7 + k, dp, place.x_peer)
        self.forward(19 + k, dp, place.sibling)

    def plane(self, k):
        place = self.place
        self.mail.arrived(3 + k, self.like())
        dp = self.shard(k, 1 - place.y, place.x)
        self.forward(11 + k, dp, place.x_peer, 0)
        self.forward(23 + k, dp, place.sibling)
        self.mail.arrived(7 + k, self.like())
        dp = self.shard(k, place.y, 1 - place.x)
        self.forward(15 + k, dp, place.y_peer, 1)
        self.forward(27 + k, dp, place.sibling)

    def corner(self, k):
        place = self.place
        self.mail.arrived(11 + k, self.like(0))
        self.mail.arrived(15 + k, self.like(1))
        self.forward(31 + k, self.shard(k, 1 - place.y, 1 - place.x), place.sibling)

    def finish(self):
        for k in range(16):
            self.mail.arrived(19 + k, self.like())
        for slot in range(GATHER_SLOTS):
            piece = 0 if 11 <= slot < 15 else 1 if 15 <= slot < 19 else None
            self.mail.left(slot, self.like(piece))

    def columns(self):
        for k in NEAR_FIRST:
            self.column(k)

    def planes(self):
        for k in NEAR_FIRST:
            self.plane(k)

    def corners(self):
        for k in (0, *NEAR_FIRST):
            self.corner(k)


SCATTER_SLOTS = 43
Z_ORDER = (2, 1, 3, 0)


class Scatter:
    def __init__(self, place, parts, hold, firsts, seconds, last, cut, send_sem, recv_sem):
        self.place, self.parts, self.hold = place, parts, hold
        self.firsts, self.seconds, self.last = firsts, seconds, last
        self.mail = Mail(place, send_sem, recv_sem)
        self.pieces = (pl.ds(0, cut), pl.ds(cut, hold.shape[2] - cut))

    def shard(self, c, k):
        y, x = self.place.y, self.place.x
        column = ((1 - y, 1 - x), (y, 1 - x), (1 - y, x), (y, x))[c]
        return self.place.index((self.place.z + Z_ORDER[k]) % 4, *column)

    def piece(self, dp, p):
        return self.hold.at[dp, :, self.pieces[p]]

    def load(self, dp, p):
        return self.hold[dp, :, self.pieces[p]].astype(F32)

    def start(self):
        half = self.place.half
        for c in range(4):
            for k in range(4):
                dp = self.shard(c, k)
                self.mail.start(4 * c + k, self.parts.at[1 - half, dp], self.hold.at[dp], self.place.sibling)

    def settle(self, c, k):
        dp = self.shard(c, k)
        self.mail.arrived(4 * c + k, self.hold.at[0])
        total = self.hold[dp].astype(F32) + self.parts[self.place.half, dp].astype(F32)
        self.hold[dp] = total.astype(BF16)
        return dp

    def first_hop(self):
        place, (first_a, first_b) = self.place, self.firsts
        for k in range(4):
            dp = self.settle(0, k)
            self.mail.start(16 + k, self.piece(dp, 0), first_a.at[k], place.x_peer)
            self.mail.start(24 + k, self.piece(dp, 1), first_b.at[k], place.y_peer)
        for k in range(4):
            dp = self.settle(1, k)
            self.mail.start(20 + k, self.piece(dp, 0), first_a.at[4 + k], place.x_peer)
            dp = self.settle(2, k)
            self.mail.start(28 + k, self.piece(dp, 1), first_b.at[4 + k], place.y_peer)
        for k in range(4):
            self.settle(3, k)

    def second_hop(self):
        place, firsts, seconds = self.place, self.firsts, self.seconds
        for k in range(4):
            for p, slot, column, out, peer in ((0, 16, 2, 32, place.y_peer), (1, 24, 1, 36, place.x_peer)):
                self.mail.arrived(slot + k, firsts[p].at[0])
                dp = self.shard(column, k)
                total = self.load(dp, p) + firsts[p][k].astype(F32)
                self.hold[dp, :, self.pieces[p]] = total.astype(BF16)
                self.mail.start(out + k, self.piece(dp, p), seconds[p].at[k], peer)

    def last_hop(self, keep):
        place = self.place
        for k in range(4):
            dp = self.shard(3, k)
            totals = []
            for p, slot, second in ((0, 20, 32), (1, 28, 36)):
                self.mail.arrived(slot + k, self.firsts[p].at[0])
                self.mail.arrived(second + k, self.seconds[p].at[0])
                totals.append(self.load(dp, p) + self.firsts[p][4 + k].astype(F32) + self.seconds[p][k].astype(F32))
            for p in range(2):
                if Z_ORDER[k]:
                    self.hold[dp, :, self.pieces[p]] = totals[p].astype(BF16)
                else:
                    keep[:, self.pieces[p]] = totals[p]
            if Z_ORDER[k]:
                j = Z_ORDER[k]
                self.mail.start(40 + j - 1, self.hold.at[dp], self.last.at[j - 1], place.at_z((place.z + j) % 4))

    def finish(self, keep):
        for j in range(3):
            self.mail.arrived(40 + j, self.last.at[0])
            keep[...] = keep[...] + self.last[j].astype(F32)
        for slot in range(SCATTER_SLOTS):
            if slot < 16 or slot >= 40:
                like = self.hold.at[0]
            elif slot < 32:
                like = self.firsts[(slot - 16) // 8].at[0]
            else:
                like = self.seconds[(slot - 32) // 4].at[0]
            self.mail.left(slot, like)


class WideGather:
    SLOTS = 8

    def __init__(self, place, own, buf, cut, send_sem, recv_sem):
        self.place, self.own, self.buf = place, own, buf
        self.mail = Mail(place, send_sem, recv_sem)
        self.pieces = (pl.ds(0, cut), pl.ds(cut, own.shape[1] - cut))

    def column(self, y, x, piece=None):
        ref = self.buf.at[self.place.half, :, 2 * y + x]
        return ref if piece is None else ref.at[:, :, self.pieces[piece]]

    def send(self, slot, ref, peer):
        self.mail.start(slot, ref, ref, peer)

    def start(self):
        place = self.place
        home = self.buf.at[place.half, place.z, 2 * place.y + place.x]
        for j in NEAR_FIRST:
            self.mail.start(j - 1, self.own, home, place.at_z((place.z + j) % 4))

    def spread(self):
        place = self.place
        for j in range(3):
            self.mail.arrived(j, self.own)
        self.send(3, self.column(place.y, place.x), place.y_peer)
        self.send(4, self.column(place.y, place.x), place.x_peer)

    def corners(self):
        place = self.place
        self.mail.arrived(3, self.column(place.y, place.x))
        self.send(5, self.column(1 - place.y, place.x, 0), place.x_peer)
        self.mail.arrived(4, self.column(place.y, place.x))
        self.send(6, self.column(place.y, 1 - place.x, 1), place.y_peer)

    def share(self):
        place = self.place
        self.mail.arrived(5, self.column(place.y, place.x, 0))
        self.mail.arrived(6, self.column(place.y, place.x, 1))
        self.send(7, self.buf.at[place.half], place.sibling)

    def finish(self):
        place = self.place
        whole, column = self.buf.at[place.half], self.column(place.y, place.x)
        self.mail.arrived(7, whole)
        likes = [self.own] * 3 + [column] * 2
        likes += [self.column(place.y, place.x, 0), self.column(place.y, place.x, 1), whole]
        for slot, like in enumerate(likes):
            self.mail.left(slot, like)


class WideScatter:
    SLOTS = 10

    def __init__(self, place, parts, hold, firsts, seconds, last, cut, send_sem, recv_sem):
        self.place, self.parts, self.hold = place, parts, hold
        self.firsts, self.seconds, self.last = firsts, seconds, last
        self.mail = Mail(place, send_sem, recv_sem)
        self.pieces = (pl.ds(0, cut), pl.ds(cut, hold.shape[3] - cut))

    def column(self, y, x, piece):
        return self.hold.at[:, 2 * y + x, :, self.pieces[piece]]

    def start(self):
        self.mail.start(0, self.parts.at[1 - self.place.half], self.hold, self.place.sibling)

    def first_hop(self):
        place = self.place
        y, x = place.y, place.x
        self.mail.arrived(0, self.hold)

        def add(z, carry):
            total = self.hold[z].astype(F32) + self.parts[place.half, z].astype(F32)
            self.hold[z] = total.astype(BF16)
            return carry

        lax.fori_loop(0, self.hold.shape[0], add, 0)
        first_a, first_b = self.firsts
        self.mail.start(1, self.column(1 - y, 1 - x, 0), first_a.at[0], place.x_peer)
        self.mail.start(2, self.column(1 - y, 1 - x, 1), first_b.at[0], place.y_peer)
        self.mail.start(3, self.column(y, 1 - x, 0), first_a.at[1], place.x_peer)
        self.mail.start(4, self.column(1 - y, x, 1), first_b.at[1], place.y_peer)

    def second_hop(self):
        place = self.place
        y, x = place.y, place.x
        moves = ((0, (1 - y, x), place.y_peer), (1, (y, 1 - x), place.x_peer))
        for p, (cy, cx), peer in moves:
            self.mail.arrived(1 + p, self.firsts[p].at[0])
            lanes = self.pieces[p]
            total = self.hold[:, 2 * cy + cx, :, lanes].astype(F32) + self.firsts[p][0].astype(F32)
            self.hold[:, 2 * cy + cx, :, lanes] = total.astype(BF16)
            self.mail.start(5 + p, self.column(cy, cx, p), self.seconds[p], peer)

    def last_hop(self, keep):
        place = self.place
        home = 2 * place.y + place.x
        for p in range(2):
            self.mail.arrived(3 + p, self.firsts[p].at[1])
            self.mail.arrived(5 + p, self.seconds[p])
            lanes = self.pieces[p]
            total = self.hold[:, home, :, lanes].astype(F32) + self.firsts[p][1].astype(F32)
            self.hold[:, home, :, lanes] = (total + self.seconds[p][...].astype(F32)).astype(BF16)
        for j in NEAR_FIRST:
            z = (place.z + j) % 4
            self.mail.start(6 + j, self.hold.at[z, home], self.last.at[j - 1], place.at_z(z))
        keep[...] = self.hold[place.z, home].astype(F32)

    def finish(self, keep):
        place = self.place
        for j in range(3):
            self.mail.arrived(7 + j, self.last.at[0])
            keep[...] = keep[...] + self.last[j].astype(F32)
        likes = [self.hold] + [self.firsts[p].at[0] for p in (0, 1, 0, 1)]
        likes += [self.seconds[0], self.seconds[1]] + [self.last.at[0]] * 3
        for slot, like in enumerate(likes):
            self.mail.left(slot, like)


def wide_scratch(rows, lanes, cut):
    return [
        pltpu.VMEM((4, 4, rows, lanes), BF16),
        pltpu.VMEM((2, 4, rows, cut), BF16),
        pltpu.VMEM((2, 4, rows, lanes - cut), BF16),
        pltpu.VMEM((4, rows, cut), BF16),
        pltpu.VMEM((4, rows, lanes - cut), BF16),
        pltpu.VMEM((3, rows, lanes), BF16),
    ]


def scatter_scratch(ranks, rows, lanes, cut):
    return [
        pltpu.VMEM((ranks, rows, lanes), BF16),
        pltpu.VMEM((8, rows, cut), BF16),
        pltpu.VMEM((8, rows, lanes - cut), BF16),
        pltpu.VMEM((4, rows, cut), BF16),
        pltpu.VMEM((4, rows, lanes - cut), BF16),
        pltpu.VMEM((3, rows, lanes), BF16),
    ]


def dma(count):
    return [pltpu.SemaphoreType.DMA((count,))] * 2


SENT_CUT, FC_CUT, EARLY_CUT, LATE_CUT = 512, 768, 896, 384


def head_masks():
    lane_head = lax.broadcasted_iota(jnp.int32, (1, SLOT), 1) // HD
    return [(lane_head == s).astype(F32).astype(BF16) for s in range(3)]


def used_lanes(bucket_ref, heads_ref, image, half):
    bucket = bucket_ref[...]
    counts = jnp.zeros(bucket.shape, jnp.int32)
    for entry in range(heads_ref.shape[1]):
        counts = jnp.where(bucket == entry, heads_ref[:, entry : entry + 1], counts)
    chosen = lax.broadcasted_iota(jnp.int32, bucket.shape, 1) == image
    count = jnp.sum(jnp.where(chosen, counts.astype(F32), 0.0), axis=1, keepdims=True)
    lane_head = lax.broadcasted_iota(jnp.int32, (1, SLOT), 1) // HD
    return jnp.where(lane_head.astype(F32) < count - 3.0 * half, 1.0, 0.0)


def widen(packed, pieces):
    blank = jnp.zeros((packed.shape[0], SLOT - HEADS), packed.dtype)
    parts = []
    for piece in range(pieces):
        parts += [packed[:, piece * HEADS : (piece + 1) * HEADS], blank]
    return jnp.concatenate(parts, axis=1)


def token_copy(place, tokens_ref, tok_own, sem):
    count = tok_own.shape[0]
    start = pl.multiple_of(place.half * count, count)
    return pltpu.make_async_copy(tokens_ref.at[pl.ds(start, count)], tok_own, sem)


def own_block(step, rows):
    return pl.ds(pl.multiple_of(step * rows, rows), rows)


def attend_kernel(
    bucket_ref, heads_ref, tokens_ref, fc1_ref, fc2_ref, qkv_ref, wo_ref, vecs_ref,
    resid_ref, proj_ref, low_ref, mixed_ref, wt_ref, vec_ref, fc_buf,
    own_at, own_fc, at_buf, tok_own, turn_ref, at_send, at_recv, fc_send, fc_recv, local_sem, tok_sem,
):
    place = Place()
    step = pl.program_id(0)
    steps = pl.num_programs(0)
    rows, model = resid_ref.shape
    pack = rows // SEQ
    tok_copy = token_copy(place, tokens_ref, tok_own, tok_sem)
    slices = Gather(place, own_at, at_buf, SENT_CUT, at_send, at_recv)
    units = Gather(place, own_fc, fc_buf, FC_CUT, fc_send, fc_recv)
    local = pltpu.make_async_copy(own_fc, fc_buf.at[place.half, place.dp], local_sem)

    @pl.when(step == 0)
    def _():
        tok_copy.start()
        own_at[...] = jnp.zeros_like(own_at)
        for which in range(3):
            own_at[:, which * HEADS : (which + 1) * HEADS] = qkv_ref[which].astype(BF16)
        own_at[:, 3 * HEADS : 4 * HEADS] = wo_ref[...].astype(BF16)
        turn_ref[...] = jnp.zeros_like(turn_ref)
        turn_ref[0 : vecs_ref.shape[0], 0 : vecs_ref.shape[1]] = vecs_ref[...]
        own_at[:, AT_SENT - 128 : AT_SENT] = turn_ref[...].T[0 : own_at.shape[0]].astype(BF16)
        own_fc[:, 0 : FC // 2] = fc1_ref[...].astype(BF16)
        own_fc[:, FC // 2 : FC] = fc2_ref[...].astype(BF16)
        at_buf[place.half, place.dp] = own_at[...]
        local.start()
        meet(place)
        slices.start_column()
        slices.start_plane()
        slices.plane(0)
        slices.columns()
        units.start_column()
        slices.planes()
        units.start_plane()
        slices.corners()
        slices.finish()
        for half in range(2):
            sent = at_buf[half].astype(F32).reshape(model, AT_SENT)
            wt_ref[half, :, 0:AT_VEC] = widen(sent, 4).astype(BF16)
            wt_ref[half, :, AT_VEC:AT] = sent[:, AT_SENT - 128 : AT_SENT].astype(BF16)
        vec_ref[...] = wt_ref[0, :, AT_VEC:AT].astype(F32).T[0:8]
        tok_copy.wait()

    @pl.when(step == 2)
    def _():
        units.planes()

    @pl.when(step == steps - 1)
    def _():
        units.corners()

    masks = head_masks()
    first_image = place.half * (bucket_ref.shape[1] // 2)
    x = tok_own[own_block(step, rows)].astype(F32)
    normed_one, _ = norm_rows(x)
    hidden_one = (normed_one * vec_ref[0:1] + vec_ref[1:2]).astype(BF16)
    branch = None
    for half in range(2):
        base = half * 3 * SLOT
        proj = []
        for which in range(3):
            part = mm(hidden_one, wt_ref[half, :, which * SLOT : (which + 1) * SLOT], NN).astype(BF16)
            proj_ref[:, base + which * SLOT : base + (which + 1) * SLOT] = part
            proj.append(part)
        mixes = []
        for image in range(pack):
            span = slice(image * SEQ, (image + 1) * SEQ)
            queries, keys, values = (part[span] for part in proj)
            total = None
            for s in range(3):
                scores = mm(queries * masks[s], keys, NT) * 0.125
                top = jnp.max(scores, axis=-1, keepdims=True)
                grown = jnp.exp(scores - top)
                low = (grown * (1.0 / lane_sum(grown))).astype(BF16)
                low_ref[(image * 2 + half) * 3 + s] = low
                term = mm(low, values * masks[s], NN)
                total = term if total is None else total + term
            mixes.append((total * used_lanes(bucket_ref, heads_ref, first_image + step * pack + image, half)).astype(BF16))
        mixed = jnp.concatenate(mixes, axis=0)
        mixed_ref[:, half * SLOT : (half + 1) * SLOT] = mixed
        term = mm(mixed, wt_ref[half, :, AT_OUT:AT_VEC], NT)
        branch = term if branch is None else branch + term
        if half == 0:

            @pl.when(step == 0)
            def _():
                units.columns()
                units.plane(0)

    resid_ref[...] = x + branch + vec_ref[4:5]

    @pl.when(step == steps - 1)
    def _():
        units.finish()
        local.wait()


def const(shape, **kw):
    return pl.BlockSpec(shape, lambda i, *_: (0,) * len(shape), **kw)


def once(shape):
    return const(shape, pipeline_mode=pl.Buffered(1))


def attend_pass(bucket, heads, tokens, weights, vectors, ranks):
    model = tokens.shape[1]
    images = bucket.shape[1] // 2
    rows = weights[0].shape[0]
    count = images * SEQ
    steps = images // PAIR
    block = PAIR * SEQ

    def by_step(lanes):
        return pl.BlockSpec((block, lanes), lambda i: (i, 0))

    return pl.pallas_call(
        attend_kernel,
        out_shape=(
            jax.ShapeDtypeStruct((count, model), F32),
            jax.ShapeDtypeStruct((count, 6 * SLOT), BF16),
            jax.ShapeDtypeStruct((images * 6, SEQ, SEQ), BF16),
            jax.ShapeDtypeStruct((count, 2 * SLOT), BF16),
            jax.ShapeDtypeStruct((2, model, AT), BF16),
            jax.ShapeDtypeStruct((8, model), F32),
            jax.ShapeDtypeStruct((2, ranks, rows, FC), BF16),
        ),
        grid_spec=pltpu.PrefetchScalarGridSpec(
            num_scalar_prefetch=0,
            grid=(steps,),
            in_specs=[once(bucket.shape), once(heads.shape), pl.BlockSpec(memory_space=pl.ANY)]
            + [once(w.shape) for w in weights]
            + [once(vectors.shape)],
            out_specs=[
                by_step(model),
                by_step(6 * SLOT),
                pl.BlockSpec((PAIR * 6, SEQ, SEQ), lambda i: (i, 0, 0)),
                by_step(2 * SLOT),
                once((2, model, AT)),
                once((8, model)),
                pl.BlockSpec(memory_space=pl.ANY),
            ],
            scratch_shapes=[
                pltpu.VMEM((rows, AT_SENT), BF16),
                pltpu.VMEM((rows, FC), BF16),
                pltpu.VMEM((2, ranks, rows, AT_SENT), BF16),
                pltpu.VMEM((count, model), BF16),
                pltpu.VMEM((128, 128), F32),
            ]
            + dma(GATHER_SLOTS)
            + dma(GATHER_SLOTS)
            + [pltpu.SemaphoreType.DMA] * 2,
        ),
        compiler_params=pltpu.CompilerParams(
            collective_id=0, has_side_effects=True, vmem_limit_bytes=56 * 1024 * 1024
        ),
        name="attend_pass",
    )(bucket, heads, tokens, *weights, vectors)


def units_kernel(
    half_ref, bucket_ref, widths_ref, resid_ref, cot_ref, mixed_ref, w_ref, vec_ref,
    out_ref, gres_ref, grad_ref, gvec_ref, acc_ref, y_ref, gh_ref,
):
    step = pl.program_id(0)
    rows, model = resid_ref.shape
    pack = rows // SEQ
    first = (half_ref[0] * pl.num_programs(0) + step) * pack
    widths = [widths_ref[bucket_ref[first + image]] for image in range(pack)]
    row_ids = lax.broadcasted_iota(jnp.int32, (rows, 1), 0)
    width, row_width = widths[0], jnp.full((rows, 1), widths[0], jnp.int32)
    for image in range(1, pack):
        width = jnp.maximum(width, widths[image])
        row_width = jnp.where(row_ids >= image * SEQ, widths[image], row_width)

    @pl.when(step == 0)
    def _():
        acc_ref[...] = jnp.zeros_like(acc_ref)
        gvec_ref[...] = jnp.zeros_like(gvec_ref)

    resid = resid_ref[...]
    normed_two, factor_two = norm_rows(resid)
    hidden_two = (normed_two * vec_ref[2:3] + vec_ref[3:4]).astype(BF16)
    cot = cot_ref[...]
    hidden_two_t = hidden_two.T
    cot_t = cot.T
    y_ref[...] = resid + vec_ref[5:6]
    gh_ref[...] = jnp.zeros_like(gh_ref)
    per_half = FC2 // CHUNK
    for chunk in range(2 * per_half):
        half, part = divmod(chunk, per_half)
        one = slice(FC1 + part * CHUNK, FC1 + (part + 1) * CHUNK)
        two = slice(FC2 + part * CHUNK, FC2 + (part + 1) * CHUNK)

        def units_pass():
            pre = mm(hidden_two, w_ref[half, :, one], NN)
            units = chunk * CHUNK + lax.broadcasted_iota(jnp.int32, pre.shape, 1)
            cumulative = 0.5 + 0.5 * lax.erf(pre * 0.7071067811865476)
            density = jnp.exp(-0.5 * pre * pre) * 0.3989422804014327
            cumulative = jnp.where(units < row_width, cumulative, 0.0)
            density = jnp.where(units < row_width, density, 0.0)
            act = (pre * cumulative).astype(BF16)
            grad_act = mm(cot, w_ref[half, :, two], NN)
            grad_pre = (grad_act * (cumulative + pre * density)).astype(BF16)
            y_ref[...] += mm(act, w_ref[half, :, two], NT)
            gh_ref[...] += mm(grad_pre, w_ref[half, :, one], NT)
            acc_ref[half, :, two] += mm(cot_t, act, NN)
            acc_ref[half, :, one] += mm(hidden_two_t, grad_pre, NN)

        if chunk < 2:
            units_pass()
        else:
            pl.when(width > chunk * CHUNK)(units_pass)

    out_ref[...] = y_ref[...]
    grad_hidden_two = gh_ref[...]
    cot_f = cot.astype(F32)
    grad_resid = cot_f + norm_back(grad_hidden_two * vec_ref[2:3], normed_two, factor_two)
    gres_ref[...] = grad_resid
    resid_low_t = grad_resid.astype(BF16).T
    for half in range(2):
        acc_ref[half, :, FC:EARLY] += mm(resid_low_t, mixed_ref[:, half * SLOT : (half + 1) * SLOT], NN)
    sums = (grad_hidden_two * normed_two, grad_hidden_two, grad_resid, cot_f)
    for row, values in enumerate(sums):
        gvec_ref[2 + row : 3 + row] += jnp.sum(values, axis=0, keepdims=True)

    @pl.when(step == pl.num_programs(0) - 1)
    def _():
        grad_ref[...] = acc_ref[...].astype(BF16)


def units_pass(half, bucket, widths, resid, cotangent, mixed, packed, vec):
    count, model = resid.shape
    block = PAIR * SEQ
    steps = count // block
    placed = pl.BlockSpec((block, model), lambda i, h, b, w: (i, 0))
    picked = pl.BlockSpec((block, model), lambda i, h, b, w: (h[0] * steps + i, 0))
    blended = pl.BlockSpec((block, 2 * SLOT), lambda i, h, b, w: (i, 0))
    return pl.pallas_call(
        units_kernel,
        out_shape=(
            jax.ShapeDtypeStruct((count, model), F32),
            jax.ShapeDtypeStruct((count, model), F32),
            jax.ShapeDtypeStruct((2, model, EARLY), BF16),
            jax.ShapeDtypeStruct((8, model), F32),
        ),
        grid_spec=pltpu.PrefetchScalarGridSpec(
            num_scalar_prefetch=3,
            grid=(steps,),
            in_specs=[placed, picked, blended, once(packed.shape), once(vec.shape)],
            out_specs=[placed, placed, once((2, model, EARLY)), once((8, model))],
            scratch_shapes=[
                pltpu.VMEM((2, model, EARLY), F32),
                pltpu.VMEM((block, model), F32),
                pltpu.VMEM((block, model), F32),
            ],
        ),
        compiler_params=pltpu.CompilerParams(vmem_limit_bytes=56 * 1024 * 1024),
        name="units_pass",
    )(half, bucket, widths, resid, cotangent, mixed, packed, vec)


def back_kernel(
    bucket_ref, heads_ref, tokens_ref, gres_ref, proj_ref, low_ref, wt_ref, vec_ref, gvec_ref,
    fc_parts, fc1_ref, fc2_ref, qkv_ref, wo_ref, out_half,
    gtok_ref, grad_fc, mom_fc, grad_at, mom_at, fc_buf, at_buf, out_other,
    acc_ref, sums_ref, gtok_own, at_parts, own_fc, own_at, tok_own,
    fc_hold, fc_first_a, fc_first_b, fc_second_a, fc_second_b, fc_last,
    at_hold, at_first_a, at_first_b, at_second_a, at_second_b, at_last,
    fcs_send, fcs_recv, ats_send, ats_recv, fcg_send, fcg_recv, atg_send, atg_recv,
    side_send, side_recv, local_sems,
):
    place = Place()
    step = pl.program_id(0)
    steps = pl.num_programs(0)
    rows, model = gres_ref.shape
    tok_copy = token_copy(place, tokens_ref, tok_own, local_sems.at[0])
    pack = rows // SEQ
    count = gtok_ref.shape[0] // 2
    fc_sum = WideScatter(
        place, fc_parts, fc_hold, (fc_first_a, fc_first_b), (fc_second_a, fc_second_b), fc_last,
        EARLY_CUT, fcs_send, fcs_recv,
    )
    at_sum = Scatter(
        place, at_parts, at_hold, (at_first_a, at_first_b), (at_second_a, at_second_b), at_last,
        LATE_CUT, ats_send, ats_recv,
    )
    fc_all = WideGather(place, own_fc, fc_buf, EARLY_CUT, fcg_send, fcg_recv)
    at_all = Gather(place, own_at, at_buf, LATE_CUT, atg_send, atg_recv)
    side = Mail(place, side_send, side_recv)
    fc_home = pltpu.make_async_copy(
        own_fc, fc_buf.at[place.half, place.z, 2 * place.y + place.x], local_sems.at[1]
    )
    at_home = pltpu.make_async_copy(own_at, at_buf.at[place.half, place.dp], local_sems.at[2])

    @pl.when(step == 0)
    def _():
        tok_copy.start()
        meet(place)
        fc_sum.start()
        tok_copy.wait()
        acc_ref[...] = jnp.zeros_like(acc_ref)
        sums_ref[...] = jnp.zeros_like(sums_ref)
        sums_ref[0:8] = gvec_ref[...]

    def settle_units():
        fc_sum.finish(grad_fc)
        mom_fc[:, 0 : FC // 2] = 0.95 * fc1_ref[...]
        mom_fc[:, FC // 2 : FC] = 0.95 * fc2_ref[...]
        mom_fc[:, FC:EARLY] = jnp.zeros((mom_fc.shape[0], SLOT), F32)
        mom_fc[:, FC : FC + HEADS] = 0.95 * wo_ref[...]
        mom_fc[...] = mom_fc[...] + grad_fc[...]
        own_fc[...] = mom_fc[...].astype(BF16)
        fc_home.start()
        fc_all.start()
        side.start(0, out_half, out_other, place.sibling)

    def spread_units():
        fc_home.wait()
        fc_all.spread()

    def part_units():
        fc_all.corners()

    stages = {
        1: fc_sum.first_hop,
        6: fc_sum.second_hop,
        10: lambda: fc_sum.last_hop(grad_fc),
        15: settle_units,
    }

    def slot(quarter):
        for number, stage in stages.items():
            if number % 4 == quarter:
                pl.when(step == number // 4)(stage)

    masks = head_masks()
    first_image = place.half * (bucket_ref.shape[1] // 2)
    normed_one, factor_one = norm_rows(tok_own[own_block(step, rows)].astype(F32))
    hidden_one_t = (normed_one * vec_ref[0:1] + vec_ref[1:2]).astype(BF16).T
    grad_resid = gres_ref[...]
    resid_low = grad_resid.astype(BF16)
    grad_hidden_one = None
    for half in range(2):
        base = half * 3 * SLOT
        grad_heads = mm(resid_low, wt_ref[half, :, AT_OUT:AT_VEC], NN).astype(BF16)
        parts = []
        for image in range(pack):
            span = slice(image * SEQ, (image + 1) * SEQ)
            used = used_lanes(bucket_ref, heads_ref, first_image + step * pack + image, half).astype(BF16)
            heads = grad_heads[span] * used
            queries, keys, values = (
                proj_ref[span, base + which * SLOT : base + (which + 1) * SLOT] for which in range(3)
            )
            sums = [None, None, None]
            for s in range(3):
                own = heads * masks[s]
                low = low_ref[(image * 2 + half) * 3 + s]
                grad_probs = mm(own, values, NT)
                probs = low.astype(F32)
                weighed = probs * grad_probs
                grad_scores = (weighed - probs * lane_sum(weighed)).astype(BF16)
                terms = (
                    mm(grad_scores, keys * masks[s], NN),
                    mm(grad_scores, queries * masks[s], TN),
                    mm(low, own, TN),
                )
                sums = [t if o is None else o + t for o, t in zip(sums, terms)]
            parts.append([(v * c).astype(BF16) for v, c in zip(sums, (0.125, 0.125, 1.0))])
            if image == 0:
                slot(2 * half)
        for which in range(3):
            lanes = slice(which * SLOT, (which + 1) * SLOT)
            grad_proj = jnp.concatenate([part[which] for part in parts], axis=0)
            acc_ref[half, :, lanes] += mm(hidden_one_t, grad_proj, NN)
            term = mm(grad_proj, wt_ref[half, :, lanes], NT)
            grad_hidden_one = term if grad_hidden_one is None else grad_hidden_one + term
        if half == 0:
            slot(1)

    gtok_own[step] = grad_resid + norm_back(grad_hidden_one * vec_ref[0:1], normed_one, factor_one)
    sums_ref[0:1] += jnp.sum(grad_hidden_one * normed_one, axis=0, keepdims=True)
    sums_ref[1:2] += jnp.sum(grad_hidden_one, axis=0, keepdims=True)

    slot(3)

    def own_rows(index):
        start = place.half * count + index * rows
        return gtok_ref.at[pl.ds(pl.multiple_of(start, rows), rows)]

    @pl.when(step == steps - 1)
    def _():
        columns = sums_ref[...].T[:, 0 : LATE - TAIL].astype(BF16)
        ranks, own = at_parts.shape[1], at_parts.shape[2]
        for half in range(2):
            for which in range(3):
                piece = acc_ref[half, :, which * SLOT : which * SLOT + HEADS].astype(BF16)
                at_parts[half, :, :, which * HEADS : (which + 1) * HEADS] = piece.reshape(ranks, own, HEADS)
            at_parts[half, :, :, TAIL:LATE] = columns.reshape(ranks, own, LATE - TAIL)
        at_sum.start()
        at_sum.first_hop()
        for index in range(gtok_own.shape[0]):
            side.start(1 + index, gtok_own.at[index], own_rows(index), place.sibling)
            pltpu.make_async_copy(gtok_own.at[index], own_rows(index), local_sems.at[3 + index]).start()
        mom_at[...] = jnp.zeros_like(mom_at)
        for which in range(3):
            mom_at[:, which * HEADS : (which + 1) * HEADS] = 0.95 * qkv_ref[which]
        at_sum.second_hop()
        at_sum.last_hop(grad_at)
        spread_units()
        at_sum.finish(grad_at)
        mom_at[:, 0:TAIL] = mom_at[:, 0:TAIL] + grad_at[:, 0:TAIL]
        own_at[:, 0:TAIL] = mom_at[:, 0:TAIL].astype(BF16)
        lanes = lax.broadcasted_iota(jnp.int32, (own, LATE - TAIL), 1)
        tile = jnp.zeros(lanes.shape, F32)
        pieces = (
            grad_at[:, 0:TAIL], grad_fc[:, FC:EARLY], grad_fc[:, 0 : FC // 2],
            grad_fc[:, FC // 2 : FC], grad_at[:, TAIL:LATE],
        )
        for number, piece in enumerate(pieces):
            square = jnp.sum(lane_sum(piece * piece), axis=0, keepdims=True)
            square = jnp.broadcast_to(square * (0.5 if number == 4 else 1.0), lanes.shape)
            high = square.astype(BF16).astype(F32)
            tile = jnp.where(lanes == number, high, tile)
            tile = jnp.where(lanes == 32 + number, square - high, tile)
        own_at[:, TAIL:LATE] = tile.astype(BF16)
        at_home.start()
        at_all.start_column()
        at_all.start_plane()
        at_all.plane(0)
        at_all.columns()
        part_units()
        at_all.planes()
        at_all.corners()
        fc_all.share()
        at_all.finish()
        fc_all.finish()
        side.arrived(0, out_half)
        side.left(0, out_half)
        for index in range(gtok_own.shape[0]):
            side.arrived(1 + index, gtok_own.at[0])
            side.left(1 + index, gtok_own.at[0])
            pltpu.make_async_copy(gtok_own.at[index], own_rows(index), local_sems.at[3 + index]).wait()
        at_home.wait()


def back_pass(bucket, heads, tokens, gres, proj, low, wt, vec, gvec, fc_parts, moms, out_half):
    count, model = gres.shape
    rows = fc_parts.shape[3]
    ranks = fc_parts.shape[1] * fc_parts.shape[2]
    block = PAIR * SEQ
    steps = count // block

    def by_step(lanes):
        return pl.BlockSpec((block, lanes), lambda i: (i, 0))

    anywhere = pl.BlockSpec(memory_space=pl.ANY)
    return pl.pallas_call(
        back_kernel,
        out_shape=(
            jax.ShapeDtypeStruct((2 * count, model), F32),
            jax.ShapeDtypeStruct((rows, EARLY), F32),
            jax.ShapeDtypeStruct((rows, EARLY), F32),
            jax.ShapeDtypeStruct((rows, LATE), F32),
            jax.ShapeDtypeStruct((rows, LATE), F32),
            jax.ShapeDtypeStruct(fc_parts.shape, BF16),
            jax.ShapeDtypeStruct((2, ranks, rows, LATE), BF16),
            jax.ShapeDtypeStruct((count, model), F32),
        ),
        grid_spec=pltpu.PrefetchScalarGridSpec(
            num_scalar_prefetch=0,
            grid=(steps,),
            in_specs=[
                once(bucket.shape),
                once(heads.shape),
                anywhere,
                by_step(model),
                by_step(6 * SLOT),
                pl.BlockSpec((PAIR * 6, SEQ, SEQ), lambda i: (i, 0, 0)),
                once(wt.shape),
                once(vec.shape),
                once(gvec.shape),
                once(fc_parts.shape),
            ]
            + [once(m.shape) for m in moms]
            + [anywhere],
            out_specs=[
                anywhere,
                once((rows, EARLY)),
                once((rows, EARLY)),
                once((rows, LATE)),
                once((rows, LATE)),
                anywhere,
                anywhere,
                anywhere,
            ],
            scratch_shapes=[
                pltpu.VMEM((2, model, AT_OUT), F32),
                pltpu.VMEM((128, model), F32),
                pltpu.VMEM((steps, block, model), F32),
                pltpu.VMEM((2, ranks, rows, LATE), BF16),
                pltpu.VMEM((rows, EARLY), BF16),
                pltpu.VMEM((rows, LATE), BF16),
                pltpu.VMEM((count, model), BF16),
            ]
            + wide_scratch(rows, EARLY, EARLY_CUT)
            + scatter_scratch(ranks, rows, LATE, LATE_CUT)
            + dma(WideScatter.SLOTS)
            + dma(SCATTER_SLOTS)
            + dma(WideGather.SLOTS)
            + dma(GATHER_SLOTS)
            + dma(1 + steps)
            + [pltpu.SemaphoreType.DMA((3 + steps,))],
        ),
        compiler_params=pltpu.CompilerParams(
            collective_id=1, has_side_effects=True, vmem_limit_bytes=60 * 1024 * 1024
        ),
        name="back_pass",
    )(bucket, heads, tokens, gres, proj, low, wt, vec, gvec, fc_parts, *moms, out_half)


QUINTIC = (3.4445, -4.775, 2.0315)
RATES = (2.0, 2.0, math.sqrt(3.0), math.sqrt(32.0))
RANGES = ((0, FC // 2), (FC // 2, FC), (0, LATE), (FC, EARLY))
IN_LATE = 2


def mm3(a, b):
    return lax.dot_general(a, b, NN, precision=lax.Precision.HIGH, preferred_element_type=F32)


def eye_mask(n):
    return lax.broadcasted_iota(jnp.int32, (n, n), 0) == lax.broadcasted_iota(jnp.int32, (n, n), 1)


def chain_kernel(
    fc_ref, at_ref, grad_fc, mom_fc, grad_at, mom_at, vec_ref, first_ref, second_ref,
    fc1_ref, fc2_ref, qkv_ref, wo_ref, out_half, out_other, gtok_both,
    root_ref, norm_ref, gfc1, gfc2, gqkv, gwo, gvec, mfc1, mfc2, mqkv, mwo,
    vec_new, first_new, second_new, kept_fc, kept_at, out_ref, gtok_ref,
    gram_ref, poly_ref, rows_ref, turn_ref, out_hold, gtok_hold, sems,
):
    place = Place()
    count = out_half.shape[0]
    half = place.half
    which = 2 * place.x + half
    sources = ((out_half, out_hold.at[0]), (out_other, out_hold.at[1]), (gtok_both, gtok_hold))
    loads = [pltpu.make_async_copy(src, hold, sems.at[i]) for i, (src, hold) in enumerate(sources)]
    stores = []
    for i, part in enumerate((half, 1 - half)):
        rows = pl.ds(pl.multiple_of(part * count, 8), count)
        stores.append(pltpu.make_async_copy(out_hold.at[i], out_ref.at[rows], sems.at[3 + i]))
    stores.append(pltpu.make_async_copy(gtok_hold, gtok_ref, sems.at[5]))
    for load in loads:
        load.start()
    model = fc_ref.shape[1]
    for number, (start, stop) in enumerate(RANGES):
        buf = at_ref if number == IN_LATE else fc_ref

        @pl.when(which == number)
        def _():
            lower, upper = buf[0, :, start:stop], buf[1, :, start:stop]
            if number == IN_LATE:
                keep = (lax.broadcasted_iota(jnp.int32, (1, LATE), 1) < TAIL).astype(F32).astype(BF16)
                lower, upper = lower * keep, upper * keep
            gram_ref[...] = mm(lower, lower, NT) + mm(upper, upper, NT)

    eye = eye_mask(model)
    gram = gram_ref[...]
    total = jnp.sum(lane_sum(jnp.where(eye, gram, 0.0)), axis=0, keepdims=True)
    scale = 1.0 / (jnp.sqrt(total) + 1e-07)
    gram_ref[...] = gram * (scale * scale)
    a, b, c = QUINTIC

    def polynomial():
        gram = gram_ref[...]
        return jnp.where(eye, a, 0.0) + b * gram + c * mm3(gram, gram)

    def advance(poly):
        gram_ref[...] = mm3(mm3(gram_ref[...], poly), poly)

    poly = polynomial()
    poly_ref[...] = poly
    first_row = (place.dp // 2) * rows_ref.shape[0]
    rows_ref[...] = poly_ref[pl.ds(pl.multiple_of(first_row, 8), rows_ref.shape[0])]
    advance(poly)
    for load, store in zip(loads, stores):
        load.wait()
        store.start()

    def sweep(_, carry):
        poly = polynomial()
        rows_ref[...] = mm3(rows_ref[...], poly)
        advance(poly)
        return carry

    lax.fori_loop(0, NS_ITERS - 2, sweep, 0)
    rows, gram = rows_ref[...], gram_ref[...]
    once_more = mm3(rows, gram)
    last = (a * rows + b * once_more + c * mm3(once_more, gram)) * scale
    for part in range(root_ref.shape[0]):
        root_ref[part] = last[part * root_ref.shape[1] : (part + 1) * root_ref.shape[1]]

    wide = FC // 2
    gfc1[...], gfc2[...] = grad_fc[:, 0:wide], grad_fc[:, wide:FC]
    mfc1[...], mfc2[...] = mom_fc[:, 0:wide], mom_fc[:, wide:FC]
    gwo[...] = grad_fc[:, FC : FC + HEADS]
    mwo[...] = mom_fc[:, FC : FC + HEADS]
    kept_fc[...] = jnp.zeros_like(kept_fc)
    kept_fc[:, 0:wide] = 0.999 * fc1_ref[...]
    kept_fc[:, wide:FC] = 0.999 * fc2_ref[...]
    kept_fc[:, FC : FC + HEADS] = 0.999 * wo_ref[...]
    kept_at[...] = jnp.zeros_like(kept_at)
    for part in range(3):
        span = slice(part * HEADS, (part + 1) * HEADS)
        gqkv[part] = grad_at[:, span]
        mqkv[part] = mom_at[:, span]
        kept_at[:, span] = 0.999 * qkv_ref[part]
    own = grad_at.shape[0]
    turn_ref[...] = jnp.zeros_like(turn_ref)
    turn_ref[0:own, 0 : LATE - TAIL] = grad_at[:, TAIL:LATE]
    turned = turn_ref[...].T[0:6, 0 : vec_ref.shape[1]]
    first = 0.9 * first_ref[...] + 0.1 * turned
    second = 0.95 * second_ref[...] + 0.05 * turned * turned
    gvec[...] = turned
    first_new[...] = first
    second_new[...] = second
    vec_new[...] = vec_ref[...] - 0.5 * (first / (1.0 - 0.9**STEP)) / (
        jnp.sqrt(second / (1.0 - 0.95**STEP)) + 1e-08
    )
    tiles = at_ref[0, :, LATE - 128 : LATE].astype(F32) + at_ref[1, :, LATE - 128 : LATE].astype(F32)
    leads = lax.broadcasted_iota(jnp.int32, tiles.shape, 0) % own == 0
    squares = jnp.sum(jnp.where(leads, tiles, 0.0), axis=0, keepdims=True)
    squares = pltpu.roll(squares, 64, 1)
    norm_ref[...] = jnp.sqrt(jnp.abs(squares + pltpu.roll(squares, 96, 1)))
    for store in stores:
        store.wait()


def run_chain(fc_buf, at_buf, grad_fc, mom_fc, grad_at, mom_at, vectors, first, second, weights, wholes):
    model = fc_buf.shape[1]
    own, columns = grad_fc.shape[0], vectors.shape[1]
    count = wholes[0].shape[0]
    full = (2 * count, model)
    vmem = pl.BlockSpec(memory_space=pltpu.VMEM)
    anywhere = pl.BlockSpec(memory_space=pl.ANY)
    shapes = [(own, 768), (own, 768), (3, own, 192), (own, 192)]
    outs = [(2, own, model), (1, 128)] + shapes + [(6, columns)] + shapes + [(6, columns)] * 3
    outs += [(own, EARLY), (own, LATE)] + [full] * 2
    return pl.pallas_call(
        chain_kernel,
        out_shape=tuple(jax.ShapeDtypeStruct(shape, F32) for shape in outs),
        in_specs=[vmem] * 13 + [anywhere] * 3,
        out_specs=tuple([vmem] * (len(outs) - 2) + [anywhere] * 2),
        scratch_shapes=[
            pltpu.VMEM((model, model), F32),
            pltpu.VMEM((model, model), F32),
            pltpu.VMEM((2 * own, model), F32),
            pltpu.VMEM((128, 128), F32),
            pltpu.VMEM((2, count, model), F32),
            pltpu.VMEM(full, F32),
            pltpu.SemaphoreType.DMA((6,)),
        ],
        compiler_params=pltpu.CompilerParams(vmem_limit_bytes=60 * 1024 * 1024),
        name="run_chain",
    )(fc_buf, at_buf, grad_fc, mom_fc, grad_at, mom_at, vectors, first, second, *weights, *wholes)


def roots_kernel(
    root_ref, kept_fc, kept_at, fc_ref, at_ref,
    nfc1, nfc2, nqkv, nwo, rows_ref, fc_own, at_own, send_sem, recv_sem, load_sem,
):
    place = Place()
    x, half = place.x, place.half
    loads = [
        pltpu.make_async_copy(fc_ref.at[half], fc_own, load_sem.at[0]),
        pltpu.make_async_copy(at_ref.at[half], at_own, load_sem.at[1]),
    ]
    for load in loads:
        load.start()
    barrier = pltpu.get_barrier_semaphore()
    peers = [(1 - x, half), (x, 1 - half), (1 - x, 1 - half)]
    ids = [(place.index(place.z, place.y, px), ph) for px, ph in peers]
    for peer in ids:
        pl.semaphore_signal(barrier, inc=1, device_id=peer, device_id_type=MESH)
    pl.semaphore_wait(barrier, 3)
    mail = Mail(place, send_sem, recv_sem)
    mine = 2 * x + half
    for slot, peer in enumerate(ids):
        mail.start(slot, root_ref.at[peers[slot][0]], rows_ref.at[mine], peer)
    rows_ref[mine] = root_ref[x]
    for load in loads:
        load.wait()
    for slot in range(3):
        mail.arrived(slot, rows_ref.at[0])
    for number, (start, stop) in enumerate(RANGES):
        rows = rows_ref[number]
        high = rows.astype(BF16)
        low = (rows - high.astype(F32)).astype(BF16)
        late = number == IN_LATE
        moment = (at_own if late else fc_own)[:, start:stop]
        step = RATES[number] * (mm(high, moment, NN) + mm(low, moment, NN))
        new = (kept_at if late else kept_fc)[:, start:stop] - step
        if late:
            for part in range(3):
                nqkv[part] = new[:, part * HEADS : (part + 1) * HEADS]
        else:
            out = (nfc1, nfc2, None, nwo)[number]
            out[...] = new[:, 0 : out.shape[1]]
    for slot in range(3):
        mail.left(slot, rows_ref.at[0])


def apply_roots(root, kept_fc, kept_at, fc_buf, at_buf, weights):
    _, rows, model = root.shape
    vmem = pl.BlockSpec(memory_space=pltpu.VMEM)
    anywhere = pl.BlockSpec(memory_space=pl.ANY)
    return pl.pallas_call(
        roots_kernel,
        out_shape=tuple(jax.ShapeDtypeStruct(w.shape, F32) for w in weights),
        in_specs=[vmem] * 3 + [anywhere] * 2,
        out_specs=(vmem,) * 4,
        scratch_shapes=[
            pltpu.VMEM((4, rows, model), F32),
            pltpu.VMEM((model, EARLY), BF16),
            pltpu.VMEM((model, LATE), BF16),
        ]
        + dma(3)
        + [pltpu.SemaphoreType.DMA((2,))],
        compiler_params=pltpu.CompilerParams(
            collective_id=2, has_side_effects=True, vmem_limit_bytes=32 * 1024 * 1024
        ),
        name="apply_roots",
    )(root, kept_fc, kept_at, fc_buf, at_buf)


def flat(part):
    return part.T if part.ndim == 2 else jnp.transpose(part, (0, 2, 1))


def pack(fc1, fc2, qkv, out):
    pad = ((0, 0), (0, SLOT - out.shape[1]))
    return jnp.concatenate([fc1, fc2] + [jnp.pad(part, pad) for part in (*qkv, out)], axis=1)


def unpack(packed, like):
    fc1, fc2, qkv, out = like
    split = jnp.stack([packed[:, QKV + part * SLOT :][:, : qkv.shape[2]] for part in range(3)])
    return packed[:, FC1:FC2], packed[:, FC2:QKV], split, packed[:, OUT : OUT + out.shape[1]]


def root_of(gram):
    a, b, c = QUINTIC
    eye = eye_mask(gram.shape[0])
    scale = 1.0 / (jnp.sqrt(jnp.sum(jnp.where(eye, gram, 0.0))) + 1e-07)
    gram = gram * (scale * scale)
    root = jnp.where(eye, scale, 0.0)
    for _ in range(NS_ITERS):
        poly = jnp.where(eye, a, 0.0) + b * gram + c * mm3(gram, gram)
        root = mm3(root, poly)
        gram = mm3(mm3(gram, poly), poly)
    return root


def general(half, bucket, widths, counts, tokens, cotangent, weights, moms, vectors, vec_first, vec_second):
    dp = lax.axis_index("dp")
    rows = weights[0].shape[0]
    vec = jnp.pad(vectors.T, ((0, 0), (0, PACK - VEC - vectors.shape[0])))
    own = jnp.concatenate([pack(*weights), vec], axis=1).astype(BF16)
    packed = lax.all_gather(lax.all_gather(own, "dp", axis=0, tiled=True), "mlp")
    out_half, gtok_half, grads = image_pass(half.reshape(1), bucket, widths, counts, tokens, cotangent, packed)
    output = lax.all_gather(out_half, "mlp", axis=0, tiled=True)
    gtok = lax.all_gather(gtok_half, "mlp", axis=0, tiled=True)
    grad = lax.psum_scatter(grads.astype(F32), "mlp", scatter_dimension=0)
    grad = lax.psum_scatter(grad, "dp", scatter_dimension=0, tiled=True)
    mom = 0.95 * pack(*moms) + grad[:, 0:VEC]
    spans = ((FC1, FC2), (FC2, QKV), (QKV, OUT), (OUT, VEC))
    squares = [jnp.sum(jnp.square(grad[:, start:stop])) for start, stop in spans[2:] + spans[:2]]
    squares.append(0.5 * jnp.sum(jnp.square(grad[:, VEC:PACK])))
    norms = jnp.sqrt(lax.psum(jnp.stack(squares), ("dp", "mlp")))
    buf = lax.all_gather(lax.all_gather(mom.astype(BF16), "dp", axis=0, tiled=True), "mlp")
    ours = lax.dynamic_index_in_dim(buf, half, 0, keepdims=False)
    steps = []
    for (start, stop), rate in zip(spans, RATES):
        root = root_of(sum(mm(buf[h, :, start:stop], buf[h, :, start:stop], NT) for h in range(2)))
        root = lax.dynamic_slice_in_dim(root, dp * rows, rows, 0)
        high = root.astype(BF16)
        low = (root - high.astype(F32)).astype(BF16)
        steps.append(rate * (mm(high, ours[:, start:stop], NN) + mm(low, ours[:, start:stop], NN)))
    moved = unpack(jnp.concatenate(steps, axis=1), weights)
    gvec = grad[:, VEC : VEC + vectors.shape[0]].T
    first = 0.9 * vec_first + 0.1 * gvec
    second = 0.95 * vec_second + 0.05 * gvec * gvec
    vec_new = vectors - 0.5 * (first / (1.0 - 0.9**STEP)) / (
        jnp.sqrt(second / (1.0 - 0.95**STEP)) + 1e-08
    )

    def ordered(parts):
        fc1, fc2, qkv, out = parts
        return flat(qkv), flat(out), flat(fc1), flat(fc2)

    news = [0.999 * w - move for w, move in zip(weights, moved)]
    return (
        output, gtok, *ordered(unpack(grad, weights)), gvec,
        *ordered(unpack(mom, weights)), *ordered(news), vec_new, first, second, norms,
    )


def body(
    tokens, cotangent, image_bucket, bucket_width, bucket_heads,
    w_qkv, w_out, w_fc1, w_fc2, vectors,
    mom_qkv, mom_out, mom_fc1, mom_fc2, vec_first, vec_second,
):
    half = lax.axis_index("mlp").astype(jnp.int32)
    ranks = lax.axis_size("dp")
    model = tokens.shape[1]
    rows = w_fc1.shape[1]
    weights = [flat(w) for w in (w_fc1, w_fc2, w_qkv, w_out)]
    moms = [flat(m) for m in (mom_fc1, mom_fc2, mom_qkv, mom_out)]
    images = image_bucket.shape[0] // 2
    if ranks != 16 or images != 4 * PAIR:
        return general(
            half, image_bucket, bucket_width, bucket_heads, tokens, cotangent,
            weights, moms, vectors, vec_first, vec_second,
        )
    bucket, heads = image_bucket.reshape(1, -1), bucket_heads.reshape(1, -1)
    resid, proj, low, mixed, wt, vec_rows, fc_weights = attend_pass(bucket, heads, tokens, weights, vectors, ranks)
    out_half, gres, fc_parts, gvec_rows = units_pass(
        half.reshape(1), image_bucket, bucket_width, resid, cotangent, mixed,
        fc_weights.reshape(2, model, FC), vec_rows,
    )
    gtok_both, grad_fc, mom_fc_new, grad_at, mom_at_new, fc_buf, at_buf, out_other = back_pass(
        bucket, heads, tokens, gres, proj, low, wt, vec_rows, gvec_rows,
        fc_parts.reshape(2, 4, 4, rows, EARLY), moms, out_half,
    )
    fc_buf, at_buf = fc_buf.reshape(2, model, EARLY), at_buf.reshape(2, model, LATE)
    (
        root, norms, gfc1, gfc2, gqkv, gwo, gvec, mfc1, mfc2, mqkv, mwo,
        vec_new, first, second, kept_fc, kept_at, output, gtok,
    ) = run_chain(
        fc_buf, at_buf, grad_fc, mom_fc_new, grad_at, mom_at_new, vectors, vec_first, vec_second,
        weights, (out_half, out_other, gtok_both),
    )
    nfc1, nfc2, nqkv, nwo = apply_roots(root, kept_fc, kept_at, fc_buf, at_buf, weights)
    return (
        output, gtok,
        flat(gqkv), flat(gwo), flat(gfc1), flat(gfc2), gvec,
        flat(mqkv), flat(mwo), flat(mfc1), flat(mfc2),
        flat(nqkv), flat(nwo), flat(nfc1), flat(nfc2),
        vec_new, first, second, norms[0, 0:5],
    )


def solution(mesh):
    halves, columns = P("mlp", "dp"), P(None, "dp")
    blocks = P(None, "mlp", "dp")
    matrices = (blocks, halves, halves, halves)
    placed = (P("dp", None), P("dp", None), P("dp"), P(), P()) + matrices + (columns,) + matrices + (columns, columns)
    outs = (P("dp", None), P("dp", None)) + matrices + (columns,) + matrices + matrices + (columns,) * 3 + (P(),)
    return jax.shard_map(body, mesh=mesh, in_specs=placed, out_specs=outs, check_vma=False)
```

```python
import functools
import math

import jax
import jax.numpy as jnp
from jax import lax
from jax.experimental import pallas as pl
from jax.experimental.pallas import tpu as pltpu
from jax.sharding import PartitionSpec as P

HD = 64
NS_ITERS = 5
STEP = 10
EPSILON = 1e-06
F32 = jnp.float32
BF16 = jnp.bfloat16
NN = (((1,), (0,)), ((), ()))
NT = (((1,), (1,)), ((), ()))
TN = (((0,), (0,)), ((), ()))

FC1, FC2, QKV, OUT, VEC, PACK = 0, 768, 1536, 2304, 2560, 2688
SLOT = 256
SEQ = 256
PAIR = 2
CHUNK = 256


def mm(a, b, dims):
    return lax.dot_general(a, b, dims, preferred_element_type=F32)


def lane_sum(v):
    return jnp.sum(v, axis=-1, keepdims=True)


def norm_rows(v):
    inv = 1.0 / v.shape[-1]
    center = v - lane_sum(v) * inv
    factor = lax.rsqrt(lane_sum(center * center) * inv + EPSILON)
    return center * factor, factor


def norm_back(g, n, factor):
    inv = 1.0 / g.shape[-1]
    return factor * (g - lane_sum(g) * inv - n * (lane_sum(g * n) * inv))


def image_kernel(
    half_ref, bucket_ref, widths_ref, counts_ref,
    tok_ref, cot_ref, w_ref,
    out_ref, gtok_ref, grad_ref,
    acc_ref, vec_ref, gvec_ref, q_ref, k_ref, v_ref, mixed_ref, probs_ref, low_ref,
    y_ref, gh_ref,
):
    step = pl.program_id(0)
    rows, model = tok_ref.shape
    heads_half = 3
    pack = rows // SEQ
    first = (half_ref[0] * pl.num_programs(0) + step) * pack
    buckets = [bucket_ref[first + image] for image in range(pack)]
    widths = [widths_ref[bucket] for bucket in buckets]
    counts = [counts_ref[bucket] for bucket in buckets]
    width, count = widths[0], counts[0]
    for image in range(1, pack):
        width, count = jnp.maximum(width, widths[image]), jnp.maximum(count, counts[image])
    row_ids = lax.broadcasted_iota(jnp.int32, (rows, 1), 0)
    row_width = jnp.full((rows, 1), widths[0], jnp.int32)
    for image in range(1, pack):
        row_width = jnp.where(row_ids >= image * SEQ, widths[image], row_width)

    @pl.when(step == 0)
    def _():
        acc_ref[...] = jnp.zeros_like(acc_ref)
        gvec_ref[...] = jnp.zeros_like(gvec_ref)
        turned = w_ref[0, :, VEC:PACK].astype(F32).T
        vec_ref[...] = turned[0:8]

    lane_head = lax.broadcasted_iota(jnp.int32, (1, SLOT), 1) // HD
    masks = [(lane_head == s).astype(F32).astype(BF16) for s in range(heads_half)]

    def used_heads(image):
        return (lane_head < counts[image] - heads_half).astype(F32)

    def spans():
        return [slice(image * SEQ, (image + 1) * SEQ) for image in range(pack)]

    x = tok_ref[...].astype(F32)
    normed_one, factor_one = norm_rows(x)
    hidden_one = (normed_one * vec_ref[0:1] + vec_ref[1:2]).astype(BF16)
    for half in range(2):
        for ref, which in ((q_ref, 0), (k_ref, 1), (v_ref, 2)):
            lanes = slice(QKV + which * SLOT, QKV + (which + 1) * SLOT)
            ref[half] = mm(hidden_one, w_ref[half, :, lanes], NN).astype(BF16)

        def attend():
            for image, span in enumerate(spans()):
                total = None
                for s in range(heads_half):
                    slot = (image * 2 + half) * heads_half + s
                    scores = mm(q_ref[half, span] * masks[s], k_ref[half, span], NT) * 0.125
                    top = jnp.max(scores, axis=-1, keepdims=True)
                    grown = jnp.exp(scores - top)
                    probs = grown * (1.0 / lane_sum(grown))
                    low = probs.astype(BF16)
                    probs_ref[slot] = probs
                    low_ref[slot] = low
                    term = mm(low, v_ref[half, span] * masks[s], NN)
                    total = term if total is None else total + term
                if half:
                    total = total * used_heads(image)
                mixed_ref[half, span] = total.astype(BF16)

        if half == 0:
            attend()
        else:
            mixed_ref[half] = jnp.zeros_like(mixed_ref[half])
            pl.when(count > heads_half)(attend)

    branch = mm(mixed_ref[0], w_ref[0, :, OUT:VEC], NT) + mm(mixed_ref[1], w_ref[1, :, OUT:VEC], NT)
    resid = x + branch + vec_ref[4:5]
    normed_two, factor_two = norm_rows(resid)
    hidden_two = (normed_two * vec_ref[2:3] + vec_ref[3:4]).astype(BF16)
    cot = cot_ref[...]
    hidden_two_t = hidden_two.T
    cot_t = cot.T
    y_ref[...] = resid + vec_ref[5:6]
    gh_ref[...] = jnp.zeros_like(gh_ref)
    per_half = FC2 // CHUNK
    for chunk in range(2 * per_half):
        half, part = divmod(chunk, per_half)
        one = slice(FC1 + part * CHUNK, FC1 + (part + 1) * CHUNK)
        two = slice(FC2 + part * CHUNK, FC2 + (part + 1) * CHUNK)

        def units_pass():
            pre = mm(hidden_two, w_ref[half, :, one], NN)
            units = chunk * CHUNK + lax.broadcasted_iota(jnp.int32, pre.shape, 1)
            cumulative = 0.5 + 0.5 * lax.erf(pre * 0.7071067811865476)
            density = jnp.exp(-0.5 * pre * pre) * 0.3989422804014327
            cumulative = jnp.where(units < row_width, cumulative, 0.0)
            density = jnp.where(units < row_width, density, 0.0)
            act = (pre * cumulative).astype(BF16)
            grad_act = mm(cot, w_ref[half, :, two], NN)
            grad_pre = (grad_act * (cumulative + pre * density)).astype(BF16)
            y_ref[...] += mm(act, w_ref[half, :, two], NT)
            gh_ref[...] += mm(grad_pre, w_ref[half, :, one], NT)
            acc_ref[half, :, two] += mm(cot_t, act, NN)
            acc_ref[half, :, one] += mm(hidden_two_t, grad_pre, NN)

        if chunk < 2:
            units_pass()
        else:
            pl.when(width > chunk * CHUNK)(units_pass)

    out_ref[...] = y_ref[...]
    grad_hidden_two = gh_ref[...]
    cot_f = cot.astype(F32)
    grad_resid = cot_f + norm_back(grad_hidden_two * vec_ref[2:3], normed_two, factor_two)
    resid_low = grad_resid.astype(BF16)
    resid_low_t = resid_low.T
    hidden_one_t = hidden_one.T
    for half in range(2):
        acc_ref[half, :, OUT:VEC] += mm(resid_low_t, mixed_ref[half], NN)

        def back():
            grad_heads = mm(resid_low, w_ref[half, :, OUT:VEC], NN).astype(BF16)
            parts = []
            for image, span in enumerate(spans()):
                heads = grad_heads[span]
                if half:
                    heads = heads * used_heads(image).astype(BF16)
                sums = [None, None, None]
                for s in range(heads_half):
                    slot = (image * 2 + half) * heads_half + s
                    own = heads * masks[s]
                    grad_probs = mm(own, v_ref[half, span], NT)
                    probs = probs_ref[slot]
                    weighed = probs * grad_probs
                    grad_scores = (weighed - probs * lane_sum(weighed)).astype(BF16)
                    terms = (
                        mm(grad_scores, k_ref[half, span] * masks[s], NN),
                        mm(grad_scores, q_ref[half, span] * masks[s], TN),
                        mm(low_ref[slot], own, TN),
                    )
                    sums = [t if o is None else o + t for o, t in zip(sums, terms)]
                parts.append([(v * c).astype(BF16) for v, c in zip(sums, (0.125, 0.125, 1.0))])
            total = None
            for which in range(3):
                lanes = slice(QKV + which * SLOT, QKV + (which + 1) * SLOT)
                grad_proj = jnp.concatenate([part[which] for part in parts], axis=0)
                acc_ref[half, :, lanes] += mm(hidden_one_t, grad_proj, NN)
                term = mm(grad_proj, w_ref[half, :, lanes], NT)
                total = term if total is None else total + term
            return total

        if half == 0:
            gh_ref[...] = back()
        else:

            @pl.when(count > heads_half)
            def _():
                gh_ref[...] += back()

    grad_hidden_one = gh_ref[...]
    gtok_ref[...] = grad_resid + norm_back(grad_hidden_one * vec_ref[0:1], normed_one, factor_one)
    sums = (
        grad_hidden_one * normed_one,
        grad_hidden_one,
        grad_hidden_two * normed_two,
        grad_hidden_two,
        grad_resid,
        cot_f,
    )
    for row, values in enumerate(sums):
        gvec_ref[row : row + 1] += jnp.sum(values, axis=0, keepdims=True)

    @pl.when(step == pl.num_programs(0) - 1)
    def _():
        grad_ref[0, :, 0:VEC] = acc_ref[0].astype(BF16)
        grad_ref[1, :, 0:VEC] = acc_ref[1].astype(BF16)
        columns = gvec_ref[...].T.astype(BF16)
        grad_ref[0, :, VEC:PACK] = columns
        grad_ref[1, :, VEC:PACK] = columns


def image_pass(half, bucket, widths, counts, tokens, cotangent, packed):
    images = bucket.shape[0] // 2
    model = tokens.shape[1]
    rows = images * SEQ
    images = images // PAIR
    seq = PAIR * SEQ
    picked = pl.BlockSpec((seq, model), lambda i, h, b, w, c: (h[0] * images + i, 0))
    placed = pl.BlockSpec((seq, model), lambda i, h, b, w, c: (i, 0))
    whole = pl.BlockSpec(
        (2, model, PACK), lambda i, h, b, w, c: (0, 0, 0), pipeline_mode=pl.Buffered(1)
    )
    heads = 6
    flops = 2 * rows * model * (3 * 4 * model + 3 * 8 * model)
    return pl.pallas_call(
        image_kernel,
        out_shape=(
            jax.ShapeDtypeStruct((rows, model), F32),
            jax.ShapeDtypeStruct((rows, model), F32),
            jax.ShapeDtypeStruct((2, model, PACK), BF16),
        ),
        grid_spec=pltpu.PrefetchScalarGridSpec(
            num_scalar_prefetch=4,
            grid=(images,),
            in_specs=[picked, picked, whole],
            out_specs=[placed, placed, whole],
            scratch_shapes=[
                pltpu.VMEM((2, model, VEC), F32),
                pltpu.VMEM((8, model), F32),
                pltpu.VMEM((128, model), F32),
                pltpu.VMEM((2, seq, SLOT), BF16),
                pltpu.VMEM((2, seq, SLOT), BF16),
                pltpu.VMEM((2, seq, SLOT), BF16),
                pltpu.VMEM((2, seq, SLOT), BF16),
                pltpu.VMEM((PAIR * heads, SEQ, SEQ), F32),
                pltpu.VMEM((PAIR * heads, SEQ, SEQ), BF16),
                pltpu.VMEM((seq, model), F32),
                pltpu.VMEM((seq, model), F32),
            ],
        ),
        compiler_params=pltpu.CompilerParams(vmem_limit_bytes=56 * 1024 * 1024),
        cost_estimate=pl.CostEstimate(flops=flops, bytes_accessed=20 * rows * model, transcendentals=rows * 6144),
        name="image_pass",
    )(half, bucket, widths, counts, tokens, cotangent, packed)


MESH = pl.DeviceIdType.MESH
AT_OUT, AT_VEC, AT = 768, 1024, 1152
HEADS = 192
AT_SENT = 896
FC = 1536
EARLY = FC + SLOT
TAIL, LATE = 3 * HEADS, 640


class Place:
    def __init__(self):
        dp = lax.axis_index("dp")
        self.half = lax.axis_index("mlp")
        self.z = dp // 4
        self.y = (dp // 2) % 2
        self.x = dp % 2
        self.dp = dp
        self.y_peer = (self.index(self.z, 1 - self.y, self.x), self.half)
        self.x_peer = (self.index(self.z, self.y, 1 - self.x), self.half)
        self.sibling = (self.dp, 1 - self.half)

    def index(self, z, y, x):
        return z * 4 + y * 2 + x

    def at_z(self, z):
        return (self.index(z, self.y, self.x), self.half)


def meet(place):
    barrier = pltpu.get_barrier_semaphore()
    peers = [place.at_z((place.z + j) % 4) for j in range(1, 4)]
    peers += [place.y_peer, place.x_peer, place.sibling]
    for peer in peers:
        pl.semaphore_signal(barrier, inc=1, device_id=peer, device_id_type=MESH)
    pl.semaphore_wait(barrier, len(peers))


class Mail:
    def __init__(self, place, send_sem, recv_sem):
        self.place, self.send_sem, self.recv_sem = place, send_sem, recv_sem

    def copy(self, slot, src, dst, peer):
        return pltpu.make_async_remote_copy(
            src_ref=src,
            dst_ref=dst,
            send_sem=self.send_sem.at[slot],
            recv_sem=self.recv_sem.at[slot],
            device_id=peer,
            device_id_type=MESH,
        )

    def start(self, slot, src, dst, peer):
        self.copy(slot, src, dst, peer).start()

    def arrived(self, slot, like):
        self.copy(slot, like, like, self.place.sibling).wait_recv()

    def left(self, slot, like):
        self.copy(slot, like, like, self.place.sibling).wait_send()


GATHER_SLOTS = 35
NEAR_FIRST = (1, 3, 2)


class Gather:
    def __init__(self, place, own, buf, cut, send_sem, recv_sem):
        self.place, self.own, self.buf = place, own, buf
        self.mail = Mail(place, send_sem, recv_sem)
        self.pieces = (pl.ds(0, cut), pl.ds(cut, own.shape[1] - cut))

    def shard(self, k, y, x):
        return self.place.index((self.place.z + 4 - k) % 4, y, x)

    def forward(self, slot, dp, peer, piece=None):
        ref = self.buf.at[self.place.half, dp]
        if piece is not None:
            ref = ref.at[:, self.pieces[piece]]
        self.mail.start(slot, ref, ref, peer)

    def like(self, piece=None):
        ref = self.buf.at[0, 0]
        return ref if piece is None else ref.at[:, self.pieces[piece]]

    def start_column(self):
        place = self.place
        home = self.buf.at[place.half, place.dp]
        for j in NEAR_FIRST:
            self.mail.start(j - 1, self.own, home, place.at_z((place.z + j) % 4))

    def start_plane(self):
        place = self.place
        home = self.buf.at[place.half, place.dp]
        self.mail.start(3, self.own, home, place.y_peer)
        self.mail.start(7, self.own, home, place.x_peer)
        self.mail.start(19, self.own, home, place.sibling)

    def column(self, k):
        place = self.place
        self.mail.arrived(k - 1, self.like())
        dp = self.shard(k, place.y, place.x)
        self.forward(3 + k, dp, place.y_peer)
        self.forward(7 + k, dp, place.x_peer)
        self.forward(19 + k, dp, place.sibling)

    def plane(self, k):
        place = self.place
        self.mail.arrived(3 + k, self.like())
        dp = self.shard(k, 1 - place.y, place.x)
        self.forward(11 + k, dp, place.x_peer, 0)
        self.forward(23 + k, dp, place.sibling)
        self.mail.arrived(7 + k, self.like())
        dp = self.shard(k, place.y, 1 - place.x)
        self.forward(15 + k, dp, place.y_peer, 1)
        self.forward(27 + k, dp, place.sibling)

    def corner(self, k):
        place = self.place
        self.mail.arrived(11 + k, self.like(0))
        self.mail.arrived(15 + k, self.like(1))
        self.forward(31 + k, self.shard(k, 1 - place.y, 1 - place.x), place.sibling)

    def finish(self):
        for k in range(16):
            self.mail.arrived(19 + k, self.like())
        for slot in range(GATHER_SLOTS):
            piece = 0 if 11 <= slot < 15 else 1 if 15 <= slot < 19 else None
            self.mail.left(slot, self.like(piece))

    def columns(self):
        for k in NEAR_FIRST:
            self.column(k)

    def planes(self):
        for k in NEAR_FIRST:
            self.plane(k)

    def corners(self):
        for k in (0, *NEAR_FIRST):
            self.corner(k)


SCATTER_SLOTS = 43
Z_ORDER = (2, 1, 3, 0)


class Scatter:
    def __init__(self, place, parts, hold, firsts, seconds, last, cut, send_sem, recv_sem):
        self.place, self.parts, self.hold = place, parts, hold
        self.firsts, self.seconds, self.last = firsts, seconds, last
        self.mail = Mail(place, send_sem, recv_sem)
        self.pieces = (pl.ds(0, cut), pl.ds(cut, hold.shape[2] - cut))

    def shard(self, c, k):
        y, x = self.place.y, self.place.x
        column = ((1 - y, 1 - x), (y, 1 - x), (1 - y, x), (y, x))[c]
        return self.place.index((self.place.z + Z_ORDER[k]) % 4, *column)

    def piece(self, dp, p):
        return self.hold.at[dp, :, self.pieces[p]]

    def load(self, dp, p):
        return self.hold[dp, :, self.pieces[p]].astype(F32)

    def start(self):
        half = self.place.half
        for c in range(4):
            for k in range(4):
                dp = self.shard(c, k)
                self.mail.start(4 * c + k, self.parts.at[1 - half, dp], self.hold.at[dp], self.place.sibling)

    def settle(self, c, k):
        dp = self.shard(c, k)
        self.mail.arrived(4 * c + k, self.hold.at[0])
        total = self.hold[dp].astype(F32) + self.parts[self.place.half, dp].astype(F32)
        self.hold[dp] = total.astype(BF16)
        return dp

    def first_hop(self):
        place, (first_a, first_b) = self.place, self.firsts
        for k in range(4):
            dp = self.settle(0, k)
            self.mail.start(16 + k, self.piece(dp, 0), first_a.at[k], place.x_peer)
            self.mail.start(24 + k, self.piece(dp, 1), first_b.at[k], place.y_peer)
        for k in range(4):
            dp = self.settle(1, k)
            self.mail.start(20 + k, self.piece(dp, 0), first_a.at[4 + k], place.x_peer)
            dp = self.settle(2, k)
            self.mail.start(28 + k, self.piece(dp, 1), first_b.at[4 + k], place.y_peer)
        for k in range(4):
            self.settle(3, k)

    def second_hop(self):
        place, firsts, seconds = self.place, self.firsts, self.seconds
        for k in range(4):
            for p, slot, column, out, peer in ((0, 16, 2, 32, place.y_peer), (1, 24, 1, 36, place.x_peer)):
                self.mail.arrived(slot + k, firsts[p].at[0])
                dp = self.shard(column, k)
                total = self.load(dp, p) + firsts[p][k].astype(F32)
                self.hold[dp, :, self.pieces[p]] = total.astype(BF16)
                self.mail.start(out + k, self.piece(dp, p), seconds[p].at[k], peer)

    def last_hop(self, keep):
        place = self.place
        for k in range(4):
            dp = self.shard(3, k)
            totals = []
            for p, slot, second in ((0, 20, 32), (1, 28, 36)):
                self.mail.arrived(slot + k, self.firsts[p].at[0])
                self.mail.arrived(second + k, self.seconds[p].at[0])
                totals.append(self.load(dp, p) + self.firsts[p][4 + k].astype(F32) + self.seconds[p][k].astype(F32))
            for p in range(2):
                if Z_ORDER[k]:
                    self.hold[dp, :, self.pieces[p]] = totals[p].astype(BF16)
                else:
                    keep[:, self.pieces[p]] = totals[p]
            if Z_ORDER[k]:
                j = Z_ORDER[k]
                self.mail.start(40 + j - 1, self.hold.at[dp], self.last.at[j - 1], place.at_z((place.z + j) % 4))

    def finish(self, keep):
        for j in range(3):
            self.mail.arrived(40 + j, self.last.at[0])
            keep[...] = keep[...] + self.last[j].astype(F32)
        for slot in range(SCATTER_SLOTS):
            if slot < 16 or slot >= 40:
                like = self.hold.at[0]
            elif slot < 32:
                like = self.firsts[(slot - 16) // 8].at[0]
            else:
                like = self.seconds[(slot - 32) // 4].at[0]
            self.mail.left(slot, like)


CHAIN_LANES = (
    (pl.ds(0, FC // 2), pl.ds(FC // 2, FC // 2)),
    (pl.ds(FC, SLOT), pl.ds(FC, SLOT)),
)


class WideGather:
    SLOTS = 8

    def __init__(self, place, own, buf, cut, send_sem, recv_sem):
        self.place, self.own, self.buf = place, own, buf
        self.mail = Mail(place, send_sem, recv_sem)
        self.pieces = (pl.ds(0, cut), pl.ds(cut, own.shape[1] - cut))

    def column(self, y, x, piece=None):
        ref = self.buf.at[self.place.half, :, 2 * y + x]
        return ref if piece is None else ref.at[:, :, self.pieces[piece]]

    def send(self, slot, ref, peer):
        self.mail.start(slot, ref, ref, peer)

    def start(self):
        place = self.place
        home = self.buf.at[place.half, place.z, 2 * place.y + place.x]
        for j in NEAR_FIRST:
            self.mail.start(j - 1, self.own, home, place.at_z((place.z + j) % 4))

    def spread(self):
        place = self.place
        for j in range(3):
            self.mail.arrived(j, self.own)
        self.send(3, self.column(place.y, place.x), place.y_peer)
        self.send(4, self.column(place.y, place.x), place.x_peer)

    def corners(self):
        place = self.place
        self.mail.arrived(3, self.column(place.y, place.x))
        self.send(5, self.column(1 - place.y, place.x, 0), place.x_peer)
        self.mail.arrived(4, self.column(place.y, place.x))
        self.send(6, self.column(place.y, 1 - place.x, 1), place.y_peer)

    def share(self):
        place = self.place
        self.mail.arrived(5, self.column(place.y, place.x, 0))
        self.mail.arrived(6, self.column(place.y, place.x, 1))
        self.each_case(self.share_case)

    def each_case(self, action):
        place = self.place
        for x in range(2):
            for half in range(2):
                here = jnp.logical_and(place.x == x, place.half == half)
                pl.when(here)(functools.partial(action, half, CHAIN_LANES[x][half], CHAIN_LANES[x][1 - half]))

    def share_case(self, half, mine, theirs):
        self.send(7, self.buf.at[half, :, :, :, theirs], self.place.sibling)

    def finish_case(self, half, mine, theirs):
        self.mail.arrived(7, self.buf.at[half, :, :, :, mine])
        self.mail.left(7, self.buf.at[half, :, :, :, theirs])

    def finish(self):
        place = self.place
        column = self.column(place.y, place.x)
        self.each_case(self.finish_case)
        likes = [self.own] * 3 + [column] * 2
        likes += [self.column(place.y, place.x, 0), self.column(place.y, place.x, 1)]
        for slot, like in enumerate(likes):
            self.mail.left(slot, like)


class WideScatter:
    SLOTS = 10

    def __init__(self, place, parts, hold, firsts, seconds, last, cut, send_sem, recv_sem):
        self.place, self.parts, self.hold = place, parts, hold
        self.firsts, self.seconds, self.last = firsts, seconds, last
        self.mail = Mail(place, send_sem, recv_sem)
        self.pieces = (pl.ds(0, cut), pl.ds(cut, hold.shape[3] - cut))

    def column(self, y, x, piece):
        return self.hold.at[:, 2 * y + x, :, self.pieces[piece]]

    def start(self):
        self.mail.start(0, self.parts.at[1 - self.place.half], self.hold, self.place.sibling)

    def first_hop(self):
        place = self.place
        y, x = place.y, place.x
        self.mail.arrived(0, self.hold)

        def add(z, carry):
            total = self.hold[z].astype(F32) + self.parts[place.half, z].astype(F32)
            self.hold[z] = total.astype(BF16)
            return carry

        lax.fori_loop(0, self.hold.shape[0], add, 0)
        first_a, first_b = self.firsts
        self.mail.start(1, self.column(1 - y, 1 - x, 0), first_a.at[0], place.x_peer)
        self.mail.start(2, self.column(1 - y, 1 - x, 1), first_b.at[0], place.y_peer)
        self.mail.start(3, self.column(y, 1 - x, 0), first_a.at[1], place.x_peer)
        self.mail.start(4, self.column(1 - y, x, 1), first_b.at[1], place.y_peer)

    def second_hop(self):
        place = self.place
        y, x = place.y, place.x
        moves = ((0, (1 - y, x), place.y_peer), (1, (y, 1 - x), place.x_peer))
        for p, (cy, cx), peer in moves:
            self.mail.arrived(1 + p, self.firsts[p].at[0])
            lanes = self.pieces[p]
            total = self.hold[:, 2 * cy + cx, :, lanes].astype(F32) + self.firsts[p][0].astype(F32)
            self.hold[:, 2 * cy + cx, :, lanes] = total.astype(BF16)
            self.mail.start(5 + p, self.column(cy, cx, p), self.seconds[p], peer)

    def last_hop(self, keep):
        place = self.place
        home = 2 * place.y + place.x
        for p in range(2):
            self.mail.arrived(3 + p, self.firsts[p].at[1])
            self.mail.arrived(5 + p, self.seconds[p])
            lanes = self.pieces[p]
            total = self.hold[:, home, :, lanes].astype(F32) + self.firsts[p][1].astype(F32)
            self.hold[:, home, :, lanes] = (total + self.seconds[p][...].astype(F32)).astype(BF16)
        for j in NEAR_FIRST:
            z = (place.z + j) % 4
            self.mail.start(6 + j, self.hold.at[z, home], self.last.at[j - 1], place.at_z(z))
        keep[...] = self.hold[place.z, home].astype(F32)

    def finish(self, keep):
        place = self.place
        for j in range(3):
            self.mail.arrived(7 + j, self.last.at[0])
            keep[...] = keep[...] + self.last[j].astype(F32)
        likes = [self.hold] + [self.firsts[p].at[0] for p in (0, 1, 0, 1)]
        likes += [self.seconds[0], self.seconds[1]] + [self.last.at[0]] * 3
        for slot, like in enumerate(likes):
            self.mail.left(slot, like)


def wide_scratch(rows, lanes, cut):
    return [
        pltpu.VMEM((4, 4, rows, lanes), BF16),
        pltpu.VMEM((2, 4, rows, cut), BF16),
        pltpu.VMEM((2, 4, rows, lanes - cut), BF16),
        pltpu.VMEM((4, rows, cut), BF16),
        pltpu.VMEM((4, rows, lanes - cut), BF16),
        pltpu.VMEM((3, rows, lanes), BF16),
    ]


def scatter_scratch(ranks, rows, lanes, cut):
    return [
        pltpu.VMEM((ranks, rows, lanes), BF16),
        pltpu.VMEM((8, rows, cut), BF16),
        pltpu.VMEM((8, rows, lanes - cut), BF16),
        pltpu.VMEM((4, rows, cut), BF16),
        pltpu.VMEM((4, rows, lanes - cut), BF16),
        pltpu.VMEM((3, rows, lanes), BF16),
    ]


def dma(count):
    return [pltpu.SemaphoreType.DMA((count,))] * 2


SENT_CUT, FC_CUT, EARLY_CUT, LATE_CUT = 512, 768, 896, 384


def head_masks():
    lane_head = lax.broadcasted_iota(jnp.int32, (1, SLOT), 1) // HD
    return [(lane_head == s).astype(F32).astype(BF16) for s in range(3)]


def used_lanes(bucket_ref, heads_ref, image, half):
    bucket = bucket_ref[...]
    counts = jnp.zeros(bucket.shape, jnp.int32)
    for entry in range(heads_ref.shape[1]):
        counts = jnp.where(bucket == entry, heads_ref[:, entry : entry + 1], counts)
    chosen = lax.broadcasted_iota(jnp.int32, bucket.shape, 1) == image
    count = jnp.sum(jnp.where(chosen, counts.astype(F32), 0.0), axis=1, keepdims=True)
    lane_head = lax.broadcasted_iota(jnp.int32, (1, SLOT), 1) // HD
    return jnp.where(lane_head.astype(F32) < count - 3.0 * half, 1.0, 0.0)


def widen(packed, pieces):
    blank = jnp.zeros((packed.shape[0], SLOT - HEADS), packed.dtype)
    parts = []
    for piece in range(pieces):
        parts += [packed[:, piece * HEADS : (piece + 1) * HEADS], blank]
    return jnp.concatenate(parts, axis=1)


def token_copy(place, tokens_ref, tok_own, sem):
    count = tok_own.shape[0]
    start = pl.multiple_of(place.half * count, count)
    return pltpu.make_async_copy(tokens_ref.at[pl.ds(start, count)], tok_own, sem)


def own_block(step, rows):
    return pl.ds(pl.multiple_of(step * rows, rows), rows)


def attend_kernel(
    bucket_ref, heads_ref, tokens_ref, fc1_ref, fc2_ref, qkv_ref, wo_ref, vecs_ref,
    resid_ref, proj_ref, low_ref, mixed_ref, wt_ref, vec_ref, fc_buf,
    own_at, own_fc, at_buf, tok_own, turn_ref, at_send, at_recv, fc_send, fc_recv, local_sem, tok_sem,
):
    place = Place()
    step = pl.program_id(0)
    steps = pl.num_programs(0)
    rows, model = resid_ref.shape
    pack = rows // SEQ
    tok_copy = token_copy(place, tokens_ref, tok_own, tok_sem)
    slices = Gather(place, own_at, at_buf, SENT_CUT, at_send, at_recv)
    units = Gather(place, own_fc, fc_buf, FC_CUT, fc_send, fc_recv)
    local = pltpu.make_async_copy(own_fc, fc_buf.at[place.half, place.dp], local_sem)

    @pl.when(step == 0)
    def _():
        tok_copy.start()
        own_at[...] = jnp.zeros_like(own_at)
        for which in range(3):
            own_at[:, which * HEADS : (which + 1) * HEADS] = qkv_ref[which].astype(BF16)
        own_at[:, 3 * HEADS : 4 * HEADS] = wo_ref[...].astype(BF16)
        turn_ref[...] = jnp.zeros_like(turn_ref)
        turn_ref[0 : vecs_ref.shape[0], 0 : vecs_ref.shape[1]] = vecs_ref[...]
        own_at[:, AT_SENT - 128 : AT_SENT] = turn_ref[...].T[0 : own_at.shape[0]].astype(BF16)
        own_fc[:, 0 : FC // 2] = fc1_ref[...].astype(BF16)
        own_fc[:, FC // 2 : FC] = fc2_ref[...].astype(BF16)
        at_buf[place.half, place.dp] = own_at[...]
        local.start()
        meet(place)
        slices.start_column()
        slices.start_plane()
        slices.plane(0)
        slices.columns()
        units.start_column()
        slices.planes()
        units.start_plane()
        slices.corners()
        slices.finish()
        for half in range(2):
            sent = at_buf[half].astype(F32).reshape(model, AT_SENT)
            wt_ref[half, :, 0:AT_VEC] = widen(sent, 4).astype(BF16)
            wt_ref[half, :, AT_VEC:AT] = sent[:, AT_SENT - 128 : AT_SENT].astype(BF16)
        vec_ref[...] = wt_ref[0, :, AT_VEC:AT].astype(F32).T[0:8]
        tok_copy.wait()

    @pl.when(step == 2)
    def _():
        units.planes()

    @pl.when(step == steps - 1)
    def _():
        units.corners()

    masks = head_masks()
    first_image = place.half * (bucket_ref.shape[1] // 2)
    x = tok_own[own_block(step, rows)].astype(F32)
    normed_one, _ = norm_rows(x)
    hidden_one = (normed_one * vec_ref[0:1] + vec_ref[1:2]).astype(BF16)
    branch = None
    for half in range(2):
        base = half * 3 * SLOT
        proj = []
        for which in range(3):
            part = mm(hidden_one, wt_ref[half, :, which * SLOT : (which + 1) * SLOT], NN).astype(BF16)
            proj_ref[:, base + which * SLOT : base + (which + 1) * SLOT] = part
            proj.append(part)
        mixes = []
        for image in range(pack):
            span = slice(image * SEQ, (image + 1) * SEQ)
            queries, keys, values = (part[span] for part in proj)
            total = None
            for s in range(3):
                scores = mm(queries * masks[s], keys, NT) * 0.125
                top = jnp.max(scores, axis=-1, keepdims=True)
                grown = jnp.exp(scores - top)
                low = (grown * (1.0 / lane_sum(grown))).astype(BF16)
                low_ref[(image * 2 + half) * 3 + s] = low
                term = mm(low, values * masks[s], NN)
                total = term if total is None else total + term
            mixes.append((total * used_lanes(bucket_ref, heads_ref, first_image + step * pack + image, half)).astype(BF16))
        mixed = jnp.concatenate(mixes, axis=0)
        mixed_ref[:, half * SLOT : (half + 1) * SLOT] = mixed
        term = mm(mixed, wt_ref[half, :, AT_OUT:AT_VEC], NT)
        branch = term if branch is None else branch + term
        if half == 0:

            @pl.when(step == 0)
            def _():
                units.columns()
                units.plane(0)

    resid_ref[...] = x + branch + vec_ref[4:5]

    @pl.when(step == steps - 1)
    def _():
        units.finish()
        local.wait()


def const(shape, **kw):
    return pl.BlockSpec(shape, lambda i, *_: (0,) * len(shape), **kw)


def once(shape):
    return const(shape, pipeline_mode=pl.Buffered(1))


def attend_pass(bucket, heads, tokens, weights, vectors, ranks):
    model = tokens.shape[1]
    images = bucket.shape[1] // 2
    rows = weights[0].shape[0]
    count = images * SEQ
    steps = images // PAIR
    block = PAIR * SEQ

    def by_step(lanes):
        return pl.BlockSpec((block, lanes), lambda i: (i, 0))

    return pl.pallas_call(
        attend_kernel,
        out_shape=(
            jax.ShapeDtypeStruct((count, model), F32),
            jax.ShapeDtypeStruct((count, 6 * SLOT), BF16),
            jax.ShapeDtypeStruct((images * 6, SEQ, SEQ), BF16),
            jax.ShapeDtypeStruct((count, 2 * SLOT), BF16),
            jax.ShapeDtypeStruct((2, model, AT), BF16),
            jax.ShapeDtypeStruct((8, model), F32),
            jax.ShapeDtypeStruct((2, ranks, rows, FC), BF16),
        ),
        grid_spec=pltpu.PrefetchScalarGridSpec(
            num_scalar_prefetch=0,
            grid=(steps,),
            in_specs=[once(bucket.shape), once(heads.shape), pl.BlockSpec(memory_space=pl.ANY)]
            + [once(w.shape) for w in weights]
            + [once(vectors.shape)],
            out_specs=[
                by_step(model),
                by_step(6 * SLOT),
                pl.BlockSpec((PAIR * 6, SEQ, SEQ), lambda i: (i, 0, 0)),
                by_step(2 * SLOT),
                once((2, model, AT)),
                once((8, model)),
                pl.BlockSpec(memory_space=pl.ANY),
            ],
            scratch_shapes=[
                pltpu.VMEM((rows, AT_SENT), BF16),
                pltpu.VMEM((rows, FC), BF16),
                pltpu.VMEM((2, ranks, rows, AT_SENT), BF16),
                pltpu.VMEM((count, model), BF16),
                pltpu.VMEM((128, 128), F32),
            ]
            + dma(GATHER_SLOTS)
            + dma(GATHER_SLOTS)
            + [pltpu.SemaphoreType.DMA] * 2,
        ),
        compiler_params=pltpu.CompilerParams(
            collective_id=0, has_side_effects=True, vmem_limit_bytes=56 * 1024 * 1024
        ),
        name="attend_pass",
    )(bucket, heads, tokens, *weights, vectors)


def units_kernel(
    half_ref, bucket_ref, widths_ref, resid_ref, cot_ref, mixed_ref, w_ref, vec_ref,
    out_ref, gres_ref, grad_ref, gvec_ref, acc_ref, y_ref, gh_ref,
):
    step = pl.program_id(0)
    rows, model = resid_ref.shape
    pack = rows // SEQ
    first = (half_ref[0] * pl.num_programs(0) + step) * pack
    widths = [widths_ref[bucket_ref[first + image]] for image in range(pack)]
    row_ids = lax.broadcasted_iota(jnp.int32, (rows, 1), 0)
    width, row_width = widths[0], jnp.full((rows, 1), widths[0], jnp.int32)
    for image in range(1, pack):
        width = jnp.maximum(width, widths[image])
        row_width = jnp.where(row_ids >= image * SEQ, widths[image], row_width)

    @pl.when(step == 0)
    def _():
        acc_ref[...] = jnp.zeros_like(acc_ref)
        gvec_ref[...] = jnp.zeros_like(gvec_ref)

    resid = resid_ref[...]
    normed_two, factor_two = norm_rows(resid)
    hidden_two = (normed_two * vec_ref[2:3] + vec_ref[3:4]).astype(BF16)
    cot = cot_ref[...]
    hidden_two_t = hidden_two.T
    cot_t = cot.T
    y_ref[...] = resid + vec_ref[5:6]
    gh_ref[...] = jnp.zeros_like(gh_ref)
    per_half = FC2 // CHUNK
    for chunk in range(2 * per_half):
        half, part = divmod(chunk, per_half)
        one = slice(FC1 + part * CHUNK, FC1 + (part + 1) * CHUNK)
        two = slice(FC2 + part * CHUNK, FC2 + (part + 1) * CHUNK)

        def units_pass():
            pre = mm(hidden_two, w_ref[half, :, one], NN)
            units = chunk * CHUNK + lax.broadcasted_iota(jnp.int32, pre.shape, 1)
            cumulative = 0.5 + 0.5 * lax.erf(pre * 0.7071067811865476)
            density = jnp.exp(-0.5 * pre * pre) * 0.3989422804014327
            cumulative = jnp.where(units < row_width, cumulative, 0.0)
            density = jnp.where(units < row_width, density, 0.0)
            act = (pre * cumulative).astype(BF16)
            grad_act = mm(cot, w_ref[half, :, two], NN)
            grad_pre = (grad_act * (cumulative + pre * density)).astype(BF16)
            y_ref[...] += mm(act, w_ref[half, :, two], NT)
            gh_ref[...] += mm(grad_pre, w_ref[half, :, one], NT)
            acc_ref[half, :, two] += mm(cot_t, act, NN)
            acc_ref[half, :, one] += mm(hidden_two_t, grad_pre, NN)

        if chunk < 2:
            units_pass()
        else:
            pl.when(width > chunk * CHUNK)(units_pass)

    out_ref[...] = y_ref[...]
    grad_hidden_two = gh_ref[...]
    cot_f = cot.astype(F32)
    grad_resid = cot_f + norm_back(grad_hidden_two * vec_ref[2:3], normed_two, factor_two)
    gres_ref[...] = grad_resid
    resid_low_t = grad_resid.astype(BF16).T
    for half in range(2):
        acc_ref[half, :, FC:EARLY] += mm(resid_low_t, mixed_ref[:, half * SLOT : (half + 1) * SLOT], NN)
    sums = (grad_hidden_two * normed_two, grad_hidden_two, grad_resid, cot_f)
    for row, values in enumerate(sums):
        gvec_ref[2 + row : 3 + row] += jnp.sum(values, axis=0, keepdims=True)

    @pl.when(step == pl.num_programs(0) - 1)
    def _():
        grad_ref[...] = acc_ref[...].astype(BF16)


def units_pass(half, bucket, widths, resid, cotangent, mixed, packed, vec):
    count, model = resid.shape
    block = PAIR * SEQ
    steps = count // block
    placed = pl.BlockSpec((block, model), lambda i, h, b, w: (i, 0))
    picked = pl.BlockSpec((block, model), lambda i, h, b, w: (h[0] * steps + i, 0))
    blended = pl.BlockSpec((block, 2 * SLOT), lambda i, h, b, w: (i, 0))
    return pl.pallas_call(
        units_kernel,
        out_shape=(
            jax.ShapeDtypeStruct((count, model), F32),
            jax.ShapeDtypeStruct((count, model), F32),
            jax.ShapeDtypeStruct((2, model, EARLY), BF16),
            jax.ShapeDtypeStruct((8, model), F32),
        ),
        grid_spec=pltpu.PrefetchScalarGridSpec(
            num_scalar_prefetch=3,
            grid=(steps,),
            in_specs=[placed, picked, blended, once(packed.shape), once(vec.shape)],
            out_specs=[placed, placed, once((2, model, EARLY)), once((8, model))],
            scratch_shapes=[
                pltpu.VMEM((2, model, EARLY), F32),
                pltpu.VMEM((block, model), F32),
                pltpu.VMEM((block, model), F32),
            ],
        ),
        compiler_params=pltpu.CompilerParams(vmem_limit_bytes=56 * 1024 * 1024),
        name="units_pass",
    )(half, bucket, widths, resid, cotangent, mixed, packed, vec)


def back_kernel(
    bucket_ref, heads_ref, tokens_ref, gres_ref, proj_ref, low_ref, wt_ref, vec_ref, gvec_ref,
    fc_parts, fc1_ref, fc2_ref, qkv_ref, wo_ref, out_half,
    gtok_ref, pairs_ref, fc_buf, at_buf, out_other,
    acc_ref, sums_ref, gtok_own, at_parts, own_fc, own_at, tok_own,
    fc_hold, fc_first_a, fc_first_b, fc_second_a, fc_second_b, fc_last,
    at_hold, at_first_a, at_first_b, at_second_a, at_second_b, at_last,
    fcs_send, fcs_recv, ats_send, ats_recv, fcg_send, fcg_recv, atg_send, atg_recv,
    side_send, side_recv, local_sems,
):
    place = Place()
    step = pl.program_id(0)
    steps = pl.num_programs(0)
    rows, model = gres_ref.shape
    tok_copy = token_copy(place, tokens_ref, tok_own, local_sems.at[0])
    pack = rows // SEQ
    count = gtok_ref.shape[0] // 2
    early, late = pl.ds(0, EARLY), pl.ds(EARLY, LATE)
    grad_fc, mom_fc = pairs_ref.at[0, :, early], pairs_ref.at[1, :, early]
    grad_at, mom_at = pairs_ref.at[0, :, late], pairs_ref.at[1, :, late]
    fc_sum = WideScatter(
        place, fc_parts, fc_hold, (fc_first_a, fc_first_b), (fc_second_a, fc_second_b), fc_last,
        EARLY_CUT, fcs_send, fcs_recv,
    )
    at_sum = Scatter(
        place, at_parts, at_hold, (at_first_a, at_first_b), (at_second_a, at_second_b), at_last,
        LATE_CUT, ats_send, ats_recv,
    )
    fc_all = WideGather(place, own_fc, fc_buf, EARLY_CUT, fcg_send, fcg_recv)
    at_all = Gather(place, own_at, at_buf, LATE_CUT, atg_send, atg_recv)
    side = Mail(place, side_send, side_recv)
    fc_home = pltpu.make_async_copy(
        own_fc, fc_buf.at[place.half, place.z, 2 * place.y + place.x], local_sems.at[1]
    )
    at_home = pltpu.make_async_copy(own_at, at_buf.at[place.half, place.dp], local_sems.at[2])

    @pl.when(step == 0)
    def _():
        tok_copy.start()
        meet(place)
        fc_sum.start()
        tok_copy.wait()
        acc_ref[...] = jnp.zeros_like(acc_ref)
        sums_ref[...] = jnp.zeros_like(sums_ref)
        sums_ref[0:8] = gvec_ref[...]

    def settle_units():
        fc_sum.finish(grad_fc)
        mom_fc[:, 0 : FC // 2] = 0.95 * fc1_ref[...]
        mom_fc[:, FC // 2 : FC] = 0.95 * fc2_ref[...]
        mom_fc[:, FC:EARLY] = jnp.zeros((mom_fc.shape[0], SLOT), F32)
        mom_fc[:, FC : FC + HEADS] = 0.95 * wo_ref[...]
        mom_fc[...] = mom_fc[...] + grad_fc[...]
        own_fc[...] = mom_fc[...].astype(BF16)
        fc_home.start()
        fc_all.start()
        side.start(0, out_half, out_other, place.sibling)

    def spread_units():
        fc_home.wait()
        fc_all.spread()

    def part_units():
        fc_all.corners()

    stages = {
        1: fc_sum.first_hop,
        6: fc_sum.second_hop,
        10: lambda: fc_sum.last_hop(grad_fc),
        15: settle_units,
    }

    def slot(quarter):
        for number, stage in stages.items():
            if number % 4 == quarter:
                pl.when(step == number // 4)(stage)

    masks = head_masks()
    first_image = place.half * (bucket_ref.shape[1] // 2)
    normed_one, factor_one = norm_rows(tok_own[own_block(step, rows)].astype(F32))
    hidden_one_t = (normed_one * vec_ref[0:1] + vec_ref[1:2]).astype(BF16).T
    grad_resid = gres_ref[...]
    resid_low = grad_resid.astype(BF16)
    grad_hidden_one = None
    for half in range(2):
        base = half * 3 * SLOT
        grad_heads = mm(resid_low, wt_ref[half, :, AT_OUT:AT_VEC], NN).astype(BF16)
        parts = []
        for image in range(pack):
            span = slice(image * SEQ, (image + 1) * SEQ)
            used = used_lanes(bucket_ref, heads_ref, first_image + step * pack + image, half).astype(BF16)
            heads = grad_heads[span] * used
            queries, keys, values = (
                proj_ref[span, base + which * SLOT : base + (which + 1) * SLOT] for which in range(3)
            )
            sums = [None, None, None]
            for s in range(3):
                own = heads * masks[s]
                low = low_ref[(image * 2 + half) * 3 + s]
                grad_probs = mm(own, values, NT)
                probs = low.astype(F32)
                weighed = probs * grad_probs
                grad_scores = (weighed - probs * lane_sum(weighed)).astype(BF16)
                terms = (
                    mm(grad_scores, keys * masks[s], NN),
                    mm(grad_scores, queries * masks[s], TN),
                    mm(low, own, TN),
                )
                sums = [t if o is None else o + t for o, t in zip(sums, terms)]
            parts.append([(v * c).astype(BF16) for v, c in zip(sums, (0.125, 0.125, 1.0))])
            if image == 0:
                slot(2 * half)
        for which in range(3):
            lanes = slice(which * SLOT, (which + 1) * SLOT)
            grad_proj = jnp.concatenate([part[which] for part in parts], axis=0)
            acc_ref[half, :, lanes] += mm(hidden_one_t, grad_proj, NN)
            term = mm(grad_proj, wt_ref[half, :, lanes], NT)
            grad_hidden_one = term if grad_hidden_one is None else grad_hidden_one + term
        if half == 0:
            slot(1)

    gtok_own[step] = grad_resid + norm_back(grad_hidden_one * vec_ref[0:1], normed_one, factor_one)
    sums_ref[0:1] += jnp.sum(grad_hidden_one * normed_one, axis=0, keepdims=True)
    sums_ref[1:2] += jnp.sum(grad_hidden_one, axis=0, keepdims=True)

    slot(3)

    def own_rows(index):
        start = place.half * count + index * rows
        return gtok_ref.at[pl.ds(pl.multiple_of(start, rows), rows)]

    @pl.when(step == steps - 1)
    def _():
        columns = sums_ref[...].T[:, 0 : LATE - TAIL].astype(BF16)
        ranks, own = at_parts.shape[1], at_parts.shape[2]
        for half in range(2):
            for which in range(3):
                piece = acc_ref[half, :, which * SLOT : which * SLOT + HEADS].astype(BF16)
                at_parts[half, :, :, which * HEADS : (which + 1) * HEADS] = piece.reshape(ranks, own, HEADS)
            at_parts[half, :, :, TAIL:LATE] = columns.reshape(ranks, own, LATE - TAIL)
        at_sum.start()
        at_sum.first_hop()
        for index in range(gtok_own.shape[0]):
            side.start(1 + index, gtok_own.at[index], own_rows(index), place.sibling)
            pltpu.make_async_copy(gtok_own.at[index], own_rows(index), local_sems.at[3 + index]).start()
        mom_at[...] = jnp.zeros(mom_at.shape, F32)
        for which in range(3):
            mom_at[:, which * HEADS : (which + 1) * HEADS] = 0.95 * qkv_ref[which]
        at_sum.second_hop()
        at_sum.last_hop(grad_at)
        spread_units()
        at_sum.finish(grad_at)
        mom_at[:, 0:TAIL] = mom_at[:, 0:TAIL] + grad_at[:, 0:TAIL]
        own_at[:, 0:TAIL] = mom_at[:, 0:TAIL].astype(BF16)
        lanes = lax.broadcasted_iota(jnp.int32, (own, LATE - TAIL), 1)
        tile = jnp.zeros(lanes.shape, F32)
        pieces = (
            grad_at[:, 0:TAIL], grad_fc[:, FC:EARLY], grad_fc[:, 0 : FC // 2],
            grad_fc[:, FC // 2 : FC], grad_at[:, TAIL:LATE],
        )
        for number, piece in enumerate(pieces):
            square = jnp.sum(lane_sum(piece * piece), axis=0, keepdims=True)
            square = jnp.broadcast_to(square * (0.5 if number == 4 else 1.0), lanes.shape)
            high = square.astype(BF16).astype(F32)
            tile = jnp.where(lanes == number, high, tile)
            tile = jnp.where(lanes == 32 + number, square - high, tile)
        own_at[:, TAIL:LATE] = tile.astype(BF16)
        at_home.start()
        at_all.start_column()
        at_all.start_plane()
        at_all.plane(0)
        at_all.columns()
        part_units()
        at_all.planes()
        at_all.corners()
        fc_all.share()
        at_all.finish()
        fc_all.finish()
        side.arrived(0, out_half)
        side.left(0, out_half)
        for index in range(gtok_own.shape[0]):
            side.arrived(1 + index, gtok_own.at[0])
            side.left(1 + index, gtok_own.at[0])
            pltpu.make_async_copy(gtok_own.at[index], own_rows(index), local_sems.at[3 + index]).wait()
        at_home.wait()


def back_pass(bucket, heads, tokens, gres, proj, low, wt, vec, gvec, fc_parts, moms, out_half):
    count, model = gres.shape
    rows = fc_parts.shape[3]
    ranks = fc_parts.shape[1] * fc_parts.shape[2]
    block = PAIR * SEQ
    steps = count // block

    def by_step(lanes):
        return pl.BlockSpec((block, lanes), lambda i: (i, 0))

    anywhere = pl.BlockSpec(memory_space=pl.ANY)
    return pl.pallas_call(
        back_kernel,
        out_shape=(
            jax.ShapeDtypeStruct((2 * count, model), F32),
            jax.ShapeDtypeStruct((2, rows, EARLY + LATE), F32),
            jax.ShapeDtypeStruct(fc_parts.shape, BF16),
            jax.ShapeDtypeStruct((2, ranks, rows, LATE), BF16),
            jax.ShapeDtypeStruct((count, model), F32),
        ),
        grid_spec=pltpu.PrefetchScalarGridSpec(
            num_scalar_prefetch=0,
            grid=(steps,),
            in_specs=[
                once(bucket.shape),
                once(heads.shape),
                anywhere,
                by_step(model),
                by_step(6 * SLOT),
                pl.BlockSpec((PAIR * 6, SEQ, SEQ), lambda i: (i, 0, 0)),
                once(wt.shape),
                once(vec.shape),
                once(gvec.shape),
                once(fc_parts.shape),
            ]
            + [once(m.shape) for m in moms]
            + [anywhere],
            out_specs=[
                anywhere,
                once((2, rows, EARLY + LATE)),
                anywhere,
                anywhere,
                anywhere,
            ],
            scratch_shapes=[
                pltpu.VMEM((2, model, AT_OUT), F32),
                pltpu.VMEM((128, model), F32),
                pltpu.VMEM((steps, block, model), F32),
                pltpu.VMEM((2, ranks, rows, LATE), BF16),
                pltpu.VMEM((rows, EARLY), BF16),
                pltpu.VMEM((rows, LATE), BF16),
                pltpu.VMEM((count, model), BF16),
            ]
            + wide_scratch(rows, EARLY, EARLY_CUT)
            + scatter_scratch(ranks, rows, LATE, LATE_CUT)
            + dma(WideScatter.SLOTS)
            + dma(SCATTER_SLOTS)
            + dma(WideGather.SLOTS)
            + dma(GATHER_SLOTS)
            + dma(1 + steps)
            + [pltpu.SemaphoreType.DMA((3 + steps,))],
        ),
        compiler_params=pltpu.CompilerParams(
            collective_id=1, has_side_effects=True, vmem_limit_bytes=60 * 1024 * 1024
        ),
        name="back_pass",
    )(bucket, heads, tokens, gres, proj, low, wt, vec, gvec, fc_parts, *moms, out_half)


QUINTIC = (3.4445, -4.775, 2.0315)
RATES = (2.0, 2.0, math.sqrt(3.0), math.sqrt(32.0))
RANGES = ((0, FC // 2), (FC // 2, FC), (0, LATE), (FC, EARLY))
IN_LATE = 2


def mm3(a, b):
    return lax.dot_general(a, b, NN, precision=lax.Precision.HIGH, preferred_element_type=F32)


def eye_mask(n):
    return lax.broadcasted_iota(jnp.int32, (n, n), 0) == lax.broadcasted_iota(jnp.int32, (n, n), 1)


def chain_kernel(
    fc_ref, at_ref, pairs_ref, vec_ref, first_ref, second_ref,
    fc1_ref, fc2_ref, qkv_ref, wo_ref, out_half, out_other, gtok_both,
    root_ref, norm_ref, gfc1, gfc2, gqkv, gwo, gvec, mfc1, mfc2, mqkv, mwo,
    vec_new, first_new, second_new, kept_fc, kept_at, half_fc, half_at, out_ref, gtok_ref,
    gram_ref, poly_ref, rows_ref, turn_ref, out_hold, gtok_hold, sems,
):
    place = Place()
    count = out_half.shape[0]
    early, late = pl.ds(0, EARLY), pl.ds(EARLY, LATE)
    grad_fc, mom_fc = pairs_ref.at[0, :, early], pairs_ref.at[1, :, early]
    grad_at, mom_at = pairs_ref.at[0, :, late], pairs_ref.at[1, :, late]
    half = place.half
    which = 2 * place.x + half
    sources = ((out_half, out_hold.at[0]), (out_other, out_hold.at[1]), (gtok_both, gtok_hold))
    loads = [pltpu.make_async_copy(src, hold, sems.at[i]) for i, (src, hold) in enumerate(sources)]
    stores = []
    for i, part in enumerate((half, 1 - half)):
        rows = pl.ds(pl.multiple_of(part * count, 8), count)
        stores.append(pltpu.make_async_copy(out_hold.at[i], out_ref.at[rows], sems.at[3 + i]))
    stores.append(pltpu.make_async_copy(gtok_hold, gtok_ref, sems.at[5]))
    for load in loads:
        load.start()
    model = fc_ref.shape[1]
    for number, (start, stop) in enumerate(RANGES):
        buf = at_ref if number == IN_LATE else fc_ref

        @pl.when(which == number)
        def _():
            lower, upper = buf[0, :, start:stop], buf[1, :, start:stop]
            if number == IN_LATE:
                keep = (lax.broadcasted_iota(jnp.int32, (1, LATE), 1) < TAIL).astype(F32).astype(BF16)
                lower, upper = lower * keep, upper * keep
            gram_ref[...] = mm(lower, lower, NT) + mm(upper, upper, NT)

    eye = eye_mask(model)
    gram = gram_ref[...]
    total = jnp.sum(lane_sum(jnp.where(eye, gram, 0.0)), axis=0, keepdims=True)
    scale = 1.0 / (jnp.sqrt(total) + 1e-07)
    gram_ref[...] = gram * (scale * scale)
    a, b, c = QUINTIC

    def polynomial():
        gram = gram_ref[...]
        return jnp.where(eye, a, 0.0) + b * gram + c * mm3(gram, gram)

    def advance(poly):
        gram_ref[...] = mm3(mm3(gram_ref[...], poly), poly)

    poly = polynomial()
    poly_ref[...] = poly
    first_row = (place.dp // 2) * rows_ref.shape[0]
    rows_ref[...] = poly_ref[pl.ds(pl.multiple_of(first_row, 8), rows_ref.shape[0])]
    advance(poly)
    for load, store in zip(loads, stores):
        load.wait()
        store.start()

    def sweep(_, carry):
        poly = polynomial()
        rows_ref[...] = mm3(rows_ref[...], poly)
        advance(poly)
        return carry

    lax.fori_loop(0, NS_ITERS - 2, sweep, 0)
    rows, gram = rows_ref[...], gram_ref[...]
    once_more = mm3(rows, gram)
    last = (a * rows + b * once_more + c * mm3(once_more, gram)) * scale
    for part in range(root_ref.shape[0]):
        root_ref[part] = last[part * root_ref.shape[1] : (part + 1) * root_ref.shape[1]]

    wide = FC // 2
    gfc1[...], gfc2[...] = grad_fc[:, 0:wide], grad_fc[:, wide:FC]
    mfc1[...], mfc2[...] = mom_fc[:, 0:wide], mom_fc[:, wide:FC]
    gwo[...] = grad_fc[:, FC : FC + HEADS]
    mwo[...] = mom_fc[:, FC : FC + HEADS]
    kept_fc[...] = jnp.zeros_like(kept_fc)
    kept_fc[:, 0:wide] = 0.999 * fc1_ref[...]
    kept_fc[:, wide:FC] = 0.999 * fc2_ref[...]
    kept_fc[:, FC : FC + HEADS] = 0.999 * wo_ref[...]
    kept_at[...] = jnp.zeros_like(kept_at)
    half_fc[...] = fc_ref[half]
    half_at[...] = at_ref[half]
    for part in range(3):
        span = slice(part * HEADS, (part + 1) * HEADS)
        gqkv[part] = grad_at[:, span]
        mqkv[part] = mom_at[:, span]
        kept_at[:, span] = 0.999 * qkv_ref[part]
    own = grad_at.shape[0]
    turn_ref[...] = jnp.zeros_like(turn_ref)
    turn_ref[0:own, 0 : LATE - TAIL] = grad_at[:, TAIL:LATE]
    turned = turn_ref[...].T[0:6, 0 : vec_ref.shape[1]]
    first = 0.9 * first_ref[...] + 0.1 * turned
    second = 0.95 * second_ref[...] + 0.05 * turned * turned
    gvec[...] = turned
    first_new[...] = first
    second_new[...] = second
    vec_new[...] = vec_ref[...] - 0.5 * (first / (1.0 - 0.9**STEP)) / (
        jnp.sqrt(second / (1.0 - 0.95**STEP)) + 1e-08
    )
    tiles = at_ref[0, :, LATE - 128 : LATE].astype(F32) + at_ref[1, :, LATE - 128 : LATE].astype(F32)
    leads = lax.broadcasted_iota(jnp.int32, tiles.shape, 0) % own == 0
    squares = jnp.sum(jnp.where(leads, tiles, 0.0), axis=0, keepdims=True)
    squares = pltpu.roll(squares, 64, 1)
    norm_ref[...] = jnp.sqrt(jnp.abs(squares + pltpu.roll(squares, 96, 1)))
    for store in stores:
        store.wait()


def run_chain(fc_buf, at_buf, pairs, vectors, first, second, weights, wholes):
    model = fc_buf.shape[1]
    own, columns = pairs.shape[1], vectors.shape[1]
    count = wholes[0].shape[0]
    full = (2 * count, model)
    vmem = pl.BlockSpec(memory_space=pltpu.VMEM)
    anywhere = pl.BlockSpec(memory_space=pl.ANY)
    shapes = [(own, 768), (own, 768), (3, own, 192), (own, 192)]
    outs = [(2, own, model), (1, 128)] + shapes + [(6, columns)] + shapes + [(6, columns)] * 3
    lows = [(model, EARLY), (model, LATE)]
    outs += [(own, EARLY), (own, LATE)] + lows + [full] * 2
    return pl.pallas_call(
        chain_kernel,
        out_shape=tuple(jax.ShapeDtypeStruct(shape, BF16 if shape in lows else F32) for shape in outs),
        in_specs=[vmem] * 10 + [anywhere] * 3,
        out_specs=tuple([vmem] * (len(outs) - 2) + [anywhere] * 2),
        scratch_shapes=[
            pltpu.VMEM((model, model), F32),
            pltpu.VMEM((model, model), F32),
            pltpu.VMEM((2 * own, model), F32),
            pltpu.VMEM((128, 128), F32),
            pltpu.VMEM((2, count, model), F32),
            pltpu.VMEM(full, F32),
            pltpu.SemaphoreType.DMA((6,)),
        ],
        compiler_params=pltpu.CompilerParams(vmem_limit_bytes=44 * 1024 * 1024),
        name="run_chain",
    )(fc_buf, at_buf, pairs, vectors, first, second, *weights, *wholes)


def roots_kernel(
    root_ref, kept_fc, kept_at, fc_own, at_own,
    nfc1, nfc2, nqkv, nwo, rows_ref, send_sem, recv_sem,
):
    place = Place()
    x, half = place.x, place.half
    barrier = pltpu.get_barrier_semaphore()
    peers = [(1 - x, half), (x, 1 - half), (1 - x, 1 - half)]
    ids = [(place.index(place.z, place.y, px), ph) for px, ph in peers]
    for peer in ids:
        pl.semaphore_signal(barrier, inc=1, device_id=peer, device_id_type=MESH)
    pl.semaphore_wait(barrier, 3)
    mail = Mail(place, send_sem, recv_sem)
    mine = 2 * x + half
    for slot, peer in enumerate(ids):
        mail.start(slot, root_ref.at[peers[slot][0]], rows_ref.at[mine], peer)
    rows_ref[mine] = root_ref[x]
    for slot in range(3):
        mail.arrived(slot, rows_ref.at[0])
    for number, (start, stop) in enumerate(RANGES):
        rows = rows_ref[number]
        high = rows.astype(BF16)
        low = (rows - high.astype(F32)).astype(BF16)
        late = number == IN_LATE
        moment = (at_own if late else fc_own)[:, start:stop]
        step = RATES[number] * (mm(high, moment, NN) + mm(low, moment, NN))
        new = (kept_at if late else kept_fc)[:, start:stop] - step
        if late:
            for part in range(3):
                nqkv[part] = new[:, part * HEADS : (part + 1) * HEADS]
        else:
            out = (nfc1, nfc2, None, nwo)[number]
            out[...] = new[:, 0 : out.shape[1]]
    for slot in range(3):
        mail.left(slot, rows_ref.at[0])


def apply_roots(root, kept_fc, kept_at, half_fc, half_at, weights):
    _, rows, model = root.shape
    vmem = pl.BlockSpec(memory_space=pltpu.VMEM)
    return pl.pallas_call(
        roots_kernel,
        out_shape=tuple(jax.ShapeDtypeStruct(w.shape, F32) for w in weights),
        in_specs=[vmem] * 5,
        out_specs=(vmem,) * 4,
        scratch_shapes=[
            pltpu.VMEM((4, rows, model), F32),
        ]
        + dma(3),
        compiler_params=pltpu.CompilerParams(
            collective_id=2, has_side_effects=True, vmem_limit_bytes=32 * 1024 * 1024
        ),
        name="apply_roots",
    )(root, kept_fc, kept_at, half_fc, half_at)


def flat(part):
    return part.T if part.ndim == 2 else jnp.transpose(part, (0, 2, 1))


def pack(fc1, fc2, qkv, out):
    pad = ((0, 0), (0, SLOT - out.shape[1]))
    return jnp.concatenate([fc1, fc2] + [jnp.pad(part, pad) for part in (*qkv, out)], axis=1)


def unpack(packed, like):
    fc1, fc2, qkv, out = like
    split = jnp.stack([packed[:, QKV + part * SLOT :][:, : qkv.shape[2]] for part in range(3)])
    return packed[:, FC1:FC2], packed[:, FC2:QKV], split, packed[:, OUT : OUT + out.shape[1]]


def root_of(gram):
    a, b, c = QUINTIC
    eye = eye_mask(gram.shape[0])
    scale = 1.0 / (jnp.sqrt(jnp.sum(jnp.where(eye, gram, 0.0))) + 1e-07)
    gram = gram * (scale * scale)
    root = jnp.where(eye, scale, 0.0)
    for _ in range(NS_ITERS):
        poly = jnp.where(eye, a, 0.0) + b * gram + c * mm3(gram, gram)
        root = mm3(root, poly)
        gram = mm3(mm3(gram, poly), poly)
    return root


def general(half, bucket, widths, counts, tokens, cotangent, weights, moms, vectors, vec_first, vec_second):
    dp = lax.axis_index("dp")
    rows = weights[0].shape[0]
    vec = jnp.pad(vectors.T, ((0, 0), (0, PACK - VEC - vectors.shape[0])))
    own = jnp.concatenate([pack(*weights), vec], axis=1).astype(BF16)
    packed = lax.all_gather(lax.all_gather(own, "dp", axis=0, tiled=True), "mlp")
    out_half, gtok_half, grads = image_pass(half.reshape(1), bucket, widths, counts, tokens, cotangent, packed)
    output = lax.all_gather(out_half, "mlp", axis=0, tiled=True)
    gtok = lax.all_gather(gtok_half, "mlp", axis=0, tiled=True)
    grad = lax.psum_scatter(grads.astype(F32), "mlp", scatter_dimension=0)
    grad = lax.psum_scatter(grad, "dp", scatter_dimension=0, tiled=True)
    mom = 0.95 * pack(*moms) + grad[:, 0:VEC]
    spans = ((FC1, FC2), (FC2, QKV), (QKV, OUT), (OUT, VEC))
    squares = [jnp.sum(jnp.square(grad[:, start:stop])) for start, stop in spans[2:] + spans[:2]]
    squares.append(0.5 * jnp.sum(jnp.square(grad[:, VEC:PACK])))
    norms = jnp.sqrt(lax.psum(jnp.stack(squares), ("dp", "mlp")))
    buf = lax.all_gather(lax.all_gather(mom.astype(BF16), "dp", axis=0, tiled=True), "mlp")
    ours = lax.dynamic_index_in_dim(buf, half, 0, keepdims=False)
    steps = []
    for (start, stop), rate in zip(spans, RATES):
        root = root_of(sum(mm(buf[h, :, start:stop], buf[h, :, start:stop], NT) for h in range(2)))
        root = lax.dynamic_slice_in_dim(root, dp * rows, rows, 0)
        high = root.astype(BF16)
        low = (root - high.astype(F32)).astype(BF16)
        steps.append(rate * (mm(high, ours[:, start:stop], NN) + mm(low, ours[:, start:stop], NN)))
    moved = unpack(jnp.concatenate(steps, axis=1), weights)
    gvec = grad[:, VEC : VEC + vectors.shape[0]].T
    first = 0.9 * vec_first + 0.1 * gvec
    second = 0.95 * vec_second + 0.05 * gvec * gvec
    vec_new = vectors - 0.5 * (first / (1.0 - 0.9**STEP)) / (
        jnp.sqrt(second / (1.0 - 0.95**STEP)) + 1e-08
    )

    def ordered(parts):
        fc1, fc2, qkv, out = parts
        return flat(qkv), flat(out), flat(fc1), flat(fc2)

    news = [0.999 * w - move for w, move in zip(weights, moved)]
    return (
        output, gtok, *ordered(unpack(grad, weights)), gvec,
        *ordered(unpack(mom, weights)), *ordered(news), vec_new, first, second, norms,
    )


def body(
    tokens, cotangent, image_bucket, bucket_width, bucket_heads,
    w_qkv, w_out, w_fc1, w_fc2, vectors,
    mom_qkv, mom_out, mom_fc1, mom_fc2, vec_first, vec_second,
):
    half = lax.axis_index("mlp").astype(jnp.int32)
    ranks = lax.axis_size("dp")
    model = tokens.shape[1]
    rows = w_fc1.shape[1]
    weights = [flat(w) for w in (w_fc1, w_fc2, w_qkv, w_out)]
    moms = [flat(m) for m in (mom_fc1, mom_fc2, mom_qkv, mom_out)]
    images = image_bucket.shape[0] // 2
    if ranks != 16 or images != 4 * PAIR:
        return general(
            half, image_bucket, bucket_width, bucket_heads, tokens, cotangent,
            weights, moms, vectors, vec_first, vec_second,
        )
    bucket, heads = image_bucket.reshape(1, -1), bucket_heads.reshape(1, -1)
    resid, proj, low, mixed, wt, vec_rows, fc_weights = attend_pass(bucket, heads, tokens, weights, vectors, ranks)
    out_half, gres, fc_parts, gvec_rows = units_pass(
        half.reshape(1), image_bucket, bucket_width, resid, cotangent, mixed,
        fc_weights.reshape(2, model, FC), vec_rows,
    )
    gtok_both, pairs, fc_buf, at_buf, out_other = back_pass(
        bucket, heads, tokens, gres, proj, low, wt, vec_rows, gvec_rows,
        fc_parts.reshape(2, 4, 4, rows, EARLY), moms, out_half,
    )
    fc_buf, at_buf = fc_buf.reshape(2, model, EARLY), at_buf.reshape(2, model, LATE)
    (
        root, norms, gfc1, gfc2, gqkv, gwo, gvec, mfc1, mfc2, mqkv, mwo,
        vec_new, first, second, kept_fc, kept_at, half_fc, half_at, output, gtok,
    ) = run_chain(
        fc_buf, at_buf, pairs, vectors, vec_first, vec_second,
        weights, (out_half, out_other, gtok_both),
    )
    nfc1, nfc2, nqkv, nwo = apply_roots(root, kept_fc, kept_at, half_fc, half_at, weights)
    return (
        output, gtok,
        flat(gqkv), flat(gwo), flat(gfc1), flat(gfc2), gvec,
        flat(mqkv), flat(mwo), flat(mfc1), flat(mfc2),
        flat(nqkv), flat(nwo), flat(nfc1), flat(nfc2),
        vec_new, first, second, norms[0, 0:5],
    )


def solution(mesh):
    halves, columns = P("mlp", "dp"), P(None, "dp")
    blocks = P(None, "mlp", "dp")
    matrices = (blocks, halves, halves, halves)
    placed = (P("dp", None), P("dp", None), P("dp"), P(), P()) + matrices + (columns,) + matrices + (columns, columns)
    outs = (P("dp", None), P("dp", None)) + matrices + (columns,) + matrices + matrices + (columns,) * 3 + (P(),)
    return jax.shard_map(body, mesh=mesh, in_specs=placed, out_specs=outs, check_vma=False)
```

```python
import functools
import math

import jax
import jax.numpy as jnp
from jax import lax
from jax.experimental import pallas as pl
from jax.experimental.pallas import tpu as pltpu
from jax.sharding import PartitionSpec as P

HD = 64
NS_ITERS = 5
STEP = 10
EPSILON = 1e-06
F32 = jnp.float32
BF16 = jnp.bfloat16
NN = (((1,), (0,)), ((), ()))
NT = (((1,), (1,)), ((), ()))
TN = (((0,), (0,)), ((), ()))

FC1, FC2, QKV, OUT, VEC, PACK = 0, 768, 1536, 2304, 2560, 2688
SLOT = 256
SEQ = 256
PAIR = 2
CHUNK = 256


def mm(a, b, dims):
    return lax.dot_general(a, b, dims, preferred_element_type=F32)


def lane_sum(v):
    return jnp.sum(v, axis=-1, keepdims=True)


def norm_rows(v):
    inv = 1.0 / v.shape[-1]
    center = v - lane_sum(v) * inv
    factor = lax.rsqrt(lane_sum(center * center) * inv + EPSILON)
    return center * factor, factor


def norm_back(g, n, factor):
    inv = 1.0 / g.shape[-1]
    return factor * (g - lane_sum(g) * inv - n * (lane_sum(g * n) * inv))


def image_kernel(
    half_ref, bucket_ref, widths_ref, counts_ref,
    tok_ref, cot_ref, w_ref,
    out_ref, gtok_ref, grad_ref,
    acc_ref, vec_ref, gvec_ref, q_ref, k_ref, v_ref, mixed_ref, probs_ref, low_ref,
    y_ref, gh_ref,
):
    step = pl.program_id(0)
    rows, model = tok_ref.shape
    heads_half = 3
    pack = rows // SEQ
    first = (half_ref[0] * pl.num_programs(0) + step) * pack
    buckets = [bucket_ref[first + image] for image in range(pack)]
    widths = [widths_ref[bucket] for bucket in buckets]
    counts = [counts_ref[bucket] for bucket in buckets]
    width, count = widths[0], counts[0]
    for image in range(1, pack):
        width, count = jnp.maximum(width, widths[image]), jnp.maximum(count, counts[image])
    row_ids = lax.broadcasted_iota(jnp.int32, (rows, 1), 0)
    row_width = jnp.full((rows, 1), widths[0], jnp.int32)
    for image in range(1, pack):
        row_width = jnp.where(row_ids >= image * SEQ, widths[image], row_width)

    @pl.when(step == 0)
    def _():
        acc_ref[...] = jnp.zeros_like(acc_ref)
        gvec_ref[...] = jnp.zeros_like(gvec_ref)
        turned = w_ref[0, :, VEC:PACK].astype(F32).T
        vec_ref[...] = turned[0:8]

    lane_head = lax.broadcasted_iota(jnp.int32, (1, SLOT), 1) // HD
    masks = [(lane_head == s).astype(F32).astype(BF16) for s in range(heads_half)]

    def used_heads(image):
        return (lane_head < counts[image] - heads_half).astype(F32)

    def spans():
        return [slice(image * SEQ, (image + 1) * SEQ) for image in range(pack)]

    x = tok_ref[...].astype(F32)
    normed_one, factor_one = norm_rows(x)
    hidden_one = (normed_one * vec_ref[0:1] + vec_ref[1:2]).astype(BF16)
    for half in range(2):
        for ref, which in ((q_ref, 0), (k_ref, 1), (v_ref, 2)):
            lanes = slice(QKV + which * SLOT, QKV + (which + 1) * SLOT)
            ref[half] = mm(hidden_one, w_ref[half, :, lanes], NN).astype(BF16)

        def attend():
            for image, span in enumerate(spans()):
                total = None
                for s in range(heads_half):
                    slot = (image * 2 + half) * heads_half + s
                    scores = mm(q_ref[half, span] * masks[s], k_ref[half, span], NT) * 0.125
                    top = jnp.max(scores, axis=-1, keepdims=True)
                    grown = jnp.exp(scores - top)
                    probs = grown * (1.0 / lane_sum(grown))
                    low = probs.astype(BF16)
                    probs_ref[slot] = probs
                    low_ref[slot] = low
                    term = mm(low, v_ref[half, span] * masks[s], NN)
                    total = term if total is None else total + term
                if half:
                    total = total * used_heads(image)
                mixed_ref[half, span] = total.astype(BF16)

        if half == 0:
            attend()
        else:
            mixed_ref[half] = jnp.zeros_like(mixed_ref[half])
            pl.when(count > heads_half)(attend)

    branch = mm(mixed_ref[0], w_ref[0, :, OUT:VEC], NT) + mm(mixed_ref[1], w_ref[1, :, OUT:VEC], NT)
    resid = x + branch + vec_ref[4:5]
    normed_two, factor_two = norm_rows(resid)
    hidden_two = (normed_two * vec_ref[2:3] + vec_ref[3:4]).astype(BF16)
    cot = cot_ref[...]
    hidden_two_t = hidden_two.T
    cot_t = cot.T
    y_ref[...] = resid + vec_ref[5:6]
    gh_ref[...] = jnp.zeros_like(gh_ref)
    per_half = FC2 // CHUNK
    for chunk in range(2 * per_half):
        half, part = divmod(chunk, per_half)
        one = slice(FC1 + part * CHUNK, FC1 + (part + 1) * CHUNK)
        two = slice(FC2 + part * CHUNK, FC2 + (part + 1) * CHUNK)

        def units_pass():
            pre = mm(hidden_two, w_ref[half, :, one], NN)
            units = chunk * CHUNK + lax.broadcasted_iota(jnp.int32, pre.shape, 1)
            cumulative = 0.5 + 0.5 * lax.erf(pre * 0.7071067811865476)
            density = jnp.exp(-0.5 * pre * pre) * 0.3989422804014327
            cumulative = jnp.where(units < row_width, cumulative, 0.0)
            density = jnp.where(units < row_width, density, 0.0)
            act = (pre * cumulative).astype(BF16)
            grad_act = mm(cot, w_ref[half, :, two], NN)
            grad_pre = (grad_act * (cumulative + pre * density)).astype(BF16)
            y_ref[...] += mm(act, w_ref[half, :, two], NT)
            gh_ref[...] += mm(grad_pre, w_ref[half, :, one], NT)
            acc_ref[half, :, two] += mm(cot_t, act, NN)
            acc_ref[half, :, one] += mm(hidden_two_t, grad_pre, NN)

        if chunk < 2:
            units_pass()
        else:
            pl.when(width > chunk * CHUNK)(units_pass)

    out_ref[...] = y_ref[...]
    grad_hidden_two = gh_ref[...]
    cot_f = cot.astype(F32)
    grad_resid = cot_f + norm_back(grad_hidden_two * vec_ref[2:3], normed_two, factor_two)
    resid_low = grad_resid.astype(BF16)
    resid_low_t = resid_low.T
    hidden_one_t = hidden_one.T
    for half in range(2):
        acc_ref[half, :, OUT:VEC] += mm(resid_low_t, mixed_ref[half], NN)

        def back():
            grad_heads = mm(resid_low, w_ref[half, :, OUT:VEC], NN).astype(BF16)
            parts = []
            for image, span in enumerate(spans()):
                heads = grad_heads[span]
                if half:
                    heads = heads * used_heads(image).astype(BF16)
                sums = [None, None, None]
                for s in range(heads_half):
                    slot = (image * 2 + half) * heads_half + s
                    own = heads * masks[s]
                    grad_probs = mm(own, v_ref[half, span], NT)
                    probs = probs_ref[slot]
                    weighed = probs * grad_probs
                    grad_scores = (weighed - probs * lane_sum(weighed)).astype(BF16)
                    terms = (
                        mm(grad_scores, k_ref[half, span] * masks[s], NN),
                        mm(grad_scores, q_ref[half, span] * masks[s], TN),
                        mm(low_ref[slot], own, TN),
                    )
                    sums = [t if o is None else o + t for o, t in zip(sums, terms)]
                parts.append([(v * c).astype(BF16) for v, c in zip(sums, (0.125, 0.125, 1.0))])
            total = None
            for which in range(3):
                lanes = slice(QKV + which * SLOT, QKV + (which + 1) * SLOT)
                grad_proj = jnp.concatenate([part[which] for part in parts], axis=0)
                acc_ref[half, :, lanes] += mm(hidden_one_t, grad_proj, NN)
                term = mm(grad_proj, w_ref[half, :, lanes], NT)
                total = term if total is None else total + term
            return total

        if half == 0:
            gh_ref[...] = back()
        else:

            @pl.when(count > heads_half)
            def _():
                gh_ref[...] += back()

    grad_hidden_one = gh_ref[...]
    gtok_ref[...] = grad_resid + norm_back(grad_hidden_one * vec_ref[0:1], normed_one, factor_one)
    sums = (
        grad_hidden_one * normed_one,
        grad_hidden_one,
        grad_hidden_two * normed_two,
        grad_hidden_two,
        grad_resid,
        cot_f,
    )
    for row, values in enumerate(sums):
        gvec_ref[row : row + 1] += jnp.sum(values, axis=0, keepdims=True)

    @pl.when(step == pl.num_programs(0) - 1)
    def _():
        grad_ref[0, :, 0:VEC] = acc_ref[0].astype(BF16)
        grad_ref[1, :, 0:VEC] = acc_ref[1].astype(BF16)
        columns = gvec_ref[...].T.astype(BF16)
        grad_ref[0, :, VEC:PACK] = columns
        grad_ref[1, :, VEC:PACK] = columns


def image_pass(half, bucket, widths, counts, tokens, cotangent, packed):
    images = bucket.shape[0] // 2
    model = tokens.shape[1]
    rows = images * SEQ
    images = images // PAIR
    seq = PAIR * SEQ
    picked = pl.BlockSpec((seq, model), lambda i, h, b, w, c: (h[0] * images + i, 0))
    placed = pl.BlockSpec((seq, model), lambda i, h, b, w, c: (i, 0))
    whole = pl.BlockSpec(
        (2, model, PACK), lambda i, h, b, w, c: (0, 0, 0), pipeline_mode=pl.Buffered(1)
    )
    heads = 6
    flops = 2 * rows * model * (3 * 4 * model + 3 * 8 * model)
    return pl.pallas_call(
        image_kernel,
        out_shape=(
            jax.ShapeDtypeStruct((rows, model), F32),
            jax.ShapeDtypeStruct((rows, model), F32),
            jax.ShapeDtypeStruct((2, model, PACK), BF16),
        ),
        grid_spec=pltpu.PrefetchScalarGridSpec(
            num_scalar_prefetch=4,
            grid=(images,),
            in_specs=[picked, picked, whole],
            out_specs=[placed, placed, whole],
            scratch_shapes=[
                pltpu.VMEM((2, model, VEC), F32),
                pltpu.VMEM((8, model), F32),
                pltpu.VMEM((128, model), F32),
                pltpu.VMEM((2, seq, SLOT), BF16),
                pltpu.VMEM((2, seq, SLOT), BF16),
                pltpu.VMEM((2, seq, SLOT), BF16),
                pltpu.VMEM((2, seq, SLOT), BF16),
                pltpu.VMEM((PAIR * heads, SEQ, SEQ), F32),
                pltpu.VMEM((PAIR * heads, SEQ, SEQ), BF16),
                pltpu.VMEM((seq, model), F32),
                pltpu.VMEM((seq, model), F32),
            ],
        ),
        compiler_params=pltpu.CompilerParams(vmem_limit_bytes=56 * 1024 * 1024),
        cost_estimate=pl.CostEstimate(flops=flops, bytes_accessed=20 * rows * model, transcendentals=rows * 6144),
        name="image_pass",
    )(half, bucket, widths, counts, tokens, cotangent, packed)


MESH = pl.DeviceIdType.MESH
AT_OUT, AT_VEC, AT = 768, 1024, 1152
HEADS = 192
AT_SENT = 896
FC = 1536
EARLY = FC + SLOT
TAIL, LATE = 3 * HEADS, 640


class Place:
    def __init__(self):
        dp = lax.axis_index("dp")
        self.half = lax.axis_index("mlp")
        self.z = dp // 4
        self.y = (dp // 2) % 2
        self.x = dp % 2
        self.dp = dp
        self.y_peer = (self.index(self.z, 1 - self.y, self.x), self.half)
        self.x_peer = (self.index(self.z, self.y, 1 - self.x), self.half)
        self.sibling = (self.dp, 1 - self.half)

    def index(self, z, y, x):
        return z * 4 + y * 2 + x

    def at_z(self, z):
        return (self.index(z, self.y, self.x), self.half)


def meet(place):
    barrier = pltpu.get_barrier_semaphore()
    peers = [place.at_z((place.z + j) % 4) for j in range(1, 4)]
    peers += [place.y_peer, place.x_peer, place.sibling]
    for peer in peers:
        pl.semaphore_signal(barrier, inc=1, device_id=peer, device_id_type=MESH)
    pl.semaphore_wait(barrier, len(peers))


class Mail:
    def __init__(self, place, send_sem, recv_sem):
        self.place, self.send_sem, self.recv_sem = place, send_sem, recv_sem

    def copy(self, slot, src, dst, peer):
        return pltpu.make_async_remote_copy(
            src_ref=src,
            dst_ref=dst,
            send_sem=self.send_sem.at[slot],
            recv_sem=self.recv_sem.at[slot],
            device_id=peer,
            device_id_type=MESH,
        )

    def start(self, slot, src, dst, peer):
        self.copy(slot, src, dst, peer).start()

    def arrived(self, slot, like):
        self.copy(slot, like, like, self.place.sibling).wait_recv()

    def left(self, slot, like):
        self.copy(slot, like, like, self.place.sibling).wait_send()


GATHER_SLOTS = 35
NEAR_FIRST = (1, 3, 2)


class Gather:
    def __init__(self, place, own, buf, cut, send_sem, recv_sem):
        self.place, self.own, self.buf = place, own, buf
        self.mail = Mail(place, send_sem, recv_sem)
        self.pieces = (pl.ds(0, cut), pl.ds(cut, own.shape[1] - cut))

    def shard(self, k, y, x):
        return self.place.index((self.place.z + 4 - k) % 4, y, x)

    def forward(self, slot, dp, peer, piece=None):
        ref = self.buf.at[self.place.half, dp]
        if piece is not None:
            ref = ref.at[:, self.pieces[piece]]
        self.mail.start(slot, ref, ref, peer)

    def like(self, piece=None):
        ref = self.buf.at[0, 0]
        return ref if piece is None else ref.at[:, self.pieces[piece]]

    def start_column(self):
        place = self.place
        home = self.buf.at[place.half, place.dp]
        for j in NEAR_FIRST:
            self.mail.start(j - 1, self.own, home, place.at_z((place.z + j) % 4))

    def start_plane(self):
        place = self.place
        home = self.buf.at[place.half, place.dp]
        self.mail.start(3, self.own, home, place.y_peer)
        self.mail.start(7, self.own, home, place.x_peer)
        self.mail.start(19, self.own, home, place.sibling)

    def column(self, k):
        place = self.place
        self.mail.arrived(k - 1, self.like())
        dp = self.shard(k, place.y, place.x)
        self.forward(3 + k, dp, place.y_peer)
        self.forward(7 + k, dp, place.x_peer)
        self.forward(19 + k, dp, place.sibling)

    def plane(self, k):
        place = self.place
        self.mail.arrived(3 + k, self.like())
        dp = self.shard(k, 1 - place.y, place.x)
        self.forward(11 + k, dp, place.x_peer, 0)
        self.forward(23 + k, dp, place.sibling)
        self.mail.arrived(7 + k, self.like())
        dp = self.shard(k, place.y, 1 - place.x)
        self.forward(15 + k, dp, place.y_peer, 1)
        self.forward(27 + k, dp, place.sibling)

    def corner(self, k):
        place = self.place
        self.mail.arrived(11 + k, self.like(0))
        self.mail.arrived(15 + k, self.like(1))
        self.forward(31 + k, self.shard(k, 1 - place.y, 1 - place.x), place.sibling)

    def finish(self):
        self.receive()
        self.drain()

    def receive(self):
        for k in range(16):
            self.mail.arrived(19 + k, self.like())

    def drain(self):
        for slot in range(GATHER_SLOTS):
            piece = 0 if 11 <= slot < 15 else 1 if 15 <= slot < 19 else None
            self.mail.left(slot, self.like(piece))

    def columns(self):
        for k in NEAR_FIRST:
            self.column(k)

    def planes(self):
        for k in NEAR_FIRST:
            self.plane(k)

    def corners(self):
        for k in (0, *NEAR_FIRST):
            self.corner(k)


SCATTER_SLOTS = 43
Z_ORDER = (2, 1, 3, 0)


class Scatter:
    def __init__(self, place, parts, hold, firsts, seconds, last, cut, send_sem, recv_sem):
        self.place, self.parts, self.hold = place, parts, hold
        self.firsts, self.seconds, self.last = firsts, seconds, last
        self.mail = Mail(place, send_sem, recv_sem)
        self.pieces = (pl.ds(0, cut), pl.ds(cut, hold.shape[2] - cut))

    def shard(self, c, k):
        y, x = self.place.y, self.place.x
        column = ((1 - y, 1 - x), (y, 1 - x), (1 - y, x), (y, x))[c]
        return self.place.index((self.place.z + Z_ORDER[k]) % 4, *column)

    def piece(self, dp, p):
        return self.hold.at[dp, :, self.pieces[p]]

    def load(self, dp, p):
        return self.hold[dp, :, self.pieces[p]].astype(F32)

    def start(self):
        half = self.place.half
        for c in range(4):
            for k in range(4):
                dp = self.shard(c, k)
                self.mail.start(4 * c + k, self.parts.at[1 - half, dp], self.hold.at[dp], self.place.sibling)

    def settle(self, c, k):
        dp = self.shard(c, k)
        self.mail.arrived(4 * c + k, self.hold.at[0])
        total = self.hold[dp].astype(F32) + self.parts[self.place.half, dp].astype(F32)
        self.hold[dp] = total.astype(BF16)
        return dp

    def first_hop(self):
        place, (first_a, first_b) = self.place, self.firsts
        for k in range(4):
            dp = self.settle(0, k)
            self.mail.start(16 + k, self.piece(dp, 0), first_a.at[k], place.x_peer)
            self.mail.start(24 + k, self.piece(dp, 1), first_b.at[k], place.y_peer)
        for k in range(4):
            dp = self.settle(1, k)
            self.mail.start(20 + k, self.piece(dp, 0), first_a.at[4 + k], place.x_peer)
            dp = self.settle(2, k)
            self.mail.start(28 + k, self.piece(dp, 1), first_b.at[4 + k], place.y_peer)
        for k in range(4):
            self.settle(3, k)

    def second_hop(self):
        place, firsts, seconds = self.place, self.firsts, self.seconds
        for k in range(4):
            for p, slot, column, out, peer in ((0, 16, 2, 32, place.y_peer), (1, 24, 1, 36, place.x_peer)):
                self.mail.arrived(slot + k, firsts[p].at[0])
                dp = self.shard(column, k)
                total = self.load(dp, p) + firsts[p][k].astype(F32)
                self.hold[dp, :, self.pieces[p]] = total.astype(BF16)
                self.mail.start(out + k, self.piece(dp, p), seconds[p].at[k], peer)

    def last_hop(self, keep):
        place = self.place
        for k in range(4):
            dp = self.shard(3, k)
            totals = []
            for p, slot, second in ((0, 20, 32), (1, 28, 36)):
                self.mail.arrived(slot + k, self.firsts[p].at[0])
                self.mail.arrived(second + k, self.seconds[p].at[0])
                totals.append(self.load(dp, p) + self.firsts[p][4 + k].astype(F32) + self.seconds[p][k].astype(F32))
            for p in range(2):
                if Z_ORDER[k]:
                    self.hold[dp, :, self.pieces[p]] = totals[p].astype(BF16)
                else:
                    keep[:, self.pieces[p]] = totals[p]
            if Z_ORDER[k]:
                j = Z_ORDER[k]
                self.mail.start(40 + j - 1, self.hold.at[dp], self.last.at[j - 1], place.at_z((place.z + j) % 4))

    def finish(self, keep):
        for j in range(3):
            self.mail.arrived(40 + j, self.last.at[0])
            keep[...] = keep[...] + self.last[j].astype(F32)
        for slot in range(SCATTER_SLOTS):
            if slot < 16 or slot >= 40:
                like = self.hold.at[0]
            elif slot < 32:
                like = self.firsts[(slot - 16) // 8].at[0]
            else:
                like = self.seconds[(slot - 32) // 4].at[0]
            self.mail.left(slot, like)


CHAIN_LANES = (
    (pl.ds(0, FC // 2), pl.ds(FC // 2, FC // 2)),
    (pl.ds(FC, SLOT), pl.ds(FC, SLOT)),
)


class WideGather:
    SLOTS = 8

    def __init__(self, place, own, buf, cut, send_sem, recv_sem):
        self.place, self.own, self.buf = place, own, buf
        self.mail = Mail(place, send_sem, recv_sem)
        self.pieces = (pl.ds(0, cut), pl.ds(cut, own.shape[1] - cut))

    def column(self, y, x, piece=None):
        ref = self.buf.at[self.place.half, :, 2 * y + x]
        return ref if piece is None else ref.at[:, :, self.pieces[piece]]

    def send(self, slot, ref, peer):
        self.mail.start(slot, ref, ref, peer)

    def start(self):
        place = self.place
        home = self.buf.at[place.half, place.z, 2 * place.y + place.x]
        for j in NEAR_FIRST:
            self.mail.start(j - 1, self.own, home, place.at_z((place.z + j) % 4))

    def spread(self):
        place = self.place
        for j in range(3):
            self.mail.arrived(j, self.own)
        self.send(3, self.column(place.y, place.x), place.y_peer)
        self.send(4, self.column(place.y, place.x), place.x_peer)

    def corners(self):
        place = self.place
        self.mail.arrived(3, self.column(place.y, place.x))
        self.send(5, self.column(1 - place.y, place.x, 0), place.x_peer)
        self.mail.arrived(4, self.column(place.y, place.x))
        self.send(6, self.column(place.y, 1 - place.x, 1), place.y_peer)

    def share(self):
        place = self.place
        self.mail.arrived(5, self.column(place.y, place.x, 0))
        self.mail.arrived(6, self.column(place.y, place.x, 1))
        self.each_case(self.share_case)

    def each_case(self, action):
        place = self.place
        for x in range(2):
            for half in range(2):
                here = jnp.logical_and(place.x == x, place.half == half)
                pl.when(here)(functools.partial(action, half, CHAIN_LANES[x][half], CHAIN_LANES[x][1 - half]))

    def share_case(self, half, mine, theirs):
        self.send(7, self.buf.at[half, :, :, :, theirs], self.place.sibling)

    def finish_case(self, half, mine, theirs):
        self.mail.arrived(7, self.buf.at[half, :, :, :, mine])
        self.mail.left(7, self.buf.at[half, :, :, :, theirs])

    def finish(self):
        place = self.place
        column = self.column(place.y, place.x)
        self.each_case(self.finish_case)
        likes = [self.own] * 3 + [column] * 2
        likes += [self.column(place.y, place.x, 0), self.column(place.y, place.x, 1)]
        for slot, like in enumerate(likes):
            self.mail.left(slot, like)


class WideScatter:
    SLOTS = 10

    def __init__(self, place, parts, hold, firsts, seconds, last, cut, send_sem, recv_sem):
        self.place, self.parts, self.hold = place, parts, hold
        self.firsts, self.seconds, self.last = firsts, seconds, last
        self.mail = Mail(place, send_sem, recv_sem)
        self.pieces = (pl.ds(0, cut), pl.ds(cut, hold.shape[3] - cut))

    def column(self, y, x, piece):
        return self.hold.at[:, 2 * y + x, :, self.pieces[piece]]

    def start(self):
        self.mail.start(0, self.parts.at[1 - self.place.half], self.hold, self.place.sibling)

    def first_hop(self):
        place = self.place
        y, x = place.y, place.x
        self.mail.arrived(0, self.hold)

        def add(z, carry):
            total = self.hold[z].astype(F32) + self.parts[place.half, z].astype(F32)
            self.hold[z] = total.astype(BF16)
            return carry

        lax.fori_loop(0, self.hold.shape[0], add, 0)
        first_a, first_b = self.firsts
        self.mail.start(1, self.column(1 - y, 1 - x, 0), first_a.at[0], place.x_peer)
        self.mail.start(2, self.column(1 - y, 1 - x, 1), first_b.at[0], place.y_peer)
        self.mail.start(3, self.column(y, 1 - x, 0), first_a.at[1], place.x_peer)
        self.mail.start(4, self.column(1 - y, x, 1), first_b.at[1], place.y_peer)

    def second_hop(self):
        place = self.place
        y, x = place.y, place.x
        moves = ((0, (1 - y, x), place.y_peer), (1, (y, 1 - x), place.x_peer))
        for p, (cy, cx), peer in moves:
            self.mail.arrived(1 + p, self.firsts[p].at[0])
            lanes = self.pieces[p]
            total = self.hold[:, 2 * cy + cx, :, lanes].astype(F32) + self.firsts[p][0].astype(F32)
            self.hold[:, 2 * cy + cx, :, lanes] = total.astype(BF16)
            self.mail.start(5 + p, self.column(cy, cx, p), self.seconds[p], peer)

    def last_hop(self, keep):
        place = self.place
        home = 2 * place.y + place.x
        for p in range(2):
            self.mail.arrived(3 + p, self.firsts[p].at[1])
            self.mail.arrived(5 + p, self.seconds[p])
            lanes = self.pieces[p]
            total = self.hold[:, home, :, lanes].astype(F32) + self.firsts[p][1].astype(F32)
            self.hold[:, home, :, lanes] = (total + self.seconds[p][...].astype(F32)).astype(BF16)
        for j in NEAR_FIRST:
            z = (place.z + j) % 4
            self.mail.start(6 + j, self.hold.at[z, home], self.last.at[j - 1], place.at_z(z))
        keep[...] = self.hold[place.z, home].astype(F32)

    def finish(self, keep):
        place = self.place
        for j in range(3):
            self.mail.arrived(7 + j, self.last.at[0])
            keep[...] = keep[...] + self.last[j].astype(F32)
        likes = [self.hold] + [self.firsts[p].at[0] for p in (0, 1, 0, 1)]
        likes += [self.seconds[0], self.seconds[1]] + [self.last.at[0]] * 3
        for slot, like in enumerate(likes):
            self.mail.left(slot, like)


def wide_scratch(rows, lanes, cut):
    return [
        pltpu.VMEM((4, 4, rows, lanes), BF16),
        pltpu.VMEM((2, 4, rows, cut), BF16),
        pltpu.VMEM((2, 4, rows, lanes - cut), BF16),
        pltpu.VMEM((4, rows, cut), BF16),
        pltpu.VMEM((4, rows, lanes - cut), BF16),
        pltpu.VMEM((3, rows, lanes), BF16),
    ]


def scatter_scratch(ranks, rows, lanes, cut):
    return [
        pltpu.VMEM((ranks, rows, lanes), BF16),
        pltpu.VMEM((8, rows, cut), BF16),
        pltpu.VMEM((8, rows, lanes - cut), BF16),
        pltpu.VMEM((4, rows, cut), BF16),
        pltpu.VMEM((4, rows, lanes - cut), BF16),
        pltpu.VMEM((3, rows, lanes), BF16),
    ]


def dma(count):
    return [pltpu.SemaphoreType.DMA((count,))] * 2


SENT_CUT, FC_CUT, EARLY_CUT, LATE_CUT = 512, 768, 896, 384


def head_masks():
    lane_head = lax.broadcasted_iota(jnp.int32, (1, SLOT), 1) // HD
    return [(lane_head == s).astype(F32).astype(BF16) for s in range(3)]


def used_lanes(bucket_ref, heads_ref, image, half):
    bucket = bucket_ref[...]
    counts = jnp.zeros(bucket.shape, jnp.int32)
    for entry in range(heads_ref.shape[1]):
        counts = jnp.where(bucket == entry, heads_ref[:, entry : entry + 1], counts)
    chosen = lax.broadcasted_iota(jnp.int32, bucket.shape, 1) == image
    count = jnp.sum(jnp.where(chosen, counts.astype(F32), 0.0), axis=1, keepdims=True)
    lane_head = lax.broadcasted_iota(jnp.int32, (1, SLOT), 1) // HD
    return jnp.where(lane_head.astype(F32) < count - 3.0 * half, 1.0, 0.0)


def widen(packed, pieces):
    blank = jnp.zeros((packed.shape[0], SLOT - HEADS), packed.dtype)
    parts = []
    for piece in range(pieces):
        parts += [packed[:, piece * HEADS : (piece + 1) * HEADS], blank]
    return jnp.concatenate(parts, axis=1)


def token_copy(place, tokens_ref, tok_own, sem):
    count = tok_own.shape[0]
    start = pl.multiple_of(place.half * count, count)
    return pltpu.make_async_copy(tokens_ref.at[pl.ds(start, count)], tok_own, sem)


def own_block(step, rows):
    return pl.ds(pl.multiple_of(step * rows, rows), rows)


def attend_kernel(
    bucket_ref, heads_ref, tokens_ref, fc1_ref, fc2_ref, qkv_ref, wo_ref, vecs_ref,
    resid_ref, proj_ref, low_ref, mixed_ref, wt_ref, vec_ref, fc_buf,
    own_at, own_fc, at_buf, tok_own, turn_ref, at_send, at_recv, fc_send, fc_recv, local_sem, tok_sem,
):
    place = Place()
    step = pl.program_id(0)
    steps = pl.num_programs(0)
    rows, model = resid_ref.shape
    pack = rows // SEQ
    tok_copy = token_copy(place, tokens_ref, tok_own, tok_sem)
    slices = Gather(place, own_at, at_buf, SENT_CUT, at_send, at_recv)
    units = Gather(place, own_fc, fc_buf, FC_CUT, fc_send, fc_recv)
    local = pltpu.make_async_copy(own_fc, fc_buf.at[place.half, place.dp], local_sem)

    @pl.when(step == 0)
    def _():
        tok_copy.start()
        own_at[...] = jnp.zeros_like(own_at)
        for which in range(3):
            own_at[:, which * HEADS : (which + 1) * HEADS] = qkv_ref[which].astype(BF16)
        own_at[:, 3 * HEADS : 4 * HEADS] = wo_ref[...].astype(BF16)
        turn_ref[...] = jnp.zeros_like(turn_ref)
        turn_ref[0 : vecs_ref.shape[0], 0 : vecs_ref.shape[1]] = vecs_ref[...]
        own_at[:, AT_SENT - 128 : AT_SENT] = turn_ref[...].T[0 : own_at.shape[0]].astype(BF16)
        own_fc[:, 0 : FC // 2] = fc1_ref[...].astype(BF16)
        own_fc[:, FC // 2 : FC] = fc2_ref[...].astype(BF16)
        at_buf[place.half, place.dp] = own_at[...]
        local.start()
        meet(place)
        slices.start_column()
        slices.start_plane()
        slices.plane(0)
        slices.columns()
        units.start_column()
        slices.planes()
        units.start_plane()
        slices.corners()
        slices.receive()
        for half in range(2):
            sent = at_buf[half].astype(F32).reshape(model, AT_SENT)
            wt_ref[half, :, 0:AT_VEC] = widen(sent, 4).astype(BF16)
            wt_ref[half, :, AT_VEC:AT] = sent[:, AT_SENT - 128 : AT_SENT].astype(BF16)
        vec_ref[...] = wt_ref[0, :, AT_VEC:AT].astype(F32).T[0:8]
        tok_copy.wait()

    @pl.when(step == 2)
    def _():
        units.planes()

    @pl.when(step == steps - 1)
    def _():
        units.corners()

    masks = head_masks()
    first_image = place.half * (bucket_ref.shape[1] // 2)
    x = tok_own[own_block(step, rows)].astype(F32)
    normed_one, _ = norm_rows(x)
    hidden_one = (normed_one * vec_ref[0:1] + vec_ref[1:2]).astype(BF16)
    branch = None
    for half in range(2):
        base = half * 3 * SLOT
        proj = []
        for which in range(3):
            part = mm(hidden_one, wt_ref[half, :, which * SLOT : (which + 1) * SLOT], NN).astype(BF16)
            proj_ref[:, base + which * SLOT : base + (which + 1) * SLOT] = part
            proj.append(part)
        mixes = []
        for image in range(pack):
            span = slice(image * SEQ, (image + 1) * SEQ)
            queries, keys, values = (part[span] for part in proj)
            total = None
            for s in range(3):
                scores = mm(queries * masks[s], keys, NT) * 0.125
                top = jnp.max(scores, axis=-1, keepdims=True)
                grown = jnp.exp(scores - top)
                low = (grown * (1.0 / lane_sum(grown))).astype(BF16)
                low_ref[(image * 2 + half) * 3 + s] = low
                term = mm(low, values * masks[s], NN)
                total = term if total is None else total + term
            mixes.append((total * used_lanes(bucket_ref, heads_ref, first_image + step * pack + image, half)).astype(BF16))
        mixed = jnp.concatenate(mixes, axis=0)
        mixed_ref[:, half * SLOT : (half + 1) * SLOT] = mixed
        term = mm(mixed, wt_ref[half, :, AT_OUT:AT_VEC], NT)
        branch = term if branch is None else branch + term
        if half == 0:

            @pl.when(step == 0)
            def _():
                units.columns()
                units.plane(0)

    resid_ref[...] = x + branch + vec_ref[4:5]

    @pl.when(step == steps - 1)
    def _():
        units.finish()
        slices.drain()
        local.wait()


def const(shape, **kw):
    return pl.BlockSpec(shape, lambda i, *_: (0,) * len(shape), **kw)


def once(shape):
    return const(shape, pipeline_mode=pl.Buffered(1))


def attend_pass(bucket, heads, tokens, weights, vectors, ranks):
    model = tokens.shape[1]
    images = bucket.shape[1] // 2
    rows = weights[0].shape[0]
    count = images * SEQ
    steps = images // PAIR
    block = PAIR * SEQ

    def by_step(lanes):
        return pl.BlockSpec((block, lanes), lambda i: (i, 0))

    return pl.pallas_call(
        attend_kernel,
        out_shape=(
            jax.ShapeDtypeStruct((count, model), F32),
            jax.ShapeDtypeStruct((count, 6 * SLOT), BF16),
            jax.ShapeDtypeStruct((images * 6, SEQ, SEQ), BF16),
            jax.ShapeDtypeStruct((count, 2 * SLOT), BF16),
            jax.ShapeDtypeStruct((2, model, AT), BF16),
            jax.ShapeDtypeStruct((8, model), F32),
            jax.ShapeDtypeStruct((2, ranks, rows, FC), BF16),
        ),
        grid_spec=pltpu.PrefetchScalarGridSpec(
            num_scalar_prefetch=0,
            grid=(steps,),
            in_specs=[once(bucket.shape), once(heads.shape), pl.BlockSpec(memory_space=pl.ANY)]
            + [once(w.shape) for w in weights]
            + [once(vectors.shape)],
            out_specs=[
                by_step(model),
                by_step(6 * SLOT),
                pl.BlockSpec((PAIR * 6, SEQ, SEQ), lambda i: (i, 0, 0)),
                by_step(2 * SLOT),
                once((2, model, AT)),
                once((8, model)),
                pl.BlockSpec(memory_space=pl.ANY),
            ],
            scratch_shapes=[
                pltpu.VMEM((rows, AT_SENT), BF16),
                pltpu.VMEM((rows, FC), BF16),
                pltpu.VMEM((2, ranks, rows, AT_SENT), BF16),
                pltpu.VMEM((count, model), BF16),
                pltpu.VMEM((128, 128), F32),
            ]
            + dma(GATHER_SLOTS)
            + dma(GATHER_SLOTS)
            + [pltpu.SemaphoreType.DMA] * 2,
        ),
        compiler_params=pltpu.CompilerParams(
            collective_id=0, has_side_effects=True, vmem_limit_bytes=56 * 1024 * 1024
        ),
        name="attend_pass",
    )(bucket, heads, tokens, *weights, vectors)


def units_kernel(
    half_ref, bucket_ref, widths_ref, resid_ref, cot_ref, mixed_ref, w_ref, vec_ref,
    out_ref, gres_ref, grad_ref, gvec_ref, acc_ref, y_ref, gh_ref,
):
    step = pl.program_id(0)
    rows, model = resid_ref.shape
    pack = rows // SEQ
    first = (half_ref[0] * pl.num_programs(0) + step) * pack
    widths = [widths_ref[bucket_ref[first + image]] for image in range(pack)]
    row_ids = lax.broadcasted_iota(jnp.int32, (rows, 1), 0)
    width, row_width = widths[0], jnp.full((rows, 1), widths[0], jnp.int32)
    for image in range(1, pack):
        width = jnp.maximum(width, widths[image])
        row_width = jnp.where(row_ids >= image * SEQ, widths[image], row_width)

    @pl.when(step == 0)
    def _():
        acc_ref[...] = jnp.zeros_like(acc_ref)
        gvec_ref[...] = jnp.zeros_like(gvec_ref)

    resid = resid_ref[...]
    normed_two, factor_two = norm_rows(resid)
    hidden_two = (normed_two * vec_ref[2:3] + vec_ref[3:4]).astype(BF16)
    cot = cot_ref[...]
    hidden_two_t = hidden_two.T
    cot_t = cot.T
    y_ref[...] = resid + vec_ref[5:6]
    gh_ref[...] = jnp.zeros_like(gh_ref)
    per_half = FC2 // CHUNK
    for chunk in range(2 * per_half):
        half, part = divmod(chunk, per_half)
        one = slice(FC1 + part * CHUNK, FC1 + (part + 1) * CHUNK)
        two = slice(FC2 + part * CHUNK, FC2 + (part + 1) * CHUNK)

        def units_pass():
            pre = mm(hidden_two, w_ref[half, :, one], NN)
            units = chunk * CHUNK + lax.broadcasted_iota(jnp.int32, pre.shape, 1)
            cumulative = 0.5 + 0.5 * lax.erf(pre * 0.7071067811865476)
            density = jnp.exp(-0.5 * pre * pre) * 0.3989422804014327
            cumulative = jnp.where(units < row_width, cumulative, 0.0)
            density = jnp.where(units < row_width, density, 0.0)
            act = (pre * cumulative).astype(BF16)
            grad_act = mm(cot, w_ref[half, :, two], NN)
            grad_pre = (grad_act * (cumulative + pre * density)).astype(BF16)
            y_ref[...] += mm(act, w_ref[half, :, two], NT)
            gh_ref[...] += mm(grad_pre, w_ref[half, :, one], NT)
            acc_ref[half, :, two] += mm(cot_t, act, NN)
            acc_ref[half, :, one] += mm(hidden_two_t, grad_pre, NN)

        if chunk < 2:
            units_pass()
        else:
            pl.when(width > chunk * CHUNK)(units_pass)

    out_ref[...] = y_ref[...]
    grad_hidden_two = gh_ref[...]
    cot_f = cot.astype(F32)
    grad_resid = cot_f + norm_back(grad_hidden_two * vec_ref[2:3], normed_two, factor_two)
    gres_ref[...] = grad_resid
    resid_low_t = grad_resid.astype(BF16).T
    for half in range(2):
        acc_ref[half, :, FC:EARLY] += mm(resid_low_t, mixed_ref[:, half * SLOT : (half + 1) * SLOT], NN)
    sums = (grad_hidden_two * normed_two, grad_hidden_two, grad_resid, cot_f)
    for row, values in enumerate(sums):
        gvec_ref[2 + row : 3 + row] += jnp.sum(values, axis=0, keepdims=True)

    @pl.when(step == pl.num_programs(0) - 1)
    def _():
        grad_ref[...] = acc_ref[...].astype(BF16)


def units_pass(half, bucket, widths, resid, cotangent, mixed, packed, vec):
    count, model = resid.shape
    block = PAIR * SEQ
    steps = count // block
    placed = pl.BlockSpec((block, model), lambda i, h, b, w: (i, 0))
    picked = pl.BlockSpec((block, model), lambda i, h, b, w: (h[0] * steps + i, 0))
    blended = pl.BlockSpec((block, 2 * SLOT), lambda i, h, b, w: (i, 0))
    return pl.pallas_call(
        units_kernel,
        out_shape=(
            jax.ShapeDtypeStruct((count, model), F32),
            jax.ShapeDtypeStruct((count, model), F32),
            jax.ShapeDtypeStruct((2, model, EARLY), BF16),
            jax.ShapeDtypeStruct((8, model), F32),
        ),
        grid_spec=pltpu.PrefetchScalarGridSpec(
            num_scalar_prefetch=3,
            grid=(steps,),
            in_specs=[placed, picked, blended, once(packed.shape), once(vec.shape)],
            out_specs=[placed, placed, once((2, model, EARLY)), once((8, model))],
            scratch_shapes=[
                pltpu.VMEM((2, model, EARLY), F32),
                pltpu.VMEM((block, model), F32),
                pltpu.VMEM((block, model), F32),
            ],
        ),
        compiler_params=pltpu.CompilerParams(vmem_limit_bytes=56 * 1024 * 1024),
        name="units_pass",
    )(half, bucket, widths, resid, cotangent, mixed, packed, vec)


def back_kernel(
    bucket_ref, heads_ref, tokens_ref, gres_ref, proj_ref, low_ref, wt_ref, vec_ref, gvec_ref,
    fc_parts, fc1_ref, fc2_ref, qkv_ref, wo_ref, out_half,
    gtok_ref, pairs_ref, fc_buf, at_buf, out_other,
    acc_ref, sums_ref, gtok_own, at_parts, own_fc, own_at, tok_own,
    fc_hold, fc_first_a, fc_first_b, fc_second_a, fc_second_b, fc_last,
    at_hold, at_first_a, at_first_b, at_second_a, at_second_b, at_last,
    fcs_send, fcs_recv, ats_send, ats_recv, fcg_send, fcg_recv, atg_send, atg_recv,
    side_send, side_recv, local_sems,
):
    place = Place()
    step = pl.program_id(0)
    steps = pl.num_programs(0)
    rows, model = gres_ref.shape
    tok_copy = token_copy(place, tokens_ref, tok_own, local_sems.at[0])
    pack = rows // SEQ
    count = gtok_ref.shape[0] // 2
    early, late = pl.ds(0, EARLY), pl.ds(EARLY, LATE)
    grad_fc, mom_fc = pairs_ref.at[0, :, early], pairs_ref.at[1, :, early]
    grad_at, mom_at = pairs_ref.at[0, :, late], pairs_ref.at[1, :, late]
    fc_sum = WideScatter(
        place, fc_parts, fc_hold, (fc_first_a, fc_first_b), (fc_second_a, fc_second_b), fc_last,
        EARLY_CUT, fcs_send, fcs_recv,
    )
    at_sum = Scatter(
        place, at_parts, at_hold, (at_first_a, at_first_b), (at_second_a, at_second_b), at_last,
        LATE_CUT, ats_send, ats_recv,
    )
    fc_all = WideGather(place, own_fc, fc_buf, EARLY_CUT, fcg_send, fcg_recv)
    at_all = Gather(place, own_at, at_buf, LATE_CUT, atg_send, atg_recv)
    side = Mail(place, side_send, side_recv)
    fc_home = pltpu.make_async_copy(
        own_fc, fc_buf.at[place.half, place.z, 2 * place.y + place.x], local_sems.at[1]
    )
    at_home = pltpu.make_async_copy(own_at, at_buf.at[place.half, place.dp], local_sems.at[2])

    @pl.when(step == 0)
    def _():
        tok_copy.start()
        meet(place)
        fc_sum.start()
        tok_copy.wait()
        acc_ref[...] = jnp.zeros_like(acc_ref)
        sums_ref[...] = jnp.zeros_like(sums_ref)
        sums_ref[0:8] = gvec_ref[...]

    def settle_units():
        fc_sum.finish(grad_fc)
        mom_fc[:, 0 : FC // 2] = 0.95 * fc1_ref[...]
        mom_fc[:, FC // 2 : FC] = 0.95 * fc2_ref[...]
        mom_fc[:, FC:EARLY] = jnp.zeros((mom_fc.shape[0], SLOT), F32)
        mom_fc[:, FC : FC + HEADS] = 0.95 * wo_ref[...]
        mom_fc[...] = mom_fc[...] + grad_fc[...]
        own_fc[...] = mom_fc[...].astype(BF16)
        fc_home.start()
        fc_all.start()
        side.start(0, out_half, out_other, place.sibling)

    def spread_units():
        fc_home.wait()
        fc_all.spread()

    def part_units():
        fc_all.corners()

    stages = {
        1: fc_sum.first_hop,
        6: fc_sum.second_hop,
        10: lambda: fc_sum.last_hop(grad_fc),
        15: settle_units,
    }

    def slot(quarter):
        for number, stage in stages.items():
            if number % 4 == quarter:
                pl.when(step == number // 4)(stage)

    masks = head_masks()
    first_image = place.half * (bucket_ref.shape[1] // 2)
    normed_one, factor_one = norm_rows(tok_own[own_block(step, rows)].astype(F32))
    hidden_one_t = (normed_one * vec_ref[0:1] + vec_ref[1:2]).astype(BF16).T
    grad_resid = gres_ref[...]
    resid_low = grad_resid.astype(BF16)
    grad_hidden_one = None
    for half in range(2):
        base = half * 3 * SLOT
        grad_heads = mm(resid_low, wt_ref[half, :, AT_OUT:AT_VEC], NN).astype(BF16)
        parts = []
        for image in range(pack):
            span = slice(image * SEQ, (image + 1) * SEQ)
            used = used_lanes(bucket_ref, heads_ref, first_image + step * pack + image, half).astype(BF16)
            heads = grad_heads[span] * used
            queries, keys, values = (
                proj_ref[span, base + which * SLOT : base + (which + 1) * SLOT] for which in range(3)
            )
            sums = [None, None, None]
            for s in range(3):
                own = heads * masks[s]
                low = low_ref[(image * 2 + half) * 3 + s]
                grad_probs = mm(own, values, NT)
                probs = low.astype(F32)
                weighed = probs * grad_probs
                grad_scores = (weighed - probs * lane_sum(weighed)).astype(BF16)
                terms = (
                    mm(grad_scores, keys * masks[s], NN),
                    mm(grad_scores, queries * masks[s], TN),
                    mm(low, own, TN),
                )
                sums = [t if o is None else o + t for o, t in zip(sums, terms)]
            parts.append([(v * c).astype(BF16) for v, c in zip(sums, (0.125, 0.125, 1.0))])
            if image == 0:
                slot(2 * half)
        for which in range(3):
            lanes = slice(which * SLOT, (which + 1) * SLOT)
            grad_proj = jnp.concatenate([part[which] for part in parts], axis=0)
            acc_ref[half, :, lanes] += mm(hidden_one_t, grad_proj, NN)
            term = mm(grad_proj, wt_ref[half, :, lanes], NT)
            grad_hidden_one = term if grad_hidden_one is None else grad_hidden_one + term
        if half == 0:
            slot(1)

    gtok_own[step] = grad_resid + norm_back(grad_hidden_one * vec_ref[0:1], normed_one, factor_one)
    sums_ref[0:1] += jnp.sum(grad_hidden_one * normed_one, axis=0, keepdims=True)
    sums_ref[1:2] += jnp.sum(grad_hidden_one, axis=0, keepdims=True)

    slot(3)

    def own_rows(index):
        start = place.half * count + index * rows
        return gtok_ref.at[pl.ds(pl.multiple_of(start, rows), rows)]

    @pl.when(step == steps - 1)
    def _():
        columns = sums_ref[...].T[:, 0 : LATE - TAIL].astype(BF16)
        ranks, own = at_parts.shape[1], at_parts.shape[2]
        for half in range(2):
            for which in range(3):
                piece = acc_ref[half, :, which * SLOT : which * SLOT + HEADS].astype(BF16)
                at_parts[half, :, :, which * HEADS : (which + 1) * HEADS] = piece.reshape(ranks, own, HEADS)
            at_parts[half, :, :, TAIL:LATE] = columns.reshape(ranks, own, LATE - TAIL)
        at_sum.start()
        at_sum.first_hop()
        for index in range(gtok_own.shape[0]):
            side.start(1 + index, gtok_own.at[index], own_rows(index), place.sibling)
            pltpu.make_async_copy(gtok_own.at[index], own_rows(index), local_sems.at[3 + index]).start()
        mom_at[...] = jnp.zeros(mom_at.shape, F32)
        for which in range(3):
            mom_at[:, which * HEADS : (which + 1) * HEADS] = 0.95 * qkv_ref[which]
        at_sum.second_hop()
        at_sum.last_hop(grad_at)
        spread_units()
        at_sum.finish(grad_at)
        mom_at[:, 0:TAIL] = mom_at[:, 0:TAIL] + grad_at[:, 0:TAIL]
        own_at[:, 0:TAIL] = mom_at[:, 0:TAIL].astype(BF16)
        lanes = lax.broadcasted_iota(jnp.int32, (own, LATE - TAIL), 1)
        tile = jnp.zeros(lanes.shape, F32)
        pieces = (
            grad_at[:, 0:TAIL], grad_fc[:, FC:EARLY], grad_fc[:, 0 : FC // 2],
            grad_fc[:, FC // 2 : FC], grad_at[:, TAIL:LATE],
        )
        for number, piece in enumerate(pieces):
            square = jnp.sum(lane_sum(piece * piece), axis=0, keepdims=True)
            square = jnp.broadcast_to(square * (0.5 if number == 4 else 1.0), lanes.shape)
            high = square.astype(BF16).astype(F32)
            tile = jnp.where(lanes == number, high, tile)
            tile = jnp.where(lanes == 32 + number, square - high, tile)
        own_at[:, TAIL:LATE] = tile.astype(BF16)
        at_home.start()
        at_all.start_column()
        at_all.start_plane()
        at_all.plane(0)
        at_all.columns()
        part_units()
        at_all.planes()
        at_all.corners()
        fc_all.share()
        at_all.finish()
        fc_all.finish()
        side.arrived(0, out_half)
        side.left(0, out_half)
        for index in range(gtok_own.shape[0]):
            side.arrived(1 + index, gtok_own.at[0])
            side.left(1 + index, gtok_own.at[0])
            pltpu.make_async_copy(gtok_own.at[index], own_rows(index), local_sems.at[3 + index]).wait()
        at_home.wait()


def back_pass(bucket, heads, tokens, gres, proj, low, wt, vec, gvec, fc_parts, moms, out_half):
    count, model = gres.shape
    rows = fc_parts.shape[3]
    ranks = fc_parts.shape[1] * fc_parts.shape[2]
    block = PAIR * SEQ
    steps = count // block

    def by_step(lanes):
        return pl.BlockSpec((block, lanes), lambda i: (i, 0))

    anywhere = pl.BlockSpec(memory_space=pl.ANY)
    return pl.pallas_call(
        back_kernel,
        out_shape=(
            jax.ShapeDtypeStruct((2 * count, model), F32),
            jax.ShapeDtypeStruct((2, rows, EARLY + LATE), F32),
            jax.ShapeDtypeStruct(fc_parts.shape, BF16),
            jax.ShapeDtypeStruct((2, ranks, rows, LATE), BF16),
            jax.ShapeDtypeStruct((count, model), F32),
        ),
        grid_spec=pltpu.PrefetchScalarGridSpec(
            num_scalar_prefetch=0,
            grid=(steps,),
            in_specs=[
                once(bucket.shape),
                once(heads.shape),
                anywhere,
                by_step(model),
                by_step(6 * SLOT),
                pl.BlockSpec((PAIR * 6, SEQ, SEQ), lambda i: (i, 0, 0)),
                once(wt.shape),
                once(vec.shape),
                once(gvec.shape),
                once(fc_parts.shape),
            ]
            + [once(m.shape) for m in moms]
            + [anywhere],
            out_specs=[
                anywhere,
                once((2, rows, EARLY + LATE)),
                anywhere,
                anywhere,
                anywhere,
            ],
            scratch_shapes=[
                pltpu.VMEM((2, model, AT_OUT), F32),
                pltpu.VMEM((128, model), F32),
                pltpu.VMEM((steps, block, model), F32),
                pltpu.VMEM((2, ranks, rows, LATE), BF16),
                pltpu.VMEM((rows, EARLY), BF16),
                pltpu.VMEM((rows, LATE), BF16),
                pltpu.VMEM((count, model), BF16),
            ]
            + wide_scratch(rows, EARLY, EARLY_CUT)
            + scatter_scratch(ranks, rows, LATE, LATE_CUT)
            + dma(WideScatter.SLOTS)
            + dma(SCATTER_SLOTS)
            + dma(WideGather.SLOTS)
            + dma(GATHER_SLOTS)
            + dma(1 + steps)
            + [pltpu.SemaphoreType.DMA((3 + steps,))],
        ),
        compiler_params=pltpu.CompilerParams(
            collective_id=1, has_side_effects=True, vmem_limit_bytes=60 * 1024 * 1024
        ),
        name="back_pass",
    )(bucket, heads, tokens, gres, proj, low, wt, vec, gvec, fc_parts, *moms, out_half)


QUINTIC = (3.4445, -4.775, 2.0315)
RATES = (2.0, 2.0, math.sqrt(3.0), math.sqrt(32.0))
RANGES = ((0, FC // 2), (FC // 2, FC), (0, LATE), (FC, EARLY))
IN_LATE = 2


def mm3(a, b):
    return lax.dot_general(a, b, NN, precision=lax.Precision.HIGH, preferred_element_type=F32)


def eye_mask(n):
    return lax.broadcasted_iota(jnp.int32, (n, n), 0) == lax.broadcasted_iota(jnp.int32, (n, n), 1)


def chain_kernel(
    fc_ref, at_ref, pairs_ref, vec_ref, first_ref, second_ref,
    fc1_ref, fc2_ref, qkv_ref, wo_ref, out_half, out_other, gtok_both,
    root_ref, norm_ref, gfc1, gfc2, gqkv, gwo, gvec, mfc1, mfc2, mqkv, mwo,
    vec_new, first_new, second_new, kept_fc, kept_at, half_fc, half_at, out_ref, gtok_ref,
    gram_ref, poly_ref, rows_ref, turn_ref, out_hold, gtok_hold, sems,
):
    place = Place()
    count = out_half.shape[0]
    early, late = pl.ds(0, EARLY), pl.ds(EARLY, LATE)
    grad_fc, mom_fc = pairs_ref.at[0, :, early], pairs_ref.at[1, :, early]
    grad_at, mom_at = pairs_ref.at[0, :, late], pairs_ref.at[1, :, late]
    half = place.half
    which = 2 * place.x + half
    sources = ((out_half, out_hold.at[0]), (out_other, out_hold.at[1]), (gtok_both, gtok_hold))
    loads = [pltpu.make_async_copy(src, hold, sems.at[i]) for i, (src, hold) in enumerate(sources)]
    stores = []
    for i, part in enumerate((half, 1 - half)):
        rows = pl.ds(pl.multiple_of(part * count, 8), count)
        stores.append(pltpu.make_async_copy(out_hold.at[i], out_ref.at[rows], sems.at[3 + i]))
    stores.append(pltpu.make_async_copy(gtok_hold, gtok_ref, sems.at[5]))
    for load in loads:
        load.start()
    model = fc_ref.shape[1]
    for number, (start, stop) in enumerate(RANGES):
        buf = at_ref if number == IN_LATE else fc_ref

        @pl.when(which == number)
        def _():
            lower, upper = buf[0, :, start:stop], buf[1, :, start:stop]
            if number == IN_LATE:
                keep = (lax.broadcasted_iota(jnp.int32, (1, LATE), 1) < TAIL).astype(F32).astype(BF16)
                lower, upper = lower * keep, upper * keep
            gram_ref[...] = mm(lower, lower, NT) + mm(upper, upper, NT)

    eye = eye_mask(model)
    gram = gram_ref[...]
    total = jnp.sum(lane_sum(jnp.where(eye, gram, 0.0)), axis=0, keepdims=True)
    scale = 1.0 / (jnp.sqrt(total) + 1e-07)
    gram_ref[...] = gram * (scale * scale)
    a, b, c = QUINTIC

    def polynomial():
        gram = gram_ref[...]
        return jnp.where(eye, a, 0.0) + b * gram + c * mm3(gram, gram)

    def advance(poly):
        gram_ref[...] = mm3(mm3(gram_ref[...], poly), poly)

    poly = polynomial()
    poly_ref[...] = poly
    first_row = (place.dp // 2) * rows_ref.shape[0]
    rows_ref[...] = poly_ref[pl.ds(pl.multiple_of(first_row, 8), rows_ref.shape[0])]
    advance(poly)
    for load, store in zip(loads, stores):
        load.wait()
        store.start()

    def sweep(_, carry):
        poly = polynomial()
        rows_ref[...] = mm3(rows_ref[...], poly)
        advance(poly)
        return carry

    lax.fori_loop(0, NS_ITERS - 2, sweep, 0)
    rows, gram = rows_ref[...], gram_ref[...]
    once_more = mm3(rows, gram)
    last = (a * rows + b * once_more + c * mm3(once_more, gram)) * scale
    for part in range(root_ref.shape[0]):
        root_ref[part] = last[part * root_ref.shape[1] : (part + 1) * root_ref.shape[1]]

    wide = FC // 2
    gfc1[...], gfc2[...] = grad_fc[:, 0:wide], grad_fc[:, wide:FC]
    mfc1[...], mfc2[...] = mom_fc[:, 0:wide], mom_fc[:, wide:FC]
    gwo[...] = grad_fc[:, FC : FC + HEADS]
    mwo[...] = mom_fc[:, FC : FC + HEADS]
    kept_fc[...] = jnp.zeros_like(kept_fc)
    kept_fc[:, 0:wide] = 0.999 * fc1_ref[...]
    kept_fc[:, wide:FC] = 0.999 * fc2_ref[...]
    kept_fc[:, FC : FC + HEADS] = 0.999 * wo_ref[...]
    kept_at[...] = jnp.zeros_like(kept_at)
    half_fc[...] = fc_ref[half]
    half_at[...] = at_ref[half]
    for part in range(3):
        span = slice(part * HEADS, (part + 1) * HEADS)
        gqkv[part] = grad_at[:, span]
        mqkv[part] = mom_at[:, span]
        kept_at[:, span] = 0.999 * qkv_ref[part]
    own = grad_at.shape[0]
    turn_ref[...] = jnp.zeros_like(turn_ref)
    turn_ref[0:own, 0 : LATE - TAIL] = grad_at[:, TAIL:LATE]
    turned = turn_ref[...].T[0:6, 0 : vec_ref.shape[1]]
    first = 0.9 * first_ref[...] + 0.1 * turned
    second = 0.95 * second_ref[...] + 0.05 * turned * turned
    gvec[...] = turned
    first_new[...] = first
    second_new[...] = second
    vec_new[...] = vec_ref[...] - 0.5 * (first / (1.0 - 0.9**STEP)) / (
        jnp.sqrt(second / (1.0 - 0.95**STEP)) + 1e-08
    )
    tiles = at_ref[0, :, LATE - 128 : LATE].astype(F32) + at_ref[1, :, LATE - 128 : LATE].astype(F32)
    leads = lax.broadcasted_iota(jnp.int32, tiles.shape, 0) % own == 0
    squares = jnp.sum(jnp.where(leads, tiles, 0.0), axis=0, keepdims=True)
    squares = pltpu.roll(squares, 64, 1)
    norm_ref[...] = jnp.sqrt(jnp.abs(squares + pltpu.roll(squares, 96, 1)))[:, 0:5]
    for store in stores:
        store.wait()


def run_chain(fc_buf, at_buf, pairs, vectors, first, second, weights, wholes):
    model = fc_buf.shape[1]
    own, columns = pairs.shape[1], vectors.shape[1]
    count = wholes[0].shape[0]
    full = (2 * count, model)
    vmem = pl.BlockSpec(memory_space=pltpu.VMEM)
    anywhere = pl.BlockSpec(memory_space=pl.ANY)
    shapes = [(own, 768), (own, 768), (3, own, 192), (own, 192)]
    outs = [(2, own, model), (1, 5)] + shapes + [(6, columns)] + shapes + [(6, columns)] * 3
    lows = [(model, EARLY), (model, LATE)]
    outs += [(own, EARLY), (own, LATE)] + lows + [full] * 2
    return pl.pallas_call(
        chain_kernel,
        out_shape=tuple(jax.ShapeDtypeStruct(shape, BF16 if shape in lows else F32) for shape in outs),
        in_specs=[vmem] * 10 + [anywhere] * 3,
        out_specs=tuple([vmem] * (len(outs) - 2) + [anywhere] * 2),
        scratch_shapes=[
            pltpu.VMEM((model, model), F32),
            pltpu.VMEM((model, model), F32),
            pltpu.VMEM((2 * own, model), F32),
            pltpu.VMEM((128, 128), F32),
            pltpu.VMEM((2, count, model), F32),
            pltpu.VMEM(full, F32),
            pltpu.SemaphoreType.DMA((6,)),
        ],
        compiler_params=pltpu.CompilerParams(vmem_limit_bytes=44 * 1024 * 1024),
        name="run_chain",
    )(fc_buf, at_buf, pairs, vectors, first, second, *weights, *wholes)


def roots_kernel(
    root_ref, kept_fc, kept_at, fc_own, at_own,
    nfc1, nfc2, nqkv, nwo, rows_ref, send_sem, recv_sem,
):
    place = Place()
    x, half = place.x, place.half
    barrier = pltpu.get_barrier_semaphore()
    peers = [(1 - x, half), (x, 1 - half), (1 - x, 1 - half)]
    ids = [(place.index(place.z, place.y, px), ph) for px, ph in peers]
    for peer in ids:
        pl.semaphore_signal(barrier, inc=1, device_id=peer, device_id_type=MESH)
    pl.semaphore_wait(barrier, 3)
    mail = Mail(place, send_sem, recv_sem)
    mine = 2 * x + half
    for slot, peer in enumerate(ids):
        mail.start(slot, root_ref.at[peers[slot][0]], rows_ref.at[mine], peer)
    rows_ref[mine] = root_ref[x]
    for slot in range(3):
        mail.arrived(slot, rows_ref.at[0])
    for number, (start, stop) in enumerate(RANGES):
        rows = rows_ref[number]
        high = rows.astype(BF16)
        low = (rows - high.astype(F32)).astype(BF16)
        late = number == IN_LATE
        moment = (at_own if late else fc_own)[:, start:stop]
        step = RATES[number] * (mm(high, moment, NN) + mm(low, moment, NN))
        new = (kept_at if late else kept_fc)[:, start:stop] - step
        if late:
            for part in range(3):
                nqkv[part] = new[:, part * HEADS : (part + 1) * HEADS]
        else:
            out = (nfc1, nfc2, None, nwo)[number]
            out[...] = new[:, 0 : out.shape[1]]
    for slot in range(3):
        mail.left(slot, rows_ref.at[0])


def apply_roots(root, kept_fc, kept_at, half_fc, half_at, weights):
    _, rows, model = root.shape
    vmem = pl.BlockSpec(memory_space=pltpu.VMEM)
    return pl.pallas_call(
        roots_kernel,
        out_shape=tuple(jax.ShapeDtypeStruct(w.shape, F32) for w in weights),
        in_specs=[vmem] * 5,
        out_specs=(vmem,) * 4,
        scratch_shapes=[
            pltpu.VMEM((4, rows, model), F32),
        ]
        + dma(3),
        compiler_params=pltpu.CompilerParams(
            collective_id=2, has_side_effects=True, vmem_limit_bytes=32 * 1024 * 1024
        ),
        name="apply_roots",
    )(root, kept_fc, kept_at, half_fc, half_at)


def flat(part):
    return part.T if part.ndim == 2 else jnp.transpose(part, (0, 2, 1))


def pack(fc1, fc2, qkv, out):
    pad = ((0, 0), (0, SLOT - out.shape[1]))
    return jnp.concatenate([fc1, fc2] + [jnp.pad(part, pad) for part in (*qkv, out)], axis=1)


def unpack(packed, like):
    fc1, fc2, qkv, out = like
    split = jnp.stack([packed[:, QKV + part * SLOT :][:, : qkv.shape[2]] for part in range(3)])
    return packed[:, FC1:FC2], packed[:, FC2:QKV], split, packed[:, OUT : OUT + out.shape[1]]


def root_of(gram):
    a, b, c = QUINTIC
    eye = eye_mask(gram.shape[0])
    scale = 1.0 / (jnp.sqrt(jnp.sum(jnp.where(eye, gram, 0.0))) + 1e-07)
    gram = gram * (scale * scale)
    root = jnp.where(eye, scale, 0.0)
    for _ in range(NS_ITERS):
        poly = jnp.where(eye, a, 0.0) + b * gram + c * mm3(gram, gram)
        root = mm3(root, poly)
        gram = mm3(mm3(gram, poly), poly)
    return root


def general(half, bucket, widths, counts, tokens, cotangent, weights, moms, vectors, vec_first, vec_second):
    dp = lax.axis_index("dp")
    rows = weights[0].shape[0]
    vec = jnp.pad(vectors.T, ((0, 0), (0, PACK - VEC - vectors.shape[0])))
    own = jnp.concatenate([pack(*weights), vec], axis=1).astype(BF16)
    packed = lax.all_gather(lax.all_gather(own, "dp", axis=0, tiled=True), "mlp")
    out_half, gtok_half, grads = image_pass(half.reshape(1), bucket, widths, counts, tokens, cotangent, packed)
    output = lax.all_gather(out_half, "mlp", axis=0, tiled=True)
    gtok = lax.all_gather(gtok_half, "mlp", axis=0, tiled=True)
    grad = lax.psum_scatter(grads.astype(F32), "mlp", scatter_dimension=0)
    grad = lax.psum_scatter(grad, "dp", scatter_dimension=0, tiled=True)
    mom = 0.95 * pack(*moms) + grad[:, 0:VEC]
    spans = ((FC1, FC2), (FC2, QKV), (QKV, OUT), (OUT, VEC))
    squares = [jnp.sum(jnp.square(grad[:, start:stop])) for start, stop in spans[2:] + spans[:2]]
    squares.append(0.5 * jnp.sum(jnp.square(grad[:, VEC:PACK])))
    norms = jnp.sqrt(lax.psum(jnp.stack(squares), ("dp", "mlp")))
    buf = lax.all_gather(lax.all_gather(mom.astype(BF16), "dp", axis=0, tiled=True), "mlp")
    ours = lax.dynamic_index_in_dim(buf, half, 0, keepdims=False)
    steps = []
    for (start, stop), rate in zip(spans, RATES):
        root = root_of(sum(mm(buf[h, :, start:stop], buf[h, :, start:stop], NT) for h in range(2)))
        root = lax.dynamic_slice_in_dim(root, dp * rows, rows, 0)
        high = root.astype(BF16)
        low = (root - high.astype(F32)).astype(BF16)
        steps.append(rate * (mm(high, ours[:, start:stop], NN) + mm(low, ours[:, start:stop], NN)))
    moved = unpack(jnp.concatenate(steps, axis=1), weights)
    gvec = grad[:, VEC : VEC + vectors.shape[0]].T
    first = 0.9 * vec_first + 0.1 * gvec
    second = 0.95 * vec_second + 0.05 * gvec * gvec
    vec_new = vectors - 0.5 * (first / (1.0 - 0.9**STEP)) / (
        jnp.sqrt(second / (1.0 - 0.95**STEP)) + 1e-08
    )

    def ordered(parts):
        fc1, fc2, qkv, out = parts
        return flat(qkv), flat(out), flat(fc1), flat(fc2)

    news = [0.999 * w - move for w, move in zip(weights, moved)]
    return (
        output, gtok, *ordered(unpack(grad, weights)), gvec,
        *ordered(unpack(mom, weights)), *ordered(news), vec_new, first, second, norms,
    )


def body(
    tokens, cotangent, image_bucket, bucket_width, bucket_heads,
    w_qkv, w_out, w_fc1, w_fc2, vectors,
    mom_qkv, mom_out, mom_fc1, mom_fc2, vec_first, vec_second,
):
    half = lax.axis_index("mlp").astype(jnp.int32)
    ranks = lax.axis_size("dp")
    model = tokens.shape[1]
    rows = w_fc1.shape[1]
    weights = [flat(w) for w in (w_fc1, w_fc2, w_qkv, w_out)]
    moms = [flat(m) for m in (mom_fc1, mom_fc2, mom_qkv, mom_out)]
    images = image_bucket.shape[0] // 2
    if ranks != 16 or images != 4 * PAIR:
        return general(
            half, image_bucket, bucket_width, bucket_heads, tokens, cotangent,
            weights, moms, vectors, vec_first, vec_second,
        )
    bucket, heads = image_bucket.reshape(1, -1), bucket_heads.reshape(1, -1)
    resid, proj, low, mixed, wt, vec_rows, fc_weights = attend_pass(bucket, heads, tokens, weights, vectors, ranks)
    out_half, gres, fc_parts, gvec_rows = units_pass(
        half.reshape(1), image_bucket, bucket_width, resid, cotangent, mixed,
        fc_weights.reshape(2, model, FC), vec_rows,
    )
    gtok_both, pairs, fc_buf, at_buf, out_other = back_pass(
        bucket, heads, tokens, gres, proj, low, wt, vec_rows, gvec_rows,
        fc_parts.reshape(2, 4, 4, rows, EARLY), moms, out_half,
    )
    fc_buf, at_buf = fc_buf.reshape(2, model, EARLY), at_buf.reshape(2, model, LATE)
    (
        root, norms, gfc1, gfc2, gqkv, gwo, gvec, mfc1, mfc2, mqkv, mwo,
        vec_new, first, second, kept_fc, kept_at, half_fc, half_at, output, gtok,
    ) = run_chain(
        fc_buf, at_buf, pairs, vectors, vec_first, vec_second,
        weights, (out_half, out_other, gtok_both),
    )
    nfc1, nfc2, nqkv, nwo = apply_roots(root, kept_fc, kept_at, half_fc, half_at, weights)
    return (
        output, gtok,
        flat(gqkv), flat(gwo), flat(gfc1), flat(gfc2), gvec,
        flat(mqkv), flat(mwo), flat(mfc1), flat(mfc2),
        flat(nqkv), flat(nwo), flat(nfc1), flat(nfc2),
        vec_new, first, second, norms.reshape(5),
    )


def solution(mesh):
    halves, columns = P("mlp", "dp"), P(None, "dp")
    blocks = P(None, "mlp", "dp")
    matrices = (blocks, halves, halves, halves)
    placed = (P("dp", None), P("dp", None), P("dp"), P(), P()) + matrices + (columns,) + matrices + (columns, columns)
    outs = (P("dp", None), P("dp", None)) + matrices + (columns,) + matrices + matrices + (columns,) * 3 + (P(),)
    return jax.shard_map(body, mesh=mesh, in_specs=placed, out_specs=outs, check_vma=False)
```

```python
import functools
import math

import jax
import jax.numpy as jnp
from jax import lax
from jax.experimental import pallas as pl
from jax.experimental.pallas import tpu as pltpu
from jax.sharding import PartitionSpec as P

HD = 64
NS_ITERS = 5
STEP = 10
EPSILON = 1e-06
F32 = jnp.float32
BF16 = jnp.bfloat16
NN = (((1,), (0,)), ((), ()))
NT = (((1,), (1,)), ((), ()))
TN = (((0,), (0,)), ((), ()))

FC1, FC2, QKV, OUT, VEC, PACK = 0, 768, 1536, 2304, 2560, 2688
SLOT = 256
SEQ = 256
PAIR = 2
CHUNK = 256


def mm(a, b, dims):
    return lax.dot_general(a, b, dims, preferred_element_type=F32)


def lane_sum(v):
    return jnp.sum(v, axis=-1, keepdims=True)


def norm_rows(v):
    inv = 1.0 / v.shape[-1]
    center = v - lane_sum(v) * inv
    factor = lax.rsqrt(lane_sum(center * center) * inv + EPSILON)
    return center * factor, factor


def norm_back(g, n, factor):
    inv = 1.0 / g.shape[-1]
    return factor * (g - lane_sum(g) * inv - n * (lane_sum(g * n) * inv))


def image_kernel(
    half_ref, bucket_ref, widths_ref, counts_ref,
    tok_ref, cot_ref, w_ref,
    out_ref, gtok_ref, grad_ref,
    acc_ref, vec_ref, gvec_ref, q_ref, k_ref, v_ref, mixed_ref, probs_ref, low_ref,
    y_ref, gh_ref,
):
    step = pl.program_id(0)
    rows, model = tok_ref.shape
    heads_half = 3
    pack = rows // SEQ
    first = (half_ref[0] * pl.num_programs(0) + step) * pack
    buckets = [bucket_ref[first + image] for image in range(pack)]
    widths = [widths_ref[bucket] for bucket in buckets]
    counts = [counts_ref[bucket] for bucket in buckets]
    width, count = widths[0], counts[0]
    for image in range(1, pack):
        width, count = jnp.maximum(width, widths[image]), jnp.maximum(count, counts[image])
    row_ids = lax.broadcasted_iota(jnp.int32, (rows, 1), 0)
    row_width = jnp.full((rows, 1), widths[0], jnp.int32)
    for image in range(1, pack):
        row_width = jnp.where(row_ids >= image * SEQ, widths[image], row_width)

    @pl.when(step == 0)
    def _():
        acc_ref[...] = jnp.zeros_like(acc_ref)
        gvec_ref[...] = jnp.zeros_like(gvec_ref)
        turned = w_ref[0, :, VEC:PACK].astype(F32).T
        vec_ref[...] = turned[0:8]

    lane_head = lax.broadcasted_iota(jnp.int32, (1, SLOT), 1) // HD
    masks = [(lane_head == s).astype(F32).astype(BF16) for s in range(heads_half)]

    def used_heads(image):
        return (lane_head < counts[image] - heads_half).astype(F32)

    def spans():
        return [slice(image * SEQ, (image + 1) * SEQ) for image in range(pack)]

    x = tok_ref[...].astype(F32)
    normed_one, factor_one = norm_rows(x)
    hidden_one = (normed_one * vec_ref[0:1] + vec_ref[1:2]).astype(BF16)
    for half in range(2):
        for ref, which in ((q_ref, 0), (k_ref, 1), (v_ref, 2)):
            lanes = slice(QKV + which * SLOT, QKV + (which + 1) * SLOT)
            ref[half] = mm(hidden_one, w_ref[half, :, lanes], NN).astype(BF16)

        def attend():
            for image, span in enumerate(spans()):
                total = None
                for s in range(heads_half):
                    slot = (image * 2 + half) * heads_half + s
                    scores = mm(q_ref[half, span] * masks[s], k_ref[half, span], NT) * 0.125
                    top = jnp.max(scores, axis=-1, keepdims=True)
                    grown = jnp.exp(scores - top)
                    probs = grown * (1.0 / lane_sum(grown))
                    low = probs.astype(BF16)
                    probs_ref[slot] = probs
                    low_ref[slot] = low
                    term = mm(low, v_ref[half, span] * masks[s], NN)
                    total = term if total is None else total + term
                if half:
                    total = total * used_heads(image)
                mixed_ref[half, span] = total.astype(BF16)

        if half == 0:
            attend()
        else:
            mixed_ref[half] = jnp.zeros_like(mixed_ref[half])
            pl.when(count > heads_half)(attend)

    branch = mm(mixed_ref[0], w_ref[0, :, OUT:VEC], NT) + mm(mixed_ref[1], w_ref[1, :, OUT:VEC], NT)
    resid = x + branch + vec_ref[4:5]
    normed_two, factor_two = norm_rows(resid)
    hidden_two = (normed_two * vec_ref[2:3] + vec_ref[3:4]).astype(BF16)
    cot = cot_ref[...]
    hidden_two_t = hidden_two.T
    cot_t = cot.T
    y_ref[...] = resid + vec_ref[5:6]
    gh_ref[...] = jnp.zeros_like(gh_ref)
    per_half = FC2 // CHUNK
    for chunk in range(2 * per_half):
        half, part = divmod(chunk, per_half)
        one = slice(FC1 + part * CHUNK, FC1 + (part + 1) * CHUNK)
        two = slice(FC2 + part * CHUNK, FC2 + (part + 1) * CHUNK)

        def units_pass():
            pre = mm(hidden_two, w_ref[half, :, one], NN)
            units = chunk * CHUNK + lax.broadcasted_iota(jnp.int32, pre.shape, 1)
            cumulative = 0.5 + 0.5 * lax.erf(pre * 0.7071067811865476)
            density = jnp.exp(-0.5 * pre * pre) * 0.3989422804014327
            cumulative = jnp.where(units < row_width, cumulative, 0.0)
            density = jnp.where(units < row_width, density, 0.0)
            act = (pre * cumulative).astype(BF16)
            grad_act = mm(cot, w_ref[half, :, two], NN)
            grad_pre = (grad_act * (cumulative + pre * density)).astype(BF16)
            y_ref[...] += mm(act, w_ref[half, :, two], NT)
            gh_ref[...] += mm(grad_pre, w_ref[half, :, one], NT)
            acc_ref[half, :, two] += mm(cot_t, act, NN)
            acc_ref[half, :, one] += mm(hidden_two_t, grad_pre, NN)

        if chunk < 2:
            units_pass()
        else:
            pl.when(width > chunk * CHUNK)(units_pass)

    out_ref[...] = y_ref[...]
    grad_hidden_two = gh_ref[...]
    cot_f = cot.astype(F32)
    grad_resid = cot_f + norm_back(grad_hidden_two * vec_ref[2:3], normed_two, factor_two)
    resid_low = grad_resid.astype(BF16)
    resid_low_t = resid_low.T
    hidden_one_t = hidden_one.T
    for half in range(2):
        acc_ref[half, :, OUT:VEC] += mm(resid_low_t, mixed_ref[half], NN)

        def back():
            grad_heads = mm(resid_low, w_ref[half, :, OUT:VEC], NN).astype(BF16)
            parts = []
            for image, span in enumerate(spans()):
                heads = grad_heads[span]
                if half:
                    heads = heads * used_heads(image).astype(BF16)
                sums = [None, None, None]
                for s in range(heads_half):
                    slot = (image * 2 + half) * heads_half + s
                    own = heads * masks[s]
                    grad_probs = mm(own, v_ref[half, span], NT)
                    probs = probs_ref[slot]
                    weighed = probs * grad_probs
                    grad_scores = (weighed - probs * lane_sum(weighed)).astype(BF16)
                    terms = (
                        mm(grad_scores, k_ref[half, span] * masks[s], NN),
                        mm(grad_scores, q_ref[half, span] * masks[s], TN),
                        mm(low_ref[slot], own, TN),
                    )
                    sums = [t if o is None else o + t for o, t in zip(sums, terms)]
                parts.append([(v * c).astype(BF16) for v, c in zip(sums, (0.125, 0.125, 1.0))])
            total = None
            for which in range(3):
                lanes = slice(QKV + which * SLOT, QKV + (which + 1) * SLOT)
                grad_proj = jnp.concatenate([part[which] for part in parts], axis=0)
                acc_ref[half, :, lanes] += mm(hidden_one_t, grad_proj, NN)
                term = mm(grad_proj, w_ref[half, :, lanes], NT)
                total = term if total is None else total + term
            return total

        if half == 0:
            gh_ref[...] = back()
        else:

            @pl.when(count > heads_half)
            def _():
                gh_ref[...] += back()

    grad_hidden_one = gh_ref[...]
    gtok_ref[...] = grad_resid + norm_back(grad_hidden_one * vec_ref[0:1], normed_one, factor_one)
    sums = (
        grad_hidden_one * normed_one,
        grad_hidden_one,
        grad_hidden_two * normed_two,
        grad_hidden_two,
        grad_resid,
        cot_f,
    )
    for row, values in enumerate(sums):
        gvec_ref[row : row + 1] += jnp.sum(values, axis=0, keepdims=True)

    @pl.when(step == pl.num_programs(0) - 1)
    def _():
        grad_ref[0, :, 0:VEC] = acc_ref[0].astype(BF16)
        grad_ref[1, :, 0:VEC] = acc_ref[1].astype(BF16)
        columns = gvec_ref[...].T.astype(BF16)
        grad_ref[0, :, VEC:PACK] = columns
        grad_ref[1, :, VEC:PACK] = columns


def image_pass(half, bucket, widths, counts, tokens, cotangent, packed):
    images = bucket.shape[0] // 2
    model = tokens.shape[1]
    rows = images * SEQ
    images = images // PAIR
    seq = PAIR * SEQ
    picked = pl.BlockSpec((seq, model), lambda i, h, b, w, c: (h[0] * images + i, 0))
    placed = pl.BlockSpec((seq, model), lambda i, h, b, w, c: (i, 0))
    whole = pl.BlockSpec(
        (2, model, PACK), lambda i, h, b, w, c: (0, 0, 0), pipeline_mode=pl.Buffered(1)
    )
    heads = 6
    flops = 2 * rows * model * (3 * 4 * model + 3 * 8 * model)
    return pl.pallas_call(
        image_kernel,
        out_shape=(
            jax.ShapeDtypeStruct((rows, model), F32),
            jax.ShapeDtypeStruct((rows, model), F32),
            jax.ShapeDtypeStruct((2, model, PACK), BF16),
        ),
        grid_spec=pltpu.PrefetchScalarGridSpec(
            num_scalar_prefetch=4,
            grid=(images,),
            in_specs=[picked, picked, whole],
            out_specs=[placed, placed, whole],
            scratch_shapes=[
                pltpu.VMEM((2, model, VEC), F32),
                pltpu.VMEM((8, model), F32),
                pltpu.VMEM((128, model), F32),
                pltpu.VMEM((2, seq, SLOT), BF16),
                pltpu.VMEM((2, seq, SLOT), BF16),
                pltpu.VMEM((2, seq, SLOT), BF16),
                pltpu.VMEM((2, seq, SLOT), BF16),
                pltpu.VMEM((PAIR * heads, SEQ, SEQ), F32),
                pltpu.VMEM((PAIR * heads, SEQ, SEQ), BF16),
                pltpu.VMEM((seq, model), F32),
                pltpu.VMEM((seq, model), F32),
            ],
        ),
        compiler_params=pltpu.CompilerParams(vmem_limit_bytes=56 * 1024 * 1024),
        cost_estimate=pl.CostEstimate(flops=flops, bytes_accessed=20 * rows * model, transcendentals=rows * 6144),
        name="image_pass",
    )(half, bucket, widths, counts, tokens, cotangent, packed)


MESH = pl.DeviceIdType.MESH
AT_OUT, AT_VEC, AT = 768, 1024, 1152
HEADS = 192
AT_SENT = 896
FC = 1536
EARLY = FC + SLOT
TAIL, LATE = 3 * HEADS, 640


class Place:
    def __init__(self):
        dp = lax.axis_index("dp")
        self.half = lax.axis_index("mlp")
        self.z = dp // 4
        self.y = (dp // 2) % 2
        self.x = dp % 2
        self.dp = dp
        self.y_peer = (self.index(self.z, 1 - self.y, self.x), self.half)
        self.x_peer = (self.index(self.z, self.y, 1 - self.x), self.half)
        self.sibling = (self.dp, 1 - self.half)

    def index(self, z, y, x):
        return z * 4 + y * 2 + x

    def at_z(self, z):
        return (self.index(z, self.y, self.x), self.half)


def meet(place):
    barrier = pltpu.get_barrier_semaphore()
    peers = [place.at_z((place.z + j) % 4) for j in range(1, 4)]
    peers += [place.y_peer, place.x_peer, place.sibling]
    for peer in peers:
        pl.semaphore_signal(barrier, inc=1, device_id=peer, device_id_type=MESH)
    pl.semaphore_wait(barrier, len(peers))


class Mail:
    def __init__(self, place, send_sem, recv_sem):
        self.place, self.send_sem, self.recv_sem = place, send_sem, recv_sem

    def copy(self, slot, src, dst, peer):
        return pltpu.make_async_remote_copy(
            src_ref=src,
            dst_ref=dst,
            send_sem=self.send_sem.at[slot],
            recv_sem=self.recv_sem.at[slot],
            device_id=peer,
            device_id_type=MESH,
        )

    def start(self, slot, src, dst, peer):
        self.copy(slot, src, dst, peer).start()

    def arrived(self, slot, like):
        self.copy(slot, like, like, self.place.sibling).wait_recv()

    def left(self, slot, like):
        self.copy(slot, like, like, self.place.sibling).wait_send()


GATHER_SLOTS = 35
NEAR_FIRST = (1, 3, 2)


class Gather:
    def __init__(self, place, own, buf, cut, send_sem, recv_sem):
        self.place, self.own, self.buf = place, own, buf
        self.mail = Mail(place, send_sem, recv_sem)
        self.pieces = (pl.ds(0, cut), pl.ds(cut, own.shape[1] - cut))

    def shard(self, k, y, x):
        return self.place.index((self.place.z + 4 - k) % 4, y, x)

    def forward(self, slot, dp, peer, piece=None):
        ref = self.buf.at[self.place.half, dp]
        if piece is not None:
            ref = ref.at[:, self.pieces[piece]]
        self.mail.start(slot, ref, ref, peer)

    def like(self, piece=None):
        ref = self.buf.at[0, 0]
        return ref if piece is None else ref.at[:, self.pieces[piece]]

    def start_column(self):
        place = self.place
        home = self.buf.at[place.half, place.dp]
        for j in NEAR_FIRST:
            self.mail.start(j - 1, self.own, home, place.at_z((place.z + j) % 4))

    def start_plane(self):
        place = self.place
        home = self.buf.at[place.half, place.dp]
        self.mail.start(3, self.own, home, place.y_peer)
        self.mail.start(7, self.own, home, place.x_peer)
        self.mail.start(19, self.own, home, place.sibling)

    def column(self, k):
        place = self.place
        self.mail.arrived(k - 1, self.like())
        dp = self.shard(k, place.y, place.x)
        self.forward(3 + k, dp, place.y_peer)
        self.forward(7 + k, dp, place.x_peer)
        self.forward(19 + k, dp, place.sibling)

    def plane(self, k):
        place = self.place
        self.mail.arrived(3 + k, self.like())
        dp = self.shard(k, 1 - place.y, place.x)
        self.forward(11 + k, dp, place.x_peer, 0)
        self.forward(23 + k, dp, place.sibling)
        self.mail.arrived(7 + k, self.like())
        dp = self.shard(k, place.y, 1 - place.x)
        self.forward(15 + k, dp, place.y_peer, 1)
        self.forward(27 + k, dp, place.sibling)

    def corner(self, k):
        place = self.place
        self.mail.arrived(11 + k, self.like(0))
        self.mail.arrived(15 + k, self.like(1))
        self.forward(31 + k, self.shard(k, 1 - place.y, 1 - place.x), place.sibling)

    def finish(self):
        self.receive()
        self.drain()

    def receive(self):
        for k in range(16):
            self.mail.arrived(19 + k, self.like())

    def drain(self):
        for slot in range(GATHER_SLOTS):
            piece = 0 if 11 <= slot < 15 else 1 if 15 <= slot < 19 else None
            self.mail.left(slot, self.like(piece))

    def columns(self):
        for k in NEAR_FIRST:
            self.column(k)

    def planes(self):
        for k in NEAR_FIRST:
            self.plane(k)

    def corners(self):
        for k in (0, *NEAR_FIRST):
            self.corner(k)


SCATTER_SLOTS = 43
Z_ORDER = (2, 1, 3, 0)


class Scatter:
    def __init__(self, place, parts, hold, firsts, seconds, last, cut, send_sem, recv_sem):
        self.place, self.parts, self.hold = place, parts, hold
        self.firsts, self.seconds, self.last = firsts, seconds, last
        self.mail = Mail(place, send_sem, recv_sem)
        self.pieces = (pl.ds(0, cut), pl.ds(cut, hold.shape[2] - cut))

    def shard(self, c, k):
        y, x = self.place.y, self.place.x
        column = ((1 - y, 1 - x), (y, 1 - x), (1 - y, x), (y, x))[c]
        return self.place.index((self.place.z + Z_ORDER[k]) % 4, *column)

    def piece(self, dp, p):
        return self.hold.at[dp, :, self.pieces[p]]

    def load(self, dp, p):
        return self.hold[dp, :, self.pieces[p]].astype(F32)

    def start(self):
        half = self.place.half
        for c in range(4):
            for k in range(4):
                dp = self.shard(c, k)
                self.mail.start(4 * c + k, self.parts.at[1 - half, dp], self.hold.at[dp], self.place.sibling)

    def settle(self, c, k):
        dp = self.shard(c, k)
        self.mail.arrived(4 * c + k, self.hold.at[0])
        total = self.hold[dp].astype(F32) + self.parts[self.place.half, dp].astype(F32)
        self.hold[dp] = total.astype(BF16)
        return dp

    def first_hop(self):
        place, (first_a, first_b) = self.place, self.firsts
        for k in range(4):
            dp = self.settle(0, k)
            self.mail.start(16 + k, self.piece(dp, 0), first_a.at[k], place.x_peer)
            self.mail.start(24 + k, self.piece(dp, 1), first_b.at[k], place.y_peer)
        for k in range(4):
            dp = self.settle(1, k)
            self.mail.start(20 + k, self.piece(dp, 0), first_a.at[4 + k], place.x_peer)
            dp = self.settle(2, k)
            self.mail.start(28 + k, self.piece(dp, 1), first_b.at[4 + k], place.y_peer)
        for k in range(4):
            self.settle(3, k)

    def second_hop(self):
        place, firsts, seconds = self.place, self.firsts, self.seconds
        for k in range(4):
            for p, slot, column, out, peer in ((0, 16, 2, 32, place.y_peer), (1, 24, 1, 36, place.x_peer)):
                self.mail.arrived(slot + k, firsts[p].at[0])
                dp = self.shard(column, k)
                total = self.load(dp, p) + firsts[p][k].astype(F32)
                self.hold[dp, :, self.pieces[p]] = total.astype(BF16)
                self.mail.start(out + k, self.piece(dp, p), seconds[p].at[k], peer)

    def last_hop(self, keep):
        place = self.place
        for k in range(4):
            dp = self.shard(3, k)
            totals = []
            for p, slot, second in ((0, 20, 32), (1, 28, 36)):
                self.mail.arrived(slot + k, self.firsts[p].at[0])
                self.mail.arrived(second + k, self.seconds[p].at[0])
                totals.append(self.load(dp, p) + self.firsts[p][4 + k].astype(F32) + self.seconds[p][k].astype(F32))
            for p in range(2):
                if Z_ORDER[k]:
                    self.hold[dp, :, self.pieces[p]] = totals[p].astype(BF16)
                else:
                    keep[:, self.pieces[p]] = totals[p]
            if Z_ORDER[k]:
                j = Z_ORDER[k]
                self.mail.start(40 + j - 1, self.hold.at[dp], self.last.at[j - 1], place.at_z((place.z + j) % 4))

    def finish(self, keep):
        for j in range(3):
            self.mail.arrived(40 + j, self.last.at[0])
            keep[...] = keep[...] + self.last[j].astype(F32)
        for slot in range(SCATTER_SLOTS):
            if slot < 16 or slot >= 40:
                like = self.hold.at[0]
            elif slot < 32:
                like = self.firsts[(slot - 16) // 8].at[0]
            else:
                like = self.seconds[(slot - 32) // 4].at[0]
            self.mail.left(slot, like)


CHAIN_LANES = (
    (pl.ds(0, FC // 2), pl.ds(FC // 2, FC // 2)),
    (pl.ds(FC, SLOT), pl.ds(FC, SLOT)),
)


class WideGather:
    SLOTS = 8

    def __init__(self, place, own, buf, cut, send_sem, recv_sem):
        self.place, self.own, self.buf = place, own, buf
        self.mail = Mail(place, send_sem, recv_sem)
        self.pieces = (pl.ds(0, cut), pl.ds(cut, own.shape[1] - cut))

    def column(self, y, x, piece=None):
        ref = self.buf.at[self.place.half, :, 2 * y + x]
        return ref if piece is None else ref.at[:, :, self.pieces[piece]]

    def send(self, slot, ref, peer):
        self.mail.start(slot, ref, ref, peer)

    def start(self):
        place = self.place
        home = self.buf.at[place.half, place.z, 2 * place.y + place.x]
        for j in NEAR_FIRST:
            self.mail.start(j - 1, self.own, home, place.at_z((place.z + j) % 4))

    def spread(self):
        place = self.place
        for j in range(3):
            self.mail.arrived(j, self.own)
        self.send(3, self.column(place.y, place.x), place.y_peer)
        self.send(4, self.column(place.y, place.x), place.x_peer)

    def corners(self):
        place = self.place
        self.mail.arrived(3, self.column(place.y, place.x))
        self.send(5, self.column(1 - place.y, place.x, 0), place.x_peer)
        self.mail.arrived(4, self.column(place.y, place.x))
        self.send(6, self.column(place.y, 1 - place.x, 1), place.y_peer)

    def share(self):
        place = self.place
        self.mail.arrived(5, self.column(place.y, place.x, 0))
        self.mail.arrived(6, self.column(place.y, place.x, 1))
        self.each_case(self.share_case)

    def each_case(self, action):
        place = self.place
        for x in range(2):
            for half in range(2):
                here = jnp.logical_and(place.x == x, place.half == half)
                pl.when(here)(functools.partial(action, half, CHAIN_LANES[x][half], CHAIN_LANES[x][1 - half]))

    def share_case(self, half, mine, theirs):
        self.send(7, self.buf.at[half, :, :, :, theirs], self.place.sibling)

    def finish_case(self, half, mine, theirs):
        self.mail.arrived(7, self.buf.at[half, :, :, :, mine])
        self.mail.left(7, self.buf.at[half, :, :, :, theirs])

    def finish(self):
        place = self.place
        column = self.column(place.y, place.x)
        self.each_case(self.finish_case)
        likes = [self.own] * 3 + [column] * 2
        likes += [self.column(place.y, place.x, 0), self.column(place.y, place.x, 1)]
        for slot, like in enumerate(likes):
            self.mail.left(slot, like)


class WideScatter:
    SLOTS = 10

    def __init__(self, place, parts, hold, firsts, seconds, last, cut, send_sem, recv_sem):
        self.place, self.parts, self.hold = place, parts, hold
        self.firsts, self.seconds, self.last = firsts, seconds, last
        self.mail = Mail(place, send_sem, recv_sem)
        self.pieces = (pl.ds(0, cut), pl.ds(cut, hold.shape[3] - cut))

    def column(self, y, x, piece):
        return self.hold.at[:, 2 * y + x, :, self.pieces[piece]]

    def start(self):
        self.mail.start(0, self.parts.at[1 - self.place.half], self.hold, self.place.sibling)

    def first_hop(self):
        place = self.place
        y, x = place.y, place.x
        self.mail.arrived(0, self.hold)

        def add(z, carry):
            total = self.hold[z].astype(F32) + self.parts[place.half, z].astype(F32)
            self.hold[z] = total.astype(BF16)
            return carry

        lax.fori_loop(0, self.hold.shape[0], add, 0)
        first_a, first_b = self.firsts
        self.mail.start(1, self.column(1 - y, 1 - x, 0), first_a.at[0], place.x_peer)
        self.mail.start(2, self.column(1 - y, 1 - x, 1), first_b.at[0], place.y_peer)
        self.mail.start(3, self.column(y, 1 - x, 0), first_a.at[1], place.x_peer)
        self.mail.start(4, self.column(1 - y, x, 1), first_b.at[1], place.y_peer)

    def second_hop(self):
        place = self.place
        y, x = place.y, place.x
        moves = ((0, (1 - y, x), place.y_peer), (1, (y, 1 - x), place.x_peer))
        for p, (cy, cx), peer in moves:
            self.mail.arrived(1 + p, self.firsts[p].at[0])
            lanes = self.pieces[p]
            total = self.hold[:, 2 * cy + cx, :, lanes].astype(F32) + self.firsts[p][0].astype(F32)
            self.hold[:, 2 * cy + cx, :, lanes] = total.astype(BF16)
            self.mail.start(5 + p, self.column(cy, cx, p), self.seconds[p], peer)

    def last_hop(self, keep):
        place = self.place
        home = 2 * place.y + place.x
        for p in range(2):
            self.mail.arrived(3 + p, self.firsts[p].at[1])
            self.mail.arrived(5 + p, self.seconds[p])
            lanes = self.pieces[p]
            total = self.hold[:, home, :, lanes].astype(F32) + self.firsts[p][1].astype(F32)
            self.hold[:, home, :, lanes] = (total + self.seconds[p][...].astype(F32)).astype(BF16)
        for j in NEAR_FIRST:
            z = (place.z + j) % 4
            self.mail.start(6 + j, self.hold.at[z, home], self.last.at[j - 1], place.at_z(z))
        keep[...] = self.hold[place.z, home].astype(F32)

    def finish(self, keep):
        place = self.place
        for j in range(3):
            self.mail.arrived(7 + j, self.last.at[0])
            keep[...] = keep[...] + self.last[j].astype(F32)
        likes = [self.hold] + [self.firsts[p].at[0] for p in (0, 1, 0, 1)]
        likes += [self.seconds[0], self.seconds[1]] + [self.last.at[0]] * 3
        for slot, like in enumerate(likes):
            self.mail.left(slot, like)


def wide_scratch(rows, lanes, cut):
    return [
        pltpu.VMEM((4, 4, rows, lanes), BF16),
        pltpu.VMEM((2, 4, rows, cut), BF16),
        pltpu.VMEM((2, 4, rows, lanes - cut), BF16),
        pltpu.VMEM((4, rows, cut), BF16),
        pltpu.VMEM((4, rows, lanes - cut), BF16),
        pltpu.VMEM((3, rows, lanes), BF16),
    ]


def scatter_scratch(ranks, rows, lanes, cut):
    return [
        pltpu.VMEM((ranks, rows, lanes), BF16),
        pltpu.VMEM((8, rows, cut), BF16),
        pltpu.VMEM((8, rows, lanes - cut), BF16),
        pltpu.VMEM((4, rows, cut), BF16),
        pltpu.VMEM((4, rows, lanes - cut), BF16),
        pltpu.VMEM((3, rows, lanes), BF16),
    ]


def dma(count):
    return [pltpu.SemaphoreType.DMA((count,))] * 2


SENT_CUT, FC_CUT, EARLY_CUT, LATE_CUT = 512, 768, 896, 384


def head_masks():
    lane_head = lax.broadcasted_iota(jnp.int32, (1, SLOT), 1) // HD
    return [(lane_head == s).astype(F32).astype(BF16) for s in range(3)]


def used_lanes(bucket_ref, heads_ref, image, half):
    bucket = bucket_ref[...]
    counts = jnp.zeros(bucket.shape, jnp.int32)
    for entry in range(heads_ref.shape[1]):
        counts = jnp.where(bucket == entry, heads_ref[:, entry : entry + 1], counts)
    chosen = lax.broadcasted_iota(jnp.int32, bucket.shape, 1) == image
    count = jnp.sum(jnp.where(chosen, counts.astype(F32), 0.0), axis=1, keepdims=True)
    lane_head = lax.broadcasted_iota(jnp.int32, (1, SLOT), 1) // HD
    return jnp.where(lane_head.astype(F32) < count - 3.0 * half, 1.0, 0.0)


def widen(packed, pieces):
    blank = jnp.zeros((packed.shape[0], SLOT - HEADS), packed.dtype)
    parts = []
    for piece in range(pieces):
        parts += [packed[:, piece * HEADS : (piece + 1) * HEADS], blank]
    return jnp.concatenate(parts, axis=1)


def token_copy(place, tokens_ref, tok_own, sem):
    count = tok_own.shape[0]
    start = pl.multiple_of(place.half * count, count)
    return pltpu.make_async_copy(tokens_ref.at[pl.ds(start, count)], tok_own, sem)


def own_block(step, rows):
    return pl.ds(pl.multiple_of(step * rows, rows), rows)


def attend_kernel(
    bucket_ref, heads_ref, tokens_ref, fc1_ref, fc2_ref, qkv_ref, wo_ref, vecs_ref,
    resid_ref, proj_ref, low_ref, mixed_ref, wt_ref, vec_ref, fc_buf,
    own_at, own_fc, at_buf, tok_own, turn_ref, at_send, at_recv, fc_send, fc_recv, local_sem, tok_sem,
):
    place = Place()
    step = pl.program_id(0)
    steps = pl.num_programs(0)
    rows, model = resid_ref.shape
    pack = rows // SEQ
    tok_copy = token_copy(place, tokens_ref, tok_own, tok_sem)
    slices = Gather(place, own_at, at_buf, SENT_CUT, at_send, at_recv)
    units = Gather(place, own_fc, fc_buf, FC_CUT, fc_send, fc_recv)
    local = pltpu.make_async_copy(own_fc, fc_buf.at[place.half, place.dp], local_sem)

    @pl.when(step == 0)
    def _():
        tok_copy.start()
        own_at[...] = jnp.zeros_like(own_at)
        for which in range(3):
            own_at[:, which * HEADS : (which + 1) * HEADS] = qkv_ref[which].astype(BF16)
        own_at[:, 3 * HEADS : 4 * HEADS] = wo_ref[...].astype(BF16)
        turn_ref[...] = jnp.zeros_like(turn_ref)
        turn_ref[0 : vecs_ref.shape[0], 0 : vecs_ref.shape[1]] = vecs_ref[...]
        own_at[:, AT_SENT - 128 : AT_SENT] = turn_ref[...].T[0 : own_at.shape[0]].astype(BF16)
        own_fc[:, 0 : FC // 2] = fc1_ref[...].astype(BF16)
        own_fc[:, FC // 2 : FC] = fc2_ref[...].astype(BF16)
        at_buf[place.half, place.dp] = own_at[...]
        local.start()
        meet(place)
        slices.start_column()
        slices.start_plane()
        slices.plane(0)
        slices.columns()
        units.start_column()
        slices.planes()
        units.start_plane()
        slices.corners()
        slices.receive()
        for half in range(2):
            sent = at_buf[half].astype(F32).reshape(model, AT_SENT)
            wt_ref[half, :, 0:AT_VEC] = widen(sent, 4).astype(BF16)
            wt_ref[half, :, AT_VEC:AT] = sent[:, AT_SENT - 128 : AT_SENT].astype(BF16)
        vec_ref[...] = wt_ref[0, :, AT_VEC:AT].astype(F32).T[0:8]
        tok_copy.wait()

    @pl.when(step == 2)
    def _():
        units.planes()

    @pl.when(step == steps - 1)
    def _():
        units.corners()

    masks = head_masks()
    first_image = place.half * (bucket_ref.shape[1] // 2)
    x = tok_own[own_block(step, rows)].astype(F32)
    normed_one, _ = norm_rows(x)
    hidden_one = (normed_one * vec_ref[0:1] + vec_ref[1:2]).astype(BF16)
    branch = None
    for half in range(2):
        base = half * 3 * SLOT
        proj = []
        for which in range(3):
            part = mm(hidden_one, wt_ref[half, :, which * SLOT : (which + 1) * SLOT], NN).astype(BF16)
            proj_ref[:, base + which * SLOT : base + (which + 1) * SLOT] = part
            proj.append(part)
        mixes = []
        for image in range(pack):
            span = slice(image * SEQ, (image + 1) * SEQ)
            queries, keys, values = (part[span] for part in proj)
            total = None
            for s in range(3):
                scores = mm(queries * masks[s], keys, NT) * 0.125
                top = jnp.max(scores, axis=-1, keepdims=True)
                grown = jnp.exp(scores - top)
                low = (grown * (1.0 / lane_sum(grown))).astype(BF16)
                low_ref[(image * 2 + half) * 3 + s] = low
                term = mm(low, values * masks[s], NN)
                total = term if total is None else total + term
            mixes.append((total * used_lanes(bucket_ref, heads_ref, first_image + step * pack + image, half)).astype(BF16))
        mixed = jnp.concatenate(mixes, axis=0)
        mixed_ref[:, half * SLOT : (half + 1) * SLOT] = mixed
        term = mm(mixed, wt_ref[half, :, AT_OUT:AT_VEC], NT)
        branch = term if branch is None else branch + term
        if half == 0:

            @pl.when(step == 0)
            def _():
                units.columns()
                units.plane(0)

    resid_ref[...] = x + branch + vec_ref[4:5]

    @pl.when(step == steps - 1)
    def _():
        units.finish()
        slices.drain()
        local.wait()


def const(shape, **kw):
    return pl.BlockSpec(shape, lambda i, *_: (0,) * len(shape), **kw)


def once(shape):
    return const(shape, pipeline_mode=pl.Buffered(1))


def attend_pass(bucket, heads, tokens, weights, vectors, ranks):
    model = tokens.shape[1]
    images = bucket.shape[1] // 2
    rows = weights[0].shape[0]
    count = images * SEQ
    steps = images // PAIR
    block = PAIR * SEQ

    def by_step(lanes):
        return pl.BlockSpec((block, lanes), lambda i: (i, 0))

    return pl.pallas_call(
        attend_kernel,
        out_shape=(
            jax.ShapeDtypeStruct((count, model), F32),
            jax.ShapeDtypeStruct((count, 6 * SLOT), BF16),
            jax.ShapeDtypeStruct((images * 6, SEQ, SEQ), BF16),
            jax.ShapeDtypeStruct((count, 2 * SLOT), BF16),
            jax.ShapeDtypeStruct((2, model, AT), BF16),
            jax.ShapeDtypeStruct((8, model), F32),
            jax.ShapeDtypeStruct((2, ranks, rows, FC), BF16),
        ),
        grid_spec=pltpu.PrefetchScalarGridSpec(
            num_scalar_prefetch=0,
            grid=(steps,),
            in_specs=[once(bucket.shape), once(heads.shape), pl.BlockSpec(memory_space=pl.ANY)]
            + [once(w.shape) for w in weights]
            + [once(vectors.shape)],
            out_specs=[
                by_step(model),
                by_step(6 * SLOT),
                pl.BlockSpec((PAIR * 6, SEQ, SEQ), lambda i: (i, 0, 0)),
                by_step(2 * SLOT),
                once((2, model, AT)),
                once((8, model)),
                pl.BlockSpec(memory_space=pl.ANY),
            ],
            scratch_shapes=[
                pltpu.VMEM((rows, AT_SENT), BF16),
                pltpu.VMEM((rows, FC), BF16),
                pltpu.VMEM((2, ranks, rows, AT_SENT), BF16),
                pltpu.VMEM((count, model), BF16),
                pltpu.VMEM((128, 128), F32),
            ]
            + dma(GATHER_SLOTS)
            + dma(GATHER_SLOTS)
            + [pltpu.SemaphoreType.DMA] * 2,
        ),
        compiler_params=pltpu.CompilerParams(
            collective_id=0, has_side_effects=True, vmem_limit_bytes=56 * 1024 * 1024
        ),
        name="attend_pass",
    )(bucket, heads, tokens, *weights, vectors)


def units_kernel(
    half_ref, bucket_ref, widths_ref, resid_ref, cot_ref, mixed_ref, w_ref, vec_ref,
    out_ref, gres_ref, grad_ref, gvec_ref, acc_ref, y_ref, gh_ref,
):
    step = pl.program_id(0)
    rows, model = resid_ref.shape
    pack = rows // SEQ
    first = (half_ref[0] * pl.num_programs(0) + step) * pack
    widths = [widths_ref[bucket_ref[first + image]] for image in range(pack)]
    row_ids = lax.broadcasted_iota(jnp.int32, (rows, 1), 0)
    width, row_width = widths[0], jnp.full((rows, 1), widths[0], jnp.int32)
    for image in range(1, pack):
        width = jnp.maximum(width, widths[image])
        row_width = jnp.where(row_ids >= image * SEQ, widths[image], row_width)

    @pl.when(step == 0)
    def _():
        acc_ref[...] = jnp.zeros_like(acc_ref)
        gvec_ref[...] = jnp.zeros_like(gvec_ref)

    resid = resid_ref[...]
    normed_two, factor_two = norm_rows(resid)
    hidden_two = (normed_two * vec_ref[2:3] + vec_ref[3:4]).astype(BF16)
    cot = cot_ref[...]
    hidden_two_t = hidden_two.T
    cot_t = cot.T
    y_ref[...] = resid + vec_ref[5:6]
    gh_ref[...] = jnp.zeros_like(gh_ref)
    per_half = FC2 // CHUNK
    for chunk in range(2 * per_half):
        half, part = divmod(chunk, per_half)
        one = slice(FC1 + part * CHUNK, FC1 + (part + 1) * CHUNK)
        two = slice(FC2 + part * CHUNK, FC2 + (part + 1) * CHUNK)

        def units_pass():
            pre = mm(hidden_two, w_ref[half, :, one], NN)
            units = chunk * CHUNK + lax.broadcasted_iota(jnp.int32, pre.shape, 1)
            cumulative = 0.5 + 0.5 * lax.erf(pre * 0.7071067811865476)
            density = jnp.exp(-0.5 * pre * pre) * 0.3989422804014327
            cumulative = jnp.where(units < row_width, cumulative, 0.0)
            density = jnp.where(units < row_width, density, 0.0)
            act = (pre * cumulative).astype(BF16)
            grad_act = mm(cot, w_ref[half, :, two], NN)
            grad_pre = (grad_act * (cumulative + pre * density)).astype(BF16)
            y_ref[...] += mm(act, w_ref[half, :, two], NT)
            gh_ref[...] += mm(grad_pre, w_ref[half, :, one], NT)
            acc_ref[half, :, two] += mm(cot_t, act, NN)
            acc_ref[half, :, one] += mm(hidden_two_t, grad_pre, NN)

        if chunk < 2:
            units_pass()
        else:
            pl.when(width > chunk * CHUNK)(units_pass)

    out_ref[...] = y_ref[...]
    grad_hidden_two = gh_ref[...]
    cot_f = cot.astype(F32)
    grad_resid = cot_f + norm_back(grad_hidden_two * vec_ref[2:3], normed_two, factor_two)
    gres_ref[...] = grad_resid
    resid_low_t = grad_resid.astype(BF16).T
    for half in range(2):
        acc_ref[half, :, FC:EARLY] += mm(resid_low_t, mixed_ref[:, half * SLOT : (half + 1) * SLOT], NN)
    sums = (grad_hidden_two * normed_two, grad_hidden_two, grad_resid, cot_f)
    for row, values in enumerate(sums):
        gvec_ref[2 + row : 3 + row] += jnp.sum(values, axis=0, keepdims=True)

    @pl.when(step == pl.num_programs(0) - 1)
    def _():
        grad_ref[...] = acc_ref[...].astype(BF16)


def units_pass(half, bucket, widths, resid, cotangent, mixed, packed, vec):
    count, model = resid.shape
    block = PAIR * SEQ
    steps = count // block
    placed = pl.BlockSpec((block, model), lambda i, h, b, w: (i, 0))
    picked = pl.BlockSpec((block, model), lambda i, h, b, w: (h[0] * steps + i, 0))
    blended = pl.BlockSpec((block, 2 * SLOT), lambda i, h, b, w: (i, 0))
    return pl.pallas_call(
        units_kernel,
        out_shape=(
            jax.ShapeDtypeStruct((count, model), F32),
            jax.ShapeDtypeStruct((count, model), F32),
            jax.ShapeDtypeStruct((2, model, EARLY), BF16),
            jax.ShapeDtypeStruct((8, model), F32),
        ),
        grid_spec=pltpu.PrefetchScalarGridSpec(
            num_scalar_prefetch=3,
            grid=(steps,),
            in_specs=[placed, picked, blended, once(packed.shape), once(vec.shape)],
            out_specs=[placed, placed, once((2, model, EARLY)), once((8, model))],
            scratch_shapes=[
                pltpu.VMEM((2, model, EARLY), F32),
                pltpu.VMEM((block, model), F32),
                pltpu.VMEM((block, model), F32),
            ],
        ),
        compiler_params=pltpu.CompilerParams(vmem_limit_bytes=56 * 1024 * 1024),
        name="units_pass",
    )(half, bucket, widths, resid, cotangent, mixed, packed, vec)


def back_kernel(
    bucket_ref, heads_ref, tokens_ref, gres_ref, proj_ref, low_ref, wt_ref, vec_ref, gvec_ref,
    fc_parts, fc1_ref, fc2_ref, qkv_ref, wo_ref, out_half,
    gtok_ref, pairs_ref, fc_buf, at_buf, out_other,
    acc_ref, sums_ref, gtok_own, at_parts, own_fc, own_at, tok_own,
    fc_hold, fc_first_a, fc_first_b, fc_second_a, fc_second_b, fc_last,
    at_hold, at_first_a, at_first_b, at_second_a, at_second_b, at_last,
    fcs_send, fcs_recv, ats_send, ats_recv, fcg_send, fcg_recv, atg_send, atg_recv,
    side_send, side_recv, local_sems,
):
    place = Place()
    step = pl.program_id(0)
    steps = pl.num_programs(0)
    rows, model = gres_ref.shape
    tok_copy = token_copy(place, tokens_ref, tok_own, local_sems.at[0])
    pack = rows // SEQ
    count = gtok_ref.shape[0] // 2
    early, late = pl.ds(0, EARLY), pl.ds(EARLY, LATE)
    grad_fc, mom_fc = pairs_ref.at[0, :, early], pairs_ref.at[1, :, early]
    grad_at, mom_at = pairs_ref.at[0, :, late], pairs_ref.at[1, :, late]
    fc_sum = WideScatter(
        place, fc_parts, fc_hold, (fc_first_a, fc_first_b), (fc_second_a, fc_second_b), fc_last,
        EARLY_CUT, fcs_send, fcs_recv,
    )
    at_sum = Scatter(
        place, at_parts, at_hold, (at_first_a, at_first_b), (at_second_a, at_second_b), at_last,
        LATE_CUT, ats_send, ats_recv,
    )
    fc_all = WideGather(place, own_fc, fc_buf, EARLY_CUT, fcg_send, fcg_recv)
    at_all = Gather(place, own_at, at_buf, LATE_CUT, atg_send, atg_recv)
    side = Mail(place, side_send, side_recv)
    fc_home = pltpu.make_async_copy(
        own_fc, fc_buf.at[place.half, place.z, 2 * place.y + place.x], local_sems.at[1]
    )
    at_home = pltpu.make_async_copy(own_at, at_buf.at[place.half, place.dp], local_sems.at[2])

    @pl.when(step == 0)
    def _():
        tok_copy.start()
        meet(place)
        fc_sum.start()
        tok_copy.wait()
        acc_ref[...] = jnp.zeros_like(acc_ref)
        sums_ref[...] = jnp.zeros_like(sums_ref)
        sums_ref[0:8] = gvec_ref[...]

    def settle_units():
        fc_sum.finish(grad_fc)
        mom_fc[:, 0 : FC // 2] = 0.95 * fc1_ref[...]
        mom_fc[:, FC // 2 : FC] = 0.95 * fc2_ref[...]
        mom_fc[:, FC:EARLY] = jnp.zeros((mom_fc.shape[0], SLOT), F32)
        mom_fc[:, FC : FC + HEADS] = 0.95 * wo_ref[...]
        mom_fc[...] = mom_fc[...] + grad_fc[...]
        own_fc[...] = mom_fc[...].astype(BF16)
        fc_home.start()
        fc_all.start()
        side.start(0, out_half, out_other, place.sibling)

    def spread_units():
        fc_home.wait()
        fc_all.spread()

    def part_units():
        fc_all.corners()

    stages = {
        1: fc_sum.first_hop,
        6: fc_sum.second_hop,
        10: lambda: fc_sum.last_hop(grad_fc),
        15: settle_units,
    }

    def slot(quarter):
        for number, stage in stages.items():
            if number % 4 == quarter:
                pl.when(step == number // 4)(stage)

    def own_rows(index):
        start = place.half * count + index * rows
        return gtok_ref.at[pl.ds(pl.multiple_of(start, rows), rows)]

    def send_block(index):
        side.start(1 + index, gtok_own.at[index], own_rows(index), place.sibling)
        pltpu.make_async_copy(gtok_own.at[index], own_rows(index), local_sems.at[3 + index]).start()

    for index in range(gtok_own.shape[0] - 1):
        pl.when(step == index + 1)(functools.partial(send_block, index))

    masks = head_masks()
    first_image = place.half * (bucket_ref.shape[1] // 2)
    normed_one, factor_one = norm_rows(tok_own[own_block(step, rows)].astype(F32))
    hidden_one_t = (normed_one * vec_ref[0:1] + vec_ref[1:2]).astype(BF16).T
    grad_resid = gres_ref[...]
    resid_low = grad_resid.astype(BF16)
    grad_hidden_one = None
    for half in range(2):
        base = half * 3 * SLOT
        grad_heads = mm(resid_low, wt_ref[half, :, AT_OUT:AT_VEC], NN).astype(BF16)
        parts = []
        for image in range(pack):
            span = slice(image * SEQ, (image + 1) * SEQ)
            used = used_lanes(bucket_ref, heads_ref, first_image + step * pack + image, half).astype(BF16)
            heads = grad_heads[span] * used
            queries, keys, values = (
                proj_ref[span, base + which * SLOT : base + (which + 1) * SLOT] for which in range(3)
            )
            sums = [None, None, None]
            for s in range(3):
                own = heads * masks[s]
                low = low_ref[(image * 2 + half) * 3 + s]
                grad_probs = mm(own, values, NT)
                probs = low.astype(F32)
                weighed = probs * grad_probs
                grad_scores = (weighed - probs * lane_sum(weighed)).astype(BF16)
                terms = (
                    mm(grad_scores, keys * masks[s], NN),
                    mm(grad_scores, queries * masks[s], TN),
                    mm(low, own, TN),
                )
                sums = [t if o is None else o + t for o, t in zip(sums, terms)]
            parts.append([(v * c).astype(BF16) for v, c in zip(sums, (0.125, 0.125, 1.0))])
            if image == 0:
                slot(2 * half)
        for which in range(3):
            lanes = slice(which * SLOT, (which + 1) * SLOT)
            grad_proj = jnp.concatenate([part[which] for part in parts], axis=0)
            acc_ref[half, :, lanes] += mm(hidden_one_t, grad_proj, NN)
            term = mm(grad_proj, wt_ref[half, :, lanes], NT)
            grad_hidden_one = term if grad_hidden_one is None else grad_hidden_one + term
        if half == 0:
            slot(1)

    gtok_own[step] = grad_resid + norm_back(grad_hidden_one * vec_ref[0:1], normed_one, factor_one)
    sums_ref[0:1] += jnp.sum(grad_hidden_one * normed_one, axis=0, keepdims=True)
    sums_ref[1:2] += jnp.sum(grad_hidden_one, axis=0, keepdims=True)

    slot(3)

    @pl.when(step == steps - 1)
    def _():
        columns = sums_ref[...].T[:, 0 : LATE - TAIL].astype(BF16)
        ranks, own = at_parts.shape[1], at_parts.shape[2]
        for half in range(2):
            for which in range(3):
                piece = acc_ref[half, :, which * SLOT : which * SLOT + HEADS].astype(BF16)
                at_parts[half, :, :, which * HEADS : (which + 1) * HEADS] = piece.reshape(ranks, own, HEADS)
            at_parts[half, :, :, TAIL:LATE] = columns.reshape(ranks, own, LATE - TAIL)
        at_sum.start()
        at_sum.first_hop()
        send_block(gtok_own.shape[0] - 1)
        mom_at[...] = jnp.zeros(mom_at.shape, F32)
        for which in range(3):
            mom_at[:, which * HEADS : (which + 1) * HEADS] = 0.95 * qkv_ref[which]
        at_sum.second_hop()
        at_sum.last_hop(grad_at)
        spread_units()
        at_sum.finish(grad_at)
        mom_at[:, 0:TAIL] = mom_at[:, 0:TAIL] + grad_at[:, 0:TAIL]
        own_at[:, 0:TAIL] = mom_at[:, 0:TAIL].astype(BF16)
        lanes = lax.broadcasted_iota(jnp.int32, (own, LATE - TAIL), 1)
        tile = jnp.zeros(lanes.shape, F32)
        pieces = (
            grad_at[:, 0:TAIL], grad_fc[:, FC:EARLY], grad_fc[:, 0 : FC // 2],
            grad_fc[:, FC // 2 : FC], grad_at[:, TAIL:LATE],
        )
        for number, piece in enumerate(pieces):
            square = jnp.sum(lane_sum(piece * piece), axis=0, keepdims=True)
            square = jnp.broadcast_to(square * (0.5 if number == 4 else 1.0), lanes.shape)
            high = square.astype(BF16).astype(F32)
            tile = jnp.where(lanes == number, high, tile)
            tile = jnp.where(lanes == 32 + number, square - high, tile)
        own_at[:, TAIL:LATE] = tile.astype(BF16)
        at_home.start()
        at_all.start_column()
        at_all.start_plane()
        at_all.plane(0)
        at_all.columns()
        part_units()
        at_all.planes()
        at_all.corners()
        fc_all.share()
        at_all.finish()
        fc_all.finish()
        side.arrived(0, out_half)
        side.left(0, out_half)
        for index in range(gtok_own.shape[0]):
            side.arrived(1 + index, gtok_own.at[0])
            side.left(1 + index, gtok_own.at[0])
            pltpu.make_async_copy(gtok_own.at[index], own_rows(index), local_sems.at[3 + index]).wait()
        at_home.wait()


def back_pass(bucket, heads, tokens, gres, proj, low, wt, vec, gvec, fc_parts, moms, out_half):
    count, model = gres.shape
    rows = fc_parts.shape[3]
    ranks = fc_parts.shape[1] * fc_parts.shape[2]
    block = PAIR * SEQ
    steps = count // block

    def by_step(lanes):
        return pl.BlockSpec((block, lanes), lambda i: (i, 0))

    anywhere = pl.BlockSpec(memory_space=pl.ANY)
    return pl.pallas_call(
        back_kernel,
        out_shape=(
            jax.ShapeDtypeStruct((2 * count, model), F32),
            jax.ShapeDtypeStruct((2, rows, EARLY + LATE), F32),
            jax.ShapeDtypeStruct(fc_parts.shape, BF16),
            jax.ShapeDtypeStruct((2, ranks, rows, LATE), BF16),
            jax.ShapeDtypeStruct((count, model), F32),
        ),
        grid_spec=pltpu.PrefetchScalarGridSpec(
            num_scalar_prefetch=0,
            grid=(steps,),
            in_specs=[
                once(bucket.shape),
                once(heads.shape),
                anywhere,
                by_step(model),
                by_step(6 * SLOT),
                pl.BlockSpec((PAIR * 6, SEQ, SEQ), lambda i: (i, 0, 0)),
                once(wt.shape),
                once(vec.shape),
                once(gvec.shape),
                once(fc_parts.shape),
            ]
            + [once(m.shape) for m in moms]
            + [anywhere],
            out_specs=[
                anywhere,
                once((2, rows, EARLY + LATE)),
                anywhere,
                anywhere,
                anywhere,
            ],
            scratch_shapes=[
                pltpu.VMEM((2, model, AT_OUT), F32),
                pltpu.VMEM((128, model), F32),
                pltpu.VMEM((steps, block, model), F32),
                pltpu.VMEM((2, ranks, rows, LATE), BF16),
                pltpu.VMEM((rows, EARLY), BF16),
                pltpu.VMEM((rows, LATE), BF16),
                pltpu.VMEM((count, model), BF16),
            ]
            + wide_scratch(rows, EARLY, EARLY_CUT)
            + scatter_scratch(ranks, rows, LATE, LATE_CUT)
            + dma(WideScatter.SLOTS)
            + dma(SCATTER_SLOTS)
            + dma(WideGather.SLOTS)
            + dma(GATHER_SLOTS)
            + dma(1 + steps)
            + [pltpu.SemaphoreType.DMA((3 + steps,))],
        ),
        compiler_params=pltpu.CompilerParams(
            collective_id=1, has_side_effects=True, vmem_limit_bytes=60 * 1024 * 1024
        ),
        name="back_pass",
    )(bucket, heads, tokens, gres, proj, low, wt, vec, gvec, fc_parts, *moms, out_half)


QUINTIC = (3.4445, -4.775, 2.0315)
RATES = (2.0, 2.0, math.sqrt(3.0), math.sqrt(32.0))
RANGES = ((0, FC // 2), (FC // 2, FC), (0, LATE), (FC, EARLY))
IN_LATE = 2


def mm3(a, b):
    return lax.dot_general(a, b, NN, precision=lax.Precision.HIGH, preferred_element_type=F32)


def eye_mask(n):
    return lax.broadcasted_iota(jnp.int32, (n, n), 0) == lax.broadcasted_iota(jnp.int32, (n, n), 1)


def chain_kernel(
    fc_ref, at_ref, pairs_ref, vec_ref, first_ref, second_ref,
    fc1_ref, fc2_ref, qkv_ref, wo_ref, out_half, out_other, gtok_both,
    root_ref, norm_ref, gfc1, gfc2, gqkv, gwo, gvec, mfc1, mfc2, mqkv, mwo,
    vec_new, first_new, second_new, kept_fc, kept_at, half_fc, half_at, out_ref, gtok_ref,
    gram_ref, poly_ref, rows_ref, turn_ref, out_hold, gtok_hold, sems,
):
    place = Place()
    count = out_half.shape[0]
    early, late = pl.ds(0, EARLY), pl.ds(EARLY, LATE)
    grad_fc, mom_fc = pairs_ref.at[0, :, early], pairs_ref.at[1, :, early]
    grad_at, mom_at = pairs_ref.at[0, :, late], pairs_ref.at[1, :, late]
    half = place.half
    which = 2 * place.x + half
    sources = ((out_half, out_hold.at[0]), (out_other, out_hold.at[1]), (gtok_both, gtok_hold))
    loads = [pltpu.make_async_copy(src, hold, sems.at[i]) for i, (src, hold) in enumerate(sources)]
    stores = []
    for i, part in enumerate((half, 1 - half)):
        rows = pl.ds(pl.multiple_of(part * count, 8), count)
        stores.append(pltpu.make_async_copy(out_hold.at[i], out_ref.at[rows], sems.at[3 + i]))
    stores.append(pltpu.make_async_copy(gtok_hold, gtok_ref, sems.at[5]))
    for load in loads:
        load.start()
    model = fc_ref.shape[1]
    for number, (start, stop) in enumerate(RANGES):
        buf = at_ref if number == IN_LATE else fc_ref

        @pl.when(which == number)
        def _():
            lower, upper = buf[0, :, start:stop], buf[1, :, start:stop]
            if number == IN_LATE:
                keep = (lax.broadcasted_iota(jnp.int32, (1, LATE), 1) < TAIL).astype(F32).astype(BF16)
                lower, upper = lower * keep, upper * keep
            gram_ref[...] = mm(lower, lower, NT) + mm(upper, upper, NT)

    eye = eye_mask(model)
    gram = gram_ref[...]
    total = jnp.sum(lane_sum(jnp.where(eye, gram, 0.0)), axis=0, keepdims=True)
    scale = 1.0 / (jnp.sqrt(total) + 1e-07)
    gram_ref[...] = gram * (scale * scale)
    a, b, c = QUINTIC

    def polynomial():
        gram = gram_ref[...]
        return jnp.where(eye, a, 0.0) + b * gram + c * mm3(gram, gram)

    def advance(poly):
        gram_ref[...] = mm3(mm3(gram_ref[...], poly), poly)

    poly = polynomial()
    poly_ref[...] = poly
    first_row = (place.dp // 2) * rows_ref.shape[0]
    rows_ref[...] = poly_ref[pl.ds(pl.multiple_of(first_row, 8), rows_ref.shape[0])]
    advance(poly)
    for load, store in zip(loads, stores):
        load.wait()
        store.start()

    def sweep(_, carry):
        poly = polynomial()
        rows_ref[...] = mm3(rows_ref[...], poly)
        advance(poly)
        return carry

    lax.fori_loop(0, NS_ITERS - 2, sweep, 0)
    rows, gram = rows_ref[...], gram_ref[...]
    once_more = mm3(rows, gram)
    last = (a * rows + b * once_more + c * mm3(once_more, gram)) * scale
    for part in range(root_ref.shape[0]):
        root_ref[part] = last[part * root_ref.shape[1] : (part + 1) * root_ref.shape[1]]

    wide = FC // 2
    gfc1[...], gfc2[...] = grad_fc[:, 0:wide], grad_fc[:, wide:FC]
    mfc1[...], mfc2[...] = mom_fc[:, 0:wide], mom_fc[:, wide:FC]
    gwo[...] = grad_fc[:, FC : FC + HEADS]
    mwo[...] = mom_fc[:, FC : FC + HEADS]
    kept_fc[...] = jnp.zeros_like(kept_fc)
    kept_fc[:, 0:wide] = 0.999 * fc1_ref[...]
    kept_fc[:, wide:FC] = 0.999 * fc2_ref[...]
    kept_fc[:, FC : FC + HEADS] = 0.999 * wo_ref[...]
    kept_at[...] = jnp.zeros_like(kept_at)
    half_fc[...] = fc_ref[half]
    half_at[...] = at_ref[half]
    for part in range(3):
        span = slice(part * HEADS, (part + 1) * HEADS)
        gqkv[part] = grad_at[:, span]
        mqkv[part] = mom_at[:, span]
        kept_at[:, span] = 0.999 * qkv_ref[part]
    own = grad_at.shape[0]
    turn_ref[...] = jnp.zeros_like(turn_ref)
    turn_ref[0:own, 0 : LATE - TAIL] = grad_at[:, TAIL:LATE]
    turned = turn_ref[...].T[0:6, 0 : vec_ref.shape[1]]
    first = 0.9 * first_ref[...] + 0.1 * turned
    second = 0.95 * second_ref[...] + 0.05 * turned * turned
    gvec[...] = turned
    first_new[...] = first
    second_new[...] = second
    vec_new[...] = vec_ref[...] - 0.5 * (first / (1.0 - 0.9**STEP)) / (
        jnp.sqrt(second / (1.0 - 0.95**STEP)) + 1e-08
    )
    tiles = at_ref[0, :, LATE - 128 : LATE].astype(F32) + at_ref[1, :, LATE - 128 : LATE].astype(F32)
    leads = lax.broadcasted_iota(jnp.int32, tiles.shape, 0) % own == 0
    squares = jnp.sum(jnp.where(leads, tiles, 0.0), axis=0, keepdims=True)
    squares = pltpu.roll(squares, 64, 1)
    norm_ref[...] = jnp.sqrt(jnp.abs(squares + pltpu.roll(squares, 96, 1)))[:, 0:5]
    for store in stores:
        store.wait()


def run_chain(fc_buf, at_buf, pairs, vectors, first, second, weights, wholes):
    model = fc_buf.shape[1]
    own, columns = pairs.shape[1], vectors.shape[1]
    count = wholes[0].shape[0]
    full = (2 * count, model)
    vmem = pl.BlockSpec(memory_space=pltpu.VMEM)
    anywhere = pl.BlockSpec(memory_space=pl.ANY)
    shapes = [(own, 768), (own, 768), (3, own, 192), (own, 192)]
    outs = [(2, own, model), (1, 5)] + shapes + [(6, columns)] + shapes + [(6, columns)] * 3
    lows = [(model, EARLY), (model, LATE)]
    outs += [(own, EARLY), (own, LATE)] + lows + [full] * 2
    return pl.pallas_call(
        chain_kernel,
        out_shape=tuple(jax.ShapeDtypeStruct(shape, BF16 if shape in lows else F32) for shape in outs),
        in_specs=[vmem] * 10 + [anywhere] * 3,
        out_specs=tuple([vmem] * (len(outs) - 2) + [anywhere] * 2),
        scratch_shapes=[
            pltpu.VMEM((model, model), F32),
            pltpu.VMEM((model, model), F32),
            pltpu.VMEM((2 * own, model), F32),
            pltpu.VMEM((128, 128), F32),
            pltpu.VMEM((2, count, model), F32),
            pltpu.VMEM(full, F32),
            pltpu.SemaphoreType.DMA((6,)),
        ],
        compiler_params=pltpu.CompilerParams(vmem_limit_bytes=44 * 1024 * 1024),
        name="run_chain",
    )(fc_buf, at_buf, pairs, vectors, first, second, *weights, *wholes)


def roots_kernel(
    root_ref, kept_fc, kept_at, fc_own, at_own,
    nfc1, nfc2, nqkv, nwo, rows_ref, send_sem, recv_sem,
):
    place = Place()
    x, half = place.x, place.half
    barrier = pltpu.get_barrier_semaphore()
    peers = [(1 - x, half), (x, 1 - half), (1 - x, 1 - half)]
    ids = [(place.index(place.z, place.y, px), ph) for px, ph in peers]
    for peer in ids:
        pl.semaphore_signal(barrier, inc=1, device_id=peer, device_id_type=MESH)
    pl.semaphore_wait(barrier, 3)
    mail = Mail(place, send_sem, recv_sem)
    mine = 2 * x + half
    for slot, peer in enumerate(ids):
        mail.start(slot, root_ref.at[peers[slot][0]], rows_ref.at[mine], peer)
    rows_ref[mine] = root_ref[x]
    for slot in range(3):
        mail.arrived(slot, rows_ref.at[0])
    for number, (start, stop) in enumerate(RANGES):
        rows = rows_ref[number]
        high = rows.astype(BF16)
        low = (rows - high.astype(F32)).astype(BF16)
        late = number == IN_LATE
        moment = (at_own if late else fc_own)[:, start:stop]
        step = RATES[number] * (mm(high, moment, NN) + mm(low, moment, NN))
        new = (kept_at if late else kept_fc)[:, start:stop] - step
        if late:
            for part in range(3):
                nqkv[part] = new[:, part * HEADS : (part + 1) * HEADS]
        else:
            out = (nfc1, nfc2, None, nwo)[number]
            out[...] = new[:, 0 : out.shape[1]]
    for slot in range(3):
        mail.left(slot, rows_ref.at[0])


def apply_roots(root, kept_fc, kept_at, half_fc, half_at, weights):
    _, rows, model = root.shape
    vmem = pl.BlockSpec(memory_space=pltpu.VMEM)
    return pl.pallas_call(
        roots_kernel,
        out_shape=tuple(jax.ShapeDtypeStruct(w.shape, F32) for w in weights),
        in_specs=[vmem] * 5,
        out_specs=(vmem,) * 4,
        scratch_shapes=[
            pltpu.VMEM((4, rows, model), F32),
        ]
        + dma(3),
        compiler_params=pltpu.CompilerParams(
            collective_id=2, has_side_effects=True, vmem_limit_bytes=32 * 1024 * 1024
        ),
        name="apply_roots",
    )(root, kept_fc, kept_at, half_fc, half_at)


def flat(part):
    return part.T if part.ndim == 2 else jnp.transpose(part, (0, 2, 1))


def pack(fc1, fc2, qkv, out):
    pad = ((0, 0), (0, SLOT - out.shape[1]))
    return jnp.concatenate([fc1, fc2] + [jnp.pad(part, pad) for part in (*qkv, out)], axis=1)


def unpack(packed, like):
    fc1, fc2, qkv, out = like
    split = jnp.stack([packed[:, QKV + part * SLOT :][:, : qkv.shape[2]] for part in range(3)])
    return packed[:, FC1:FC2], packed[:, FC2:QKV], split, packed[:, OUT : OUT + out.shape[1]]


def root_of(gram):
    a, b, c = QUINTIC
    eye = eye_mask(gram.shape[0])
    scale = 1.0 / (jnp.sqrt(jnp.sum(jnp.where(eye, gram, 0.0))) + 1e-07)
    gram = gram * (scale * scale)
    root = jnp.where(eye, scale, 0.0)
    for _ in range(NS_ITERS):
        poly = jnp.where(eye, a, 0.0) + b * gram + c * mm3(gram, gram)
        root = mm3(root, poly)
        gram = mm3(mm3(gram, poly), poly)
    return root


def general(half, bucket, widths, counts, tokens, cotangent, weights, moms, vectors, vec_first, vec_second):
    dp = lax.axis_index("dp")
    rows = weights[0].shape[0]
    vec = jnp.pad(vectors.T, ((0, 0), (0, PACK - VEC - vectors.shape[0])))
    own = jnp.concatenate([pack(*weights), vec], axis=1).astype(BF16)
    packed = lax.all_gather(lax.all_gather(own, "dp", axis=0, tiled=True), "mlp")
    out_half, gtok_half, grads = image_pass(half.reshape(1), bucket, widths, counts, tokens, cotangent, packed)
    output = lax.all_gather(out_half, "mlp", axis=0, tiled=True)
    gtok = lax.all_gather(gtok_half, "mlp", axis=0, tiled=True)
    grad = lax.psum_scatter(grads.astype(F32), "mlp", scatter_dimension=0)
    grad = lax.psum_scatter(grad, "dp", scatter_dimension=0, tiled=True)
    mom = 0.95 * pack(*moms) + grad[:, 0:VEC]
    spans = ((FC1, FC2), (FC2, QKV), (QKV, OUT), (OUT, VEC))
    squares = [jnp.sum(jnp.square(grad[:, start:stop])) for start, stop in spans[2:] + spans[:2]]
    squares.append(0.5 * jnp.sum(jnp.square(grad[:, VEC:PACK])))
    norms = jnp.sqrt(lax.psum(jnp.stack(squares), ("dp", "mlp")))
    buf = lax.all_gather(lax.all_gather(mom.astype(BF16), "dp", axis=0, tiled=True), "mlp")
    ours = lax.dynamic_index_in_dim(buf, half, 0, keepdims=False)
    steps = []
    for (start, stop), rate in zip(spans, RATES):
        root = root_of(sum(mm(buf[h, :, start:stop], buf[h, :, start:stop], NT) for h in range(2)))
        root = lax.dynamic_slice_in_dim(root, dp * rows, rows, 0)
        high = root.astype(BF16)
        low = (root - high.astype(F32)).astype(BF16)
        steps.append(rate * (mm(high, ours[:, start:stop], NN) + mm(low, ours[:, start:stop], NN)))
    moved = unpack(jnp.concatenate(steps, axis=1), weights)
    gvec = grad[:, VEC : VEC + vectors.shape[0]].T
    first = 0.9 * vec_first + 0.1 * gvec
    second = 0.95 * vec_second + 0.05 * gvec * gvec
    vec_new = vectors - 0.5 * (first / (1.0 - 0.9**STEP)) / (
        jnp.sqrt(second / (1.0 - 0.95**STEP)) + 1e-08
    )

    def ordered(parts):
        fc1, fc2, qkv, out = parts
        return flat(qkv), flat(out), flat(fc1), flat(fc2)

    news = [0.999 * w - move for w, move in zip(weights, moved)]
    return (
        output, gtok, *ordered(unpack(grad, weights)), gvec,
        *ordered(unpack(mom, weights)), *ordered(news), vec_new, first, second, norms,
    )


def body(
    tokens, cotangent, image_bucket, bucket_width, bucket_heads,
    w_qkv, w_out, w_fc1, w_fc2, vectors,
    mom_qkv, mom_out, mom_fc1, mom_fc2, vec_first, vec_second,
):
    half = lax.axis_index("mlp").astype(jnp.int32)
    ranks = lax.axis_size("dp")
    model = tokens.shape[1]
    rows = w_fc1.shape[1]
    weights = [flat(w) for w in (w_fc1, w_fc2, w_qkv, w_out)]
    moms = [flat(m) for m in (mom_fc1, mom_fc2, mom_qkv, mom_out)]
    images = image_bucket.shape[0] // 2
    if ranks != 16 or images != 4 * PAIR:
        return general(
            half, image_bucket, bucket_width, bucket_heads, tokens, cotangent,
            weights, moms, vectors, vec_first, vec_second,
        )
    bucket, heads = image_bucket.reshape(1, -1), bucket_heads.reshape(1, -1)
    resid, proj, low, mixed, wt, vec_rows, fc_weights = attend_pass(bucket, heads, tokens, weights, vectors, ranks)
    out_half, gres, fc_parts, gvec_rows = units_pass(
        half.reshape(1), image_bucket, bucket_width, resid, cotangent, mixed,
        fc_weights.reshape(2, model, FC), vec_rows,
    )
    gtok_both, pairs, fc_buf, at_buf, out_other = back_pass(
        bucket, heads, tokens, gres, proj, low, wt, vec_rows, gvec_rows,
        fc_parts.reshape(2, 4, 4, rows, EARLY), moms, out_half,
    )
    fc_buf, at_buf = fc_buf.reshape(2, model, EARLY), at_buf.reshape(2, model, LATE)
    (
        root, norms, gfc1, gfc2, gqkv, gwo, gvec, mfc1, mfc2, mqkv, mwo,
        vec_new, first, second, kept_fc, kept_at, half_fc, half_at, output, gtok,
    ) = run_chain(
        fc_buf, at_buf, pairs, vectors, vec_first, vec_second,
        weights, (out_half, out_other, gtok_both),
    )
    nfc1, nfc2, nqkv, nwo = apply_roots(root, kept_fc, kept_at, half_fc, half_at, weights)
    return (
        output, gtok,
        flat(gqkv), flat(gwo), flat(gfc1), flat(gfc2), gvec,
        flat(mqkv), flat(mwo), flat(mfc1), flat(mfc2),
        flat(nqkv), flat(nwo), flat(nfc1), flat(nfc2),
        vec_new, first, second, norms.reshape(5),
    )


def solution(mesh):
    halves, columns = P("mlp", "dp"), P(None, "dp")
    blocks = P(None, "mlp", "dp")
    matrices = (blocks, halves, halves, halves)
    placed = (P("dp", None), P("dp", None), P("dp"), P(), P()) + matrices + (columns,) + matrices + (columns, columns)
    outs = (P("dp", None), P("dp", None)) + matrices + (columns,) + matrices + matrices + (columns,) * 3 + (P(),)
    return jax.shard_map(body, mesh=mesh, in_specs=placed, out_specs=outs, check_vma=False)
```
